32 devices in a mesh: loop: 4 (over y, x), bulk: 8 (over z, core).
Axes of the slice: x: 2, y: 2, z: 4, core: 2. Of those that a mesh axis runs over, the one named last changes fastest.
Arguments:
- series: float32 [4224, 3072], P('loop', 'bulk'), may hold values from -64 to 64
Outputs:
- correlation: float32 [4, 1056, 4224], P(None, 'bulk', 'loop')
The draws below stay inside these ranges and needn't reach their ends.
All inputs are finite; a program needn't handle non-finite values.
Results may differ from the reference program's by a relative error of at most 0.0011.
Values may be sent and summed in bfloat16 or wider, within the bound.
A program may use at most 64 MiB of HBM per device.

```python
import jax
import jax.numpy as jnp
from jax import lax

ROWS_DEV = 1056
TIME = 3072
GRAY = 4224
N_LOOP = 4


def draw_series(key, part):
    keys = jax.random.split(key, 3)
    position = (jnp.arange(TIME, dtype=jnp.float32) + 0.5) / TIME
    ramp = (0.5 + position)[None, :]
    drift = jax.random.truncated_normal(keys[1], -3.0, 3.0, (GRAY, 1), jnp.float32)
    scale_row = jnp.exp(jax.random.uniform(keys[0], (GRAY, 1), jnp.float32, 0.0, jnp.log(10.0)))
    noise = jax.random.truncated_normal(keys[2], -4.0, 4.0, (GRAY, TIME), jnp.float32)
    values = scale_row * (drift * ramp + jnp.sqrt(ramp) * noise)
    return jnp.clip(values, -64.0, 64.0)


def setup_inputs(seed: int = 0) -> dict:
    key_of = jax.random.split(jax.random.key(seed), 2)
    series = draw_series(jax.random.fold_in(key_of[1], 71), 0)
    return dict(series=series)


epsilon = 1e-06

def reference(series):
    average = lax.optimization_barrier(jnp.sum(series, axis=1, keepdims=True)) / TIME
    centered = series - average
    variance = lax.optimization_barrier(jnp.sum(centered * centered, axis=1, keepdims=True)) / TIME
    zscore = (centered * lax.rsqrt(variance + epsilon)).astype(jnp.bfloat16)
    gray_blocks = zscore.reshape(N_LOOP, ROWS_DEV, TIME)

    def block_product(gray_block):
        product = lax.dot_general(gray_block, zscore, (((1,), (1,)), ((), ())), preferred_element_type=jnp.float32)
        return product / TIME
    return lax.map(block_product, gray_blocks)
```

```python
import functools
import jax
import jax.numpy as jnp
from jax import lax
from jax.experimental import pallas as pl
from jax.experimental.pallas import tpu as pltpu
from jax.sharding import PartitionSpec as P

epsilon = 1e-06
MESH = pl.DeviceIdType.MESH
NT = (((1,), (1,)), ((), ()))
TN = (((0,), (0,)), ((), ()))


def up_to(value, unit):
    return -(-value // unit) * unit


def largest_tile(rows, limit):
    return max(t for t in range(16, limit + 1, 16) if rows % t == 0)


def kernel(L, B, PIECES, x_hbm, o_ref, zbuf, shr, acc, cols, stats, x_ref,
           z_recv, up_send, down_send, mate_send, shr_recv, shr_send, st_recv, st_send, x_sem):
    R, T = x_hbm.shape
    total = T * B
    Q = B // 2
    share = R // B
    SP = shr.shape[2]
    W = min(up_to(share + 15, 16), R)
    bounds = [up_to(R * i // PIECES, 128) for i in range(PIECES)] + [R]
    tile = largest_tile(R, 128)
    l, b = lax.axis_index("loop"), lax.axis_index("bulk")
    q, c = b // 2, b % 2
    mate = q * 2 + (1 - c)

    barrier = pltpu.get_barrier_semaphore()
    for d in range(1, B):
        pl.semaphore_signal(barrier, inc=1, device_id=(l, lax.rem(b + d, B)), device_id_type=MESH)
    for d in range(1, L):
        pl.semaphore_signal(barrier, inc=1, device_id=(lax.rem(l + d, L), b), device_id_type=MESH)

    def load(i):
        rows = pl.ds(pl.multiple_of(i * tile, tile), tile)
        return pltpu.make_async_copy(x_hbm.at[rows, :], x_ref.at[rows, :], x_sem.at[i])

    @pl.loop(0, R // tile)
    def _(i):
        load(i).start()

    lane = lax.broadcasted_iota(jnp.int32, (tile, 128), 1)

    @pl.loop(0, R // tile)
    def _(i):
        rows = pl.ds(pl.multiple_of(i * tile, tile), tile)
        load(i).wait()
        v = x_ref[rows, :]
        mean = jnp.sum(v, axis=1, keepdims=True) / T
        dev = v - mean
        m2 = jnp.sum(dev * dev, axis=1, keepdims=True)
        cols[rows, :] = jnp.where(lane == 0, mean, jnp.where(lane == 1, m2, 0.0))

    pick = (lax.broadcasted_iota(jnp.int32, (8, 128), 0)
            == lax.broadcasted_iota(jnp.int32, (8, 128), 1)).astype(jnp.float32)
    line = lax.dot_general(pick, cols[...], NT, precision=lax.Precision.HIGHEST,
                           preferred_element_type=jnp.float32)
    stats[b] = line[:2]

    pl.semaphore_wait(barrier, B - 1 + L - 1)

    def stat_copy(source, peer):
        return pltpu.make_async_remote_copy(
            src_ref=stats.at[source], dst_ref=stats.at[source],
            send_sem=st_send.at[peer], recv_sem=st_recv.at[source],
            device_id=(l, peer), device_id_type=MESH)

    for d in range(1, B):
        stat_copy(b, lax.rem(b + d, B)).start()
    for d in range(1, B):
        other = lax.rem(b + d, B)
        stat_copy(other, other).wait_recv()

    mean = stats[0, 0:1]
    for k in range(1, B):
        mean = mean + stats[k, 0:1]
    mean = mean / B
    square = jnp.zeros_like(mean)
    for k in range(B):
        shift = stats[k, 0:1] - mean
        square = square + (stats[k, 1:2] + T * (shift * shift))
    scale = lax.rsqrt(square / total + epsilon)
    sub = lax.broadcasted_iota(jnp.int32, (8, R), 0)
    both = jnp.where(sub == 0, mean, jnp.where(sub == 1, scale, 0.0))
    cols[...] = lax.dot_general(both, pick, TN, precision=lax.Precision.HIGHEST,
                                preferred_element_type=jnp.float32)

    def normalise(piece):
        size = bounds[piece + 1] - bounds[piece]
        step = largest_tile(size, 128)

        @pl.loop(0, size // step)
        def _(i):
            rows = pl.ds(pl.multiple_of(bounds[piece] + i * step, 16), step)
            z = (x_ref[rows, :] - cols[rows, 0:1]) * cols[rows, 1:2]
            zbuf[b, rows, :] = z.astype(jnp.bfloat16)

    def piece_copy(k, piece, send_sem, peer):
        part = zbuf.at[k, pl.ds(bounds[piece], bounds[piece + 1] - bounds[piece]), :]
        return pltpu.make_async_remote_copy(
            src_ref=part, dst_ref=part, send_sem=send_sem.at[k, piece],
            recv_sem=z_recv.at[k, piece], device_id=(l, peer), device_id_type=MESH)

    def share_copy(k, block, peer):
        return pltpu.make_async_remote_copy(
            src_ref=shr.at[k, block], dst_ref=shr.at[k, block], send_sem=shr_send.at[k, peer],
            recv_sem=shr_recv.at[k, block], device_id=(peer, b), device_id_type=MESH)

    has_up, has_down = q + 1 < Q, q >= 1
    start = b * share
    first = pl.multiple_of(jnp.minimum(start // 16 * 16, R - W), 16)
    need_below = PIECES - 1 - sum((first >= x).astype(jnp.int32) for x in bounds[1:-1])
    need_above = sum((first + W > x).astype(jnp.int32) for x in bounds[1:-1])

    def extract(k):
        window = zbuf[k, pl.ds(first, W), :]
        hot = (lax.broadcasted_iota(jnp.int32, (SP, W), 1)
               == lax.broadcasted_iota(jnp.int32, (SP, W), 0) + (start - first))
        inside = lax.broadcasted_iota(jnp.int32, (SP, W), 0) < share
        hot = jnp.where(hot & inside, 1.0, 0.0).astype(jnp.bfloat16)
        rows = lax.dot_general(hot, window, (((1,), (0,)), ((), ())),
                               preferred_element_type=jnp.float32)
        shr[k, l] = rows.astype(jnp.bfloat16)
        for d in range(1, L):
            share_copy(k, l, lax.rem(l + d, L)).start()

    def wait_shares(place):
        for core in range(2):
            k = place * 2 + core
            for d in range(1, L):
                other = lax.rem(l + d, L)
                share_copy(k, other, other).wait_recv()

    def multiply(place):
        part = None
        wait_shares(place)
        for core in range(2):
            k = place * 2 + core
            a = shr[k].reshape(L * SP, T)
            term = lax.dot_general(a, zbuf[k], NT, preferred_element_type=jnp.float32)
            part = term if part is None else part + term
        acc[...] += part

    def multiply_step(s):
        @pl.loop(0, 2)
        def _(n):
            place = q - (1 - 2 * n) * s

            @pl.when((place >= 0) & (place < Q) & ((s > 0) | (n < 1)))
            def _():
                multiply(place)

    def send_own(up_first):
        done = set()

        def send(up, i):
            piece = PIECES - 1 - i if up else i
            if piece not in done:
                done.add(piece)
                normalise(piece)

            @pl.when(has_up if up else has_down)
            def _():
                if up:
                    piece_copy(b, piece, up_send, b + 2).start()
                else:
                    piece_copy(b, piece, down_send, b - 2).start()

        for i in range(PIECES):
            send(up_first, i)
            send(not up_first, i)

    @pl.when(q >= Q // 2)
    def _():
        send_own(True)

    @pl.when(q < Q // 2)
    def _():
        send_own(False)

    for i in range(PIECES):
        piece_copy(b, i, mate_send, mate).start()

    acc[...] = jnp.zeros_like(acc)
    extract(b)

    for i in range(PIECES):
        piece_copy(mate, i, mate_send, mate).wait_recv()

    extract(mate)

    def arrive(s, i, between=None):
        below, above = b - 2 * s, b + 2 * s
        from_below, from_above = q - s >= 0, q + s < Q
        down_piece = PIECES - 1 - i

        @pl.when(from_below)
        def _():
            piece_copy(below, down_piece, up_send, b).wait_recv()

            @pl.when(has_up)
            def _():
                piece_copy(below, down_piece, up_send, b + 2).start()
            piece_copy(below, down_piece, mate_send, mate).start()

        @pl.when(from_above)
        def _():
            piece_copy(above, i, down_send, b).wait_recv()

            @pl.when(has_down)
            def _():
                piece_copy(above, i, down_send, b - 2).start()
            piece_copy(above, i, mate_send, mate).start()

        @pl.when(from_below & (i == need_below))
        def _():
            extract(below)

        @pl.when(from_above & (i == need_above))
        def _():
            extract(above)

        if between is not None:
            between()

        @pl.when(from_below)
        def _():
            piece_copy(mate - 2 * s, down_piece, mate_send, mate).wait_recv()

            @pl.when(i == need_below)
            def _():
                extract(mate - 2 * s)

        @pl.when(from_above)
        def _():
            piece_copy(mate + 2 * s, i, mate_send, mate).wait_recv()

            @pl.when(i == need_above)
            def _():
                extract(mate + 2 * s)

        if i == 0:
            multiply_step(s - 1)

    def finish(piece, place):
        lo, hi = bounds[piece], bounds[piece + 1]
        part = acc[:, lo:hi]
        if place is not None:
            for core in range(2):
                k = place * 2 + core
                a = shr[k].reshape(L * SP, T)
                part = part + lax.dot_general(a, zbuf[k, lo:hi, :], NT,
                                              preferred_element_type=jnp.float32)
        part = part / total
        for j in range(L):
            o_ref[:, j, lo:hi] = part[j * SP:j * SP + share]

    @pl.loop(1, Q - 1)
    def _(s):
        for i in range(PIECES):
            arrive(s, i)

    def finish_ends(steps):
        for end, place in ((Q - 1, 0), (0, Q - 1)):
            @pl.when(q == end)
            def _():
                for i in steps:
                    finish(PIECES - 1 - i if end else i, place)

    def finish_early():
        for end, place in ((Q - 1, 0), (0, Q - 1)):
            @pl.when(q == end)
            def _():
                wait_shares(place)

        finish_ends(range(PIECES - 1))

    for i in range(PIECES):
        arrive(Q - 1, i, finish_early if i == PIECES - 1 else None)
    finish_ends([PIECES - 1])

    @pl.when((q > 0) & (q < Q - 1))
    def _():
        for i in range(PIECES):
            finish(i, None)

    for d in range(1, B):
        other = lax.rem(b + d, B)
        stat_copy(b, other).wait_send()

    @pl.loop(0, Q)
    def _(s):
        below, above = b - 2 * s, b + 2 * s
        from_below, from_above = q - s >= 0, q + s < Q

        for i in range(PIECES):
            @pl.when(from_below & has_up)
            def _():
                piece_copy(below, i, up_send, b + 2).wait_send()

            @pl.when(from_above & has_down)
            def _():
                piece_copy(above, i, down_send, b - 2).wait_send()

            @pl.when(from_below)
            def _():
                piece_copy(below, i, mate_send, mate).wait_send()

            @pl.when(from_above & (s > 0))
            def _():
                piece_copy(above, i, mate_send, mate).wait_send()

    @pl.loop(0, B)
    def _(k):
        for d in range(1, L):
            other = lax.rem(l + d, L)
            share_copy(k, l, other).wait_send()


D, S, A2, A1 = range(4)


def line_kernel(L, B, x_hbm, o_ref, zbuf, shr, acc_t, acc_r, tile_send, tile_recv, cols, stats, x_ref,
                z_recv, out_send, in_send, mate_send, shr_recv, shr_send, diag_recv, t_recv, t_send,
                st_recv, st_send, x_sem):
    R, T = x_hbm.shape
    total = T * B
    share = R // B
    half = 2 * share
    SP = shr.shape[2]
    pad = share - 128
    W = min(up_to(share + 15, 16), R)
    skip_lo, skip_hi = up_to(R // 2 + pad, 16), (3 * half - pad) // 16 * 16
    middle = up_to(skip_lo // 2, 16)
    up_start = {D: skip_hi, S: skip_lo, A2: middle, A1: 0}
    size = {D: R - skip_hi, S: skip_hi - skip_lo, A2: skip_lo - middle, A1: middle}
    tile = largest_tile(R, 128)
    NTL, NR = acc_t.shape[1], acc_r.shape[1]
    l, b = lax.axis_index("loop"), lax.axis_index("bulk")
    q, c = b // 2, b % 2
    mate = q * 2 + (1 - c)
    upper = q >= 2
    inner = (q == 1) | (q == 2)
    outer = (q == 0) | (q == 3)
    step = jnp.where(upper, 1, -1)
    H = [jnp.where(upper, h, 3 - h) for h in range(4)]
    out_nbr, in_nbr = b + 2 * step, b - 2 * step
    lx, ly, ld = l + 1 - 2 * (l % 2), lax.rem(l + 2, 4), 3 - l

    def align(value, unit=16):
        return pl.multiple_of(value, unit)

    down_start = {p: R - up_start[p] - size[p] for p in up_start}
    so = {p: align(jnp.where(upper, up_start[p], down_start[p])) for p in up_start}
    si = {p: align(jnp.where(upper, down_start[p], up_start[p])) for p in up_start}
    start_t = align(jnp.where(upper, R - NTL, 0), 128)
    start_r = align(jnp.where(upper, 0, R - NR), 128)

    barrier = pltpu.get_barrier_semaphore()
    for d in range(1, B):
        pl.semaphore_signal(barrier, inc=1, device_id=(l, lax.rem(b + d, B)), device_id_type=MESH)
    facing = jnp.where(inner, H[3], H[2])
    for d in range(1, L):
        other = lax.rem(l + d, L)
        pl.semaphore_signal(barrier, inc=1, device_id=(other, b), device_id_type=MESH)
        for core in range(2):
            pl.semaphore_signal(barrier, inc=1, device_id=(other, facing * 2 + core), device_id_type=MESH)

    def load(i):
        rows = pl.ds(pl.multiple_of(i * tile, tile), tile)
        return pltpu.make_async_copy(x_hbm.at[rows, :], x_ref.at[rows, :], x_sem.at[i])

    @pl.loop(0, R // tile)
    def _(i):
        load(i).start()

    lane = lax.broadcasted_iota(jnp.int32, (tile, 128), 1)

    @pl.loop(0, R // tile)
    def _(i):
        rows = pl.ds(pl.multiple_of(i * tile, tile), tile)
        load(i).wait()
        v = x_ref[rows, :]
        mean = jnp.sum(v, axis=1, keepdims=True) / T
        dev = v - mean
        m2 = jnp.sum(dev * dev, axis=1, keepdims=True)
        cols[rows, :] = jnp.where(lane == 0, mean, jnp.where(lane == 1, m2, 0.0))

    pick = (lax.broadcasted_iota(jnp.int32, (8, 128), 0)
            == lax.broadcasted_iota(jnp.int32, (8, 128), 1)).astype(jnp.float32)
    line = lax.dot_general(pick, cols[...], NT, precision=lax.Precision.HIGHEST,
                           preferred_element_type=jnp.float32)
    stats[b] = line[:2]

    pl.semaphore_wait(barrier, B - 1 + 3 * (L - 1))

    def stat_copy(source, peer):
        return pltpu.make_async_remote_copy(
            src_ref=stats.at[source], dst_ref=stats.at[source],
            send_sem=st_send.at[peer], recv_sem=st_recv.at[source],
            device_id=(l, peer), device_id_type=MESH)

    for d in range(1, B):
        stat_copy(b, lax.rem(b + d, B)).start()
    for d in range(1, B):
        other = lax.rem(b + d, B)
        stat_copy(other, other).wait_recv()

    mean = stats[0, 0:1]
    for k in range(1, B):
        mean = mean + stats[k, 0:1]
    mean = mean / B
    square = jnp.zeros_like(mean)
    for k in range(B):
        shift = stats[k, 0:1] - mean
        square = square + (stats[k, 1:2] + T * (shift * shift))
    scale = lax.rsqrt(square / total + epsilon)
    sub = lax.broadcasted_iota(jnp.int32, (8, R), 0)
    both = jnp.where(sub == 0, mean, jnp.where(sub == 1, scale, 0.0))
    cols[...] = lax.dot_general(both, pick, TN, precision=lax.Precision.HIGHEST,
                                preferred_element_type=jnp.float32)

    def normalise(start, rows_all):
        unit = largest_tile(rows_all, 128)

        @pl.loop(0, rows_all // unit)
        def _(i):
            rows = pl.ds(pl.multiple_of(start + i * unit, 16), unit)
            z = (x_ref[rows, :] - cols[rows, 0:1]) * cols[rows, 1:2]
            zbuf[b, rows, :] = z.astype(jnp.bfloat16)

    def z_copy(k, start, p, send_sem, peer, rows=None):
        part = zbuf.at[k, pl.ds(start, size[p] if rows is None else rows), :]
        return pltpu.make_async_remote_copy(
            src_ref=part, dst_ref=part, send_sem=send_sem.at[k, p],
            recv_sem=z_recv.at[k, p], device_id=(l, peer), device_id_type=MESH)

    def send_out(k, p):
        return z_copy(k, so[p], p, out_send, out_nbr)

    def send_in(k, p):
        return z_copy(k, si[p], p, in_send, in_nbr)

    def mate_copy(k, p, start):
        return z_copy(k, start[p], p, mate_send, mate)

    def mate_own(k):
        return z_copy(k, 0, 0, mate_send, mate, R)

    def share_copy(k, block, peer, way):
        return pltpu.make_async_remote_copy(
            src_ref=shr.at[k, block], dst_ref=shr.at[k, block], send_sem=shr_send.at[k, way],
            recv_sem=shr_recv.at[k, way], device_id=(peer, b), device_id_type=MESH)

    cut = up_to(SP // 2, 16)

    def diag_copy(k, block, peer, way):
        rows = pl.ds(0, cut) if way == 0 else pl.ds(cut, SP - cut)
        part = shr.at[k, block, rows, :]
        return pltpu.make_async_remote_copy(
            src_ref=part, dst_ref=part, send_sem=shr_send.at[k, 2 + way],
            recv_sem=diag_recv.at[k, way], device_id=(peer, b), device_id_type=MESH)

    first = align(jnp.minimum(b * share // 16 * 16, jnp.where(q == 0, size[D], R) - W))

    def extract(place):
        @pl.loop(0, 2)
        def _(core):
            k = place * 2 + core
            window = zbuf[k, pl.ds(first, W), :]
            row = lax.broadcasted_iota(jnp.int32, (SP, W), 0)
            hot = lax.broadcasted_iota(jnp.int32, (SP, W), 1) == row + (b * share - first)
            hot = jnp.where(hot & (row < share), 1.0, 0.0).astype(jnp.bfloat16)
            rows = lax.dot_general(hot, window, (((1,), (0,)), ((), ())),
                                   preferred_element_type=jnp.float32)
            shr[k, l] = rows.astype(jnp.bfloat16)
            share_copy(k, l, lx, 0).start()
            share_copy(k, l, ly, 1).start()

    def pass_on(place):
        @pl.loop(0, 2)
        def _(core):
            k = place * 2 + core
            share_copy(k, lx, lx, 0).wait_recv()
            diag_copy(k, lx, ly, 0).start()
            share_copy(k, ly, ly, 1).wait_recv()
            diag_copy(k, ly, lx, 1).start()

    def wait_diag(place):
        @pl.loop(0, 2)
        def _(core):
            k = place * 2 + core
            for way in range(2):
                diag_copy(k, ld, ld, way).wait_recv()

    def product(place, start, width):
        part = None
        for core in range(2):
            k = place * 2 + core
            term = lax.dot_general(shr[k].reshape(L * SP, T), zbuf[k, pl.ds(start, width), :], NT,
                                   preferred_element_type=jnp.float32)
            part = term if part is None else part + term
        return part

    def own(h):
        return H[h] * 2 + c

    def other(h):
        return H[h] * 2 + (1 - c)

    def take(h, p, start, onward=None):
        z_copy(own(h), start[p], p, mate_send, mate).wait_recv()
        if onward is not None:
            onward(own(h), p).start()
        mate_copy(own(h), p, start).start()

    def mate_take(h, pieces, start):
        for p in pieces:
            mate_copy(other(h), p, start).wait_recv()

    normalise(so[D], size[D])

    @pl.when(inner)
    def _():
        send_out(b, D).start()
    normalise(align(jnp.where(upper, 0, size[D])), R - size[D])

    @pl.when(inner)
    def _():
        for p in (D, S, A2):
            send_in(b, p).start()
        for p in (A2, A1):
            send_out(b, p).start()

    @pl.when(outer)
    def _():
        for p in (D, S, A2, A1):
            send_in(b, p).start()
    mate_own(b).start()
    mate_own(mate).wait_recv()
    extract(q)

    @pl.when(inner)
    def _():
        take(1, D, so, send_out)
        take(3, D, si, send_in)
        pass_on(q)
        take(1, S, so)
        take(3, S, si, send_in)
        take(1, A2, so, send_out)
        take(3, A2, si, send_in)
        send_in(b, A1).start()
        mate_take(1, (D, S, A2), so)
        extract(H[1])

    @pl.when(outer)
    def _():
        take(2, D, so)
        mate_take(2, (D,), so)
        extract(H[2])
        pass_on(q)
        take(2, A2, so)
        take(2, A1, so)
        mate_take(2, (A2, A1), so)
    wait_diag(q)
    acc_t[...] = product(q, start_t, NTL)
    acc_r[...] = product(q, start_r, NR)

    @pl.when(inner)
    def _():
        take(0, D, so, send_out)
        take(3, A1, si, send_in)
        mate_take(3, (D, S, A2, A1), si)
        extract(H[3])
        pass_on(H[1])
        take(0, S, so)
        take(0, A2, so, send_out)
        mate_take(0, (D, S, A2), so)
        extract(H[0])
        pass_on(H[3])

    @pl.when(outer)
    def _():
        pass_on(H[2])
        take(1, D, so)
        mate_take(1, (D,), so)
        extract(H[1])
        take(1, A2, so)
        pass_on(H[1])
        take(0, D, so)
        mate_take(0, (D,), so)
        extract(H[0])
    second, third = jnp.where(inner, H[1], H[2]), jnp.where(inner, H[3], H[1])
    wait_diag(second)
    acc_t[...] += product(second, start_t, NTL)

    @pl.when(inner)
    def _():
        take(1, A1, so, send_out)
        mate_take(1, (A1,), so)

    @pl.when(outer)
    def _():
        take(0, A2, so)
        pass_on(H[0])
        take(1, A1, so)
        mate_take(1, (A2, A1), so)
    acc_r[...] += product(second, start_r, NR)
    wait_diag(third)
    acc_t[...] += product(third, start_t, NTL)
    acc_r[...] += product(third, start_r, NR)

    @pl.when(inner)
    def _():
        pass_on(H[0])
        take(0, A1, so, send_out)

    @pl.when(outer)
    def _():
        take(0, A1, so)
        mate_take(0, (A2, A1), so)
    wait_diag(H[0])
    acc_t[...] += product(H[0], start_t, NTL)

    def tile_copy(j, core, block, slot):
        return pltpu.make_async_remote_copy(
            src_ref=tile_send.at[j, pl.ds(core * SP, SP), :],
            dst_ref=tile_recv.at[block, :, pl.ds(pl.multiple_of(slot * 128, 128), 128)],
            send_sem=t_send.at[j, core], recv_sem=t_recv.at[block, slot],
            device_id=(j, H[3] * 2 + core), device_id_type=MESH)

    @pl.when(inner)
    def _():
        value = (acc_t[...] / total).astype(jnp.bfloat16)
        row = lax.broadcasted_iota(jnp.int32, (2 * SP, NTL), 0)
        lower = row < SP
        want = jnp.where(lower, row, row - SP + share) + jnp.where(upper, NTL - half, 0)
        keep = jnp.where(lower, row, row - SP) < share
        hot = (lax.broadcasted_iota(jnp.int32, (2 * SP, NTL), 1) == want) & keep
        hot = jnp.where(hot, 1.0, 0.0).astype(jnp.bfloat16)
        picked = lax.dot_general(value, hot, NT, preferred_element_type=jnp.float32)
        picked = picked.astype(jnp.bfloat16)
        shift = (lax.broadcasted_iota(jnp.int32, (SP, 128), 0)
                 == lax.broadcasted_iota(jnp.int32, (SP, 128), 1) + jnp.where(c == 0, pad, 0))
        shift = jnp.where(shift, 1.0, 0.0).astype(jnp.bfloat16)
        for j in range(L):
            turned = lax.dot_general(picked[j * SP:(j + 1) * SP], shift, TN,
                                     preferred_element_type=jnp.float32)
            tile_send[j] = turned.astype(jnp.bfloat16)
        for d in (1, 2, 3, 0):
            for core in range(2):
                tile_copy(lax.rem(l + d, L), core, l, c).start()
        mate_take(0, (A1,), so)
    acc_r[...] += product(H[0], start_r, NR)

    def put(j, lo, hi, part):
        o_ref[:, j, lo:hi] = part

    def near(ref, j, lo, hi):
        return ref[j * SP:j * SP + share, lo:hi] / total

    t_lo, r_lo = R - NTL, R - NR
    @pl.when(upper)
    def _():
        for j in range(L):
            put(j, 0, t_lo, near(acc_r, j, 0, t_lo))
            put(j, t_lo, R, near(acc_t, j, 0, NTL))

    @pl.when(q < 2)
    def _():
        for j in range(L):
            put(j, 0, r_lo, near(acc_t, j, 0, r_lo))
            put(j, r_lo, R, near(acc_r, j, 0, NR))

    @pl.when(outer)
    def _():
        from_up, from_down = R // 2 + pad, half + pad
        base_up, base_down = from_up // 128 * 128, from_down // 128 * 128
        width = up_to(max(from_up - base_up, from_down - base_down) + 256, 128)
        offset = jnp.where(upper, from_up - base_up, from_down - base_down)
        hot = (lax.broadcasted_iota(jnp.int32, (256, width), 1)
               == lax.broadcasted_iota(jnp.int32, (256, width), 0) + offset)
        hot = jnp.where(hot, 1.0, 0.0).astype(jnp.bfloat16)
        place = lax.broadcasted_iota(jnp.int32, (share, width), 1)
        inside = (place >= offset) & (place < offset + 256)
        for d in range(L):
            for slot in range(2):
                tile_copy(l, 0, d, slot).wait_recv()
            placed = lax.dot_general(tile_recv[d], hot, (((1,), (0,)), ((), ())),
                                     preferred_element_type=jnp.float32)[:share]
            for side, lo in ((3, base_up), (0, base_down)):
                @pl.when(q == side)
                def _():
                    o_ref[:, d, lo:lo + width] = jnp.where(inside, placed, o_ref[:, d, lo:lo + width])

    for d in range(1, B):
        stat_copy(b, lax.rem(b + d, B)).wait_send()
    mate_own(b).wait_send()

    @pl.when(inner)
    def _():
        for h in (2, 1, 0):
            for p in (D, A2, A1):
                send_out(own(h), p).wait_send()
        for h in (2, 3):
            for p in (D, S, A2, A1):
                send_in(own(h), p).wait_send()
        for h, start in ((1, so), (0, so), (3, si)):
            for p in (D, S, A2, A1):
                mate_copy(own(h), p, start).wait_send()
        for j in range(L):
            for core in range(2):
                tile_copy(j, core, l, c).wait_send()

    @pl.when(outer)
    def _():
        for p in (D, S, A2, A1):
            send_in(b, p).wait_send()
        for h in (2, 1, 0):
            for p in (D, A2, A1):
                mate_copy(own(h), p, so).wait_send()

    @pl.loop(0, B)
    def _(k):
        share_copy(k, l, lx, 0).wait_send()
        share_copy(k, l, ly, 1).wait_send()
        diag_copy(k, lx, ly, 0).wait_send()
        diag_copy(k, ly, lx, 1).wait_send()


def line_call(L, B, series):
    R, T = series.shape
    share = R // B
    SP = up_to(share, 16)
    pad = share - 128
    skip_hi = (3 * 2 * share - pad) // 16 * 16
    t_lo = skip_hi // 128 * 128
    r_lo = (R - t_lo) // 128 * 128
    vmem = pl.BlockSpec(memory_space=pltpu.VMEM)
    dma = pltpu.SemaphoreType.DMA
    return pl.pallas_call(
        functools.partial(line_kernel, L, B),
        out_shape=jax.ShapeDtypeStruct((share, L, R), jnp.float32),
        in_specs=[pl.BlockSpec(memory_space=pltpu.HBM)],
        out_specs=vmem,
        scratch_shapes=[
            pltpu.VMEM((B, R, T), jnp.bfloat16),
            pltpu.VMEM((B, L, SP, T), jnp.bfloat16),
            pltpu.VMEM((L * SP, R - t_lo), jnp.float32),
            pltpu.VMEM((L * SP, R - r_lo), jnp.float32),
            pltpu.VMEM((L, 2 * SP, 128), jnp.bfloat16),
            pltpu.VMEM((L, SP, 256), jnp.bfloat16),
            pltpu.VMEM((R, 128), jnp.float32),
            pltpu.VMEM((B, 2, R), jnp.float32),
            pltpu.VMEM((R, T), jnp.float32),
            dma((B, 4)), dma((B, 4)), dma((B, 4)), dma((B, 4)),
            dma((B, 2)), dma((B, 4)), dma((B, 2)), dma((L, 2)), dma((L, 2)),
            dma((B,)), dma((B,)), dma((R // largest_tile(R, 128),)),
        ],
        compiler_params=pltpu.CompilerParams(
            collective_id=0, has_side_effects=True, vmem_limit_bytes=34 * 1024 * 1024),
    )(pltpu.with_memory_space_constraint(series, pltpu.HBM)).transpose(1, 0, 2)


def solution(mesh):
    L, B = mesh.shape["loop"], mesh.shape["bulk"]

    def on_device(series):
        R, T = series.shape
        share = R // B
        if L == 4 and B == 8 and R % 16 == 0 and T % 128 == 0 and 128 <= share <= 144:
            return line_call(L, B, series)
        SP = up_to(share, 16)
        pieces = 3
        vmem = pl.BlockSpec(memory_space=pltpu.VMEM)
        dma = pltpu.SemaphoreType.DMA
        return pl.pallas_call(
            functools.partial(kernel, L, B, pieces),
            out_shape=jax.ShapeDtypeStruct((share, L, R), jnp.float32),
            in_specs=[pl.BlockSpec(memory_space=pltpu.HBM)],
            out_specs=vmem,
            scratch_shapes=[
                pltpu.VMEM((B, R, T), jnp.bfloat16),
                pltpu.VMEM((B, L, SP, T), jnp.bfloat16),
                pltpu.VMEM((L * SP, R), jnp.float32),
                pltpu.VMEM((R, 128), jnp.float32),
                pltpu.VMEM((B, 2, R), jnp.float32),
                pltpu.VMEM((R, T), jnp.float32),
                dma((B, pieces)), dma((B, pieces)), dma((B, pieces)), dma((B, pieces)),
                dma((B, L)), dma((B, L)), dma((B,)), dma((B,)), dma((R // largest_tile(R, 128),)),
            ],
            compiler_params=pltpu.CompilerParams(
                collective_id=0, has_side_effects=True, vmem_limit_bytes=26 * 1024 * 1024),
        )(pltpu.with_memory_space_constraint(series, pltpu.HBM)).transpose(1, 0, 2)

    return jax.shard_map(
        on_device, mesh=mesh, in_specs=(P("loop", "bulk"),),
        out_specs=P(None, "bulk", "loop"), check_vma=False)
```

```python
import functools
import jax
import jax.numpy as jnp
from jax import lax
from jax.experimental import pallas as pl
from jax.experimental.pallas import tpu as pltpu
from jax.sharding import PartitionSpec as P

epsilon = 1e-06
MESH = pl.DeviceIdType.MESH
NT = (((1,), (1,)), ((), ()))
TN = (((0,), (0,)), ((), ()))


def up_to(value, unit):
    return -(-value // unit) * unit


def largest_tile(rows, limit):
    return max(t for t in range(16, limit + 1, 16) if rows % t == 0)


def kernel(L, B, PIECES, x_hbm, o_ref, zbuf, shr, acc, cols, stats, x_ref,
           z_recv, up_send, down_send, mate_send, shr_recv, shr_send, st_recv, st_send, x_sem):
    R, T = x_hbm.shape
    total = T * B
    Q = B // 2
    share = R // B
    SP = shr.shape[2]
    W = min(up_to(share + 15, 16), R)
    bounds = [up_to(R * i // PIECES, 128) for i in range(PIECES)] + [R]
    tile = largest_tile(R, 128)
    l, b = lax.axis_index("loop"), lax.axis_index("bulk")
    q, c = b // 2, b % 2
    mate = q * 2 + (1 - c)

    barrier = pltpu.get_barrier_semaphore()
    for d in range(1, B):
        pl.semaphore_signal(barrier, inc=1, device_id=(l, lax.rem(b + d, B)), device_id_type=MESH)
    for d in range(1, L):
        pl.semaphore_signal(barrier, inc=1, device_id=(lax.rem(l + d, L), b), device_id_type=MESH)

    def load(i):
        rows = pl.ds(pl.multiple_of(i * tile, tile), tile)
        return pltpu.make_async_copy(x_hbm.at[rows, :], x_ref.at[rows, :], x_sem.at[i])

    @pl.loop(0, R // tile)
    def _(i):
        load(i).start()

    lane = lax.broadcasted_iota(jnp.int32, (tile, 128), 1)

    @pl.loop(0, R // tile)
    def _(i):
        rows = pl.ds(pl.multiple_of(i * tile, tile), tile)
        load(i).wait()
        v = x_ref[rows, :]
        mean = jnp.sum(v, axis=1, keepdims=True) / T
        dev = v - mean
        m2 = jnp.sum(dev * dev, axis=1, keepdims=True)
        cols[rows, :] = jnp.where(lane == 0, mean, jnp.where(lane == 1, m2, 0.0))

    pick = (lax.broadcasted_iota(jnp.int32, (8, 128), 0)
            == lax.broadcasted_iota(jnp.int32, (8, 128), 1)).astype(jnp.float32)
    line = lax.dot_general(pick, cols[...], NT, precision=lax.Precision.HIGHEST,
                           preferred_element_type=jnp.float32)
    stats[b] = line[:2]

    pl.semaphore_wait(barrier, B - 1 + L - 1)

    def stat_copy(source, peer):
        return pltpu.make_async_remote_copy(
            src_ref=stats.at[source], dst_ref=stats.at[source],
            send_sem=st_send.at[peer], recv_sem=st_recv.at[source],
            device_id=(l, peer), device_id_type=MESH)

    for d in range(1, B):
        stat_copy(b, lax.rem(b + d, B)).start()
    for d in range(1, B):
        other = lax.rem(b + d, B)
        stat_copy(other, other).wait_recv()

    mean = stats[0, 0:1]
    for k in range(1, B):
        mean = mean + stats[k, 0:1]
    mean = mean / B
    square = jnp.zeros_like(mean)
    for k in range(B):
        shift = stats[k, 0:1] - mean
        square = square + (stats[k, 1:2] + T * (shift * shift))
    scale = lax.rsqrt(square / total + epsilon)
    sub = lax.broadcasted_iota(jnp.int32, (8, R), 0)
    both = jnp.where(sub == 0, mean, jnp.where(sub == 1, scale, 0.0))
    cols[...] = lax.dot_general(both, pick, TN, precision=lax.Precision.HIGHEST,
                                preferred_element_type=jnp.float32)

    def normalise(piece):
        size = bounds[piece + 1] - bounds[piece]
        step = largest_tile(size, 128)

        @pl.loop(0, size // step)
        def _(i):
            rows = pl.ds(pl.multiple_of(bounds[piece] + i * step, 16), step)
            z = (x_ref[rows, :] - cols[rows, 0:1]) * cols[rows, 1:2]
            zbuf[b, rows, :] = z.astype(jnp.bfloat16)

    def piece_copy(k, piece, send_sem, peer):
        part = zbuf.at[k, pl.ds(bounds[piece], bounds[piece + 1] - bounds[piece]), :]
        return pltpu.make_async_remote_copy(
            src_ref=part, dst_ref=part, send_sem=send_sem.at[k, piece],
            recv_sem=z_recv.at[k, piece], device_id=(l, peer), device_id_type=MESH)

    def share_copy(k, block, peer):
        return pltpu.make_async_remote_copy(
            src_ref=shr.at[k, block], dst_ref=shr.at[k, block], send_sem=shr_send.at[k, peer],
            recv_sem=shr_recv.at[k, block], device_id=(peer, b), device_id_type=MESH)

    has_up, has_down = q + 1 < Q, q >= 1
    start = b * share
    first = pl.multiple_of(jnp.minimum(start // 16 * 16, R - W), 16)
    need_below = PIECES - 1 - sum((first >= x).astype(jnp.int32) for x in bounds[1:-1])
    need_above = sum((first + W > x).astype(jnp.int32) for x in bounds[1:-1])

    def extract(k):
        window = zbuf[k, pl.ds(first, W), :]
        hot = (lax.broadcasted_iota(jnp.int32, (SP, W), 1)
               == lax.broadcasted_iota(jnp.int32, (SP, W), 0) + (start - first))
        inside = lax.broadcasted_iota(jnp.int32, (SP, W), 0) < share
        hot = jnp.where(hot & inside, 1.0, 0.0).astype(jnp.bfloat16)
        rows = lax.dot_general(hot, window, (((1,), (0,)), ((), ())),
                               preferred_element_type=jnp.float32)
        shr[k, l] = rows.astype(jnp.bfloat16)
        for d in range(1, L):
            share_copy(k, l, lax.rem(l + d, L)).start()

    def wait_shares(place):
        for core in range(2):
            k = place * 2 + core
            for d in range(1, L):
                other = lax.rem(l + d, L)
                share_copy(k, other, other).wait_recv()

    def multiply(place):
        part = None
        wait_shares(place)
        for core in range(2):
            k = place * 2 + core
            a = shr[k].reshape(L * SP, T)
            term = lax.dot_general(a, zbuf[k], NT, preferred_element_type=jnp.float32)
            part = term if part is None else part + term
        acc[...] += part

    def multiply_step(s):
        @pl.loop(0, 2)
        def _(n):
            place = q - (1 - 2 * n) * s

            @pl.when((place >= 0) & (place < Q) & ((s > 0) | (n < 1)))
            def _():
                multiply(place)

    def send_own(up_first):
        done = set()

        def send(up, i):
            piece = PIECES - 1 - i if up else i
            if piece not in done:
                done.add(piece)
                normalise(piece)

            @pl.when(has_up if up else has_down)
            def _():
                if up:
                    piece_copy(b, piece, up_send, b + 2).start()
                else:
                    piece_copy(b, piece, down_send, b - 2).start()

        for i in range(PIECES):
            send(up_first, i)
            send(not up_first, i)

    @pl.when(q >= Q // 2)
    def _():
        send_own(True)

    @pl.when(q < Q // 2)
    def _():
        send_own(False)

    for i in range(PIECES):
        piece_copy(b, i, mate_send, mate).start()

    acc[...] = jnp.zeros_like(acc)
    extract(b)

    for i in range(PIECES):
        piece_copy(mate, i, mate_send, mate).wait_recv()

    extract(mate)

    def arrive(s, i, between=None):
        below, above = b - 2 * s, b + 2 * s
        from_below, from_above = q - s >= 0, q + s < Q
        down_piece = PIECES - 1 - i

        @pl.when(from_below)
        def _():
            piece_copy(below, down_piece, up_send, b).wait_recv()

            @pl.when(has_up)
            def _():
                piece_copy(below, down_piece, up_send, b + 2).start()
            piece_copy(below, down_piece, mate_send, mate).start()

        @pl.when(from_above)
        def _():
            piece_copy(above, i, down_send, b).wait_recv()

            @pl.when(has_down)
            def _():
                piece_copy(above, i, down_send, b - 2).start()
            piece_copy(above, i, mate_send, mate).start()

        @pl.when(from_below & (i == need_below))
        def _():
            extract(below)

        @pl.when(from_above & (i == need_above))
        def _():
            extract(above)

        if between is not None:
            between()

        @pl.when(from_below)
        def _():
            piece_copy(mate - 2 * s, down_piece, mate_send, mate).wait_recv()

            @pl.when(i == need_below)
            def _():
                extract(mate - 2 * s)

        @pl.when(from_above)
        def _():
            piece_copy(mate + 2 * s, i, mate_send, mate).wait_recv()

            @pl.when(i == need_above)
            def _():
                extract(mate + 2 * s)

        if i == 0:
            multiply_step(s - 1)

    def finish(piece, place):
        lo, hi = bounds[piece], bounds[piece + 1]
        part = acc[:, lo:hi]
        if place is not None:
            for core in range(2):
                k = place * 2 + core
                a = shr[k].reshape(L * SP, T)
                part = part + lax.dot_general(a, zbuf[k, lo:hi, :], NT,
                                              preferred_element_type=jnp.float32)
        part = part / total
        for j in range(L):
            o_ref[:, j, lo:hi] = part[j * SP:j * SP + share]

    @pl.loop(1, Q - 1)
    def _(s):
        for i in range(PIECES):
            arrive(s, i)

    def finish_ends(steps):
        for end, place in ((Q - 1, 0), (0, Q - 1)):
            @pl.when(q == end)
            def _():
                for i in steps:
                    finish(PIECES - 1 - i if end else i, place)

    def finish_early():
        for end, place in ((Q - 1, 0), (0, Q - 1)):
            @pl.when(q == end)
            def _():
                wait_shares(place)

        finish_ends(range(PIECES - 1))

    for i in range(PIECES):
        arrive(Q - 1, i, finish_early if i == PIECES - 1 else None)
    finish_ends([PIECES - 1])

    @pl.when((q > 0) & (q < Q - 1))
    def _():
        for i in range(PIECES):
            finish(i, None)

    for d in range(1, B):
        other = lax.rem(b + d, B)
        stat_copy(b, other).wait_send()

    @pl.loop(0, Q)
    def _(s):
        below, above = b - 2 * s, b + 2 * s
        from_below, from_above = q - s >= 0, q + s < Q

        for i in range(PIECES):
            @pl.when(from_below & has_up)
            def _():
                piece_copy(below, i, up_send, b + 2).wait_send()

            @pl.when(from_above & has_down)
            def _():
                piece_copy(above, i, down_send, b - 2).wait_send()

            @pl.when(from_below)
            def _():
                piece_copy(below, i, mate_send, mate).wait_send()

            @pl.when(from_above & (s > 0))
            def _():
                piece_copy(above, i, mate_send, mate).wait_send()

    @pl.loop(0, B)
    def _(k):
        for d in range(1, L):
            other = lax.rem(l + d, L)
            share_copy(k, l, other).wait_send()


D, S, A2, A1 = range(4)


def line_kernel(L, B, x_hbm, o_ref, zbuf, shr, acc_t, acc_r, tile_send, tile_recv, hot_ref, shift_ref, cols, stats, x_ref,
                z_recv, out_send, in_send, mate_send, shr_recv, shr_send, diag_recv, t_recv, t_send,
                st_recv, st_send, x_sem):
    R, T = x_hbm.shape
    total = T * B
    share = R // B
    half = 2 * share
    SP = shr.shape[2]
    pad = share - 128
    W = min(up_to(share + 15, 16), R)
    skip_lo, skip_hi = up_to(R // 2 + pad, 16), (3 * half - pad) // 16 * 16
    middle = up_to(skip_lo // 2, 16)
    up_start = {D: skip_hi, S: skip_lo, A2: middle, A1: 0}
    size = {D: R - skip_hi, S: skip_hi - skip_lo, A2: skip_lo - middle, A1: middle}
    tile = largest_tile(R, 128)
    NTL, NR = acc_t.shape[1], acc_r.shape[1]
    l, b = lax.axis_index("loop"), lax.axis_index("bulk")
    q, c = b // 2, b % 2
    mate = q * 2 + (1 - c)
    upper = q >= 2
    inner = (q == 1) | (q == 2)
    outer = (q == 0) | (q == 3)
    step = jnp.where(upper, 1, -1)
    H = [jnp.where(upper, h, 3 - h) for h in range(4)]
    out_nbr, in_nbr = b + 2 * step, b - 2 * step
    lx, ly, ld = l + 1 - 2 * (l % 2), lax.rem(l + 2, 4), 3 - l

    def align(value, unit=16):
        return pl.multiple_of(value, unit)

    down_start = {p: R - up_start[p] - size[p] for p in up_start}
    so = {p: align(jnp.where(upper, up_start[p], down_start[p])) for p in up_start}
    si = {p: align(jnp.where(upper, down_start[p], up_start[p])) for p in up_start}
    start_t = align(jnp.where(upper, R - NTL, 0), 128)
    start_r = align(jnp.where(upper, 0, R - NR), 128)

    barrier = pltpu.get_barrier_semaphore()
    for d in range(1, B):
        pl.semaphore_signal(barrier, inc=1, device_id=(l, lax.rem(b + d, B)), device_id_type=MESH)
    facing = jnp.where(inner, H[3], H[2])
    for d in range(1, L):
        other = lax.rem(l + d, L)
        pl.semaphore_signal(barrier, inc=1, device_id=(other, b), device_id_type=MESH)
        for core in range(2):
            pl.semaphore_signal(barrier, inc=1, device_id=(other, facing * 2 + core), device_id_type=MESH)

    def load(i):
        rows = pl.ds(pl.multiple_of(i * tile, tile), tile)
        return pltpu.make_async_copy(x_hbm.at[rows, :], x_ref.at[rows, :], x_sem.at[i])

    @pl.loop(0, R // tile)
    def _(i):
        load(i).start()

    lane = lax.broadcasted_iota(jnp.int32, (tile, 128), 1)

    @pl.loop(0, R // tile)
    def _(i):
        rows = pl.ds(pl.multiple_of(i * tile, tile), tile)
        load(i).wait()
        v = x_ref[rows, :]
        mean = jnp.sum(v, axis=1, keepdims=True) / T
        dev = v - mean
        m2 = jnp.sum(dev * dev, axis=1, keepdims=True)
        cols[rows, :] = jnp.where(lane == 0, mean, jnp.where(lane == 1, m2, 0.0))

    pick = (lax.broadcasted_iota(jnp.int32, (8, 128), 0)
            == lax.broadcasted_iota(jnp.int32, (8, 128), 1)).astype(jnp.float32)
    line = lax.dot_general(pick, cols[...], NT, precision=lax.Precision.HIGHEST,
                           preferred_element_type=jnp.float32)
    stats[b] = line[:2]

    pl.semaphore_wait(barrier, B - 1 + 3 * (L - 1))

    def stat_copy(source, peer):
        return pltpu.make_async_remote_copy(
            src_ref=stats.at[source], dst_ref=stats.at[source],
            send_sem=st_send.at[peer], recv_sem=st_recv.at[source],
            device_id=(l, peer), device_id_type=MESH)

    for d in range(1, B):
        stat_copy(b, lax.rem(b + d, B)).start()
    for d in range(1, B):
        other = lax.rem(b + d, B)
        stat_copy(other, other).wait_recv()

    mean = stats[0, 0:1]
    for k in range(1, B):
        mean = mean + stats[k, 0:1]
    mean = mean / B
    square = jnp.zeros_like(mean)
    for k in range(B):
        shift = stats[k, 0:1] - mean
        square = square + (stats[k, 1:2] + T * (shift * shift))
    scale = lax.rsqrt(square / total + epsilon)
    sub = lax.broadcasted_iota(jnp.int32, (8, R), 0)
    both = jnp.where(sub == 0, mean, jnp.where(sub == 1, scale, 0.0))
    cols[...] = lax.dot_general(both, pick, TN, precision=lax.Precision.HIGHEST,
                                preferred_element_type=jnp.float32)

    def normalise(start, count):
        unit = count if count <= 288 else largest_tile(count, 128)

        def chunk(i):
            rows = pl.ds(pl.multiple_of(start + i * unit, 16), unit)
            z = (x_ref[rows, :] - cols[rows, 0:1]) * cols[rows, 1:2]
            zbuf[b, rows, :] = z.astype(jnp.bfloat16)

        if unit == count:
            chunk(0)
        else:
            pl.loop(0, count // unit)(chunk)

    def z_copy(k, start, p, send_sem, peer, rows=None):
        part = zbuf.at[k, pl.ds(start, size[p] if rows is None else rows), :]
        return pltpu.make_async_remote_copy(
            src_ref=part, dst_ref=part, send_sem=send_sem.at[k, p],
            recv_sem=z_recv.at[k, p], device_id=(l, peer), device_id_type=MESH)

    def send_out(k, p):
        return z_copy(k, so[p], p, out_send, out_nbr)

    def send_in(k, p):
        return z_copy(k, si[p], p, in_send, in_nbr)

    def mate_copy(k, p, start):
        return z_copy(k, start[p], p, mate_send, mate)

    def mate_own(k):
        return z_copy(k, 0, 0, mate_send, mate, R)

    def share_copy(k, block, peer, way):
        return pltpu.make_async_remote_copy(
            src_ref=shr.at[k, block], dst_ref=shr.at[k, block], send_sem=shr_send.at[k, way],
            recv_sem=shr_recv.at[k, way], device_id=(peer, b), device_id_type=MESH)

    cut = up_to(SP // 2, 16)

    def diag_copy(k, block, peer, way):
        rows = pl.ds(0, cut) if way == 0 else pl.ds(cut, SP - cut)
        part = shr.at[k, block, rows, :]
        return pltpu.make_async_remote_copy(
            src_ref=part, dst_ref=part, send_sem=shr_send.at[k, 2 + way],
            recv_sem=diag_recv.at[k, way], device_id=(peer, b), device_id_type=MESH)

    first = align(jnp.minimum(b * share // 16 * 16, jnp.where(q == 0, size[D], R) - W))

    def extract(place):
        @pl.loop(0, 2)
        def _(core):
            k = place * 2 + core
            window = zbuf[k, pl.ds(first, W), :]
            row = lax.broadcasted_iota(jnp.int32, (SP, W), 0)
            hot = lax.broadcasted_iota(jnp.int32, (SP, W), 1) == row + (b * share - first)
            hot = jnp.where(hot & (row < share), 1.0, 0.0).astype(jnp.bfloat16)
            rows = lax.dot_general(hot, window, (((1,), (0,)), ((), ())),
                                   preferred_element_type=jnp.float32)
            shr[k, l] = rows.astype(jnp.bfloat16)
            share_copy(k, l, lx, 0).start()
            share_copy(k, l, ly, 1).start()

    def pass_on(place):
        @pl.loop(0, 2)
        def _(core):
            k = place * 2 + core
            share_copy(k, lx, lx, 0).wait_recv()
            diag_copy(k, lx, ly, 0).start()
            share_copy(k, ly, ly, 1).wait_recv()
            diag_copy(k, ly, lx, 1).start()

    def wait_diag(place):
        @pl.loop(0, 2)
        def _(core):
            k = place * 2 + core
            for way in range(2):
                diag_copy(k, ld, ld, way).wait_recv()

    def product(place, start, width):
        part = None
        for core in range(2):
            k = place * 2 + core
            term = lax.dot_general(shr[k].reshape(L * SP, T), zbuf[k, pl.ds(start, width), :], NT,
                                   preferred_element_type=jnp.float32)
            part = term if part is None else part + term
        return part

    def own(h):
        return H[h] * 2 + c

    def other(h):
        return H[h] * 2 + (1 - c)

    def take(h, p, start, onward=None):
        z_copy(own(h), start[p], p, mate_send, mate).wait_recv()
        if onward is not None:
            onward(own(h), p).start()
        mate_copy(own(h), p, start).start()

    def mate_take(h, pieces, start):
        for p in pieces:
            mate_copy(other(h), p, start).wait_recv()

    def tile_copy(j, core, block, slot):
        return pltpu.make_async_remote_copy(
            src_ref=tile_send.at[j, pl.ds(core * SP, SP), :],
            dst_ref=tile_recv.at[block, :, pl.ds(pl.multiple_of(slot * 128, 128), 128)],
            send_sem=t_send.at[j, core], recv_sem=t_recv.at[block, slot],
            device_id=(j, H[3] * 2 + core), device_id_type=MESH)

    def make_hot():
        row = lax.broadcasted_iota(jnp.int32, (2 * SP, NTL), 0)
        lower = row < SP
        want = jnp.where(lower, row, row - SP + share) + jnp.where(upper, NTL - half, 0)
        keep = jnp.where(lower, row, row - SP) < share
        hot = (lax.broadcasted_iota(jnp.int32, (2 * SP, NTL), 1) == want) & keep
        hot_ref[...] = jnp.where(hot, 1.0, 0.0).astype(jnp.bfloat16)
        shift = (lax.broadcasted_iota(jnp.int32, (SP, 128), 0)
                 == lax.broadcasted_iota(jnp.int32, (SP, 128), 1) + jnp.where(c == 0, pad, 0))
        shift_ref[...] = jnp.where(shift, 1.0, 0.0).astype(jnp.bfloat16)

    def finish_tile(j):
        rows = pl.ds(pl.multiple_of(j * SP, SP), SP)
        value = acc_t[rows, :]
        for core in range(2):
            k = H[0] * 2 + core
            value = value + lax.dot_general(shr[k, j], zbuf[k, pl.ds(start_t, NTL), :], NT,
                                            preferred_element_type=jnp.float32)
        acc_t[rows, :] = value
        turned = lax.dot_general((value / total).astype(jnp.bfloat16), shift_ref[...], TN,
                                 preferred_element_type=jnp.float32)
        picked = lax.dot_general(hot_ref[...], turned.astype(jnp.bfloat16), (((1,), (0,)), ((), ())),
                                 preferred_element_type=jnp.float32)
        tile_send[j] = picked.astype(jnp.bfloat16)
        for core in range(2):
            tile_copy(j, core, l, c).start()

    normalise(so[D], size[D])

    @pl.when(inner)
    def _():
        send_out(b, D).start()
    normalise(align(jnp.where(upper, 0, size[D])), R - size[D])

    @pl.when(inner)
    def _():
        for p in (D, S, A2):
            send_in(b, p).start()
        for p in (A2, A1):
            send_out(b, p).start()

    @pl.when(outer)
    def _():
        for p in (A2, A1, D, S):
            send_in(b, p).start()
    mate_own(b).start()
    make_hot()
    mate_own(mate).wait_recv()
    extract(q)

    @pl.when(inner)
    def _():
        take(1, D, so, send_out)
        take(3, A2, si, send_in)
        pass_on(q)
        take(1, S, so)
        take(3, A1, si)
        mate_take(3, (A2, A1), si)
        extract(H[3])
        take(1, A2, so, send_out)
        take(3, D, si, send_in)
        mate_take(1, (D, S, A2), so)
        extract(H[1])

    @pl.when(outer)
    def _():
        take(2, D, so)
        mate_take(2, (D,), so)
        extract(H[2])
        pass_on(q)
        take(2, A2, so)
        pass_on(H[2])
        take(2, A1, so)
        mate_take(2, (A2, A1), so)
    wait_diag(q)
    acc_t[...] = product(q, start_t, NTL)
    acc_r[...] = product(q, start_r, NR)

    second, third = jnp.where(inner, H[3], H[2]), H[1]

    @pl.when(inner)
    def _():
        pass_on(H[3])
        take(0, A2, so, send_out)
        take(3, S, si, send_in)
        send_in(b, A1).start()
        send_in(own(3), A1).start()
        mate_take(3, (D, S), si)
        pass_on(H[1])
        take(0, D, so, send_out)

    @pl.when(outer)
    def _():
        take(1, D, so)
        mate_take(1, (D,), so)
        extract(H[1])
    wait_diag(second)
    acc_t[...] += product(second, start_t, NTL)
    acc_r[...] += product(second, start_r, NR)

    @pl.when(inner)
    def _():
        take(0, S, so)
        mate_take(0, (A2, D, S), so)
        extract(H[0])

    @pl.when(outer)
    def _():
        take(1, A2, so)
        pass_on(H[1])
        take(0, A2, so)
        take(0, D, so)
        mate_take(0, (D,), so)
        extract(H[0])
        take(1, A1, so)
        mate_take(1, (A2, A1), so)
    wait_diag(third)
    acc_t[...] += product(third, start_t, NTL)

    @pl.when(inner)
    def _():
        finish_tile(l)
        take(1, A1, so, send_out)
        mate_take(1, (A1,), so)
    acc_r[...] += product(third, start_r, NR)

    @pl.when(inner)
    def _():
        pass_on(H[0])

        @pl.loop(0, 2)
        def _(n):
            finish_tile(jnp.where(n == 0, lx, ly))
        take(0, A1, so, send_out)
        wait_diag(H[0])
        finish_tile(ld)
        mate_take(0, (A1,), so)

    @pl.when(outer)
    def _():
        pass_on(H[0])
        take(0, A1, so)
        mate_take(0, (A2, A1), so)
        wait_diag(H[0])
        acc_t[...] += product(H[0], start_t, NTL)
    acc_r[...] += product(H[0], start_r, NR)

    def put(j, lo, hi, part):
        o_ref[:, j, lo:hi] = part

    def near(ref, j, lo, hi):
        return ref[j * SP:j * SP + share, lo:hi] / total

    t_lo, r_lo = R - NTL, R - NR
    @pl.when(upper)
    def _():
        for j in range(L):
            put(j, 0, t_lo, near(acc_r, j, 0, t_lo))
            put(j, t_lo, R, near(acc_t, j, 0, NTL))

    @pl.when(q < 2)
    def _():
        for j in range(L):
            put(j, 0, r_lo, near(acc_t, j, 0, r_lo))
            put(j, r_lo, R, near(acc_r, j, 0, NR))

    @pl.when(outer)
    def _():
        from_up, from_down = R // 2 + pad, half + pad
        base_up, base_down = from_up // 128 * 128, from_down // 128 * 128
        width = up_to(max(from_up - base_up, from_down - base_down) + 256, 128)
        offset = jnp.where(upper, from_up - base_up, from_down - base_down)
        hot = (lax.broadcasted_iota(jnp.int32, (256, width), 1)
               == lax.broadcasted_iota(jnp.int32, (256, width), 0) + offset)
        hot = jnp.where(hot, 1.0, 0.0).astype(jnp.bfloat16)
        place = lax.broadcasted_iota(jnp.int32, (share, width), 1)
        inside = (place >= offset) & (place < offset + 256)
        for d in (l, lx, ly, ld):
            for slot in range(2):
                tile_copy(l, 0, d, slot).wait_recv()
            placed = lax.dot_general(tile_recv[d], hot, (((1,), (0,)), ((), ())),
                                     preferred_element_type=jnp.float32)[:share]
            for side, lo in ((3, base_up), (0, base_down)):
                @pl.when(q == side)
                def _():
                    o_ref[:, d, lo:lo + width] = jnp.where(inside, placed, o_ref[:, d, lo:lo + width])

    for d in range(1, B):
        stat_copy(b, lax.rem(b + d, B)).wait_send()
    mate_own(b).wait_send()

    @pl.when(inner)
    def _():
        for h in (2, 1, 0):
            for p in (D, A2, A1):
                send_out(own(h), p).wait_send()
        for h in (2, 3):
            for p in (D, S, A2, A1):
                send_in(own(h), p).wait_send()
        for h, start in ((1, so), (0, so), (3, si)):
            for p in (D, S, A2, A1):
                mate_copy(own(h), p, start).wait_send()
        for j in range(L):
            for core in range(2):
                tile_copy(j, core, l, c).wait_send()

    @pl.when(outer)
    def _():
        for p in (D, S, A2, A1):
            send_in(b, p).wait_send()
        for h in (2, 1, 0):
            for p in (D, A2, A1):
                mate_copy(own(h), p, so).wait_send()

    @pl.loop(0, B)
    def _(k):
        share_copy(k, l, lx, 0).wait_send()
        share_copy(k, l, ly, 1).wait_send()
        diag_copy(k, lx, ly, 0).wait_send()
        diag_copy(k, ly, lx, 1).wait_send()


def line_call(L, B, series):
    R, T = series.shape
    share = R // B
    SP = up_to(share, 16)
    pad = share - 128
    skip_hi = (3 * 2 * share - pad) // 16 * 16
    t_lo = skip_hi // 128 * 128
    r_lo = (R - t_lo) // 128 * 128
    vmem = pl.BlockSpec(memory_space=pltpu.VMEM)
    dma = pltpu.SemaphoreType.DMA
    return pl.pallas_call(
        functools.partial(line_kernel, L, B),
        out_shape=jax.ShapeDtypeStruct((share, L, R), jnp.float32),
        in_specs=[pl.BlockSpec(memory_space=pltpu.HBM)],
        out_specs=vmem,
        scratch_shapes=[
            pltpu.VMEM((B, R, T), jnp.bfloat16),
            pltpu.VMEM((B, L, SP, T), jnp.bfloat16),
            pltpu.VMEM((L * SP, R - t_lo), jnp.float32),
            pltpu.VMEM((L * SP, R - r_lo), jnp.float32),
            pltpu.VMEM((L, 2 * SP, 128), jnp.bfloat16),
            pltpu.VMEM((L, SP, 256), jnp.bfloat16),
            pltpu.VMEM((2 * SP, R - t_lo), jnp.bfloat16),
            pltpu.VMEM((SP, 128), jnp.bfloat16),
            pltpu.VMEM((R, 128), jnp.float32),
            pltpu.VMEM((B, 2, R), jnp.float32),
            pltpu.VMEM((R, T), jnp.float32),
            dma((B, 4)), dma((B, 4)), dma((B, 4)), dma((B, 4)),
            dma((B, 2)), dma((B, 4)), dma((B, 2)), dma((L, 2)), dma((L, 2)),
            dma((B,)), dma((B,)), dma((R // largest_tile(R, 128),)),
        ],
        compiler_params=pltpu.CompilerParams(
            collective_id=0, has_side_effects=True, vmem_limit_bytes=34 * 1024 * 1024),
    )(pltpu.with_memory_space_constraint(series, pltpu.HBM)).transpose(1, 0, 2)


def solution(mesh):
    L, B = mesh.shape["loop"], mesh.shape["bulk"]

    def on_device(series):
        R, T = series.shape
        share = R // B
        if L == 4 and B == 8 and R % 16 == 0 and T % 128 == 0 and 128 <= share <= 144:
            return line_call(L, B, series)
        SP = up_to(share, 16)
        pieces = 3
        vmem = pl.BlockSpec(memory_space=pltpu.VMEM)
        dma = pltpu.SemaphoreType.DMA
        return pl.pallas_call(
            functools.partial(kernel, L, B, pieces),
            out_shape=jax.ShapeDtypeStruct((share, L, R), jnp.float32),
            in_specs=[pl.BlockSpec(memory_space=pltpu.HBM)],
            out_specs=vmem,
            scratch_shapes=[
                pltpu.VMEM((B, R, T), jnp.bfloat16),
                pltpu.VMEM((B, L, SP, T), jnp.bfloat16),
                pltpu.VMEM((L * SP, R), jnp.float32),
                pltpu.VMEM((R, 128), jnp.float32),
                pltpu.VMEM((B, 2, R), jnp.float32),
                pltpu.VMEM((R, T), jnp.float32),
                dma((B, pieces)), dma((B, pieces)), dma((B, pieces)), dma((B, pieces)),
                dma((B, L)), dma((B, L)), dma((B,)), dma((B,)), dma((R // largest_tile(R, 128),)),
            ],
            compiler_params=pltpu.CompilerParams(
                collective_id=0, has_side_effects=True, vmem_limit_bytes=26 * 1024 * 1024),
        )(pltpu.with_memory_space_constraint(series, pltpu.HBM)).transpose(1, 0, 2)

    return jax.shard_map(
        on_device, mesh=mesh, in_specs=(P("loop", "bulk"),),
        out_specs=P(None, "bulk", "loop"), check_vma=False)
```

```python
import functools
import jax
import jax.numpy as jnp
from jax import lax
from jax.experimental import pallas as pl
from jax.experimental.pallas import tpu as pltpu
from jax.sharding import PartitionSpec as P

epsilon = 1e-06
MESH = pl.DeviceIdType.MESH
NT = (((1,), (1,)), ((), ()))
TN = (((0,), (0,)), ((), ()))


def up_to(value, unit):
    return -(-value // unit) * unit


def largest_tile(rows, limit):
    return max(t for t in range(16, limit + 1, 16) if rows % t == 0)


def kernel(L, B, PIECES, x_hbm, o_ref, zbuf, shr, acc, cols, stats, x_ref,
           z_recv, up_send, down_send, mate_send, shr_recv, shr_send, st_recv, st_send, x_sem):
    R, T = x_hbm.shape
    total = T * B
    Q = B // 2
    share = R // B
    SP = shr.shape[2]
    W = min(up_to(share + 15, 16), R)
    bounds = [up_to(R * i // PIECES, 128) for i in range(PIECES)] + [R]
    tile = largest_tile(R, 128)
    l, b = lax.axis_index("loop"), lax.axis_index("bulk")
    q, c = b // 2, b % 2
    mate = q * 2 + (1 - c)

    barrier = pltpu.get_barrier_semaphore()
    for d in range(1, B):
        pl.semaphore_signal(barrier, inc=1, device_id=(l, lax.rem(b + d, B)), device_id_type=MESH)
    for d in range(1, L):
        pl.semaphore_signal(barrier, inc=1, device_id=(lax.rem(l + d, L), b), device_id_type=MESH)

    def load(i):
        rows = pl.ds(pl.multiple_of(i * tile, tile), tile)
        return pltpu.make_async_copy(x_hbm.at[rows, :], x_ref.at[rows, :], x_sem.at[i])

    @pl.loop(0, R // tile)
    def _(i):
        load(i).start()

    lane = lax.broadcasted_iota(jnp.int32, (tile, 128), 1)

    @pl.loop(0, R // tile)
    def _(i):
        rows = pl.ds(pl.multiple_of(i * tile, tile), tile)
        load(i).wait()
        v = x_ref[rows, :]
        mean = jnp.sum(v, axis=1, keepdims=True) / T
        dev = v - mean
        m2 = jnp.sum(dev * dev, axis=1, keepdims=True)
        cols[rows, :] = jnp.where(lane == 0, mean, jnp.where(lane == 1, m2, 0.0))

    pick = (lax.broadcasted_iota(jnp.int32, (8, 128), 0)
            == lax.broadcasted_iota(jnp.int32, (8, 128), 1)).astype(jnp.float32)
    line = lax.dot_general(pick, cols[...], NT, precision=lax.Precision.HIGHEST,
                           preferred_element_type=jnp.float32)
    stats[b] = line[:2]

    pl.semaphore_wait(barrier, B - 1 + L - 1)

    def stat_copy(source, peer):
        return pltpu.make_async_remote_copy(
            src_ref=stats.at[source], dst_ref=stats.at[source],
            send_sem=st_send.at[peer], recv_sem=st_recv.at[source],
            device_id=(l, peer), device_id_type=MESH)

    for d in range(1, B):
        stat_copy(b, lax.rem(b + d, B)).start()
    for d in range(1, B):
        other = lax.rem(b + d, B)
        stat_copy(other, other).wait_recv()

    mean = stats[0, 0:1]
    for k in range(1, B):
        mean = mean + stats[k, 0:1]
    mean = mean / B
    square = jnp.zeros_like(mean)
    for k in range(B):
        shift = stats[k, 0:1] - mean
        square = square + (stats[k, 1:2] + T * (shift * shift))
    scale = lax.rsqrt(square / total + epsilon)
    sub = lax.broadcasted_iota(jnp.int32, (8, R), 0)
    both = jnp.where(sub == 0, mean, jnp.where(sub == 1, scale, 0.0))
    cols[...] = lax.dot_general(both, pick, TN, precision=lax.Precision.HIGHEST,
                                preferred_element_type=jnp.float32)

    def normalise(piece):
        size = bounds[piece + 1] - bounds[piece]
        step = largest_tile(size, 128)

        @pl.loop(0, size // step)
        def _(i):
            rows = pl.ds(pl.multiple_of(bounds[piece] + i * step, 16), step)
            z = (x_ref[rows, :] - cols[rows, 0:1]) * cols[rows, 1:2]
            zbuf[b, rows, :] = z.astype(jnp.bfloat16)

    def piece_copy(k, piece, send_sem, peer):
        part = zbuf.at[k, pl.ds(bounds[piece], bounds[piece + 1] - bounds[piece]), :]
        return pltpu.make_async_remote_copy(
            src_ref=part, dst_ref=part, send_sem=send_sem.at[k, piece],
            recv_sem=z_recv.at[k, piece], device_id=(l, peer), device_id_type=MESH)

    def share_copy(k, block, peer):
        return pltpu.make_async_remote_copy(
            src_ref=shr.at[k, block], dst_ref=shr.at[k, block], send_sem=shr_send.at[k, peer],
            recv_sem=shr_recv.at[k, block], device_id=(peer, b), device_id_type=MESH)

    has_up, has_down = q + 1 < Q, q >= 1
    start = b * share
    first = pl.multiple_of(jnp.minimum(start // 16 * 16, R - W), 16)
    need_below = PIECES - 1 - sum((first >= x).astype(jnp.int32) for x in bounds[1:-1])
    need_above = sum((first + W > x).astype(jnp.int32) for x in bounds[1:-1])

    def extract(k):
        window = zbuf[k, pl.ds(first, W), :]
        hot = (lax.broadcasted_iota(jnp.int32, (SP, W), 1)
               == lax.broadcasted_iota(jnp.int32, (SP, W), 0) + (start - first))
        inside = lax.broadcasted_iota(jnp.int32, (SP, W), 0) < share
        hot = jnp.where(hot & inside, 1.0, 0.0).astype(jnp.bfloat16)
        rows = lax.dot_general(hot, window, (((1,), (0,)), ((), ())),
                               preferred_element_type=jnp.float32)
        shr[k, l] = rows.astype(jnp.bfloat16)
        for d in range(1, L):
            share_copy(k, l, lax.rem(l + d, L)).start()

    def wait_shares(place):
        for core in range(2):
            k = place * 2 + core
            for d in range(1, L):
                other = lax.rem(l + d, L)
                share_copy(k, other, other).wait_recv()

    def multiply(place):
        part = None
        wait_shares(place)
        for core in range(2):
            k = place * 2 + core
            a = shr[k].reshape(L * SP, T)
            term = lax.dot_general(a, zbuf[k], NT, preferred_element_type=jnp.float32)
            part = term if part is None else part + term
        acc[...] += part

    def multiply_step(s):
        @pl.loop(0, 2)
        def _(n):
            place = q - (1 - 2 * n) * s

            @pl.when((place >= 0) & (place < Q) & ((s > 0) | (n < 1)))
            def _():
                multiply(place)

    def send_own(up_first):
        done = set()

        def send(up, i):
            piece = PIECES - 1 - i if up else i
            if piece not in done:
                done.add(piece)
                normalise(piece)

            @pl.when(has_up if up else has_down)
            def _():
                if up:
                    piece_copy(b, piece, up_send, b + 2).start()
                else:
                    piece_copy(b, piece, down_send, b - 2).start()

        for i in range(PIECES):
            send(up_first, i)
            send(not up_first, i)

    @pl.when(q >= Q // 2)
    def _():
        send_own(True)

    @pl.when(q < Q // 2)
    def _():
        send_own(False)

    for i in range(PIECES):
        piece_copy(b, i, mate_send, mate).start()

    acc[...] = jnp.zeros_like(acc)
    extract(b)

    for i in range(PIECES):
        piece_copy(mate, i, mate_send, mate).wait_recv()

    extract(mate)

    def arrive(s, i, between=None):
        below, above = b - 2 * s, b + 2 * s
        from_below, from_above = q - s >= 0, q + s < Q
        down_piece = PIECES - 1 - i

        @pl.when(from_below)
        def _():
            piece_copy(below, down_piece, up_send, b).wait_recv()

            @pl.when(has_up)
            def _():
                piece_copy(below, down_piece, up_send, b + 2).start()
            piece_copy(below, down_piece, mate_send, mate).start()

        @pl.when(from_above)
        def _():
            piece_copy(above, i, down_send, b).wait_recv()

            @pl.when(has_down)
            def _():
                piece_copy(above, i, down_send, b - 2).start()
            piece_copy(above, i, mate_send, mate).start()

        @pl.when(from_below & (i == need_below))
        def _():
            extract(below)

        @pl.when(from_above & (i == need_above))
        def _():
            extract(above)

        if between is not None:
            between()

        @pl.when(from_below)
        def _():
            piece_copy(mate - 2 * s, down_piece, mate_send, mate).wait_recv()

            @pl.when(i == need_below)
            def _():
                extract(mate - 2 * s)

        @pl.when(from_above)
        def _():
            piece_copy(mate + 2 * s, i, mate_send, mate).wait_recv()

            @pl.when(i == need_above)
            def _():
                extract(mate + 2 * s)

        if i == 0:
            multiply_step(s - 1)

    def finish(piece, place):
        lo, hi = bounds[piece], bounds[piece + 1]
        part = acc[:, lo:hi]
        if place is not None:
            for core in range(2):
                k = place * 2 + core
                a = shr[k].reshape(L * SP, T)
                part = part + lax.dot_general(a, zbuf[k, lo:hi, :], NT,
                                              preferred_element_type=jnp.float32)
        part = part / total
        for j in range(L):
            o_ref[:, j, lo:hi] = part[j * SP:j * SP + share]

    @pl.loop(1, Q - 1)
    def _(s):
        for i in range(PIECES):
            arrive(s, i)

    def finish_ends(steps):
        for end, place in ((Q - 1, 0), (0, Q - 1)):
            @pl.when(q == end)
            def _():
                for i in steps:
                    finish(PIECES - 1 - i if end else i, place)

    def finish_early():
        for end, place in ((Q - 1, 0), (0, Q - 1)):
            @pl.when(q == end)
            def _():
                wait_shares(place)

        finish_ends(range(PIECES - 1))

    for i in range(PIECES):
        arrive(Q - 1, i, finish_early if i == PIECES - 1 else None)
    finish_ends([PIECES - 1])

    @pl.when((q > 0) & (q < Q - 1))
    def _():
        for i in range(PIECES):
            finish(i, None)

    for d in range(1, B):
        other = lax.rem(b + d, B)
        stat_copy(b, other).wait_send()

    @pl.loop(0, Q)
    def _(s):
        below, above = b - 2 * s, b + 2 * s
        from_below, from_above = q - s >= 0, q + s < Q

        for i in range(PIECES):
            @pl.when(from_below & has_up)
            def _():
                piece_copy(below, i, up_send, b + 2).wait_send()

            @pl.when(from_above & has_down)
            def _():
                piece_copy(above, i, down_send, b - 2).wait_send()

            @pl.when(from_below)
            def _():
                piece_copy(below, i, mate_send, mate).wait_send()

            @pl.when(from_above & (s > 0))
            def _():
                piece_copy(above, i, mate_send, mate).wait_send()

    @pl.loop(0, B)
    def _(k):
        for d in range(1, L):
            other = lax.rem(l + d, L)
            share_copy(k, l, other).wait_send()


D, S, A2, A1 = range(4)


def line_kernel(L, B, x_hbm, o_ref, zbuf, shr, acc_t, acc_r, tile_send, tile_recv, hot_ref, shift_ref, cols, stats, x_ref,
                z_recv, out_send, in_send, mate_send, own_send, shr_recv, shr_send, diag_recv, diag_send, t_recv, t_send,
                st_recv, st_send, x_sem):
    R, T = x_hbm.shape
    total = T * B
    share = R // B
    half = 2 * share
    SP = shr.shape[2]
    pad = share - 128
    W = min(up_to(share + 15, 16), R)
    skip_lo, skip_hi = up_to(R // 2 + pad, 16), (3 * half - pad) // 16 * 16
    middle = up_to(skip_lo // 2, 16)
    up_start = {D: skip_hi, S: skip_lo, A2: middle, A1: 0}
    size = {D: R - skip_hi, S: skip_hi - skip_lo, A2: skip_lo - middle, A1: middle}
    tile = largest_tile(R, 352)
    NTL, NR = acc_t.shape[1], acc_r.shape[1]
    l, b = lax.axis_index("loop"), lax.axis_index("bulk")
    q, c = b // 2, b % 2
    mate = q * 2 + (1 - c)
    upper = q >= 2
    inner = (q == 1) | (q == 2)
    outer = (q == 0) | (q == 3)
    step = jnp.where(upper, 1, -1)
    H = [jnp.where(upper, h, 3 - h) for h in range(4)]
    out_nbr, in_nbr = b + 2 * step, b - 2 * step
    lx, ly, ld = l + 1 - 2 * (l % 2), lax.rem(l + 2, 4), 3 - l

    def align(value, unit=16):
        return pl.multiple_of(value, unit)

    down_start = {p: R - up_start[p] - size[p] for p in up_start}
    so = {p: align(jnp.where(upper, up_start[p], down_start[p])) for p in up_start}
    si = {p: align(jnp.where(upper, down_start[p], up_start[p])) for p in up_start}
    start_t = align(jnp.where(upper, R - NTL, 0), 128)
    start_r = align(jnp.where(upper, 0, R - NR), 128)

    barrier = pltpu.get_barrier_semaphore()
    for d in range(1, B):
        pl.semaphore_signal(barrier, inc=1, device_id=(l, lax.rem(b + d, B)), device_id_type=MESH)
    facing = jnp.where(inner, H[3], H[2])
    for d in range(1, L):
        other = lax.rem(l + d, L)
        pl.semaphore_signal(barrier, inc=1, device_id=(other, b), device_id_type=MESH)
        for core in range(2):
            pl.semaphore_signal(barrier, inc=1, device_id=(other, facing * 2 + core), device_id_type=MESH)

    def load(i):
        rows = pl.ds(pl.multiple_of(i * tile, tile), tile)
        return pltpu.make_async_copy(x_hbm.at[rows, :], x_ref.at[rows, :], x_sem.at[i])

    @pl.loop(0, R // tile)
    def _(i):
        load(i).start()

    lane = lax.broadcasted_iota(jnp.int32, (tile, 128), 1)

    @pl.loop(0, R // tile)
    def _(i):
        rows = pl.ds(pl.multiple_of(i * tile, tile), tile)
        load(i).wait()
        v = x_ref[rows, :]
        mean = jnp.sum(v, axis=1, keepdims=True) / T
        dev = v - mean
        m2 = jnp.sum(dev * dev, axis=1, keepdims=True)
        cols[rows, :] = jnp.where(lane == 0, mean, jnp.where(lane == 1, m2, 0.0))

    pick = (lax.broadcasted_iota(jnp.int32, (8, 128), 0)
            == lax.broadcasted_iota(jnp.int32, (8, 128), 1)).astype(jnp.float32)
    line = lax.dot_general(pick, cols[...], NT, precision=lax.Precision.HIGHEST,
                           preferred_element_type=jnp.float32)
    stats[b] = line[:2]

    pl.semaphore_wait(barrier, B - 1 + 3 * (L - 1))

    def stat_copy(source, peer):
        return pltpu.make_async_remote_copy(
            src_ref=stats.at[source], dst_ref=stats.at[source],
            send_sem=st_send, recv_sem=st_recv,
            device_id=(l, peer), device_id_type=MESH)

    for d in range(1, B):
        stat_copy(b, lax.rem(b + d, B)).start()
    gathered = stats.at[pl.ds(0, B - 1)]
    all_stats = pltpu.make_async_remote_copy(
        src_ref=gathered, dst_ref=gathered, send_sem=st_send, recv_sem=st_recv,
        device_id=(l, b), device_id_type=MESH)
    all_stats.wait_recv()

    mean = stats[0, 0:1]
    for k in range(1, B):
        mean = mean + stats[k, 0:1]
    mean = mean / B
    square = jnp.zeros_like(mean)
    for k in range(B):
        shift = stats[k, 0:1] - mean
        square = square + (stats[k, 1:2] + T * (shift * shift))
    scale = lax.rsqrt(square / total + epsilon)
    sub = lax.broadcasted_iota(jnp.int32, (8, R), 0)
    both = jnp.where(sub == 0, mean, jnp.where(sub == 1, scale, 0.0))
    cols[...] = lax.dot_general(both, pick, TN, precision=lax.Precision.HIGHEST,
                                preferred_element_type=jnp.float32)

    def normalise(start, count):
        unit = count if count <= 288 else largest_tile(count, 128)

        def chunk(i):
            rows = pl.ds(pl.multiple_of(start + i * unit, 16), unit)
            z = (x_ref[rows, :] - cols[rows, 0:1]) * cols[rows, 1:2]
            zbuf[b, rows, :] = z.astype(jnp.bfloat16)

        if unit == count:
            chunk(0)
        else:
            pl.loop(0, count // unit)(chunk)

    def z_copy(k, start, p, send_sem, peer, rows=None):
        part = zbuf.at[k, pl.ds(start, size[p] if rows is None else rows), :]
        return pltpu.make_async_remote_copy(
            src_ref=part, dst_ref=part, send_sem=send_sem,
            recv_sem=z_recv.at[k, p], device_id=(l, peer), device_id_type=MESH)

    def send_out(k, p):
        return z_copy(k, so[p], p, out_send, out_nbr)

    def send_in(k, p):
        return z_copy(k, si[p], p, in_send, in_nbr)

    def mate_copy(k, p, start):
        return z_copy(k, start[p], p, mate_send, mate)

    def mate_own(k):
        return z_copy(k, 0, 0, own_send, mate, R)

    def share_copy(k, block, peer, way):
        return pltpu.make_async_remote_copy(
            src_ref=shr.at[k, block], dst_ref=shr.at[k, block], send_sem=shr_send,
            recv_sem=shr_recv.at[k, way], device_id=(peer, b), device_id_type=MESH)

    cut = up_to(SP // 2, 16)

    def diag_copy(k, block, peer, way):
        rows = pl.ds(0, cut) if way == 0 else pl.ds(cut, SP - cut)
        part = shr.at[k, block, rows, :]
        return pltpu.make_async_remote_copy(
            src_ref=part, dst_ref=part, send_sem=diag_send,
            recv_sem=diag_recv.at[k // 2], device_id=(peer, b), device_id_type=MESH)

    first = align(jnp.minimum(b * share // 16 * 16, jnp.where(q == 0, size[D], R) - W))

    def extract(place):
        @pl.loop(0, 2)
        def _(core):
            k = place * 2 + core
            window = zbuf[k, pl.ds(first, W), :]
            row = lax.broadcasted_iota(jnp.int32, (SP, W), 0)
            hot = lax.broadcasted_iota(jnp.int32, (SP, W), 1) == row + (b * share - first)
            hot = jnp.where(hot & (row < share), 1.0, 0.0).astype(jnp.bfloat16)
            rows = lax.dot_general(hot, window, (((1,), (0,)), ((), ())),
                                   preferred_element_type=jnp.float32)
            shr[k, l] = rows.astype(jnp.bfloat16)
            share_copy(k, l, lx, 0).start()
            share_copy(k, l, ly, 1).start()

    def pass_on(place):
        @pl.loop(0, 2)
        def _(core):
            k = place * 2 + core
            share_copy(k, lx, lx, 0).wait_recv()
            diag_copy(k, lx, ly, 0).start()
            share_copy(k, ly, ly, 1).wait_recv()
            diag_copy(k, ly, lx, 1).start()

    def wait_diag(place):
        part = shr.at[pl.ds(place * 2, 2), ld]
        pltpu.make_async_remote_copy(
            src_ref=part, dst_ref=part, send_sem=diag_send, recv_sem=diag_recv.at[place],
            device_id=(l, b), device_id_type=MESH).wait_recv()

    def product(place, start, width):
        part = None
        for core in range(2):
            k = place * 2 + core
            term = lax.dot_general(shr[k].reshape(L * SP, T), zbuf[k, pl.ds(start, width), :], NT,
                                   preferred_element_type=jnp.float32)
            part = term if part is None else part + term
        return part

    def own(h):
        return H[h] * 2 + c

    def other(h):
        return H[h] * 2 + (1 - c)

    def take(h, p, start, onward=None):
        z_copy(own(h), start[p], p, mate_send, mate).wait_recv()
        if onward is not None:
            onward(own(h), p).start()
        mate_copy(own(h), p, start).start()

    def mate_take(h, pieces, start):
        for p in pieces:
            mate_copy(other(h), p, start).wait_recv()

    def tile_copy(j, core, block, slot):
        return pltpu.make_async_remote_copy(
            src_ref=tile_send.at[j, pl.ds(core * SP, SP), :],
            dst_ref=tile_recv.at[block, :, pl.ds(pl.multiple_of(slot * 128, 128), 128)],
            send_sem=t_send, recv_sem=t_recv.at[block],
            device_id=(j, H[3] * 2 + core), device_id_type=MESH)

    def make_hot():
        row = lax.broadcasted_iota(jnp.int32, (2 * SP, NTL), 0)
        lower = row < SP
        want = jnp.where(lower, row, row - SP + share) + jnp.where(upper, NTL - half, 0)
        keep = jnp.where(lower, row, row - SP) < share
        hot = (lax.broadcasted_iota(jnp.int32, (2 * SP, NTL), 1) == want) & keep
        hot_ref[...] = jnp.where(hot, 1.0, 0.0).astype(jnp.bfloat16)
        shift = (lax.broadcasted_iota(jnp.int32, (SP, 128), 0)
                 == lax.broadcasted_iota(jnp.int32, (SP, 128), 1) + jnp.where(c == 0, pad, 0))
        shift_ref[...] = jnp.where(shift, 1.0, 0.0).astype(jnp.bfloat16)

    def finish_tile(j):
        rows = pl.ds(pl.multiple_of(j * SP, SP), SP)
        value = acc_t[rows, :]
        for core in range(2):
            k = H[0] * 2 + core
            value = value + lax.dot_general(shr[k, j], zbuf[k, pl.ds(start_t, NTL), :], NT,
                                            preferred_element_type=jnp.float32)
        acc_t[rows, :] = value
        turned = lax.dot_general((value / total).astype(jnp.bfloat16), shift_ref[...], TN,
                                 preferred_element_type=jnp.float32)
        picked = lax.dot_general(hot_ref[...], turned.astype(jnp.bfloat16), (((1,), (0,)), ((), ())),
                                 preferred_element_type=jnp.float32)
        tile_send[j] = picked.astype(jnp.bfloat16)

    def start_tile(j):
        for core in range(2):
            tile_copy(j, core, l, c).start()

    def wait_tile(block):
        part = tile_recv.at[block]
        pltpu.make_async_remote_copy(
            src_ref=part, dst_ref=part, send_sem=t_send, recv_sem=t_recv.at[block],
            device_id=(l, b), device_id_type=MESH).wait_recv()

    normalise(so[D], size[D])

    @pl.when(inner)
    def _():
        send_out(b, D).start()
    normalise(align(jnp.where(upper, 0, size[D])), R - size[D])

    @pl.when(inner)
    def _():
        for p in (D, S, A2):
            send_in(b, p).start()
        for p in (A2, A1):
            send_out(b, p).start()

    @pl.when(outer)
    def _():
        for p in (A2, A1, D, S):
            send_in(b, p).start()
    mate_own(b).start()
    make_hot()
    mate_own(mate).wait_recv()
    extract(q)

    @pl.when(inner)
    def _():
        take(1, D, so, send_out)
        take(3, A2, si, send_in)
        pass_on(q)
        take(1, S, so)
        take(3, A1, si)
        mate_take(3, (A2, A1), si)
        extract(H[3])
        take(1, A2, so, send_out)
        take(3, D, si, send_in)
        mate_take(1, (D, S, A2), so)
        extract(H[1])

    @pl.when(outer)
    def _():
        take(2, D, so)
        mate_take(2, (D,), so)
        extract(H[2])
        pass_on(q)
        take(2, A2, so)
        pass_on(H[2])
        take(2, A1, so)
        mate_take(2, (A2, A1), so)
    wait_diag(q)
    acc_t[...] = product(q, start_t, NTL)
    acc_r[...] = product(q, start_r, NR)

    second, third = jnp.where(inner, H[3], H[2]), H[1]

    @pl.when(inner)
    def _():
        pass_on(H[3])
        take(0, A2, so, send_out)
        take(3, S, si, send_in)
        send_in(b, A1).start()
        send_in(own(3), A1).start()
        mate_take(3, (D, S), si)
        pass_on(H[1])
        take(0, D, so, send_out)

    @pl.when(outer)
    def _():
        take(1, D, so)
        mate_take(1, (D,), so)
        extract(H[1])
    wait_diag(second)
    acc_t[...] += product(second, start_t, NTL)
    acc_r[...] += product(second, start_r, NR)

    @pl.when(inner)
    def _():
        take(0, S, so)
        mate_take(0, (A2, D, S), so)
        extract(H[0])

    @pl.when(outer)
    def _():
        take(1, A2, so)
        pass_on(H[1])
        take(0, A2, so)
        take(0, D, so)
        mate_take(0, (D,), so)
        extract(H[0])
        pass_on(H[0])
        take(1, A1, so)
        mate_take(1, (A2, A1), so)
    wait_diag(third)
    acc_t[...] += product(third, start_t, NTL)

    @pl.when(inner)
    def _():
        finish_tile(l)
        take(1, A1, so, send_out)
        mate_take(1, (A1,), so)
    acc_r[...] += product(third, start_r, NR)

    @pl.when(inner)
    def _():
        pass_on(H[0])

        @pl.loop(0, 2)
        def _(n):
            finish_tile(jnp.where(n == 0, lx, ly))
        take(0, A1, so, send_out)
        for j in (lx, ly, l):
            start_tile(j)
        wait_diag(H[0])
        finish_tile(ld)
        start_tile(ld)
        mate_take(0, (A1,), so)

    @pl.when(outer)
    def _():
        wait_diag(H[0])
        acc_t[...] += product(H[0], start_t, NTL)
        take(0, A1, so)
        mate_take(0, (A2, A1), so)
    acc_r[...] += product(H[0], start_r, NR)

    def put(j, lo, hi, part):
        o_ref[:, j, lo:hi] = part

    def near(ref, j, lo, hi):
        return ref[j * SP:j * SP + share, lo:hi] / total

    t_lo, r_lo = R - NTL, R - NR
    @pl.when(upper)
    def _():
        for j in range(L):
            put(j, 0, t_lo, near(acc_r, j, 0, t_lo))
            put(j, t_lo, R, near(acc_t, j, 0, NTL))

    @pl.when(q < 2)
    def _():
        for j in range(L):
            put(j, 0, r_lo, near(acc_t, j, 0, r_lo))
            put(j, r_lo, R, near(acc_r, j, 0, NR))

    @pl.when(outer)
    def _():
        from_up, from_down = R // 2 + pad, half + pad
        base_up, base_down = from_up // 128 * 128, from_down // 128 * 128
        width = up_to(max(from_up - base_up, from_down - base_down) + 256, 128)
        offset = jnp.where(upper, from_up - base_up, from_down - base_down)
        hot = (lax.broadcasted_iota(jnp.int32, (256, width), 1)
               == lax.broadcasted_iota(jnp.int32, (256, width), 0) + offset)
        hot = jnp.where(hot, 1.0, 0.0).astype(jnp.bfloat16)
        place = lax.broadcasted_iota(jnp.int32, (share, width), 1)
        inside = (place >= offset) & (place < offset + 256)
        for d in (l, lx, ly, ld):
            wait_tile(d)
            placed = lax.dot_general(tile_recv[d], hot, (((1,), (0,)), ((), ())),
                                     preferred_element_type=jnp.float32)[:share]
            for side, lo in ((3, base_up), (0, base_down)):
                @pl.when(q == side)
                def _():
                    o_ref[:, d, lo:lo + width] = jnp.where(inside, placed, o_ref[:, d, lo:lo + width])

    all_stats.wait_send()
    mate_own(b).wait_send()

    def sent(part, sem):
        pltpu.make_async_remote_copy(
            src_ref=part, dst_ref=part, send_sem=sem, recv_sem=st_recv,
            device_id=(l, b), device_id_type=MESH).wait_send()

    near_end = R - size[S]

    @pl.when(inner)
    def _():
        sent(zbuf.at[pl.ds(0, 3), pl.ds(0, near_end), :], out_send)
        sent(zbuf.at[pl.ds(0, 2)], in_send)
        sent(zbuf.at[pl.ds(0, 3)], mate_send)
        sent(tile_send, t_send)

    @pl.when(outer)
    def _():
        sent(zbuf.at[pl.ds(0, 1)], in_send)
        sent(zbuf.at[pl.ds(0, 3), pl.ds(0, near_end), :], mate_send)

    sent(shr.at[pl.ds(0, L)], shr_send)
    sent(shr.at[pl.ds(0, B // L)], diag_send)


def line_call(L, B, series):
    R, T = series.shape
    share = R // B
    SP = up_to(share, 16)
    pad = share - 128
    skip_hi = (3 * 2 * share - pad) // 16 * 16
    t_lo = skip_hi // 128 * 128
    r_lo = (R - t_lo) // 128 * 128
    vmem = pl.BlockSpec(memory_space=pltpu.VMEM)
    dma = pltpu.SemaphoreType.DMA
    return pl.pallas_call(
        functools.partial(line_kernel, L, B),
        out_shape=jax.ShapeDtypeStruct((share, L, R), jnp.float32),
        in_specs=[pl.BlockSpec(memory_space=pltpu.HBM)],
        out_specs=vmem,
        scratch_shapes=[
            pltpu.VMEM((B, R, T), jnp.bfloat16),
            pltpu.VMEM((B, L, SP, T), jnp.bfloat16),
            pltpu.VMEM((L * SP, R - t_lo), jnp.float32),
            pltpu.VMEM((L * SP, R - r_lo), jnp.float32),
            pltpu.VMEM((L, 2 * SP, 128), jnp.bfloat16),
            pltpu.VMEM((L, SP, 256), jnp.bfloat16),
            pltpu.VMEM((2 * SP, R - t_lo), jnp.bfloat16),
            pltpu.VMEM((SP, 128), jnp.bfloat16),
            pltpu.VMEM((R, 128), jnp.float32),
            pltpu.VMEM((B, 2, R), jnp.float32),
            pltpu.VMEM((R, T), jnp.float32),
            dma((B, 4)), dma, dma, dma, dma,
            dma((B, 2)), dma, dma((B // 2,)), dma, dma((L,)), dma,
            dma, dma, dma((R // largest_tile(R, 352),)),
        ],
        compiler_params=pltpu.CompilerParams(
            collective_id=0, has_side_effects=True, vmem_limit_bytes=34 * 1024 * 1024),
    )(pltpu.with_memory_space_constraint(series, pltpu.HBM)).transpose(1, 0, 2)


def solution(mesh):
    L, B = mesh.shape["loop"], mesh.shape["bulk"]

    def on_device(series):
        R, T = series.shape
        share = R // B
        if L == 4 and B == 8 and R % 16 == 0 and T % 128 == 0 and 128 <= share <= 144:
            return line_call(L, B, series)
        SP = up_to(share, 16)
        pieces = 3
        vmem = pl.BlockSpec(memory_space=pltpu.VMEM)
        dma = pltpu.SemaphoreType.DMA
        return pl.pallas_call(
            functools.partial(kernel, L, B, pieces),
            out_shape=jax.ShapeDtypeStruct((share, L, R), jnp.float32),
            in_specs=[pl.BlockSpec(memory_space=pltpu.HBM)],
            out_specs=vmem,
            scratch_shapes=[
                pltpu.VMEM((B, R, T), jnp.bfloat16),
                pltpu.VMEM((B, L, SP, T), jnp.bfloat16),
                pltpu.VMEM((L * SP, R), jnp.float32),
                pltpu.VMEM((R, 128), jnp.float32),
                pltpu.VMEM((B, 2, R), jnp.float32),
                pltpu.VMEM((R, T), jnp.float32),
                dma((B, pieces)), dma((B, pieces)), dma((B, pieces)), dma((B, pieces)),
                dma((B, L)), dma((B, L)), dma((B,)), dma((B,)), dma((R // largest_tile(R, 128),)),
            ],
            compiler_params=pltpu.CompilerParams(
                collective_id=0, has_side_effects=True, vmem_limit_bytes=26 * 1024 * 1024),
        )(pltpu.with_memory_space_constraint(series, pltpu.HBM)).transpose(1, 0, 2)

    return jax.shard_map(
        on_device, mesh=mesh, in_specs=(P("loop", "bulk"),),
        out_specs=P(None, "bulk", "loop"), check_vma=False)
```

```python
import functools
import jax
import jax.numpy as jnp
from jax import lax
from jax.experimental import pallas as pl
from jax.experimental.pallas import tpu as pltpu
from jax.sharding import PartitionSpec as P

epsilon = 1e-06
MESH = pl.DeviceIdType.MESH
NT = (((1,), (1,)), ((), ()))
TN = (((0,), (0,)), ((), ()))


def up_to(value, unit):
    return -(-value // unit) * unit


def largest_tile(rows, limit):
    return max(t for t in range(16, limit + 1, 16) if rows % t == 0)


def kernel(L, B, PIECES, x_hbm, o_ref, zbuf, shr, acc, cols, stats, x_ref,
           z_recv, up_send, down_send, mate_send, shr_recv, shr_send, st_recv, st_send, x_sem):
    R, T = x_hbm.shape
    total = T * B
    Q = B // 2
    share = R // B
    SP = shr.shape[2]
    W = min(up_to(share + 15, 16), R)
    bounds = [up_to(R * i // PIECES, 128) for i in range(PIECES)] + [R]
    tile = largest_tile(R, 128)
    l, b = lax.axis_index("loop"), lax.axis_index("bulk")
    q, c = b // 2, b % 2
    mate = q * 2 + (1 - c)

    barrier = pltpu.get_barrier_semaphore()
    for d in range(1, B):
        pl.semaphore_signal(barrier, inc=1, device_id=(l, lax.rem(b + d, B)), device_id_type=MESH)
    for d in range(1, L):
        pl.semaphore_signal(barrier, inc=1, device_id=(lax.rem(l + d, L), b), device_id_type=MESH)

    def load(i):
        rows = pl.ds(pl.multiple_of(i * tile, tile), tile)
        return pltpu.make_async_copy(x_hbm.at[rows, :], x_ref.at[rows, :], x_sem.at[i])

    @pl.loop(0, R // tile)
    def _(i):
        load(i).start()

    lane = lax.broadcasted_iota(jnp.int32, (tile, 128), 1)

    @pl.loop(0, R // tile)
    def _(i):
        rows = pl.ds(pl.multiple_of(i * tile, tile), tile)
        load(i).wait()
        v = x_ref[rows, :]
        mean = jnp.sum(v, axis=1, keepdims=True) / T
        dev = v - mean
        m2 = jnp.sum(dev * dev, axis=1, keepdims=True)
        cols[rows, :] = jnp.where(lane == 0, mean, jnp.where(lane == 1, m2, 0.0))

    pick = (lax.broadcasted_iota(jnp.int32, (8, 128), 0)
            == lax.broadcasted_iota(jnp.int32, (8, 128), 1)).astype(jnp.float32)
    line = lax.dot_general(pick, cols[...], NT, precision=lax.Precision.HIGHEST,
                           preferred_element_type=jnp.float32)
    stats[b] = line[:2]

    pl.semaphore_wait(barrier, B - 1 + L - 1)

    def stat_copy(source, peer):
        return pltpu.make_async_remote_copy(
            src_ref=stats.at[source], dst_ref=stats.at[source],
            send_sem=st_send.at[peer], recv_sem=st_recv.at[source],
            device_id=(l, peer), device_id_type=MESH)

    for d in range(1, B):
        stat_copy(b, lax.rem(b + d, B)).start()
    for d in range(1, B):
        other = lax.rem(b + d, B)
        stat_copy(other, other).wait_recv()

    mean = stats[0, 0:1]
    for k in range(1, B):
        mean = mean + stats[k, 0:1]
    mean = mean / B
    square = jnp.zeros_like(mean)
    for k in range(B):
        shift = stats[k, 0:1] - mean
        square = square + (stats[k, 1:2] + T * (shift * shift))
    scale = lax.rsqrt(square / total + epsilon)
    sub = lax.broadcasted_iota(jnp.int32, (8, R), 0)
    both = jnp.where(sub == 0, mean, jnp.where(sub == 1, scale, 0.0))
    cols[...] = lax.dot_general(both, pick, TN, precision=lax.Precision.HIGHEST,
                                preferred_element_type=jnp.float32)

    def normalise(piece):
        size = bounds[piece + 1] - bounds[piece]
        step = largest_tile(size, 128)

        @pl.loop(0, size // step)
        def _(i):
            rows = pl.ds(pl.multiple_of(bounds[piece] + i * step, 16), step)
            z = (x_ref[rows, :] - cols[rows, 0:1]) * cols[rows, 1:2]
            zbuf[b, rows, :] = z.astype(jnp.bfloat16)

    def piece_copy(k, piece, send_sem, peer):
        part = zbuf.at[k, pl.ds(bounds[piece], bounds[piece + 1] - bounds[piece]), :]
        return pltpu.make_async_remote_copy(
            src_ref=part, dst_ref=part, send_sem=send_sem.at[k, piece],
            recv_sem=z_recv.at[k, piece], device_id=(l, peer), device_id_type=MESH)

    def share_copy(k, block, peer):
        return pltpu.make_async_remote_copy(
            src_ref=shr.at[k, block], dst_ref=shr.at[k, block], send_sem=shr_send.at[k, peer],
            recv_sem=shr_recv.at[k, block], device_id=(peer, b), device_id_type=MESH)

    has_up, has_down = q + 1 < Q, q >= 1
    start = b * share
    first = pl.multiple_of(jnp.minimum(start // 16 * 16, R - W), 16)
    need_below = PIECES - 1 - sum((first >= x).astype(jnp.int32) for x in bounds[1:-1])
    need_above = sum((first + W > x).astype(jnp.int32) for x in bounds[1:-1])

    def extract(k):
        window = zbuf[k, pl.ds(first, W), :]
        hot = (lax.broadcasted_iota(jnp.int32, (SP, W), 1)
               == lax.broadcasted_iota(jnp.int32, (SP, W), 0) + (start - first))
        inside = lax.broadcasted_iota(jnp.int32, (SP, W), 0) < share
        hot = jnp.where(hot & inside, 1.0, 0.0).astype(jnp.bfloat16)
        rows = lax.dot_general(hot, window, (((1,), (0,)), ((), ())),
                               preferred_element_type=jnp.float32)
        shr[k, l] = rows.astype(jnp.bfloat16)
        for d in range(1, L):
            share_copy(k, l, lax.rem(l + d, L)).start()

    def wait_shares(place):
        for core in range(2):
            k = place * 2 + core
            for d in range(1, L):
                other = lax.rem(l + d, L)
                share_copy(k, other, other).wait_recv()

    def multiply(place):
        part = None
        wait_shares(place)
        for core in range(2):
            k = place * 2 + core
            a = shr[k].reshape(L * SP, T)
            term = lax.dot_general(a, zbuf[k], NT, preferred_element_type=jnp.float32)
            part = term if part is None else part + term
        acc[...] += part

    def multiply_step(s):
        @pl.loop(0, 2)
        def _(n):
            place = q - (1 - 2 * n) * s

            @pl.when((place >= 0) & (place < Q) & ((s > 0) | (n < 1)))
            def _():
                multiply(place)

    def send_own(up_first):
        done = set()

        def send(up, i):
            piece = PIECES - 1 - i if up else i
            if piece not in done:
                done.add(piece)
                normalise(piece)

            @pl.when(has_up if up else has_down)
            def _():
                if up:
                    piece_copy(b, piece, up_send, b + 2).start()
                else:
                    piece_copy(b, piece, down_send, b - 2).start()

        for i in range(PIECES):
            send(up_first, i)
            send(not up_first, i)

    @pl.when(q >= Q // 2)
    def _():
        send_own(True)

    @pl.when(q < Q // 2)
    def _():
        send_own(False)

    for i in range(PIECES):
        piece_copy(b, i, mate_send, mate).start()

    acc[...] = jnp.zeros_like(acc)
    extract(b)

    for i in range(PIECES):
        piece_copy(mate, i, mate_send, mate).wait_recv()

    extract(mate)

    def arrive(s, i, between=None):
        below, above = b - 2 * s, b + 2 * s
        from_below, from_above = q - s >= 0, q + s < Q
        down_piece = PIECES - 1 - i

        @pl.when(from_below)
        def _():
            piece_copy(below, down_piece, up_send, b).wait_recv()

            @pl.when(has_up)
            def _():
                piece_copy(below, down_piece, up_send, b + 2).start()
            piece_copy(below, down_piece, mate_send, mate).start()

        @pl.when(from_above)
        def _():
            piece_copy(above, i, down_send, b).wait_recv()

            @pl.when(has_down)
            def _():
                piece_copy(above, i, down_send, b - 2).start()
            piece_copy(above, i, mate_send, mate).start()

        @pl.when(from_below & (i == need_below))
        def _():
            extract(below)

        @pl.when(from_above & (i == need_above))
        def _():
            extract(above)

        if between is not None:
            between()

        @pl.when(from_below)
        def _():
            piece_copy(mate - 2 * s, down_piece, mate_send, mate).wait_recv()

            @pl.when(i == need_below)
            def _():
                extract(mate - 2 * s)

        @pl.when(from_above)
        def _():
            piece_copy(mate + 2 * s, i, mate_send, mate).wait_recv()

            @pl.when(i == need_above)
            def _():
                extract(mate + 2 * s)

        if i == 0:
            multiply_step(s - 1)

    def finish(piece, place):
        lo, hi = bounds[piece], bounds[piece + 1]
        part = acc[:, lo:hi]
        if place is not None:
            for core in range(2):
                k = place * 2 + core
                a = shr[k].reshape(L * SP, T)
                part = part + lax.dot_general(a, zbuf[k, lo:hi, :], NT,
                                              preferred_element_type=jnp.float32)
        part = part / total
        for j in range(L):
            o_ref[:, j, lo:hi] = part[j * SP:j * SP + share]

    @pl.loop(1, Q - 1)
    def _(s):
        for i in range(PIECES):
            arrive(s, i)

    def finish_ends(steps):
        for end, place in ((Q - 1, 0), (0, Q - 1)):
            @pl.when(q == end)
            def _():
                for i in steps:
                    finish(PIECES - 1 - i if end else i, place)

    def finish_early():
        for end, place in ((Q - 1, 0), (0, Q - 1)):
            @pl.when(q == end)
            def _():
                wait_shares(place)

        finish_ends(range(PIECES - 1))

    for i in range(PIECES):
        arrive(Q - 1, i, finish_early if i == PIECES - 1 else None)
    finish_ends([PIECES - 1])

    @pl.when((q > 0) & (q < Q - 1))
    def _():
        for i in range(PIECES):
            finish(i, None)

    for d in range(1, B):
        other = lax.rem(b + d, B)
        stat_copy(b, other).wait_send()

    @pl.loop(0, Q)
    def _(s):
        below, above = b - 2 * s, b + 2 * s
        from_below, from_above = q - s >= 0, q + s < Q

        for i in range(PIECES):
            @pl.when(from_below & has_up)
            def _():
                piece_copy(below, i, up_send, b + 2).wait_send()

            @pl.when(from_above & has_down)
            def _():
                piece_copy(above, i, down_send, b - 2).wait_send()

            @pl.when(from_below)
            def _():
                piece_copy(below, i, mate_send, mate).wait_send()

            @pl.when(from_above & (s > 0))
            def _():
                piece_copy(above, i, mate_send, mate).wait_send()

    @pl.loop(0, B)
    def _(k):
        for d in range(1, L):
            other = lax.rem(l + d, L)
            share_copy(k, l, other).wait_send()


D, S, A2, A1 = range(4)


def line_kernel(L, B, x_hbm, o_ref, zbuf, shr, acc_t, acc_r, tile_send, tile_recv, hot_ref, shift_ref, cols, stats, x_ref, raw,
                z_recv, out_send, in_send, mate_send, own_send, own_out, own_in, first_send, raw_recv, raw_send, shr_recv, shr_send, diag_recv, diag_send, t_recv, t_send,
                st_recv, st_send, x_sem):
    R, T = x_hbm.shape
    total = T * B
    share = R // B
    half = 2 * share
    SP = shr.shape[2]
    pad = share - 128
    W = min(up_to(share + 15, 16), R)
    skip_lo, skip_hi = up_to(R // 2 + pad, 16), (3 * half - pad) // 16 * 16
    middle = up_to(skip_lo // 2, 16)
    up_start = {D: skip_hi, S: skip_lo, A2: middle, A1: 0}
    size = {D: R - skip_hi, S: skip_hi - skip_lo, A2: skip_lo - middle, A1: middle}
    tile = largest_tile(R, 352)
    RAW = raw.shape[1]
    NTL, NR = acc_t.shape[1], acc_r.shape[1]
    l, b = lax.axis_index("loop"), lax.axis_index("bulk")
    q, c = b // 2, b % 2
    mate = q * 2 + (1 - c)
    upper = q >= 2
    inner = (q == 1) | (q == 2)
    outer = (q == 0) | (q == 3)
    step = jnp.where(upper, 1, -1)
    H = [jnp.where(upper, h, 3 - h) for h in range(4)]
    out_nbr, in_nbr = b + 2 * step, b - 2 * step
    lx, ly, ld = l + 1 - 2 * (l % 2), lax.rem(l + 2, 4), 3 - l

    def align(value, unit=16):
        return pl.multiple_of(value, unit)

    down_start = {p: R - up_start[p] - size[p] for p in up_start}
    so = {p: align(jnp.where(upper, up_start[p], down_start[p])) for p in up_start}
    si = {p: align(jnp.where(upper, down_start[p], up_start[p])) for p in up_start}
    start_t = align(jnp.where(upper, R - NTL, 0), 128)
    start_r = align(jnp.where(upper, 0, R - NR), 128)

    barrier = pltpu.get_barrier_semaphore()
    for d in range(1, B):
        pl.semaphore_signal(barrier, inc=1, device_id=(l, lax.rem(b + d, B)), device_id_type=MESH)
    facing = jnp.where(inner, H[3], H[2])
    for d in range(1, L):
        other = lax.rem(l + d, L)
        pl.semaphore_signal(barrier, inc=1, device_id=(other, b), device_id_type=MESH)
        for core in range(2):
            pl.semaphore_signal(barrier, inc=1, device_id=(other, facing * 2 + core), device_id_type=MESH)

    def load(i):
        rows = pl.ds(pl.multiple_of(i * tile, tile), tile)
        return pltpu.make_async_copy(x_hbm.at[rows, :], x_ref.at[rows, :], x_sem.at[i])

    @pl.loop(0, R // tile)
    def _(i):
        load(i).start()

    lane = lax.broadcasted_iota(jnp.int32, (tile, 128), 1)

    @pl.loop(0, R // tile)
    def _(i):
        rows = pl.ds(pl.multiple_of(i * tile, tile), tile)
        load(i).wait()
        v = x_ref[rows, :]
        mean = jnp.sum(v, axis=1, keepdims=True) / T
        dev = v - mean
        m2 = jnp.sum(dev * dev, axis=1, keepdims=True)
        cols[rows, :] = jnp.where(lane == 0, mean, jnp.where(lane == 1, m2, 0.0))

    pick = (lax.broadcasted_iota(jnp.int32, (8, 128), 0)
            == lax.broadcasted_iota(jnp.int32, (8, 128), 1)).astype(jnp.float32)
    line = lax.dot_general(pick, cols[...], NT, precision=lax.Precision.HIGHEST,
                           preferred_element_type=jnp.float32)
    stats[b] = line[:2]

    pl.semaphore_wait(barrier, B - 1 + 3 * (L - 1))

    def stat_copy(source, peer):
        return pltpu.make_async_remote_copy(
            src_ref=stats.at[source], dst_ref=stats.at[source],
            send_sem=st_send, recv_sem=st_recv,
            device_id=(l, peer), device_id_type=MESH)

    for d in range(1, B):
        stat_copy(b, lax.rem(b + d, B)).start()
    def raw_copy(start, slot, peer):
        return pltpu.make_async_remote_copy(
            src_ref=x_ref.at[pl.ds(start, RAW), :], dst_ref=raw.at[slot], send_sem=raw_send,
            recv_sem=raw_recv.at[slot], device_id=(l, peer), device_id_type=MESH)

    @pl.when(inner)
    def _():
        raw_copy(so[D], 0, out_nbr).start()
        raw_copy(si[D], 0, in_nbr).start()

    @pl.when(outer)
    def _():
        raw_copy(si[A2], 1, in_nbr).start()

    gathered = stats.at[pl.ds(0, B - 1)]
    all_stats = pltpu.make_async_remote_copy(
        src_ref=gathered, dst_ref=gathered, send_sem=st_send, recv_sem=st_recv,
        device_id=(l, b), device_id_type=MESH)
    all_stats.wait_recv()

    mean = stats[0, 0:1]
    for k in range(1, B):
        mean = mean + stats[k, 0:1]
    mean = mean / B
    square = jnp.zeros_like(mean)
    for k in range(B):
        shift = stats[k, 0:1] - mean
        square = square + (stats[k, 1:2] + T * (shift * shift))
    scale = lax.rsqrt(square / total + epsilon)
    sub = lax.broadcasted_iota(jnp.int32, (8, R), 0)
    both = jnp.where(sub == 0, mean, jnp.where(sub == 1, scale, 0.0))
    cols[...] = lax.dot_general(both, pick, TN, precision=lax.Precision.HIGHEST,
                                preferred_element_type=jnp.float32)

    def normalise(start, count):
        unit = count if count <= 288 else largest_tile(count, 128)

        def chunk(i):
            rows = pl.ds(pl.multiple_of(start + i * unit, 16), unit)
            z = (x_ref[rows, :] - cols[rows, 0:1]) * cols[rows, 1:2]
            zbuf[b, rows, :] = z.astype(jnp.bfloat16)

        if unit == count:
            chunk(0)
        else:
            pl.loop(0, count // unit)(chunk)

    def z_copy(k, start, p, send_sem, peer, rows=None):
        part = zbuf.at[k, pl.ds(start, size[p] if rows is None else rows), :]
        return pltpu.make_async_remote_copy(
            src_ref=part, dst_ref=part, send_sem=send_sem,
            recv_sem=z_recv.at[k, p], device_id=(l, peer), device_id_type=MESH)

    def first_copy(k, p, start, peer):
        return z_copy(k, align(start[p] + RAW), p, first_send, peer, size[p] - RAW)

    def unpack(slot, k, start):
        raw_copy(start, slot, b).wait_recv()
        rows = pl.ds(start, RAW)
        z = (raw[slot] - cols[rows, 0:1]) * cols[rows, 1:2]
        zbuf[k, rows, :] = z.astype(jnp.bfloat16)

    def send_out(k, p):
        return z_copy(k, so[p], p, out_send, out_nbr)

    def send_in(k, p):
        return z_copy(k, si[p], p, in_send, in_nbr)

    def mate_copy(k, p, start):
        return z_copy(k, start[p], p, mate_send, mate)

    def mate_own(k):
        return z_copy(k, 0, 0, own_send, mate, R)

    def share_copy(k, block, peer, way):
        return pltpu.make_async_remote_copy(
            src_ref=shr.at[k, block], dst_ref=shr.at[k, block], send_sem=shr_send,
            recv_sem=shr_recv.at[k, way], device_id=(peer, b), device_id_type=MESH)

    cut = up_to(SP // 2, 16)

    def diag_copy(k, block, peer, way):
        rows = pl.ds(0, cut) if way == 0 else pl.ds(cut, SP - cut)
        part = shr.at[k, block, rows, :]
        return pltpu.make_async_remote_copy(
            src_ref=part, dst_ref=part, send_sem=diag_send,
            recv_sem=diag_recv.at[k // 2], device_id=(peer, b), device_id_type=MESH)

    first = align(jnp.minimum(b * share // 16 * 16, jnp.where(q == 0, size[D], R) - W))

    def extract(place):
        @pl.loop(0, 2)
        def _(core):
            k = place * 2 + core
            window = zbuf[k, pl.ds(first, W), :]
            row = lax.broadcasted_iota(jnp.int32, (SP, W), 0)
            hot = lax.broadcasted_iota(jnp.int32, (SP, W), 1) == row + (b * share - first)
            hot = jnp.where(hot & (row < share), 1.0, 0.0).astype(jnp.bfloat16)
            rows = lax.dot_general(hot, window, (((1,), (0,)), ((), ())),
                                   preferred_element_type=jnp.float32)
            shr[k, l] = rows.astype(jnp.bfloat16)
            share_copy(k, l, lx, 0).start()
            share_copy(k, l, ly, 1).start()

    def pass_on(place):
        @pl.loop(0, 2)
        def _(core):
            k = place * 2 + core
            share_copy(k, lx, lx, 0).wait_recv()
            diag_copy(k, lx, ly, 0).start()
            share_copy(k, ly, ly, 1).wait_recv()
            diag_copy(k, ly, lx, 1).start()

    def wait_diag(place):
        part = shr.at[pl.ds(place * 2, 2), ld]
        pltpu.make_async_remote_copy(
            src_ref=part, dst_ref=part, send_sem=diag_send, recv_sem=diag_recv.at[place],
            device_id=(l, b), device_id_type=MESH).wait_recv()

    def product(place, start, width):
        part = None
        for core in range(2):
            k = place * 2 + core
            term = lax.dot_general(shr[k].reshape(L * SP, T), zbuf[k, pl.ds(start, width), :], NT,
                                   preferred_element_type=jnp.float32)
            part = term if part is None else part + term
        return part

    def own(h):
        return H[h] * 2 + c

    def other(h):
        return H[h] * 2 + (1 - c)

    def take(h, p, start, onward=None, first=False):
        if first:
            first_copy(own(h), p, start, mate).wait_recv()
        else:
            z_copy(own(h), start[p], p, mate_send, mate).wait_recv()
        if onward is not None:
            onward(own(h), p).start()
        mate_copy(own(h), p, start).start()

    def mate_take(h, pieces, start):
        for p in pieces:
            mate_copy(other(h), p, start).wait_recv()

    def tile_copy(j, core, block, slot):
        return pltpu.make_async_remote_copy(
            src_ref=tile_send.at[j, pl.ds(core * SP, SP), :],
            dst_ref=tile_recv.at[block, :, pl.ds(pl.multiple_of(slot * 128, 128), 128)],
            send_sem=t_send, recv_sem=t_recv.at[block],
            device_id=(j, H[3] * 2 + core), device_id_type=MESH)

    def make_hot():
        row = lax.broadcasted_iota(jnp.int32, (2 * SP, NTL), 0)
        lower = row < SP
        want = jnp.where(lower, row, row - SP + share) + jnp.where(upper, NTL - half, 0)
        keep = jnp.where(lower, row, row - SP) < share
        hot = (lax.broadcasted_iota(jnp.int32, (2 * SP, NTL), 1) == want) & keep
        hot_ref[...] = jnp.where(hot, 1.0, 0.0).astype(jnp.bfloat16)
        shift = (lax.broadcasted_iota(jnp.int32, (SP, 128), 0)
                 == lax.broadcasted_iota(jnp.int32, (SP, 128), 1) + jnp.where(c == 0, pad, 0))
        shift_ref[...] = jnp.where(shift, 1.0, 0.0).astype(jnp.bfloat16)

    def finish_tile(j):
        rows = pl.ds(pl.multiple_of(j * SP, SP), SP)
        value = acc_t[rows, :]
        for core in range(2):
            k = H[0] * 2 + core
            value = value + lax.dot_general(shr[k, j], zbuf[k, pl.ds(start_t, NTL), :], NT,
                                            preferred_element_type=jnp.float32)
        acc_t[rows, :] = value
        turned = lax.dot_general((value / total).astype(jnp.bfloat16), shift_ref[...], TN,
                                 preferred_element_type=jnp.float32)
        picked = lax.dot_general(hot_ref[...], turned.astype(jnp.bfloat16), (((1,), (0,)), ((), ())),
                                 preferred_element_type=jnp.float32)
        tile_send[j] = picked.astype(jnp.bfloat16)

    def start_tile(j):
        for core in range(2):
            tile_copy(j, core, l, c).start()

    def wait_tile(block):
        part = tile_recv.at[block]
        pltpu.make_async_remote_copy(
            src_ref=part, dst_ref=part, send_sem=t_send, recv_sem=t_recv.at[block],
            device_id=(l, b), device_id_type=MESH).wait_recv()

    normalise(so[D], size[D])

    @pl.when(inner)
    def _():
        first_copy(b, D, so, out_nbr).start()
    normalise(align(jnp.where(upper, 0, size[D])), R - size[D])

    @pl.when(inner)
    def _():
        first_copy(b, D, si, in_nbr).start()
        for p in (S, A2):
            z_copy(b, si[p], p, own_in, in_nbr).start()
        for p in (A2, A1):
            z_copy(b, so[p], p, own_out, out_nbr).start()

    @pl.when(outer)
    def _():
        first_copy(b, A2, si, in_nbr).start()
        for p in (A1, D, S):
            z_copy(b, si[p], p, own_in, in_nbr).start()
    mate_own(b).start()
    make_hot()
    mate_own(mate).wait_recv()
    extract(q)

    @pl.when(inner)
    def _():
        unpack(0, own(1), so[D])
        unpack(1, own(3), si[A2])
        take(1, D, so, send_out, True)
        take(3, A2, si, send_in, True)
        pass_on(q)
        take(1, S, so)
        take(3, A1, si)
        mate_take(3, (A2, A1), si)
        extract(H[3])
        take(1, A2, so, send_out)
        take(3, D, si, send_in)
        mate_take(1, (D, S, A2), so)
        extract(H[1])

    @pl.when(outer)
    def _():
        unpack(0, own(2), so[D])
        take(2, D, so, None, True)
        mate_take(2, (D,), so)
        extract(H[2])
        pass_on(q)
        take(2, A2, so)
        pass_on(H[2])
        take(2, A1, so)
        mate_take(2, (A2, A1), so)
    wait_diag(q)
    acc_t[...] = product(q, start_t, NTL)
    acc_r[...] = product(q, start_r, NR)

    second, third = jnp.where(inner, H[3], H[2]), H[1]

    @pl.when(inner)
    def _():
        pass_on(H[3])
        take(0, A2, so, send_out)
        take(3, S, si, send_in)
        z_copy(b, si[A1], A1, own_in, in_nbr).start()
        send_in(own(3), A1).start()
        mate_take(3, (D, S), si)
        pass_on(H[1])
        take(0, D, so, send_out)

    @pl.when(outer)
    def _():
        take(1, D, so)
        mate_take(1, (D,), so)
        extract(H[1])
    wait_diag(second)
    acc_t[...] += product(second, start_t, NTL)
    acc_r[...] += product(second, start_r, NR)

    @pl.when(inner)
    def _():
        take(0, S, so)
        mate_take(0, (A2, D, S), so)
        extract(H[0])

    @pl.when(outer)
    def _():
        take(1, A2, so)
        pass_on(H[1])
        take(0, A2, so)
        take(0, D, so)
        mate_take(0, (D,), so)
        extract(H[0])
        pass_on(H[0])
        take(1, A1, so)
        mate_take(1, (A2, A1), so)
    wait_diag(third)
    acc_t[...] += product(third, start_t, NTL)

    @pl.when(inner)
    def _():
        finish_tile(l)
        take(1, A1, so, send_out)
        start_tile(l)
        mate_take(1, (A1,), so)
    acc_r[...] += product(third, start_r, NR)

    @pl.when(inner)
    def _():
        pass_on(H[0])

        @pl.loop(0, 2)
        def _(n):
            finish_tile(jnp.where(n == 0, lx, ly))
        take(0, A1, so, send_out)
        for j in (lx, ly):
            start_tile(j)
        wait_diag(H[0])
        finish_tile(ld)
        start_tile(ld)
        mate_take(0, (A1,), so)

    @pl.when(outer)
    def _():
        wait_diag(H[0])
        acc_t[...] += product(H[0], start_t, NTL)
        take(0, A1, so)
        mate_take(0, (A2, A1), so)
    acc_r[...] += product(H[0], start_r, NR)

    def put(j, lo, hi, part):
        o_ref[:, j, lo:hi] = part

    def near(ref, j, lo, hi):
        return ref[j * SP:j * SP + share, lo:hi] / total

    t_lo, r_lo = R - NTL, R - NR
    @pl.when(upper)
    def _():
        for j in range(L):
            put(j, 0, t_lo, near(acc_r, j, 0, t_lo))
            put(j, t_lo, R, near(acc_t, j, 0, NTL))

    @pl.when(q < 2)
    def _():
        for j in range(L):
            put(j, 0, r_lo, near(acc_t, j, 0, r_lo))
            put(j, r_lo, R, near(acc_r, j, 0, NR))

    @pl.when(outer)
    def _():
        from_up, from_down = R // 2 + pad, half + pad
        base_up, base_down = from_up // 128 * 128, from_down // 128 * 128
        width = up_to(max(from_up - base_up, from_down - base_down) + 256, 128)
        offset = jnp.where(upper, from_up - base_up, from_down - base_down)
        hot = (lax.broadcasted_iota(jnp.int32, (256, width), 1)
               == lax.broadcasted_iota(jnp.int32, (256, width), 0) + offset)
        hot = jnp.where(hot, 1.0, 0.0).astype(jnp.bfloat16)
        place = lax.broadcasted_iota(jnp.int32, (share, width), 1)
        inside = (place >= offset) & (place < offset + 256)
        for d in (l, lx, ly, ld):
            wait_tile(d)
            placed = lax.dot_general(tile_recv[d], hot, (((1,), (0,)), ((), ())),
                                     preferred_element_type=jnp.float32)[:share]
            for side, lo in ((3, base_up), (0, base_down)):
                @pl.when(q == side)
                def _():
                    o_ref[:, d, lo:lo + width] = jnp.where(inside, placed, o_ref[:, d, lo:lo + width])

    all_stats.wait_send()
    mate_own(b).wait_send()

    def sent(part, sem):
        pltpu.make_async_remote_copy(
            src_ref=part, dst_ref=part, send_sem=sem, recv_sem=st_recv,
            device_id=(l, b), device_id_type=MESH).wait_send()

    near_end = R - size[S]

    @pl.when(inner)
    def _():
        sent(zbuf.at[0, pl.ds(0, size[A2] + size[A1]), :], own_out)
        sent(zbuf.at[0, pl.ds(0, R - size[D]), :], own_in)
        sent(zbuf.at[pl.ds(0, 2), pl.ds(0, size[D] - RAW), :], first_send)
        sent(raw, raw_send)
        sent(zbuf.at[pl.ds(0, 2), pl.ds(0, near_end), :], out_send)
        sent(zbuf.at[pl.ds(0, 1)], in_send)
        sent(zbuf.at[pl.ds(0, 3)], mate_send)
        sent(tile_send, t_send)

    @pl.when(outer)
    def _():
        sent(zbuf.at[0, pl.ds(0, R - size[A2]), :], own_in)
        sent(zbuf.at[0, pl.ds(0, size[A2] - RAW), :], first_send)
        sent(raw.at[0], raw_send)
        sent(zbuf.at[pl.ds(0, 3), pl.ds(0, near_end), :], mate_send)

    sent(shr.at[pl.ds(0, L)], shr_send)
    sent(shr.at[pl.ds(0, B // L)], diag_send)


def line_call(L, B, series):
    R, T = series.shape
    share = R // B
    SP = up_to(share, 16)
    pad = share - 128
    skip_hi = (3 * 2 * share - pad) // 16 * 16
    t_lo = skip_hi // 128 * 128
    r_lo = (R - t_lo) // 128 * 128
    vmem = pl.BlockSpec(memory_space=pltpu.VMEM)
    dma = pltpu.SemaphoreType.DMA
    return pl.pallas_call(
        functools.partial(line_kernel, L, B),
        out_shape=jax.ShapeDtypeStruct((share, L, R), jnp.float32),
        in_specs=[pl.BlockSpec(memory_space=pltpu.HBM)],
        out_specs=vmem,
        scratch_shapes=[
            pltpu.VMEM((B, R, T), jnp.bfloat16),
            pltpu.VMEM((B, L, SP, T), jnp.bfloat16),
            pltpu.VMEM((L * SP, R - t_lo), jnp.float32),
            pltpu.VMEM((L * SP, R - r_lo), jnp.float32),
            pltpu.VMEM((L, 2 * SP, 128), jnp.bfloat16),
            pltpu.VMEM((L, SP, 256), jnp.bfloat16),
            pltpu.VMEM((2 * SP, R - t_lo), jnp.bfloat16),
            pltpu.VMEM((SP, 128), jnp.bfloat16),
            pltpu.VMEM((R, 128), jnp.float32),
            pltpu.VMEM((B, 2, R), jnp.float32),
            pltpu.VMEM((R, T), jnp.float32),
            pltpu.VMEM((2, (R - skip_hi) // 32 * 16, T), jnp.float32),
            dma((B, 4)), dma, dma, dma, dma, dma, dma, dma, dma((2,)), dma,
            dma((B, 2)), dma, dma((B // 2,)), dma, dma((L,)), dma,
            dma, dma, dma((R // largest_tile(R, 352),)),
        ],
        compiler_params=pltpu.CompilerParams(
            collective_id=0, has_side_effects=True, vmem_limit_bytes=34 * 1024 * 1024),
    )(pltpu.with_memory_space_constraint(series, pltpu.HBM)).transpose(1, 0, 2)


def solution(mesh):
    L, B = mesh.shape["loop"], mesh.shape["bulk"]

    def on_device(series):
        R, T = series.shape
        share = R // B
        if L == 4 and B == 8 and R % 16 == 0 and T % 128 == 0 and 128 <= share <= 144:
            return line_call(L, B, series)
        SP = up_to(share, 16)
        pieces = 3
        vmem = pl.BlockSpec(memory_space=pltpu.VMEM)
        dma = pltpu.SemaphoreType.DMA
        return pl.pallas_call(
            functools.partial(kernel, L, B, pieces),
            out_shape=jax.ShapeDtypeStruct((share, L, R), jnp.float32),
            in_specs=[pl.BlockSpec(memory_space=pltpu.HBM)],
            out_specs=vmem,
            scratch_shapes=[
                pltpu.VMEM((B, R, T), jnp.bfloat16),
                pltpu.VMEM((B, L, SP, T), jnp.bfloat16),
                pltpu.VMEM((L * SP, R), jnp.float32),
                pltpu.VMEM((R, 128), jnp.float32),
                pltpu.VMEM((B, 2, R), jnp.float32),
                pltpu.VMEM((R, T), jnp.float32),
                dma((B, pieces)), dma((B, pieces)), dma((B, pieces)), dma((B, pieces)),
                dma((B, L)), dma((B, L)), dma((B,)), dma((B,)), dma((R // largest_tile(R, 128),)),
            ],
            compiler_params=pltpu.CompilerParams(
                collective_id=0, has_side_effects=True, vmem_limit_bytes=26 * 1024 * 1024),
        )(pltpu.with_memory_space_constraint(series, pltpu.HBM)).transpose(1, 0, 2)

    return jax.shard_map(
        on_device, mesh=mesh, in_specs=(P("loop", "bulk"),),
        out_specs=P(None, "bulk", "loop"), check_vma=False)
```

```python
import functools
import jax
import jax.numpy as jnp
from jax import lax
from jax.experimental import pallas as pl
from jax.experimental.pallas import tpu as pltpu
from jax.sharding import PartitionSpec as P

epsilon = 1e-06
MESH = pl.DeviceIdType.MESH
NT = (((1,), (1,)), ((), ()))
TN = (((0,), (0,)), ((), ()))


def up_to(value, unit):
    return -(-value // unit) * unit


def largest_tile(rows, limit):
    return max(t for t in range(16, limit + 1, 16) if rows % t == 0)


def kernel(L, B, PIECES, x_hbm, o_ref, zbuf, shr, acc, cols, stats, x_ref,
           z_recv, up_send, down_send, mate_send, shr_recv, shr_send, st_recv, st_send, x_sem):
    R, T = x_hbm.shape
    total = T * B
    Q = B // 2
    share = R // B
    SP = shr.shape[2]
    W = min(up_to(share + 15, 16), R)
    bounds = [up_to(R * i // PIECES, 128) for i in range(PIECES)] + [R]
    tile = largest_tile(R, 128)
    l, b = lax.axis_index("loop"), lax.axis_index("bulk")
    q, c = b // 2, b % 2
    mate = q * 2 + (1 - c)

    barrier = pltpu.get_barrier_semaphore()
    for d in range(1, B):
        pl.semaphore_signal(barrier, inc=1, device_id=(l, lax.rem(b + d, B)), device_id_type=MESH)
    for d in range(1, L):
        pl.semaphore_signal(barrier, inc=1, device_id=(lax.rem(l + d, L), b), device_id_type=MESH)

    def load(i):
        rows = pl.ds(pl.multiple_of(i * tile, tile), tile)
        return pltpu.make_async_copy(x_hbm.at[rows, :], x_ref.at[rows, :], x_sem.at[i])

    @pl.loop(0, R // tile)
    def _(i):
        load(i).start()

    lane = lax.broadcasted_iota(jnp.int32, (tile, 128), 1)

    @pl.loop(0, R // tile)
    def _(i):
        rows = pl.ds(pl.multiple_of(i * tile, tile), tile)
        load(i).wait()
        v = x_ref[rows, :]
        mean = jnp.sum(v, axis=1, keepdims=True) / T
        dev = v - mean
        m2 = jnp.sum(dev * dev, axis=1, keepdims=True)
        cols[rows, :] = jnp.where(lane == 0, mean, jnp.where(lane == 1, m2, 0.0))

    pick = (lax.broadcasted_iota(jnp.int32, (8, 128), 0)
            == lax.broadcasted_iota(jnp.int32, (8, 128), 1)).astype(jnp.float32)
    line = lax.dot_general(pick, cols[...], NT, precision=lax.Precision.HIGHEST,
                           preferred_element_type=jnp.float32)
    stats[b] = line[:2]

    pl.semaphore_wait(barrier, B - 1 + L - 1)

    def stat_copy(source, peer):
        return pltpu.make_async_remote_copy(
            src_ref=stats.at[source], dst_ref=stats.at[source],
            send_sem=st_send.at[peer], recv_sem=st_recv.at[source],
            device_id=(l, peer), device_id_type=MESH)

    for d in range(1, B):
        stat_copy(b, lax.rem(b + d, B)).start()
    for d in range(1, B):
        other = lax.rem(b + d, B)
        stat_copy(other, other).wait_recv()

    mean = stats[0, 0:1]
    for k in range(1, B):
        mean = mean + stats[k, 0:1]
    mean = mean / B
    square = jnp.zeros_like(mean)
    for k in range(B):
        shift = stats[k, 0:1] - mean
        square = square + (stats[k, 1:2] + T * (shift * shift))
    scale = lax.rsqrt(square / total + epsilon)
    sub = lax.broadcasted_iota(jnp.int32, (8, R), 0)
    both = jnp.where(sub == 0, mean, jnp.where(sub == 1, scale, 0.0))
    cols[...] = lax.dot_general(both, pick, TN, precision=lax.Precision.HIGHEST,
                                preferred_element_type=jnp.float32)

    def normalise(piece):
        size = bounds[piece + 1] - bounds[piece]
        step = largest_tile(size, 128)

        @pl.loop(0, size // step)
        def _(i):
            rows = pl.ds(pl.multiple_of(bounds[piece] + i * step, 16), step)
            z = (x_ref[rows, :] - cols[rows, 0:1]) * cols[rows, 1:2]
            zbuf[b, rows, :] = z.astype(jnp.bfloat16)

    def piece_copy(k, piece, send_sem, peer):
        part = zbuf.at[k, pl.ds(bounds[piece], bounds[piece + 1] - bounds[piece]), :]
        return pltpu.make_async_remote_copy(
            src_ref=part, dst_ref=part, send_sem=send_sem.at[k, piece],
            recv_sem=z_recv.at[k, piece], device_id=(l, peer), device_id_type=MESH)

    def share_copy(k, block, peer):
        return pltpu.make_async_remote_copy(
            src_ref=shr.at[k, block], dst_ref=shr.at[k, block], send_sem=shr_send.at[k, peer],
            recv_sem=shr_recv.at[k, block], device_id=(peer, b), device_id_type=MESH)

    has_up, has_down = q + 1 < Q, q >= 1
    start = b * share
    first = pl.multiple_of(jnp.minimum(start // 16 * 16, R - W), 16)
    need_below = PIECES - 1 - sum((first >= x).astype(jnp.int32) for x in bounds[1:-1])
    need_above = sum((first + W > x).astype(jnp.int32) for x in bounds[1:-1])

    def extract(k):
        window = zbuf[k, pl.ds(first, W), :]
        hot = (lax.broadcasted_iota(jnp.int32, (SP, W), 1)
               == lax.broadcasted_iota(jnp.int32, (SP, W), 0) + (start - first))
        inside = lax.broadcasted_iota(jnp.int32, (SP, W), 0) < share
        hot = jnp.where(hot & inside, 1.0, 0.0).astype(jnp.bfloat16)
        rows = lax.dot_general(hot, window, (((1,), (0,)), ((), ())),
                               preferred_element_type=jnp.float32)
        shr[k, l] = rows.astype(jnp.bfloat16)
        for d in range(1, L):
            share_copy(k, l, lax.rem(l + d, L)).start()

    def wait_shares(place):
        for core in range(2):
            k = place * 2 + core
            for d in range(1, L):
                other = lax.rem(l + d, L)
                share_copy(k, other, other).wait_recv()

    def multiply(place):
        part = None
        wait_shares(place)
        for core in range(2):
            k = place * 2 + core
            a = shr[k].reshape(L * SP, T)
            term = lax.dot_general(a, zbuf[k], NT, preferred_element_type=jnp.float32)
            part = term if part is None else part + term
        acc[...] += part

    def multiply_step(s):
        @pl.loop(0, 2)
        def _(n):
            place = q - (1 - 2 * n) * s

            @pl.when((place >= 0) & (place < Q) & ((s > 0) | (n < 1)))
            def _():
                multiply(place)

    def send_own(up_first):
        done = set()

        def send(up, i):
            piece = PIECES - 1 - i if up else i
            if piece not in done:
                done.add(piece)
                normalise(piece)

            @pl.when(has_up if up else has_down)
            def _():
                if up:
                    piece_copy(b, piece, up_send, b + 2).start()
                else:
                    piece_copy(b, piece, down_send, b - 2).start()

        for i in range(PIECES):
            send(up_first, i)
            send(not up_first, i)

    @pl.when(q >= Q // 2)
    def _():
        send_own(True)

    @pl.when(q < Q // 2)
    def _():
        send_own(False)

    for i in range(PIECES):
        piece_copy(b, i, mate_send, mate).start()

    acc[...] = jnp.zeros_like(acc)
    extract(b)

    for i in range(PIECES):
        piece_copy(mate, i, mate_send, mate).wait_recv()

    extract(mate)

    def arrive(s, i, between=None):
        below, above = b - 2 * s, b + 2 * s
        from_below, from_above = q - s >= 0, q + s < Q
        down_piece = PIECES - 1 - i

        @pl.when(from_below)
        def _():
            piece_copy(below, down_piece, up_send, b).wait_recv()

            @pl.when(has_up)
            def _():
                piece_copy(below, down_piece, up_send, b + 2).start()
            piece_copy(below, down_piece, mate_send, mate).start()

        @pl.when(from_above)
        def _():
            piece_copy(above, i, down_send, b).wait_recv()

            @pl.when(has_down)
            def _():
                piece_copy(above, i, down_send, b - 2).start()
            piece_copy(above, i, mate_send, mate).start()

        @pl.when(from_below & (i == need_below))
        def _():
            extract(below)

        @pl.when(from_above & (i == need_above))
        def _():
            extract(above)

        if between is not None:
            between()

        @pl.when(from_below)
        def _():
            piece_copy(mate - 2 * s, down_piece, mate_send, mate).wait_recv()

            @pl.when(i == need_below)
            def _():
                extract(mate - 2 * s)

        @pl.when(from_above)
        def _():
            piece_copy(mate + 2 * s, i, mate_send, mate).wait_recv()

            @pl.when(i == need_above)
            def _():
                extract(mate + 2 * s)

        if i == 0:
            multiply_step(s - 1)

    def finish(piece, place):
        lo, hi = bounds[piece], bounds[piece + 1]
        part = acc[:, lo:hi]
        if place is not None:
            for core in range(2):
                k = place * 2 + core
                a = shr[k].reshape(L * SP, T)
                part = part + lax.dot_general(a, zbuf[k, lo:hi, :], NT,
                                              preferred_element_type=jnp.float32)
        part = part / total
        for j in range(L):
            o_ref[:, j, lo:hi] = part[j * SP:j * SP + share]

    @pl.loop(1, Q - 1)
    def _(s):
        for i in range(PIECES):
            arrive(s, i)

    def finish_ends(steps):
        for end, place in ((Q - 1, 0), (0, Q - 1)):
            @pl.when(q == end)
            def _():
                for i in steps:
                    finish(PIECES - 1 - i if end else i, place)

    def finish_early():
        for end, place in ((Q - 1, 0), (0, Q - 1)):
            @pl.when(q == end)
            def _():
                wait_shares(place)

        finish_ends(range(PIECES - 1))

    for i in range(PIECES):
        arrive(Q - 1, i, finish_early if i == PIECES - 1 else None)
    finish_ends([PIECES - 1])

    @pl.when((q > 0) & (q < Q - 1))
    def _():
        for i in range(PIECES):
            finish(i, None)

    for d in range(1, B):
        other = lax.rem(b + d, B)
        stat_copy(b, other).wait_send()

    @pl.loop(0, Q)
    def _(s):
        below, above = b - 2 * s, b + 2 * s
        from_below, from_above = q - s >= 0, q + s < Q

        for i in range(PIECES):
            @pl.when(from_below & has_up)
            def _():
                piece_copy(below, i, up_send, b + 2).wait_send()

            @pl.when(from_above & has_down)
            def _():
                piece_copy(above, i, down_send, b - 2).wait_send()

            @pl.when(from_below)
            def _():
                piece_copy(below, i, mate_send, mate).wait_send()

            @pl.when(from_above & (s > 0))
            def _():
                piece_copy(above, i, mate_send, mate).wait_send()

    @pl.loop(0, B)
    def _(k):
        for d in range(1, L):
            other = lax.rem(l + d, L)
            share_copy(k, l, other).wait_send()


F, M, C, N, D = range(5)


def line_kernel(L, B, x_hbm, o_ref, zbuf, shr, acc_lo, acc_hi, acc_mid, tile_send, tile_recv, shift_ref, place_ref,
                cols, stats, x_ref, raw,
                z_recv, out_send, in_send, mate_send, own_send, own_out, own_in, first_send, raw_recv, raw_send, shr_recv, shr_send, diag_recv, diag_send, t_recv, t_send,
                st_recv, st_send, x_sem):
    R, T = x_hbm.shape
    total = T * B
    share = R // B
    half = 2 * share
    SP = shr.shape[2]
    pad = share - 128
    W = min(up_to(share + 15, 16), R)
    low, high = R - (3 * half - pad) // 16 * 16, (3 * half - pad) // 16 * 16
    edges = [0, low, (R // 2 - pad) // 16 * 16, up_to(R // 2 + pad, 16), high, R]
    size = [edges[p + 1] - edges[p] for p in range(5)]
    far = size[F] + size[C] + size[D]
    tile = largest_tile(R, 352)
    RAW = raw.shape[1]
    WS = acc_lo.shape[1]
    hi_lane, mid_lane = R - WS, WS // 128 * 128
    WM = acc_mid.shape[1]
    l, b = lax.axis_index("loop"), lax.axis_index("bulk")
    q, c = b // 2, b % 2
    mate = q * 2 + (1 - c)
    upper = q >= 2
    inner = (q == 1) | (q == 2)
    outer = (q == 0) | (q == 3)
    step = jnp.where(upper, 1, -1)
    H = [jnp.where(upper, h, 3 - h) for h in range(4)]
    out_nbr, in_nbr = b + 2 * step, b - 2 * step
    lx, ly, ld = l + 1 - 2 * (l % 2), lax.rem(l + 2, 4), 3 - l

    def align(value, unit=16):
        return pl.multiple_of(value, unit)

    start = [align(jnp.where(upper, edges[p], edges[4 - p])) for p in range(5)]

    barrier = pltpu.get_barrier_semaphore()
    for d in range(1, B):
        pl.semaphore_signal(barrier, inc=1, device_id=(l, lax.rem(b + d, B)), device_id_type=MESH)
    facing = [jnp.where(inner, 3 * side, 1 + side) for side in range(2)]
    for d in range(1, L):
        other = lax.rem(l + d, L)
        pl.semaphore_signal(barrier, inc=1, device_id=(other, b), device_id_type=MESH)
        for side in range(2):
            for core in range(2):
                pl.semaphore_signal(barrier, inc=1, device_id=(other, facing[side] * 2 + core),
                                    device_id_type=MESH)

    def load(i):
        rows = pl.ds(pl.multiple_of(i * tile, tile), tile)
        return pltpu.make_async_copy(x_hbm.at[rows, :], x_ref.at[rows, :], x_sem.at[i])

    @pl.loop(0, R // tile)
    def _(i):
        load(i).start()

    lane = lax.broadcasted_iota(jnp.int32, (tile, 128), 1)

    @pl.loop(0, R // tile)
    def _(i):
        rows = pl.ds(pl.multiple_of(i * tile, tile), tile)
        load(i).wait()
        v = x_ref[rows, :]
        mean = jnp.sum(v, axis=1, keepdims=True) / T
        dev = v - mean
        m2 = jnp.sum(dev * dev, axis=1, keepdims=True)
        cols[rows, :] = jnp.where(lane == 0, mean, jnp.where(lane == 1, m2, 0.0))

    pick = (lax.broadcasted_iota(jnp.int32, (8, 128), 0)
            == lax.broadcasted_iota(jnp.int32, (8, 128), 1)).astype(jnp.float32)
    line = lax.dot_general(pick, cols[...], NT, precision=lax.Precision.HIGHEST,
                           preferred_element_type=jnp.float32)
    stats[b] = line[:2]

    pl.semaphore_wait(barrier, B - 1 + 5 * (L - 1))

    def stat_copy(source, peer):
        return pltpu.make_async_remote_copy(
            src_ref=stats.at[source], dst_ref=stats.at[source],
            send_sem=st_send, recv_sem=st_recv,
            device_id=(l, peer), device_id_type=MESH)

    for d in range(1, B):
        stat_copy(b, lax.rem(b + d, B)).start()
    def raw_copy(p, slot, peer):
        return pltpu.make_async_remote_copy(
            src_ref=x_ref.at[pl.ds(start[p], RAW), :], dst_ref=raw.at[slot], send_sem=raw_send,
            recv_sem=raw_recv.at[slot], device_id=(l, peer), device_id_type=MESH)

    @pl.when(inner)
    def _():
        raw_copy(D, 0, out_nbr).start()
        raw_copy(F, 0, in_nbr).start()

    @pl.when(outer)
    def _():
        raw_copy(D, 1, in_nbr).start()

    gathered = stats.at[pl.ds(0, B - 1)]
    all_stats = pltpu.make_async_remote_copy(
        src_ref=gathered, dst_ref=gathered, send_sem=st_send, recv_sem=st_recv,
        device_id=(l, b), device_id_type=MESH)
    all_stats.wait_recv()

    mean = stats[0, 0:1]
    for k in range(1, B):
        mean = mean + stats[k, 0:1]
    mean = mean / B
    square = jnp.zeros_like(mean)
    for k in range(B):
        shift = stats[k, 0:1] - mean
        square = square + (stats[k, 1:2] + T * (shift * shift))
    scale = lax.rsqrt(square / total + epsilon)
    sub = lax.broadcasted_iota(jnp.int32, (8, R), 0)
    both = jnp.where(sub == 0, mean, jnp.where(sub == 1, scale, 0.0))
    cols[...] = lax.dot_general(both, pick, TN, precision=lax.Precision.HIGHEST,
                                preferred_element_type=jnp.float32)

    def normalise(begin, count):
        unit = count if count <= 288 else largest_tile(count, 128)

        def chunk(i):
            rows = pl.ds(pl.multiple_of(begin + i * unit, 16), unit)
            z = (x_ref[rows, :] - cols[rows, 0:1]) * cols[rows, 1:2]
            zbuf[b, rows, :] = z.astype(jnp.bfloat16)

        if unit == count:
            chunk(0)
        else:
            pl.loop(0, count // unit)(chunk)

    def z_copy(k, p, send_sem, peer, skip=0):
        part = zbuf.at[k, pl.ds(align(start[p] + skip), size[p] - skip), :]
        return pltpu.make_async_remote_copy(
            src_ref=part, dst_ref=part, send_sem=send_sem,
            recv_sem=z_recv.at[k, jnp.where(upper, p, 4 - p)], device_id=(l, peer), device_id_type=MESH)

    def first_copy(k, p, peer):
        return z_copy(k, p, first_send, peer, RAW)

    def unpack(slot, k):
        raw_copy(D, slot, b).wait_recv()
        rows = pl.ds(start[D], RAW)
        z = (raw[slot] - cols[rows, 0:1]) * cols[rows, 1:2]
        zbuf[k, rows, :] = z.astype(jnp.bfloat16)

    def send_out(k, p):
        return z_copy(k, p, out_send, out_nbr)

    def send_in(k, p):
        return z_copy(k, p, in_send, in_nbr)

    def mate_copy(k, p):
        return z_copy(k, p, mate_send, mate)

    def mate_own(k):
        part = zbuf.at[k]
        return pltpu.make_async_remote_copy(
            src_ref=part, dst_ref=part, send_sem=own_send, recv_sem=z_recv.at[k, 0],
            device_id=(l, mate), device_id_type=MESH)

    def share_copy(k, block, peer, way):
        return pltpu.make_async_remote_copy(
            src_ref=shr.at[k, block], dst_ref=shr.at[k, block], send_sem=shr_send,
            recv_sem=shr_recv.at[k, way], device_id=(peer, b), device_id_type=MESH)

    cut = up_to(SP // 2, 16)

    def diag_copy(k, block, peer, way):
        rows = pl.ds(0, cut) if way == 0 else pl.ds(cut, SP - cut)
        part = shr.at[k, block, rows, :]
        return pltpu.make_async_remote_copy(
            src_ref=part, dst_ref=part, send_sem=diag_send,
            recv_sem=diag_recv.at[k // 2], device_id=(peer, b), device_id_type=MESH)

    first = align(jnp.minimum(b * share // 16 * 16, jnp.where(q == 0, size[D], R) - W))

    def extract(place):
        @pl.loop(0, 2)
        def _(core):
            k = place * 2 + core
            window = zbuf[k, pl.ds(first, W), :]
            row = lax.broadcasted_iota(jnp.int32, (SP, W), 0)
            hot = lax.broadcasted_iota(jnp.int32, (SP, W), 1) == row + (b * share - first)
            hot = jnp.where(hot & (row < share), 1.0, 0.0).astype(jnp.bfloat16)
            rows = lax.dot_general(hot, window, (((1,), (0,)), ((), ())),
                                   preferred_element_type=jnp.float32)
            shr[k, l] = rows.astype(jnp.bfloat16)
            share_copy(k, l, lx, 0).start()
            share_copy(k, l, ly, 1).start()

    def pass_on(place):
        @pl.loop(0, 2)
        def _(core):
            k = place * 2 + core
            share_copy(k, lx, lx, 0).wait_recv()
            diag_copy(k, lx, ly, 0).start()
            share_copy(k, ly, ly, 1).wait_recv()
            diag_copy(k, ly, lx, 1).start()

    def wait_diag(place):
        part = shr.at[pl.ds(place * 2, 2), ld]
        pltpu.make_async_remote_copy(
            src_ref=part, dst_ref=part, send_sem=diag_send, recv_sem=diag_recv.at[place],
            device_id=(l, b), device_id_type=MESH).wait_recv()

    def product(place, begin, width):
        part = None
        for core in range(2):
            k = place * 2 + core
            term = lax.dot_general(shr[k].reshape(L * SP, T), zbuf[k, begin:begin + width, :], NT,
                                   preferred_element_type=jnp.float32)
            part = term if part is None else part + term
        return part

    def add_sides(place):
        acc_lo[...] += product(place, 0, WS)
        acc_hi[...] += product(place, hi_lane, WS)

    def add_middle(place):
        acc_mid[...] += product(place, mid_lane, WM)

    def own(h):
        return H[h] * 2 + c

    def other(h):
        return H[h] * 2 + (1 - c)

    def take(h, p, onward=None, first=False):
        if first:
            first_copy(own(h), p, mate).wait_recv()
        else:
            mate_copy(own(h), p).wait_recv()
        if onward is not None:
            onward(own(h), p).start()
        mate_copy(own(h), p).start()

    def mate_take(h, pieces):
        for p in pieces:
            mate_copy(other(h), p).wait_recv()

    def tile_copy(side, j, core, block, slot):
        return pltpu.make_async_remote_copy(
            src_ref=tile_send.at[side, j, pl.ds(core * SP, SP), :],
            dst_ref=tile_recv.at[block, :, pl.ds(pl.multiple_of(slot * 128, 128), 128)],
            send_sem=t_send, recv_sem=t_recv.at[block],
            device_id=(j, 6 * side + core), device_id_type=MESH)

    def make_hot():
        shift = (lax.broadcasted_iota(jnp.int32, (SP, 128), 0)
                 == lax.broadcasted_iota(jnp.int32, (SP, 128), 1) + jnp.where(c == 0, pad, 0))
        shift_ref[...] = jnp.where(shift, 1.0, 0.0).astype(jnp.bfloat16)
        row = lax.broadcasted_iota(jnp.int32, (512, WM), 0)
        lane = jnp.where(row < 256, row + half + pad, row - 256 + R // 2 + pad) - mid_lane
        hot = lax.broadcasted_iota(jnp.int32, (512, WM), 1) == lane
        place_ref[...] = jnp.where(hot, 1.0, 0.0).astype(jnp.bfloat16)

    def finish_tiles(j):
        rows = pl.ds(pl.multiple_of(j * SP, SP), SP)
        for side, acc, begin in ((0, acc_lo, 0), (1, acc_hi, hi_lane)):
            value = acc[rows, :]
            for core in range(2):
                k = H[0] * 2 + core
                value = value + lax.dot_general(shr[k, j], zbuf[k, begin:begin + WS, :], NT,
                                                preferred_element_type=jnp.float32)
            acc[rows, :] = value
            turned = lax.dot_general((value / total).astype(jnp.bfloat16), shift_ref[...], TN,
                                     preferred_element_type=jnp.float32)
            for core in range(2):
                at = (WS - half if side else 0) + core * share
                tile_send[side, j, core * SP:core * SP + share, :] = turned[at:at + share].astype(jnp.bfloat16)

    def start_tiles(j):
        for side in range(2):
            for core in range(2):
                tile_copy(side, j, core, l, b - 2).start()

    def wait_tile(block):
        part = tile_recv.at[block]
        pltpu.make_async_remote_copy(
            src_ref=part, dst_ref=part, send_sem=t_send, recv_sem=t_recv.at[block],
            device_id=(l, b), device_id_type=MESH).wait_recv()

    normalise(start[D], size[D])

    @pl.when(inner)
    def _():
        first_copy(b, D, out_nbr).start()

    @pl.when(outer)
    def _():
        first_copy(b, D, in_nbr).start()
    normalise(start[F], size[F])

    @pl.when(inner)
    def _():
        first_copy(b, F, in_nbr).start()
    normalise(low, high - low)

    @pl.when(inner)
    def _():
        for p in (M, C, D):
            z_copy(b, p, own_in, in_nbr).start()
        for p in (F, C):
            z_copy(b, p, own_out, out_nbr).start()

    @pl.when(outer)
    def _():
        for p in (N, C, F, M):
            z_copy(b, p, own_in, in_nbr).start()
    mate_own(b).start()
    make_hot()
    mate_own(mate).wait_recv()
    extract(q)

    @pl.when(inner)
    def _():
        unpack(0, own(1))
        unpack(1, own(3))
        take(1, D, send_out, True)
        take(3, D, None, True)
        pass_on(q)
        take(1, N)
        take(3, N)
        take(1, C, send_out)
        take(3, C)
        mate_take(3, (D, N, C))
        extract(H[3])
        mate_take(1, (D, N, C))
        extract(H[1])

    @pl.when(outer)
    def _():
        unpack(0, own(2))
        take(2, D, None, True)
        mate_take(2, (D,))
        extract(H[2])
        pass_on(q)
        take(2, F)
        take(2, C)
        mate_take(2, (F, C))
    wait_diag(q)
    acc_lo[...] = product(q, 0, WS)
    acc_hi[...] = product(q, hi_lane, WS)
    acc_mid[...] = product(q, mid_lane, WM)

    second, third = jnp.where(inner, H[3], H[2]), H[1]

    @pl.when(inner)
    def _():
        take(1, F, send_out)
        take(3, F, send_in)
        send_in(own(3), C).start()
        pass_on(H[3])
        take(3, M, send_in)
        send_in(own(3), D).start()
        take(0, D, send_out)
        take(0, C, send_out)
        pass_on(H[1])
        take(0, N)
        mate_take(3, (F, M))
        mate_take(0, (D, C, N))
        extract(H[0])

    @pl.when(outer)
    def _():
        pass_on(H[2])
        take(1, D)
        mate_take(1, (D,))
        extract(H[1])
        take(1, C)
    wait_diag(second)
    add_sides(second)
    add_middle(second)

    @pl.when(inner)
    def _():
        take(0, F, send_out)
        z_copy(b, N, own_in, in_nbr).start()
        mate_take(1, (F,))
        mate_take(0, (F,))

    @pl.when(outer)
    def _():
        take(1, F)
        pass_on(H[1])
        take(0, D)
        mate_take(0, (D,))
        extract(H[0])
        take(0, C)
        mate_take(1, (C, F))
    wait_diag(third)
    add_sides(third)

    pass_on(H[0])

    @pl.when(inner)
    def _():
        finish_tiles(l)
        start_tiles(l)

        @pl.loop(0, 2)
        def _(n):
            j = jnp.where(n == 0, lx, ly)
            finish_tiles(j)
            start_tiles(j)
        send_in(own(3), N).start()
        take(1, M)
        wait_diag(H[0])
        finish_tiles(ld)
        start_tiles(ld)
        mate_take(1, (M,))
    add_middle(third)

    @pl.when(inner)
    def _():
        take(0, M)
        mate_take(0, (M,))

    @pl.when(outer)
    def _():
        take(0, F)
        mate_take(0, (C, F))
        wait_diag(H[0])
        add_sides(H[0])
    add_middle(H[0])

    for j in range(L):
        rows = slice(j * SP, j * SP + share)
        o_ref[:, j, :mid_lane] = acc_lo[rows, :mid_lane] / total
        o_ref[:, j, mid_lane:mid_lane + WM] = acc_mid[rows, :] / total
        o_ref[:, j, mid_lane + WM:] = acc_hi[rows, :][:, mid_lane + WM - hi_lane:] / total

    @pl.when(outer)
    def _():
        place = lax.broadcasted_iota(jnp.int32, (share, WM), 1) + mid_lane
        inside = ((place >= half + pad) & (place < half + pad + 256)
                  | (place >= R // 2 + pad) & (place < R // 2 + pad + 256))
        for d in (l, lx, ly, ld):
            wait_tile(d)
            placed = lax.dot_general(tile_recv[d], place_ref[...], (((1,), (0,)), ((), ())),
                                     preferred_element_type=jnp.float32)[:share]
            middle = pl.ds(mid_lane, WM)
            o_ref[:, d, middle] = jnp.where(inside, placed, o_ref[:, d, middle])

    all_stats.wait_send()
    mate_own(b).wait_send()

    def sent(part, sem):
        pltpu.make_async_remote_copy(
            src_ref=part, dst_ref=part, send_sem=sem, recv_sem=st_recv,
            device_id=(l, b), device_id_type=MESH).wait_send()

    @pl.when(inner)
    def _():
        sent(zbuf.at[0, pl.ds(0, size[F] + size[C]), :], own_out)
        sent(zbuf.at[pl.ds(0, 2), pl.ds(0, size[D] - RAW), :], first_send)
        sent(raw, raw_send)
        sent(zbuf.at[pl.ds(0, 2), pl.ds(0, far), :], out_send)
        sent(zbuf.at[0], in_send)
        sent(zbuf.at[pl.ds(0, 3)], mate_send)
        sent(tile_send, t_send)

    @pl.when(outer)
    def _():
        sent(zbuf.at[0, pl.ds(0, size[D] - RAW), :], first_send)
        sent(raw.at[0], raw_send)
        sent(zbuf.at[pl.ds(0, 3), pl.ds(0, far), :], mate_send)

    sent(zbuf.at[0, pl.ds(0, R - size[D]), :], own_in)
    sent(shr.at[pl.ds(0, L)], shr_send)
    sent(shr.at[pl.ds(0, B // L)], diag_send)


def line_call(L, B, series):
    R, T = series.shape
    share = R // B
    SP = up_to(share, 16)
    pad = share - 128
    high = (3 * 2 * share - pad) // 16 * 16
    WS = R - high
    mid_lane = WS // 128 * 128
    WM = up_to(R // 2 + pad + 256, 128) - mid_lane
    vmem = pl.BlockSpec(memory_space=pltpu.VMEM)
    dma = pltpu.SemaphoreType.DMA
    return pl.pallas_call(
        functools.partial(line_kernel, L, B),
        out_shape=jax.ShapeDtypeStruct((share, L, R), jnp.float32),
        in_specs=[pl.BlockSpec(memory_space=pltpu.HBM)],
        out_specs=vmem,
        scratch_shapes=[
            pltpu.VMEM((B, R, T), jnp.bfloat16),
            pltpu.VMEM((B, L, SP, T), jnp.bfloat16),
            pltpu.VMEM((L * SP, WS), jnp.float32),
            pltpu.VMEM((L * SP, WS), jnp.float32),
            pltpu.VMEM((L * SP, WM), jnp.float32),
            pltpu.VMEM((2, L, 2 * SP, 128), jnp.bfloat16),
            pltpu.VMEM((L, SP, 512), jnp.bfloat16),
            pltpu.VMEM((SP, 128), jnp.bfloat16),
            pltpu.VMEM((512, WM), jnp.bfloat16),
            pltpu.VMEM((R, 128), jnp.float32),
            pltpu.VMEM((B, 2, R), jnp.float32),
            pltpu.VMEM((R, T), jnp.float32),
            pltpu.VMEM((2, (R - high) // 32 * 16, T), jnp.float32),
            dma((B, 5)), dma, dma, dma, dma, dma, dma, dma, dma((2,)), dma,
            dma((B, 2)), dma, dma((B // 2,)), dma, dma((L,)), dma,
            dma, dma, dma((R // largest_tile(R, 352),)),
        ],
        compiler_params=pltpu.CompilerParams(
            collective_id=0, has_side_effects=True, vmem_limit_bytes=34 * 1024 * 1024),
    )(pltpu.with_memory_space_constraint(series, pltpu.HBM)).transpose(1, 0, 2)


def solution(mesh):
    L, B = mesh.shape["loop"], mesh.shape["bulk"]

    def on_device(series):
        R, T = series.shape
        share = R // B
        if L == 4 and B == 8 and R % 16 == 0 and T % 128 == 0 and 128 <= share <= 144:
            return line_call(L, B, series)
        SP = up_to(share, 16)
        pieces = 3
        vmem = pl.BlockSpec(memory_space=pltpu.VMEM)
        dma = pltpu.SemaphoreType.DMA
        return pl.pallas_call(
            functools.partial(kernel, L, B, pieces),
            out_shape=jax.ShapeDtypeStruct((share, L, R), jnp.float32),
            in_specs=[pl.BlockSpec(memory_space=pltpu.HBM)],
            out_specs=vmem,
            scratch_shapes=[
                pltpu.VMEM((B, R, T), jnp.bfloat16),
                pltpu.VMEM((B, L, SP, T), jnp.bfloat16),
                pltpu.VMEM((L * SP, R), jnp.float32),
                pltpu.VMEM((R, 128), jnp.float32),
                pltpu.VMEM((B, 2, R), jnp.float32),
                pltpu.VMEM((R, T), jnp.float32),
                dma((B, pieces)), dma((B, pieces)), dma((B, pieces)), dma((B, pieces)),
                dma((B, L)), dma((B, L)), dma((B,)), dma((B,)), dma((R // largest_tile(R, 128),)),
            ],
            compiler_params=pltpu.CompilerParams(
                collective_id=0, has_side_effects=True, vmem_limit_bytes=26 * 1024 * 1024),
        )(pltpu.with_memory_space_constraint(series, pltpu.HBM)).transpose(1, 0, 2)

    return jax.shard_map(
        on_device, mesh=mesh, in_specs=(P("loop", "bulk"),),
        out_specs=P(None, "bulk", "loop"), check_vma=False)
```

```python
import functools
import jax
import jax.numpy as jnp
from jax import lax
from jax.experimental import pallas as pl
from jax.experimental.pallas import tpu as pltpu
from jax.sharding import PartitionSpec as P

epsilon = 1e-06
MESH = pl.DeviceIdType.MESH
NT = (((1,), (1,)), ((), ()))
TN = (((0,), (0,)), ((), ()))


def up_to(value, unit):
    return -(-value // unit) * unit


def largest_tile(rows, limit):
    return max(t for t in range(16, limit + 1, 16) if rows % t == 0)


def kernel(L, B, PIECES, x_hbm, o_ref, zbuf, shr, acc, cols, stats, x_ref,
           z_recv, up_send, down_send, mate_send, shr_recv, shr_send, st_recv, st_send, x_sem):
    R, T = x_hbm.shape
    total = T * B
    Q = B // 2
    share = R // B
    SP = shr.shape[2]
    W = min(up_to(share + 15, 16), R)
    bounds = [up_to(R * i // PIECES, 128) for i in range(PIECES)] + [R]
    tile = largest_tile(R, 128)
    l, b = lax.axis_index("loop"), lax.axis_index("bulk")
    q, c = b // 2, b % 2
    mate = q * 2 + (1 - c)

    barrier = pltpu.get_barrier_semaphore()
    for d in range(1, B):
        pl.semaphore_signal(barrier, inc=1, device_id=(l, lax.rem(b + d, B)), device_id_type=MESH)
    for d in range(1, L):
        pl.semaphore_signal(barrier, inc=1, device_id=(lax.rem(l + d, L), b), device_id_type=MESH)

    def load(i):
        rows = pl.ds(pl.multiple_of(i * tile, tile), tile)
        return pltpu.make_async_copy(x_hbm.at[rows, :], x_ref.at[rows, :], x_sem.at[i])

    @pl.loop(0, R // tile)
    def _(i):
        load(i).start()

    lane = lax.broadcasted_iota(jnp.int32, (tile, 128), 1)

    @pl.loop(0, R // tile)
    def _(i):
        rows = pl.ds(pl.multiple_of(i * tile, tile), tile)
        load(i).wait()
        v = x_ref[rows, :]
        mean = jnp.sum(v, axis=1, keepdims=True) / T
        dev = v - mean
        m2 = jnp.sum(dev * dev, axis=1, keepdims=True)
        cols[rows, :] = jnp.where(lane == 0, mean, jnp.where(lane == 1, m2, 0.0))

    pick = (lax.broadcasted_iota(jnp.int32, (8, 128), 0)
            == lax.broadcasted_iota(jnp.int32, (8, 128), 1)).astype(jnp.float32)
    line = lax.dot_general(pick, cols[...], NT, precision=lax.Precision.HIGHEST,
                           preferred_element_type=jnp.float32)
    stats[b] = line[:2]

    pl.semaphore_wait(barrier, B - 1 + L - 1)

    def stat_copy(source, peer):
        return pltpu.make_async_remote_copy(
            src_ref=stats.at[source], dst_ref=stats.at[source],
            send_sem=st_send.at[peer], recv_sem=st_recv.at[source],
            device_id=(l, peer), device_id_type=MESH)

    for d in range(1, B):
        stat_copy(b, lax.rem(b + d, B)).start()
    for d in range(1, B):
        other = lax.rem(b + d, B)
        stat_copy(other, other).wait_recv()

    mean = stats[0, 0:1]
    for k in range(1, B):
        mean = mean + stats[k, 0:1]
    mean = mean / B
    square = jnp.zeros_like(mean)
    for k in range(B):
        shift = stats[k, 0:1] - mean
        square = square + (stats[k, 1:2] + T * (shift * shift))
    scale = lax.rsqrt(square / total + epsilon)
    sub = lax.broadcasted_iota(jnp.int32, (8, R), 0)
    both = jnp.where(sub == 0, mean, jnp.where(sub == 1, scale, 0.0))
    cols[...] = lax.dot_general(both, pick, TN, precision=lax.Precision.HIGHEST,
                                preferred_element_type=jnp.float32)

    def normalise(piece):
        size = bounds[piece + 1] - bounds[piece]
        step = largest_tile(size, 128)

        @pl.loop(0, size // step)
        def _(i):
            rows = pl.ds(pl.multiple_of(bounds[piece] + i * step, 16), step)
            z = (x_ref[rows, :] - cols[rows, 0:1]) * cols[rows, 1:2]
            zbuf[b, rows, :] = z.astype(jnp.bfloat16)

    def piece_copy(k, piece, send_sem, peer):
        part = zbuf.at[k, pl.ds(bounds[piece], bounds[piece + 1] - bounds[piece]), :]
        return pltpu.make_async_remote_copy(
            src_ref=part, dst_ref=part, send_sem=send_sem.at[k, piece],
            recv_sem=z_recv.at[k, piece], device_id=(l, peer), device_id_type=MESH)

    def share_copy(k, block, peer):
        return pltpu.make_async_remote_copy(
            src_ref=shr.at[k, block], dst_ref=shr.at[k, block], send_sem=shr_send.at[k, peer],
            recv_sem=shr_recv.at[k, block], device_id=(peer, b), device_id_type=MESH)

    has_up, has_down = q + 1 < Q, q >= 1
    start = b * share
    first = pl.multiple_of(jnp.minimum(start // 16 * 16, R - W), 16)
    need_below = PIECES - 1 - sum((first >= x).astype(jnp.int32) for x in bounds[1:-1])
    need_above = sum((first + W > x).astype(jnp.int32) for x in bounds[1:-1])

    def extract(k):
        window = zbuf[k, pl.ds(first, W), :]
        hot = (lax.broadcasted_iota(jnp.int32, (SP, W), 1)
               == lax.broadcasted_iota(jnp.int32, (SP, W), 0) + (start - first))
        inside = lax.broadcasted_iota(jnp.int32, (SP, W), 0) < share
        hot = jnp.where(hot & inside, 1.0, 0.0).astype(jnp.bfloat16)
        rows = lax.dot_general(hot, window, (((1,), (0,)), ((), ())),
                               preferred_element_type=jnp.float32)
        shr[k, l] = rows.astype(jnp.bfloat16)
        for d in range(1, L):
            share_copy(k, l, lax.rem(l + d, L)).start()

    def wait_shares(place):
        for core in range(2):
            k = place * 2 + core
            for d in range(1, L):
                other = lax.rem(l + d, L)
                share_copy(k, other, other).wait_recv()

    def multiply(place):
        part = None
        wait_shares(place)
        for core in range(2):
            k = place * 2 + core
            a = shr[k].reshape(L * SP, T)
            term = lax.dot_general(a, zbuf[k], NT, preferred_element_type=jnp.float32)
            part = term if part is None else part + term
        acc[...] += part

    def multiply_step(s):
        @pl.loop(0, 2)
        def _(n):
            place = q - (1 - 2 * n) * s

            @pl.when((place >= 0) & (place < Q) & ((s > 0) | (n < 1)))
            def _():
                multiply(place)

    def send_own(up_first):
        done = set()

        def send(up, i):
            piece = PIECES - 1 - i if up else i
            if piece not in done:
                done.add(piece)
                normalise(piece)

            @pl.when(has_up if up else has_down)
            def _():
                if up:
                    piece_copy(b, piece, up_send, b + 2).start()
                else:
                    piece_copy(b, piece, down_send, b - 2).start()

        for i in range(PIECES):
            send(up_first, i)
            send(not up_first, i)

    @pl.when(q >= Q // 2)
    def _():
        send_own(True)

    @pl.when(q < Q // 2)
    def _():
        send_own(False)

    for i in range(PIECES):
        piece_copy(b, i, mate_send, mate).start()

    acc[...] = jnp.zeros_like(acc)
    extract(b)

    for i in range(PIECES):
        piece_copy(mate, i, mate_send, mate).wait_recv()

    extract(mate)

    def arrive(s, i, between=None):
        below, above = b - 2 * s, b + 2 * s
        from_below, from_above = q - s >= 0, q + s < Q
        down_piece = PIECES - 1 - i

        @pl.when(from_below)
        def _():
            piece_copy(below, down_piece, up_send, b).wait_recv()

            @pl.when(has_up)
            def _():
                piece_copy(below, down_piece, up_send, b + 2).start()
            piece_copy(below, down_piece, mate_send, mate).start()

        @pl.when(from_above)
        def _():
            piece_copy(above, i, down_send, b).wait_recv()

            @pl.when(has_down)
            def _():
                piece_copy(above, i, down_send, b - 2).start()
            piece_copy(above, i, mate_send, mate).start()

        @pl.when(from_below & (i == need_below))
        def _():
            extract(below)

        @pl.when(from_above & (i == need_above))
        def _():
            extract(above)

        if between is not None:
            between()

        @pl.when(from_below)
        def _():
            piece_copy(mate - 2 * s, down_piece, mate_send, mate).wait_recv()

            @pl.when(i == need_below)
            def _():
                extract(mate - 2 * s)

        @pl.when(from_above)
        def _():
            piece_copy(mate + 2 * s, i, mate_send, mate).wait_recv()

            @pl.when(i == need_above)
            def _():
                extract(mate + 2 * s)

        if i == 0:
            multiply_step(s - 1)

    def finish(piece, place):
        lo, hi = bounds[piece], bounds[piece + 1]
        part = acc[:, lo:hi]
        if place is not None:
            for core in range(2):
                k = place * 2 + core
                a = shr[k].reshape(L * SP, T)
                part = part + lax.dot_general(a, zbuf[k, lo:hi, :], NT,
                                              preferred_element_type=jnp.float32)
        part = part / total
        for j in range(L):
            o_ref[:, j, lo:hi] = part[j * SP:j * SP + share]

    @pl.loop(1, Q - 1)
    def _(s):
        for i in range(PIECES):
            arrive(s, i)

    def finish_ends(steps):
        for end, place in ((Q - 1, 0), (0, Q - 1)):
            @pl.when(q == end)
            def _():
                for i in steps:
                    finish(PIECES - 1 - i if end else i, place)

    def finish_early():
        for end, place in ((Q - 1, 0), (0, Q - 1)):
            @pl.when(q == end)
            def _():
                wait_shares(place)

        finish_ends(range(PIECES - 1))

    for i in range(PIECES):
        arrive(Q - 1, i, finish_early if i == PIECES - 1 else None)
    finish_ends([PIECES - 1])

    @pl.when((q > 0) & (q < Q - 1))
    def _():
        for i in range(PIECES):
            finish(i, None)

    for d in range(1, B):
        other = lax.rem(b + d, B)
        stat_copy(b, other).wait_send()

    @pl.loop(0, Q)
    def _(s):
        below, above = b - 2 * s, b + 2 * s
        from_below, from_above = q - s >= 0, q + s < Q

        for i in range(PIECES):
            @pl.when(from_below & has_up)
            def _():
                piece_copy(below, i, up_send, b + 2).wait_send()

            @pl.when(from_above & has_down)
            def _():
                piece_copy(above, i, down_send, b - 2).wait_send()

            @pl.when(from_below)
            def _():
                piece_copy(below, i, mate_send, mate).wait_send()

            @pl.when(from_above & (s > 0))
            def _():
                piece_copy(above, i, mate_send, mate).wait_send()

    @pl.loop(0, B)
    def _(k):
        for d in range(1, L):
            other = lax.rem(l + d, L)
            share_copy(k, l, other).wait_send()


F, M, C, N, D = range(5)


def line_kernel(L, B, x_hbm, o_ref, zbuf, shr, acc_lo, acc_hi, acc_mid, tile_send, tile_recv, shift_ref, place_ref,
                cols, stats, x_ref, raw,
                z_recv, out_send, in_send, mate_send, own_send, own_out, own_in, first_send, raw_recv, raw_send, shr_recv, shr_send, diag_recv, diag_send, t_recv, t_send,
                st_recv, st_send, x_sem):
    R, T = x_hbm.shape
    total = T * B
    share = R // B
    half = 2 * share
    SP = shr.shape[2]
    pad = share - 128
    W = min(up_to(share + 15, 16), R)
    low, high = R - (3 * half - pad) // 16 * 16, (3 * half - pad) // 16 * 16
    edges = [0, low, (R // 2 - pad) // 16 * 16, up_to(R // 2 + pad, 16), high, R]
    size = [edges[p + 1] - edges[p] for p in range(5)]
    far = size[F] + size[C] + size[D]
    tile = largest_tile(R, 352)
    RAW = raw.shape[1]
    WS = acc_lo.shape[1]
    hi_lane, mid_lane = R - WS, WS // 128 * 128
    WM = acc_mid.shape[1]
    l, b = lax.axis_index("loop"), lax.axis_index("bulk")
    q, c = b // 2, b % 2
    mate = q * 2 + (1 - c)
    upper = q >= 2
    inner = (q == 1) | (q == 2)
    outer = (q == 0) | (q == 3)
    step = jnp.where(upper, 1, -1)
    H = [jnp.where(upper, h, 3 - h) for h in range(4)]
    out_nbr, in_nbr = b + 2 * step, b - 2 * step
    lx, ly, ld = l + 1 - 2 * (l % 2), lax.rem(l + 2, 4), 3 - l

    def align(value, unit=16):
        return pl.multiple_of(value, unit)

    start = [align(jnp.where(upper, edges[p], edges[4 - p])) for p in range(5)]

    barrier = pltpu.get_barrier_semaphore()
    for d in range(1, B):
        pl.semaphore_signal(barrier, inc=1, device_id=(l, lax.rem(b + d, B)), device_id_type=MESH)
    for line in (lx, ly):
        pl.semaphore_signal(barrier, inc=1, device_id=(line, b), device_id_type=MESH)

    def load(i):
        rows = pl.ds(pl.multiple_of(i * tile, tile), tile)
        return pltpu.make_async_copy(x_hbm.at[rows, :], x_ref.at[rows, :], x_sem.at[i])

    @pl.loop(0, R // tile)
    def _(i):
        load(i).start()

    lane = lax.broadcasted_iota(jnp.int32, (tile, 128), 1)

    @pl.loop(0, R // tile)
    def _(i):
        rows = pl.ds(pl.multiple_of(i * tile, tile), tile)
        load(i).wait()
        v = x_ref[rows, :]
        mean = jnp.sum(v, axis=1, keepdims=True) / T
        dev = v - mean
        m2 = jnp.sum(dev * dev, axis=1, keepdims=True)
        cols[rows, :] = jnp.where(lane == 0, mean, jnp.where(lane == 1, m2, 0.0))

    pick = (lax.broadcasted_iota(jnp.int32, (8, 128), 0)
            == lax.broadcasted_iota(jnp.int32, (8, 128), 1)).astype(jnp.float32)
    line = lax.dot_general(pick, cols[...], NT, precision=lax.Precision.HIGHEST,
                           preferred_element_type=jnp.float32)
    stats[b] = line[:2]

    pl.semaphore_wait(barrier, B - 1 + 2)

    def stat_copy(source, peer):
        return pltpu.make_async_remote_copy(
            src_ref=stats.at[source], dst_ref=stats.at[source],
            send_sem=st_send, recv_sem=st_recv,
            device_id=(l, peer), device_id_type=MESH)

    for d in range(1, B):
        stat_copy(b, lax.rem(b + d, B)).start()
    def raw_copy(p, slot, peer):
        return pltpu.make_async_remote_copy(
            src_ref=x_ref.at[pl.ds(start[p], RAW), :], dst_ref=raw.at[slot], send_sem=raw_send,
            recv_sem=raw_recv.at[slot], device_id=(l, peer), device_id_type=MESH)

    @pl.when(inner)
    def _():
        raw_copy(D, 0, out_nbr).start()
        raw_copy(F, 0, in_nbr).start()

    @pl.when(outer)
    def _():
        raw_copy(D, 1, in_nbr).start()

    gathered = stats.at[pl.ds(0, B - 1)]
    all_stats = pltpu.make_async_remote_copy(
        src_ref=gathered, dst_ref=gathered, send_sem=st_send, recv_sem=st_recv,
        device_id=(l, b), device_id_type=MESH)
    all_stats.wait_recv()

    mean = stats[0, 0:1]
    for k in range(1, B):
        mean = mean + stats[k, 0:1]
    mean = mean / B
    square = jnp.zeros_like(mean)
    for k in range(B):
        shift = stats[k, 0:1] - mean
        square = square + (stats[k, 1:2] + T * (shift * shift))
    scale = lax.rsqrt(square / total + epsilon)
    sub = lax.broadcasted_iota(jnp.int32, (8, R), 0)
    both = jnp.where(sub == 0, mean, jnp.where(sub == 1, scale, 0.0))
    cols[...] = lax.dot_general(both, pick, TN, precision=lax.Precision.HIGHEST,
                                preferred_element_type=jnp.float32)

    def normalise(begin, count):
        unit = count if count <= 288 else largest_tile(count, 128)

        def chunk(i):
            rows = pl.ds(pl.multiple_of(begin + i * unit, 16), unit)
            z = (x_ref[rows, :] - cols[rows, 0:1]) * cols[rows, 1:2]
            zbuf[b, rows, :] = z.astype(jnp.bfloat16)

        if unit == count:
            chunk(0)
        else:
            pl.loop(0, count // unit)(chunk)

    def z_copy(k, p, send_sem, peer, skip=0):
        part = zbuf.at[k, pl.ds(align(start[p] + skip), size[p] - skip), :]
        return pltpu.make_async_remote_copy(
            src_ref=part, dst_ref=part, send_sem=send_sem,
            recv_sem=z_recv.at[k, jnp.where(upper, p, 4 - p)], device_id=(l, peer), device_id_type=MESH)

    def first_copy(k, p, peer):
        return z_copy(k, p, first_send, peer, RAW)

    def unpack(slot, k):
        raw_copy(D, slot, b).wait_recv()
        rows = pl.ds(start[D], RAW)
        z = (raw[slot] - cols[rows, 0:1]) * cols[rows, 1:2]
        zbuf[k, rows, :] = z.astype(jnp.bfloat16)

    def send_out(k, p):
        return z_copy(k, p, out_send, out_nbr)

    def send_in(k, p):
        return z_copy(k, p, in_send, in_nbr)

    def mate_copy(k, p):
        return z_copy(k, p, mate_send, mate)

    def mate_own(k):
        part = zbuf.at[k]
        return pltpu.make_async_remote_copy(
            src_ref=part, dst_ref=part, send_sem=own_send, recv_sem=z_recv.at[k, 0],
            device_id=(l, mate), device_id_type=MESH)

    def share_copy(k, block, peer, way):
        return pltpu.make_async_remote_copy(
            src_ref=shr.at[k, block], dst_ref=shr.at[k, block], send_sem=shr_send,
            recv_sem=shr_recv.at[k, way], device_id=(peer, b), device_id_type=MESH)

    cut = up_to(SP // 2, 16)

    def diag_copy(k, block, peer, way):
        rows = pl.ds(0, cut) if way == 0 else pl.ds(cut, SP - cut)
        part = shr.at[k, block, rows, :]
        return pltpu.make_async_remote_copy(
            src_ref=part, dst_ref=part, send_sem=diag_send,
            recv_sem=diag_recv.at[k // 2], device_id=(peer, b), device_id_type=MESH)

    first = align(jnp.minimum(b * share // 16 * 16, jnp.where(q == 0, size[D], R) - W))

    def extract_one(k):
        window = zbuf[k, pl.ds(first, W), :]
        row = lax.broadcasted_iota(jnp.int32, (SP, W), 0)
        hot = lax.broadcasted_iota(jnp.int32, (SP, W), 1) == row + (b * share - first)
        hot = jnp.where(hot & (row < share), 1.0, 0.0).astype(jnp.bfloat16)
        rows = lax.dot_general(hot, window, (((1,), (0,)), ((), ())),
                               preferred_element_type=jnp.float32)
        shr[k, l] = rows.astype(jnp.bfloat16)
        share_copy(k, l, lx, 0).start()
        share_copy(k, l, ly, 1).start()

    def extract(place):
        @pl.loop(0, 2)
        def _(core):
            extract_one(place * 2 + core)

    def pass_on(place):
        @pl.loop(0, 2)
        def _(core):
            k = place * 2 + core
            share_copy(k, lx, lx, 0).wait_recv()
            diag_copy(k, lx, ly, 0).start()
            share_copy(k, ly, ly, 1).wait_recv()
            diag_copy(k, ly, lx, 1).start()

    def wait_diag(place):
        part = shr.at[pl.ds(place * 2, 2), ld]
        pltpu.make_async_remote_copy(
            src_ref=part, dst_ref=part, send_sem=diag_send, recv_sem=diag_recv.at[place],
            device_id=(l, b), device_id_type=MESH).wait_recv()

    def product(place, begin, width):
        part = None
        for core in range(2):
            k = place * 2 + core
            term = lax.dot_general(shr[k].reshape(L * SP, T), zbuf[k, begin:begin + width, :], NT,
                                   preferred_element_type=jnp.float32)
            part = term if part is None else part + term
        return part

    def add_sides(place):
        acc_lo[...] += product(place, 0, WS)
        acc_hi[...] += product(place, hi_lane, WS)

    def add_middle(place):
        acc_mid[...] += product(place, mid_lane, WM)

    def own(h):
        return H[h] * 2 + c

    def other(h):
        return H[h] * 2 + (1 - c)

    def take(h, p, onward=None, first=False):
        if first:
            first_copy(own(h), p, mate).wait_recv()
        else:
            mate_copy(own(h), p).wait_recv()
        if onward is not None:
            onward(own(h), p).start()
        mate_copy(own(h), p).start()

    def mate_take(h, pieces):
        for p in pieces:
            mate_copy(other(h), p).wait_recv()

    def tile_copy(side, j, core, block, slot):
        return pltpu.make_async_remote_copy(
            src_ref=tile_send.at[side, j, pl.ds(core * SP, SP), :],
            dst_ref=tile_recv.at[block, :, pl.ds(pl.multiple_of(slot * 128, 128), 128)],
            send_sem=t_send, recv_sem=t_recv.at[block],
            device_id=(j, 6 * side + core), device_id_type=MESH)

    def make_hot():
        shift = (lax.broadcasted_iota(jnp.int32, (SP, 128), 0)
                 == lax.broadcasted_iota(jnp.int32, (SP, 128), 1) + jnp.where(c == 0, pad, 0))
        shift_ref[...] = jnp.where(shift, 1.0, 0.0).astype(jnp.bfloat16)
        row = lax.broadcasted_iota(jnp.int32, (512, WM), 0)
        lane = jnp.where(row < 256, row + half + pad, row - 256 + R // 2 + pad) - mid_lane
        hot = lax.broadcasted_iota(jnp.int32, (512, WM), 1) == lane
        place_ref[...] = jnp.where(hot, 1.0, 0.0).astype(jnp.bfloat16)

    def finish_tiles(j):
        rows = pl.ds(pl.multiple_of(j * SP, SP), SP)
        for side, acc, begin in ((0, acc_lo, 0), (1, acc_hi, hi_lane)):
            value = acc[rows, :]
            for core in range(2):
                k = H[0] * 2 + core
                value = value + lax.dot_general(shr[k, j], zbuf[k, begin:begin + WS, :], NT,
                                                preferred_element_type=jnp.float32)
            acc[rows, :] = value
            turned = lax.dot_general((value / total).astype(jnp.bfloat16), shift_ref[...], TN,
                                     preferred_element_type=jnp.float32)
            for core in range(2):
                at = (WS - half if side else 0) + core * share
                tile_send[side, j, core * SP:core * SP + share, :] = turned[at:at + share].astype(jnp.bfloat16)

    def start_tiles(j):
        for side in range(2):
            for core in range(2):
                tile_copy(side, j, core, l, b - 2).start()

    def wait_tile(block):
        part = tile_recv.at[block]
        pltpu.make_async_remote_copy(
            src_ref=part, dst_ref=part, send_sem=t_send, recv_sem=t_recv.at[block],
            device_id=(l, b), device_id_type=MESH).wait_recv()

    normalise(start[D], size[D])

    @pl.when(inner)
    def _():
        first_copy(b, D, out_nbr).start()

    @pl.when(outer)
    def _():
        first_copy(b, D, in_nbr).start()
    normalise(start[F], size[F])

    @pl.when(inner)
    def _():
        first_copy(b, F, in_nbr).start()
    normalise(low, high - low)

    @pl.when(inner)
    def _():
        for p in (M, C, D):
            z_copy(b, p, own_in, in_nbr).start()
        for p in (F, C):
            z_copy(b, p, own_out, out_nbr).start()

    @pl.when(outer)
    def _():
        for p in (N, C, F, M):
            z_copy(b, p, own_in, in_nbr).start()
    mate_own(b).start()
    extract_one(b)
    make_hot()
    mate_own(mate).wait_recv()
    extract_one(mate)

    @pl.when(inner)
    def _():
        unpack(0, own(1))
        unpack(1, own(3))
        take(1, D, send_out, True)
        take(3, D, None, True)
        pass_on(q)
        take(1, N)
        take(3, N)
        take(1, C, send_out)
        take(3, C)
        mate_take(3, (D, N, C))
        extract(H[3])
        mate_take(1, (D, N, C))
        extract(H[1])
        take(1, F, send_out)
        take(3, F, send_in)
        send_in(own(3), C).start()

    @pl.when(outer)
    def _():
        unpack(0, own(2))
        take(2, D, None, True)
        mate_take(2, (D,))
        extract(H[2])
        pass_on(q)
        take(2, F)
        take(2, C)
        take(1, D)
        mate_take(1, (D,))
        extract(H[1])
        pass_on(H[2])
        mate_take(2, (F, C))
    wait_diag(q)
    acc_lo[...] = product(q, 0, WS)
    acc_hi[...] = product(q, hi_lane, WS)
    acc_mid[...] = product(q, mid_lane, WM)

    second, third = jnp.where(inner, H[3], H[2]), H[1]

    @pl.when(inner)
    def _():
        pass_on(H[3])
        take(3, M, send_in)
        send_in(own(3), D).start()
        take(0, D, send_out)
        take(0, C, send_out)
        z_copy(b, N, own_in, in_nbr).start()
        pass_on(H[1])
        take(0, N)
        mate_take(3, (F, M))
        mate_take(0, (D, C, N))
        extract(H[0])
        mate_take(1, (F,))

    @pl.when(outer)
    def _():
        take(1, C)
        take(1, F)
        take(0, D)
        mate_take(0, (D,))
        extract(H[0])
        pass_on(H[1])
        take(0, C)
        mate_take(1, (C, F))
    wait_diag(second)
    add_sides(second)
    wait_diag(third)
    add_sides(third)

    @pl.when(inner)
    def _():
        take(0, F, send_out)
        mate_take(0, (F,))
        finish_tiles(l)
        start_tiles(l)
    pass_on(H[0])

    @pl.when(inner)
    def _():
        @pl.loop(0, 2)
        def _(n):
            j = jnp.where(n == 0, lx, ly)
            finish_tiles(j)
            start_tiles(j)
        send_in(own(3), N).start()
        wait_diag(H[0])
        finish_tiles(ld)
        start_tiles(ld)
        take(1, M)
        mate_take(1, (M,))
    add_middle(second)
    add_middle(third)

    @pl.when(inner)
    def _():
        take(0, M)
        mate_take(0, (M,))

    @pl.when(outer)
    def _():
        take(0, F)
        mate_take(0, (C, F))
        wait_diag(H[0])
        add_sides(H[0])
    add_middle(H[0])

    for j in range(L):
        rows = slice(j * SP, j * SP + share)
        o_ref[:, j, :mid_lane] = acc_lo[rows, :mid_lane] / total
        o_ref[:, j, mid_lane:mid_lane + WM] = acc_mid[rows, :] / total
        o_ref[:, j, mid_lane + WM:] = acc_hi[rows, :][:, mid_lane + WM - hi_lane:] / total

    @pl.when(outer)
    def _():
        place = lax.broadcasted_iota(jnp.int32, (share, WM), 1) + mid_lane
        inside = ((place >= half + pad) & (place < half + pad + 256)
                  | (place >= R // 2 + pad) & (place < R // 2 + pad + 256))
        for d in (l, lx, ly, ld):
            wait_tile(d)
            placed = lax.dot_general(tile_recv[d], place_ref[...], (((1,), (0,)), ((), ())),
                                     preferred_element_type=jnp.float32)[:share]
            middle = pl.ds(mid_lane, WM)
            o_ref[:, d, middle] = jnp.where(inside, placed, o_ref[:, d, middle])

    all_stats.wait_send()
    mate_own(b).wait_send()

    def sent(part, sem):
        pltpu.make_async_remote_copy(
            src_ref=part, dst_ref=part, send_sem=sem, recv_sem=st_recv,
            device_id=(l, b), device_id_type=MESH).wait_send()

    @pl.when(inner)
    def _():
        sent(zbuf.at[0, pl.ds(0, size[F] + size[C]), :], own_out)
        sent(zbuf.at[pl.ds(0, 2), pl.ds(0, size[D] - RAW), :], first_send)
        sent(raw, raw_send)
        sent(zbuf.at[pl.ds(0, 2), pl.ds(0, far), :], out_send)
        sent(zbuf.at[0], in_send)
        sent(zbuf.at[pl.ds(0, 3)], mate_send)
        sent(tile_send, t_send)

    @pl.when(outer)
    def _():
        sent(zbuf.at[0, pl.ds(0, size[D] - RAW), :], first_send)
        sent(raw.at[0], raw_send)
        sent(zbuf.at[pl.ds(0, 3), pl.ds(0, far), :], mate_send)

    sent(zbuf.at[0, pl.ds(0, R - size[D]), :], own_in)
    sent(shr.at[pl.ds(0, L)], shr_send)
    sent(shr.at[pl.ds(0, B // L)], diag_send)


def line_call(L, B, series):
    R, T = series.shape
    share = R // B
    SP = up_to(share, 16)
    pad = share - 128
    high = (3 * 2 * share - pad) // 16 * 16
    WS = R - high
    mid_lane = WS // 128 * 128
    WM = up_to(R // 2 + pad + 256, 128) - mid_lane
    vmem = pl.BlockSpec(memory_space=pltpu.VMEM)
    dma = pltpu.SemaphoreType.DMA
    return pl.pallas_call(
        functools.partial(line_kernel, L, B),
        out_shape=jax.ShapeDtypeStruct((share, L, R), jnp.float32),
        in_specs=[pl.BlockSpec(memory_space=pltpu.HBM)],
        out_specs=vmem,
        scratch_shapes=[
            pltpu.VMEM((B, R, T), jnp.bfloat16),
            pltpu.VMEM((B, L, SP, T), jnp.bfloat16),
            pltpu.VMEM((L * SP, WS), jnp.float32),
            pltpu.VMEM((L * SP, WS), jnp.float32),
            pltpu.VMEM((L * SP, WM), jnp.float32),
            pltpu.VMEM((2, L, 2 * SP, 128), jnp.bfloat16),
            pltpu.VMEM((L, SP, 512), jnp.bfloat16),
            pltpu.VMEM((SP, 128), jnp.bfloat16),
            pltpu.VMEM((512, WM), jnp.bfloat16),
            pltpu.VMEM((R, 128), jnp.float32),
            pltpu.VMEM((B, 2, R), jnp.float32),
            pltpu.VMEM((R, T), jnp.float32),
            pltpu.VMEM((2, (R - high) // 32 * 16, T), jnp.float32),
            dma((B, 5)), dma, dma, dma, dma, dma, dma, dma, dma((2,)), dma,
            dma((B, 2)), dma, dma((B // 2,)), dma, dma((L,)), dma,
            dma, dma, dma((R // largest_tile(R, 352),)),
        ],
        compiler_params=pltpu.CompilerParams(
            collective_id=0, has_side_effects=True, vmem_limit_bytes=34 * 1024 * 1024),
    )(pltpu.with_memory_space_constraint(series, pltpu.HBM)).transpose(1, 0, 2)


def solution(mesh):
    L, B = mesh.shape["loop"], mesh.shape["bulk"]

    def on_device(series):
        R, T = series.shape
        share = R // B
        if L == 4 and B == 8 and R % 16 == 0 and T % 128 == 0 and 128 <= share <= 144:
            return line_call(L, B, series)
        SP = up_to(share, 16)
        pieces = 3
        vmem = pl.BlockSpec(memory_space=pltpu.VMEM)
        dma = pltpu.SemaphoreType.DMA
        return pl.pallas_call(
            functools.partial(kernel, L, B, pieces),
            out_shape=jax.ShapeDtypeStruct((share, L, R), jnp.float32),
            in_specs=[pl.BlockSpec(memory_space=pltpu.HBM)],
            out_specs=vmem,
            scratch_shapes=[
                pltpu.VMEM((B, R, T), jnp.bfloat16),
                pltpu.VMEM((B, L, SP, T), jnp.bfloat16),
                pltpu.VMEM((L * SP, R), jnp.float32),
                pltpu.VMEM((R, 128), jnp.float32),
                pltpu.VMEM((B, 2, R), jnp.float32),
                pltpu.VMEM((R, T), jnp.float32),
                dma((B, pieces)), dma((B, pieces)), dma((B, pieces)), dma((B, pieces)),
                dma((B, L)), dma((B, L)), dma((B,)), dma((B,)), dma((R // largest_tile(R, 128),)),
            ],
            compiler_params=pltpu.CompilerParams(
                collective_id=0, has_side_effects=True, vmem_limit_bytes=26 * 1024 * 1024),
        )(pltpu.with_memory_space_constraint(series, pltpu.HBM)).transpose(1, 0, 2)

    return jax.shard_map(
        on_device, mesh=mesh, in_specs=(P("loop", "bulk"),),
        out_specs=P(None, "bulk", "loop"), check_vma=False)
```

```python
import functools
import jax
import jax.numpy as jnp
from jax import lax
from jax.experimental import pallas as pl
from jax.experimental.pallas import tpu as pltpu
from jax.sharding import PartitionSpec as P

epsilon = 1e-06
MESH = pl.DeviceIdType.MESH
NT = (((1,), (1,)), ((), ()))
TN = (((0,), (0,)), ((), ()))


def up_to(value, unit):
    return -(-value // unit) * unit


def largest_tile(rows, limit):
    return max(t for t in range(16, limit + 1, 16) if rows % t == 0)


def kernel(L, B, PIECES, x_hbm, o_ref, zbuf, shr, acc, cols, stats, x_ref,
           z_recv, up_send, down_send, mate_send, shr_recv, shr_send, st_recv, st_send, x_sem):
    R, T = x_hbm.shape
    total = T * B
    Q = B // 2
    share = R // B
    SP = shr.shape[2]
    W = min(up_to(share + 15, 16), R)
    bounds = [up_to(R * i // PIECES, 128) for i in range(PIECES)] + [R]
    tile = largest_tile(R, 128)
    l, b = lax.axis_index("loop"), lax.axis_index("bulk")
    q, c = b // 2, b % 2
    mate = q * 2 + (1 - c)

    barrier = pltpu.get_barrier_semaphore()
    for d in range(1, B):
        pl.semaphore_signal(barrier, inc=1, device_id=(l, lax.rem(b + d, B)), device_id_type=MESH)
    for d in range(1, L):
        pl.semaphore_signal(barrier, inc=1, device_id=(lax.rem(l + d, L), b), device_id_type=MESH)

    def load(i):
        rows = pl.ds(pl.multiple_of(i * tile, tile), tile)
        return pltpu.make_async_copy(x_hbm.at[rows, :], x_ref.at[rows, :], x_sem.at[i])

    @pl.loop(0, R // tile)
    def _(i):
        load(i).start()

    lane = lax.broadcasted_iota(jnp.int32, (tile, 128), 1)

    @pl.loop(0, R // tile)
    def _(i):
        rows = pl.ds(pl.multiple_of(i * tile, tile), tile)
        load(i).wait()
        v = x_ref[rows, :]
        mean = jnp.sum(v, axis=1, keepdims=True) / T
        dev = v - mean
        m2 = jnp.sum(dev * dev, axis=1, keepdims=True)
        cols[rows, :] = jnp.where(lane == 0, mean, jnp.where(lane == 1, m2, 0.0))

    pick = (lax.broadcasted_iota(jnp.int32, (8, 128), 0)
            == lax.broadcasted_iota(jnp.int32, (8, 128), 1)).astype(jnp.float32)
    line = lax.dot_general(pick, cols[...], NT, precision=lax.Precision.HIGHEST,
                           preferred_element_type=jnp.float32)
    stats[b] = line[:2]

    pl.semaphore_wait(barrier, B - 1 + L - 1)

    def stat_copy(source, peer):
        return pltpu.make_async_remote_copy(
            src_ref=stats.at[source], dst_ref=stats.at[source],
            send_sem=st_send.at[peer], recv_sem=st_recv.at[source],
            device_id=(l, peer), device_id_type=MESH)

    for d in range(1, B):
        stat_copy(b, lax.rem(b + d, B)).start()
    for d in range(1, B):
        other = lax.rem(b + d, B)
        stat_copy(other, other).wait_recv()

    mean = stats[0, 0:1]
    for k in range(1, B):
        mean = mean + stats[k, 0:1]
    mean = mean / B
    square = jnp.zeros_like(mean)
    for k in range(B):
        shift = stats[k, 0:1] - mean
        square = square + (stats[k, 1:2] + T * (shift * shift))
    scale = lax.rsqrt(square / total + epsilon)
    sub = lax.broadcasted_iota(jnp.int32, (8, R), 0)
    both = jnp.where(sub == 0, mean, jnp.where(sub == 1, scale, 0.0))
    cols[...] = lax.dot_general(both, pick, TN, precision=lax.Precision.HIGHEST,
                                preferred_element_type=jnp.float32)

    def normalise(piece):
        size = bounds[piece + 1] - bounds[piece]
        step = largest_tile(size, 128)

        @pl.loop(0, size // step)
        def _(i):
            rows = pl.ds(pl.multiple_of(bounds[piece] + i * step, 16), step)
            z = (x_ref[rows, :] - cols[rows, 0:1]) * cols[rows, 1:2]
            zbuf[b, rows, :] = z.astype(jnp.bfloat16)

    def piece_copy(k, piece, send_sem, peer):
        part = zbuf.at[k, pl.ds(bounds[piece], bounds[piece + 1] - bounds[piece]), :]
        return pltpu.make_async_remote_copy(
            src_ref=part, dst_ref=part, send_sem=send_sem.at[k, piece],
            recv_sem=z_recv.at[k, piece], device_id=(l, peer), device_id_type=MESH)

    def share_copy(k, block, peer):
        return pltpu.make_async_remote_copy(
            src_ref=shr.at[k, block], dst_ref=shr.at[k, block], send_sem=shr_send.at[k, peer],
            recv_sem=shr_recv.at[k, block], device_id=(peer, b), device_id_type=MESH)

    has_up, has_down = q + 1 < Q, q >= 1
    start = b * share
    first = pl.multiple_of(jnp.minimum(start // 16 * 16, R - W), 16)
    need_below = PIECES - 1 - sum((first >= x).astype(jnp.int32) for x in bounds[1:-1])
    need_above = sum((first + W > x).astype(jnp.int32) for x in bounds[1:-1])

    def extract(k):
        window = zbuf[k, pl.ds(first, W), :]
        hot = (lax.broadcasted_iota(jnp.int32, (SP, W), 1)
               == lax.broadcasted_iota(jnp.int32, (SP, W), 0) + (start - first))
        inside = lax.broadcasted_iota(jnp.int32, (SP, W), 0) < share
        hot = jnp.where(hot & inside, 1.0, 0.0).astype(jnp.bfloat16)
        rows = lax.dot_general(hot, window, (((1,), (0,)), ((), ())),
                               preferred_element_type=jnp.float32)
        shr[k, l] = rows.astype(jnp.bfloat16)
        for d in range(1, L):
            share_copy(k, l, lax.rem(l + d, L)).start()

    def wait_shares(place):
        for core in range(2):
            k = place * 2 + core
            for d in range(1, L):
                other = lax.rem(l + d, L)
                share_copy(k, other, other).wait_recv()

    def multiply(place):
        part = None
        wait_shares(place)
        for core in range(2):
            k = place * 2 + core
            a = shr[k].reshape(L * SP, T)
            term = lax.dot_general(a, zbuf[k], NT, preferred_element_type=jnp.float32)
            part = term if part is None else part + term
        acc[...] += part

    def multiply_step(s):
        @pl.loop(0, 2)
        def _(n):
            place = q - (1 - 2 * n) * s

            @pl.when((place >= 0) & (place < Q) & ((s > 0) | (n < 1)))
            def _():
                multiply(place)

    def send_own(up_first):
        done = set()

        def send(up, i):
            piece = PIECES - 1 - i if up else i
            if piece not in done:
                done.add(piece)
                normalise(piece)

            @pl.when(has_up if up else has_down)
            def _():
                if up:
                    piece_copy(b, piece, up_send, b + 2).start()
                else:
                    piece_copy(b, piece, down_send, b - 2).start()

        for i in range(PIECES):
            send(up_first, i)
            send(not up_first, i)

    @pl.when(q >= Q // 2)
    def _():
        send_own(True)

    @pl.when(q < Q // 2)
    def _():
        send_own(False)

    for i in range(PIECES):
        piece_copy(b, i, mate_send, mate).start()

    acc[...] = jnp.zeros_like(acc)
    extract(b)

    for i in range(PIECES):
        piece_copy(mate, i, mate_send, mate).wait_recv()

    extract(mate)

    def arrive(s, i, between=None):
        below, above = b - 2 * s, b + 2 * s
        from_below, from_above = q - s >= 0, q + s < Q
        down_piece = PIECES - 1 - i

        @pl.when(from_below)
        def _():
            piece_copy(below, down_piece, up_send, b).wait_recv()

            @pl.when(has_up)
            def _():
                piece_copy(below, down_piece, up_send, b + 2).start()
            piece_copy(below, down_piece, mate_send, mate).start()

        @pl.when(from_above)
        def _():
            piece_copy(above, i, down_send, b).wait_recv()

            @pl.when(has_down)
            def _():
                piece_copy(above, i, down_send, b - 2).start()
            piece_copy(above, i, mate_send, mate).start()

        @pl.when(from_below & (i == need_below))
        def _():
            extract(below)

        @pl.when(from_above & (i == need_above))
        def _():
            extract(above)

        if between is not None:
            between()

        @pl.when(from_below)
        def _():
            piece_copy(mate - 2 * s, down_piece, mate_send, mate).wait_recv()

            @pl.when(i == need_below)
            def _():
                extract(mate - 2 * s)

        @pl.when(from_above)
        def _():
            piece_copy(mate + 2 * s, i, mate_send, mate).wait_recv()

            @pl.when(i == need_above)
            def _():
                extract(mate + 2 * s)

        if i == 0:
            multiply_step(s - 1)

    def finish(piece, place):
        lo, hi = bounds[piece], bounds[piece + 1]
        part = acc[:, lo:hi]
        if place is not None:
            for core in range(2):
                k = place * 2 + core
                a = shr[k].reshape(L * SP, T)
                part = part + lax.dot_general(a, zbuf[k, lo:hi, :], NT,
                                              preferred_element_type=jnp.float32)
        part = part / total
        for j in range(L):
            o_ref[:, j, lo:hi] = part[j * SP:j * SP + share]

    @pl.loop(1, Q - 1)
    def _(s):
        for i in range(PIECES):
            arrive(s, i)

    def finish_ends(steps):
        for end, place in ((Q - 1, 0), (0, Q - 1)):
            @pl.when(q == end)
            def _():
                for i in steps:
                    finish(PIECES - 1 - i if end else i, place)

    def finish_early():
        for end, place in ((Q - 1, 0), (0, Q - 1)):
            @pl.when(q == end)
            def _():
                wait_shares(place)

        finish_ends(range(PIECES - 1))

    for i in range(PIECES):
        arrive(Q - 1, i, finish_early if i == PIECES - 1 else None)
    finish_ends([PIECES - 1])

    @pl.when((q > 0) & (q < Q - 1))
    def _():
        for i in range(PIECES):
            finish(i, None)

    for d in range(1, B):
        other = lax.rem(b + d, B)
        stat_copy(b, other).wait_send()

    @pl.loop(0, Q)
    def _(s):
        below, above = b - 2 * s, b + 2 * s
        from_below, from_above = q - s >= 0, q + s < Q

        for i in range(PIECES):
            @pl.when(from_below & has_up)
            def _():
                piece_copy(below, i, up_send, b + 2).wait_send()

            @pl.when(from_above & has_down)
            def _():
                piece_copy(above, i, down_send, b - 2).wait_send()

            @pl.when(from_below)
            def _():
                piece_copy(below, i, mate_send, mate).wait_send()

            @pl.when(from_above & (s > 0))
            def _():
                piece_copy(above, i, mate_send, mate).wait_send()

    @pl.loop(0, B)
    def _(k):
        for d in range(1, L):
            other = lax.rem(l + d, L)
            share_copy(k, l, other).wait_send()


F, M, C, N, D = range(5)


def line_kernel(L, B, x_hbm, o_ref, zbuf, shr, acc_lo, acc_hi, acc_mid, tile_send, tile_recv, shift_ref, place_ref,
                cols, stats, x_ref, raw,
                z_recv, out_send, in_send, mate_send, own_send, own_out, own_in, first_send, raw_recv, raw_send, shr_recv, shr_send, diag_recv, diag_send, t_recv, t_send,
                st_recv, st_send, x_sem):
    R, T = x_hbm.shape
    total = T * B
    share = R // B
    half = 2 * share
    SP = shr.shape[2]
    pad = share - 128
    W = min(up_to(share + 15, 16), R)
    low, high = R - (3 * half - pad) // 16 * 16, (3 * half - pad) // 16 * 16
    edges = [0, low, (R // 2 - pad) // 16 * 16, up_to(R // 2 + pad, 16), high, R]
    size = [edges[p + 1] - edges[p] for p in range(5)]
    far = size[F] + size[C] + size[D]
    tile = largest_tile(R, 352)
    RAW = raw.shape[1]
    WS = acc_lo.shape[1]
    hi_lane, mid_lane = R - WS, WS // 128 * 128
    WM = acc_mid.shape[1]
    l, b = lax.axis_index("loop"), lax.axis_index("bulk")
    q, c = b // 2, b % 2
    mate = q * 2 + (1 - c)
    upper = q >= 2
    inner = (q == 1) | (q == 2)
    outer = (q == 0) | (q == 3)
    step = jnp.where(upper, 1, -1)
    H = [jnp.where(upper, h, 3 - h) for h in range(4)]
    out_nbr, in_nbr = b + 2 * step, b - 2 * step
    lx, ly, ld = l + 1 - 2 * (l % 2), lax.rem(l + 2, 4), 3 - l

    def align(value, unit=16):
        return pl.multiple_of(value, unit)

    start = [align(jnp.where(upper, edges[p], edges[4 - p])) for p in range(5)]

    barrier = pltpu.get_barrier_semaphore()
    for d in range(1, B):
        pl.semaphore_signal(barrier, inc=1, device_id=(l, lax.rem(b + d, B)), device_id_type=MESH)
    for line in (lx, ly):
        pl.semaphore_signal(barrier, inc=1, device_id=(line, b), device_id_type=MESH)

    def load(i):
        rows = pl.ds(pl.multiple_of(i * tile, tile), tile)
        return pltpu.make_async_copy(x_hbm.at[rows, :], x_ref.at[rows, :], x_sem.at[i])

    @pl.loop(0, R // tile)
    def _(i):
        load(i).start()

    lane = lax.broadcasted_iota(jnp.int32, (tile, 128), 1)

    @pl.loop(0, R // tile)
    def _(i):
        rows = pl.ds(pl.multiple_of(i * tile, tile), tile)
        load(i).wait()
        v = x_ref[rows, :]
        mean = jnp.sum(v, axis=1, keepdims=True) / T
        dev = v - mean
        m2 = jnp.sum(dev * dev, axis=1, keepdims=True)
        cols[rows, :] = jnp.where(lane == 0, mean, jnp.where(lane == 1, m2, 0.0))

    pick = (lax.broadcasted_iota(jnp.int32, (8, 128), 0)
            == lax.broadcasted_iota(jnp.int32, (8, 128), 1)).astype(jnp.float32)
    line = lax.dot_general(pick, cols[...], NT, precision=lax.Precision.HIGHEST,
                           preferred_element_type=jnp.float32)
    stats[b] = line[:2]

    pl.semaphore_wait(barrier, B - 1 + 2)

    def stat_copy(source, peer):
        return pltpu.make_async_remote_copy(
            src_ref=stats.at[source], dst_ref=stats.at[source],
            send_sem=st_send, recv_sem=st_recv,
            device_id=(l, peer), device_id_type=MESH)

    for d in range(1, B):
        stat_copy(b, lax.rem(b + d, B)).start()
    def raw_copy(p, slot, peer):
        return pltpu.make_async_remote_copy(
            src_ref=x_ref.at[pl.ds(start[p], RAW), :], dst_ref=raw.at[slot], send_sem=raw_send,
            recv_sem=raw_recv.at[slot], device_id=(l, peer), device_id_type=MESH)

    @pl.when(inner)
    def _():
        raw_copy(D, 0, out_nbr).start()
        raw_copy(F, 0, in_nbr).start()

    @pl.when(outer)
    def _():
        raw_copy(D, 1, in_nbr).start()

    gathered = stats.at[pl.ds(0, B - 1)]
    all_stats = pltpu.make_async_remote_copy(
        src_ref=gathered, dst_ref=gathered, send_sem=st_send, recv_sem=st_recv,
        device_id=(l, b), device_id_type=MESH)
    all_stats.wait_recv()

    mean = stats[0, 0:1]
    for k in range(1, B):
        mean = mean + stats[k, 0:1]
    mean = mean / B
    square = jnp.zeros_like(mean)
    for k in range(B):
        shift = stats[k, 0:1] - mean
        square = square + (stats[k, 1:2] + T * (shift * shift))
    scale = lax.rsqrt(square / total + epsilon)
    sub = lax.broadcasted_iota(jnp.int32, (8, R), 0)
    both = jnp.where(sub == 0, mean, jnp.where(sub == 1, scale, 0.0))
    cols[...] = lax.dot_general(both, pick, TN, precision=lax.Precision.HIGHEST,
                                preferred_element_type=jnp.float32)

    def normalise(begin, count):
        unit = count if count <= 288 else largest_tile(count, 128)

        def chunk(i):
            rows = pl.ds(pl.multiple_of(begin + i * unit, 16), unit)
            z = (x_ref[rows, :] - cols[rows, 0:1]) * cols[rows, 1:2]
            zbuf[b, rows, :] = z.astype(jnp.bfloat16)

        if unit == count:
            chunk(0)
        else:
            pl.loop(0, count // unit)(chunk)

    def z_copy(k, p, send_sem, peer, skip=0):
        part = zbuf.at[k, pl.ds(align(start[p] + skip), size[p] - skip), :]
        return pltpu.make_async_remote_copy(
            src_ref=part, dst_ref=part, send_sem=send_sem,
            recv_sem=z_recv.at[k, jnp.where(upper, p, 4 - p)], device_id=(l, peer), device_id_type=MESH)

    def first_copy(k, p, peer):
        return z_copy(k, p, first_send, peer, RAW)

    def unpack(slot, k):
        raw_copy(D, slot, b).wait_recv()
        rows = pl.ds(start[D], RAW)
        z = (raw[slot] - cols[rows, 0:1]) * cols[rows, 1:2]
        zbuf[k, rows, :] = z.astype(jnp.bfloat16)

    def send_out(k, p):
        return z_copy(k, p, out_send, out_nbr)

    def send_in(k, p):
        return z_copy(k, p, in_send, in_nbr)

    def mate_copy(k, p):
        return z_copy(k, p, mate_send, mate)

    def mate_own(k):
        part = zbuf.at[k]
        return pltpu.make_async_remote_copy(
            src_ref=part, dst_ref=part, send_sem=own_send, recv_sem=z_recv.at[k, 0],
            device_id=(l, mate), device_id_type=MESH)

    def share_copy(k, block, peer, way):
        part = shr.at[k, block, pl.ds(0, SR), :]
        return pltpu.make_async_remote_copy(
            src_ref=part, dst_ref=part, send_sem=shr_send,
            recv_sem=shr_recv.at[k, way], device_id=(peer, b), device_id_type=MESH)

    SR = up_to(share, 8)
    cut = up_to(share // 2, 16)

    def diag_copy(k, block, peer, way):
        rows = pl.ds(0, cut) if way == 0 else pl.ds(cut, SR - cut)
        part = shr.at[k, block, rows, :]
        return pltpu.make_async_remote_copy(
            src_ref=part, dst_ref=part, send_sem=diag_send,
            recv_sem=diag_recv.at[k // 2], device_id=(peer, b), device_id_type=MESH)

    first = align(jnp.minimum(b * share // 16 * 16, jnp.where(q == 0, size[D], R) - W))

    def extract_one(k):
        window = zbuf[k, pl.ds(first, W), :]
        row = lax.broadcasted_iota(jnp.int32, (SP, W), 0)
        hot = lax.broadcasted_iota(jnp.int32, (SP, W), 1) == row + (b * share - first)
        hot = jnp.where(hot & (row < share), 1.0, 0.0).astype(jnp.bfloat16)
        rows = lax.dot_general(hot, window, (((1,), (0,)), ((), ())),
                               preferred_element_type=jnp.float32)
        shr[k, l] = rows.astype(jnp.bfloat16)
        share_copy(k, l, lx, 0).start()
        share_copy(k, l, ly, 1).start()

    def extract(place):
        @pl.loop(0, 2)
        def _(core):
            extract_one(place * 2 + core)

    def pass_on(place):
        @pl.loop(0, 2)
        def _(core):
            k = place * 2 + core
            share_copy(k, lx, lx, 0).wait_recv()
            diag_copy(k, lx, ly, 0).start()
            share_copy(k, ly, ly, 1).wait_recv()
            diag_copy(k, ly, lx, 1).start()

    def wait_diag(place):
        part = shr.at[pl.ds(place * 2, 2), ld, pl.ds(0, SR), :]
        pltpu.make_async_remote_copy(
            src_ref=part, dst_ref=part, send_sem=diag_send, recv_sem=diag_recv.at[place],
            device_id=(l, b), device_id_type=MESH).wait_recv()

    def product(place, begin, width):
        part = None
        for core in range(2):
            k = place * 2 + core
            term = lax.dot_general(shr[k].reshape(L * SP, T), zbuf[k, begin:begin + width, :], NT,
                                   preferred_element_type=jnp.float32)
            part = term if part is None else part + term
        return part

    def add_sides(place):
        acc_lo[...] += product(place, 0, WS)
        acc_hi[...] += product(place, hi_lane, WS)

    def add_middle(place):
        acc_mid[...] += product(place, mid_lane, WM)

    def own(h):
        return H[h] * 2 + c

    def other(h):
        return H[h] * 2 + (1 - c)

    def take(h, p, onward=None, first=False):
        if first:
            first_copy(own(h), p, mate).wait_recv()
        else:
            mate_copy(own(h), p).wait_recv()
        if onward is not None:
            onward(own(h), p).start()
        mate_copy(own(h), p).start()

    def mate_take(h, pieces):
        for p in pieces:
            mate_copy(other(h), p).wait_recv()

    def tile_copy(side, j, core, block, slot):
        return pltpu.make_async_remote_copy(
            src_ref=tile_send.at[side, j, core, pl.ds(0, SR), :],
            dst_ref=tile_recv.at[block, pl.ds(0, SR), pl.ds(pl.multiple_of(slot * 128, 128), 128)],
            send_sem=t_send, recv_sem=t_recv.at[block],
            device_id=(j, 6 * side + core), device_id_type=MESH)

    def make_hot():
        shift = (lax.broadcasted_iota(jnp.int32, (SR, 128), 0)
                 == lax.broadcasted_iota(jnp.int32, (SR, 128), 1) + jnp.where(c == 0, pad, 0))
        shift_ref[...] = jnp.where(shift, 1.0, 0.0).astype(jnp.bfloat16)
        row = lax.broadcasted_iota(jnp.int32, (512, WM), 0)
        lane = jnp.where(row < 256, row + half + pad, row - 256 + R // 2 + pad) - mid_lane
        hot = lax.broadcasted_iota(jnp.int32, (512, WM), 1) == lane
        place_ref[...] = jnp.where(hot, 1.0, 0.0).astype(jnp.bfloat16)

    def finish_tiles(j):
        rows = pl.ds(pl.multiple_of(j * SP, SP), SP)
        for side, acc, begin in ((0, acc_lo, 0), (1, acc_hi, hi_lane)):
            value = acc[rows, :]
            for core in range(2):
                k = H[0] * 2 + core
                value = value + lax.dot_general(shr[k, j], zbuf[k, begin:begin + WS, :], NT,
                                                preferred_element_type=jnp.float32)
            acc[rows, :] = value
            turned = lax.dot_general((value[:SR] / total).astype(jnp.bfloat16), shift_ref[...], TN,
                                     preferred_element_type=jnp.float32)
            for core in range(2):
                at = (WS - half if side else 0) + core * share
                tile_send[side, j, core, :share, :] = turned[at:at + share].astype(jnp.bfloat16)

    def start_tiles(j):
        for side in range(2):
            for core in range(2):
                tile_copy(side, j, core, l, b - 2).start()

    def wait_tile(block):
        part = tile_recv.at[block, pl.ds(0, SR), :]
        pltpu.make_async_remote_copy(
            src_ref=part, dst_ref=part, send_sem=t_send, recv_sem=t_recv.at[block],
            device_id=(l, b), device_id_type=MESH).wait_recv()

    normalise(start[D], size[D])

    @pl.when(inner)
    def _():
        first_copy(b, D, out_nbr).start()

    @pl.when(outer)
    def _():
        first_copy(b, D, in_nbr).start()
    normalise(start[F], size[F])

    @pl.when(inner)
    def _():
        first_copy(b, F, in_nbr).start()
    normalise(low, high - low)

    @pl.when(inner)
    def _():
        for p in (M, C, D):
            z_copy(b, p, own_in, in_nbr).start()
        for p in (F, C):
            z_copy(b, p, own_out, out_nbr).start()

    @pl.when(outer)
    def _():
        for p in (N, C, F, M):
            z_copy(b, p, own_in, in_nbr).start()
    mate_own(b).start()
    extract_one(b)
    make_hot()
    mate_own(mate).wait_recv()
    extract_one(mate)

    @pl.when(inner)
    def _():
        unpack(0, own(1))
        unpack(1, own(3))
        take(1, D, send_out, True)
        take(3, D, None, True)
        pass_on(q)
        take(1, N)
        take(3, N)
        take(1, C, send_out)
        take(3, C)
        mate_take(3, (D, N, C))
        extract(H[3])
        mate_take(1, (D, N, C))
        extract(H[1])
        take(1, F, send_out)
        take(3, F, send_in)
        send_in(own(3), C).start()

    @pl.when(outer)
    def _():
        unpack(0, own(2))
        take(2, D, None, True)
        mate_take(2, (D,))
        extract(H[2])
        pass_on(q)
        take(2, F)
        take(2, C)
        take(1, D)
        mate_take(1, (D,))
        extract(H[1])
        pass_on(H[2])
        mate_take(2, (F, C))
    wait_diag(q)
    acc_lo[...] = product(q, 0, WS)
    acc_hi[...] = product(q, hi_lane, WS)
    acc_mid[...] = product(q, mid_lane, WM)

    second, third = jnp.where(inner, H[3], H[2]), H[1]

    @pl.when(inner)
    def _():
        pass_on(H[3])
        take(3, M, send_in)
        send_in(own(3), D).start()
        take(0, D, send_out)
        take(0, C, send_out)
        z_copy(b, N, own_in, in_nbr).start()
        pass_on(H[1])
        take(0, N)
        mate_take(3, (F, M))
        mate_take(0, (D, C, N))
        extract(H[0])
        mate_take(1, (F,))

    @pl.when(outer)
    def _():
        take(1, C)
        take(1, F)
        pass_on(H[1])
        mate_take(1, (C, F))
    wait_diag(second)
    add_sides(second)

    @pl.when(inner)
    def _():
        take(0, F, send_out)
    wait_diag(third)
    add_sides(third)

    @pl.when(inner)
    def _():
        mate_take(0, (F,))
        finish_tiles(l)
        start_tiles(l)

    @pl.when(outer)
    def _():
        take(0, D)
        mate_take(0, (D,))
        extract(H[0])
        take(0, C)
    pass_on(H[0])

    @pl.when(inner)
    def _():
        @pl.loop(0, 2)
        def _(n):
            j = jnp.where(n == 0, lx, ly)
            finish_tiles(j)
            start_tiles(j)
        send_in(own(3), N).start()
        wait_diag(H[0])
        finish_tiles(ld)
        start_tiles(ld)
        take(1, M)
        mate_take(1, (M,))
    add_middle(second)
    add_middle(third)

    @pl.when(inner)
    def _():
        take(0, M)
        mate_take(0, (M,))

    @pl.when(outer)
    def _():
        take(0, F)
        mate_take(0, (C, F))
        wait_diag(H[0])
        add_sides(H[0])
    add_middle(H[0])

    for j in range(L):
        rows = slice(j * SP, j * SP + share)
        o_ref[:, j, :mid_lane] = acc_lo[rows, :mid_lane] / total
        o_ref[:, j, mid_lane:mid_lane + WM] = acc_mid[rows, :] / total
        o_ref[:, j, mid_lane + WM:] = acc_hi[rows, :][:, mid_lane + WM - hi_lane:] / total

    @pl.when(outer)
    def _():
        place = lax.broadcasted_iota(jnp.int32, (share, WM), 1) + mid_lane
        inside = ((place >= half + pad) & (place < half + pad + 256)
                  | (place >= R // 2 + pad) & (place < R // 2 + pad + 256))
        for d in (l, lx, ly, ld):
            wait_tile(d)
            placed = lax.dot_general(tile_recv[d], place_ref[...], (((1,), (0,)), ((), ())),
                                     preferred_element_type=jnp.float32)[:share]
            middle = pl.ds(mid_lane, WM)
            o_ref[:, d, middle] = jnp.where(inside, placed, o_ref[:, d, middle])

    all_stats.wait_send()
    mate_own(b).wait_send()

    def sent(part, sem):
        pltpu.make_async_remote_copy(
            src_ref=part, dst_ref=part, send_sem=sem, recv_sem=st_recv,
            device_id=(l, b), device_id_type=MESH).wait_send()

    @pl.when(inner)
    def _():
        sent(zbuf.at[0, pl.ds(0, size[F] + size[C]), :], own_out)
        sent(zbuf.at[pl.ds(0, 2), pl.ds(0, size[D] - RAW), :], first_send)
        sent(raw, raw_send)
        sent(zbuf.at[pl.ds(0, 2), pl.ds(0, far), :], out_send)
        sent(zbuf.at[0], in_send)
        sent(zbuf.at[pl.ds(0, 3)], mate_send)
        sent(tile_send.at[:, :, :, pl.ds(0, SR), :], t_send)

    @pl.when(outer)
    def _():
        sent(zbuf.at[0, pl.ds(0, size[D] - RAW), :], first_send)
        sent(raw.at[0], raw_send)
        sent(zbuf.at[pl.ds(0, 3), pl.ds(0, far), :], mate_send)

    sent(zbuf.at[0, pl.ds(0, R - size[D]), :], own_in)
    sent(shr.at[pl.ds(0, L), :, pl.ds(0, SR), :], shr_send)
    sent(shr.at[pl.ds(0, B // L), :, pl.ds(0, SR), :], diag_send)


def line_call(L, B, series):
    R, T = series.shape
    share = R // B
    SP = up_to(share, 16)
    pad = share - 128
    high = (3 * 2 * share - pad) // 16 * 16
    WS = R - high
    mid_lane = WS // 128 * 128
    WM = up_to(R // 2 + pad + 256, 128) - mid_lane
    vmem = pl.BlockSpec(memory_space=pltpu.VMEM)
    dma = pltpu.SemaphoreType.DMA
    return pl.pallas_call(
        functools.partial(line_kernel, L, B),
        out_shape=jax.ShapeDtypeStruct((share, L, R), jnp.float32),
        in_specs=[pl.BlockSpec(memory_space=pltpu.HBM)],
        out_specs=vmem,
        scratch_shapes=[
            pltpu.VMEM((B, R, T), jnp.bfloat16),
            pltpu.VMEM((B, L, SP, T), jnp.bfloat16),
            pltpu.VMEM((L * SP, WS), jnp.float32),
            pltpu.VMEM((L * SP, WS), jnp.float32),
            pltpu.VMEM((L * SP, WM), jnp.float32),
            pltpu.VMEM((2, L, 2, SP, 128), jnp.bfloat16),
            pltpu.VMEM((L, SP, 512), jnp.bfloat16),
            pltpu.VMEM((up_to(share, 8), 128), jnp.bfloat16),
            pltpu.VMEM((512, WM), jnp.bfloat16),
            pltpu.VMEM((R, 128), jnp.float32),
            pltpu.VMEM((B, 2, R), jnp.float32),
            pltpu.VMEM((R, T), jnp.float32),
            pltpu.VMEM((2, (R - high) // 32 * 16, T), jnp.float32),
            dma((B, 5)), dma, dma, dma, dma, dma, dma, dma, dma((2,)), dma,
            dma((B, 2)), dma, dma((B // 2,)), dma, dma((L,)), dma,
            dma, dma, dma((R // largest_tile(R, 352),)),
        ],
        compiler_params=pltpu.CompilerParams(
            collective_id=0, has_side_effects=True, vmem_limit_bytes=34 * 1024 * 1024),
    )(pltpu.with_memory_space_constraint(series, pltpu.HBM)).transpose(1, 0, 2)


def solution(mesh):
    L, B = mesh.shape["loop"], mesh.shape["bulk"]

    def on_device(series):
        R, T = series.shape
        share = R // B
        if L == 4 and B == 8 and R % 16 == 0 and T % 128 == 0 and 128 <= share <= 144:
            return line_call(L, B, series)
        SP = up_to(share, 16)
        pieces = 3
        vmem = pl.BlockSpec(memory_space=pltpu.VMEM)
        dma = pltpu.SemaphoreType.DMA
        return pl.pallas_call(
            functools.partial(kernel, L, B, pieces),
            out_shape=jax.ShapeDtypeStruct((share, L, R), jnp.float32),
            in_specs=[pl.BlockSpec(memory_space=pltpu.HBM)],
            out_specs=vmem,
            scratch_shapes=[
                pltpu.VMEM((B, R, T), jnp.bfloat16),
                pltpu.VMEM((B, L, SP, T), jnp.bfloat16),
                pltpu.VMEM((L * SP, R), jnp.float32),
                pltpu.VMEM((R, 128), jnp.float32),
                pltpu.VMEM((B, 2, R), jnp.float32),
                pltpu.VMEM((R, T), jnp.float32),
                dma((B, pieces)), dma((B, pieces)), dma((B, pieces)), dma((B, pieces)),
                dma((B, L)), dma((B, L)), dma((B,)), dma((B,)), dma((R // largest_tile(R, 128),)),
            ],
            compiler_params=pltpu.CompilerParams(
                collective_id=0, has_side_effects=True, vmem_limit_bytes=26 * 1024 * 1024),
        )(pltpu.with_memory_space_constraint(series, pltpu.HBM)).transpose(1, 0, 2)

    return jax.shard_map(
        on_device, mesh=mesh, in_specs=(P("loop", "bulk"),),
        out_specs=P(None, "bulk", "loop"), check_vma=False)
```

```python
import functools
import jax
import jax.numpy as jnp
from jax import lax
from jax.experimental import pallas as pl
from jax.experimental.pallas import tpu as pltpu
from jax.sharding import PartitionSpec as P

epsilon = 1e-06
MESH = pl.DeviceIdType.MESH
NT = (((1,), (1,)), ((), ()))
TN = (((0,), (0,)), ((), ()))


def up_to(value, unit):
    return -(-value // unit) * unit


def largest_tile(rows, limit):
    return max(t for t in range(16, limit + 1, 16) if rows % t == 0)


def kernel(L, B, PIECES, x_hbm, o_ref, zbuf, shr, acc, cols, stats, x_ref,
           z_recv, up_send, down_send, mate_send, shr_recv, shr_send, st_recv, st_send, x_sem):
    R, T = x_hbm.shape
    total = T * B
    Q = B // 2
    share = R // B
    SP = shr.shape[2]
    W = min(up_to(share + 15, 16), R)
    bounds = [up_to(R * i // PIECES, 128) for i in range(PIECES)] + [R]
    tile = largest_tile(R, 128)
    l, b = lax.axis_index("loop"), lax.axis_index("bulk")
    q, c = b // 2, b % 2
    mate = q * 2 + (1 - c)

    barrier = pltpu.get_barrier_semaphore()
    for d in range(1, B):
        pl.semaphore_signal(barrier, inc=1, device_id=(l, lax.rem(b + d, B)), device_id_type=MESH)
    for d in range(1, L):
        pl.semaphore_signal(barrier, inc=1, device_id=(lax.rem(l + d, L), b), device_id_type=MESH)

    def load(i):
        rows = pl.ds(pl.multiple_of(i * tile, tile), tile)
        return pltpu.make_async_copy(x_hbm.at[rows, :], x_ref.at[rows, :], x_sem.at[i])

    @pl.loop(0, R // tile)
    def _(i):
        load(i).start()

    lane = lax.broadcasted_iota(jnp.int32, (tile, 128), 1)

    @pl.loop(0, R // tile)
    def _(i):
        rows = pl.ds(pl.multiple_of(i * tile, tile), tile)
        load(i).wait()
        v = x_ref[rows, :]
        mean = jnp.sum(v, axis=1, keepdims=True) / T
        dev = v - mean
        m2 = jnp.sum(dev * dev, axis=1, keepdims=True)
        cols[rows, :] = jnp.where(lane == 0, mean, jnp.where(lane == 1, m2, 0.0))

    pick = (lax.broadcasted_iota(jnp.int32, (8, 128), 0)
            == lax.broadcasted_iota(jnp.int32, (8, 128), 1)).astype(jnp.float32)
    line = lax.dot_general(pick, cols[...], NT, precision=lax.Precision.HIGHEST,
                           preferred_element_type=jnp.float32)
    stats[b] = line[:2]

    pl.semaphore_wait(barrier, B - 1 + L - 1)

    def stat_copy(source, peer):
        return pltpu.make_async_remote_copy(
            src_ref=stats.at[source], dst_ref=stats.at[source],
            send_sem=st_send.at[peer], recv_sem=st_recv.at[source],
            device_id=(l, peer), device_id_type=MESH)

    for d in range(1, B):
        stat_copy(b, lax.rem(b + d, B)).start()
    for d in range(1, B):
        other = lax.rem(b + d, B)
        stat_copy(other, other).wait_recv()

    mean = stats[0, 0:1]
    for k in range(1, B):
        mean = mean + stats[k, 0:1]
    mean = mean / B
    square = jnp.zeros_like(mean)
    for k in range(B):
        shift = stats[k, 0:1] - mean
        square = square + (stats[k, 1:2] + T * (shift * shift))
    scale = lax.rsqrt(square / total + epsilon)
    sub = lax.broadcasted_iota(jnp.int32, (8, R), 0)
    both = jnp.where(sub == 0, mean, jnp.where(sub == 1, scale, 0.0))
    cols[...] = lax.dot_general(both, pick, TN, precision=lax.Precision.HIGHEST,
                                preferred_element_type=jnp.float32)

    def normalise(piece):
        size = bounds[piece + 1] - bounds[piece]
        step = largest_tile(size, 128)

        @pl.loop(0, size // step)
        def _(i):
            rows = pl.ds(pl.multiple_of(bounds[piece] + i * step, 16), step)
            z = (x_ref[rows, :] - cols[rows, 0:1]) * cols[rows, 1:2]
            zbuf[b, rows, :] = z.astype(jnp.bfloat16)

    def piece_copy(k, piece, send_sem, peer):
        part = zbuf.at[k, pl.ds(bounds[piece], bounds[piece + 1] - bounds[piece]), :]
        return pltpu.make_async_remote_copy(
            src_ref=part, dst_ref=part, send_sem=send_sem.at[k, piece],
            recv_sem=z_recv.at[k, piece], device_id=(l, peer), device_id_type=MESH)

    def share_copy(k, block, peer):
        return pltpu.make_async_remote_copy(
            src_ref=shr.at[k, block], dst_ref=shr.at[k, block], send_sem=shr_send.at[k, peer],
            recv_sem=shr_recv.at[k, block], device_id=(peer, b), device_id_type=MESH)

    has_up, has_down = q + 1 < Q, q >= 1
    start = b * share
    first = pl.multiple_of(jnp.minimum(start // 16 * 16, R - W), 16)
    need_below = PIECES - 1 - sum((first >= x).astype(jnp.int32) for x in bounds[1:-1])
    need_above = sum((first + W > x).astype(jnp.int32) for x in bounds[1:-1])

    def extract(k):
        window = zbuf[k, pl.ds(first, W), :]
        hot = (lax.broadcasted_iota(jnp.int32, (SP, W), 1)
               == lax.broadcasted_iota(jnp.int32, (SP, W), 0) + (start - first))
        inside = lax.broadcasted_iota(jnp.int32, (SP, W), 0) < share
        hot = jnp.where(hot & inside, 1.0, 0.0).astype(jnp.bfloat16)
        rows = lax.dot_general(hot, window, (((1,), (0,)), ((), ())),
                               preferred_element_type=jnp.float32)
        shr[k, l] = rows.astype(jnp.bfloat16)
        for d in range(1, L):
            share_copy(k, l, lax.rem(l + d, L)).start()

    def wait_shares(place):
        for core in range(2):
            k = place * 2 + core
            for d in range(1, L):
                other = lax.rem(l + d, L)
                share_copy(k, other, other).wait_recv()

    def multiply(place):
        part = None
        wait_shares(place)
        for core in range(2):
            k = place * 2 + core
            a = shr[k].reshape(L * SP, T)
            term = lax.dot_general(a, zbuf[k], NT, preferred_element_type=jnp.float32)
            part = term if part is None else part + term
        acc[...] += part

    def multiply_step(s):
        @pl.loop(0, 2)
        def _(n):
            place = q - (1 - 2 * n) * s

            @pl.when((place >= 0) & (place < Q) & ((s > 0) | (n < 1)))
            def _():
                multiply(place)

    def send_own(up_first):
        done = set()

        def send(up, i):
            piece = PIECES - 1 - i if up else i
            if piece not in done:
                done.add(piece)
                normalise(piece)

            @pl.when(has_up if up else has_down)
            def _():
                if up:
                    piece_copy(b, piece, up_send, b + 2).start()
                else:
                    piece_copy(b, piece, down_send, b - 2).start()

        for i in range(PIECES):
            send(up_first, i)
            send(not up_first, i)

    @pl.when(q >= Q // 2)
    def _():
        send_own(True)

    @pl.when(q < Q // 2)
    def _():
        send_own(False)

    for i in range(PIECES):
        piece_copy(b, i, mate_send, mate).start()

    acc[...] = jnp.zeros_like(acc)
    extract(b)

    for i in range(PIECES):
        piece_copy(mate, i, mate_send, mate).wait_recv()

    extract(mate)

    def arrive(s, i, between=None):
        below, above = b - 2 * s, b + 2 * s
        from_below, from_above = q - s >= 0, q + s < Q
        down_piece = PIECES - 1 - i

        @pl.when(from_below)
        def _():
            piece_copy(below, down_piece, up_send, b).wait_recv()

            @pl.when(has_up)
            def _():
                piece_copy(below, down_piece, up_send, b + 2).start()
            piece_copy(below, down_piece, mate_send, mate).start()

        @pl.when(from_above)
        def _():
            piece_copy(above, i, down_send, b).wait_recv()

            @pl.when(has_down)
            def _():
                piece_copy(above, i, down_send, b - 2).start()
            piece_copy(above, i, mate_send, mate).start()

        @pl.when(from_below & (i == need_below))
        def _():
            extract(below)

        @pl.when(from_above & (i == need_above))
        def _():
            extract(above)

        if between is not None:
            between()

        @pl.when(from_below)
        def _():
            piece_copy(mate - 2 * s, down_piece, mate_send, mate).wait_recv()

            @pl.when(i == need_below)
            def _():
                extract(mate - 2 * s)

        @pl.when(from_above)
        def _():
            piece_copy(mate + 2 * s, i, mate_send, mate).wait_recv()

            @pl.when(i == need_above)
            def _():
                extract(mate + 2 * s)

        if i == 0:
            multiply_step(s - 1)

    def finish(piece, place):
        lo, hi = bounds[piece], bounds[piece + 1]
        part = acc[:, lo:hi]
        if place is not None:
            for core in range(2):
                k = place * 2 + core
                a = shr[k].reshape(L * SP, T)
                part = part + lax.dot_general(a, zbuf[k, lo:hi, :], NT,
                                              preferred_element_type=jnp.float32)
        part = part / total
        for j in range(L):
            o_ref[:, j, lo:hi] = part[j * SP:j * SP + share]

    @pl.loop(1, Q - 1)
    def _(s):
        for i in range(PIECES):
            arrive(s, i)

    def finish_ends(steps):
        for end, place in ((Q - 1, 0), (0, Q - 1)):
            @pl.when(q == end)
            def _():
                for i in steps:
                    finish(PIECES - 1 - i if end else i, place)

    def finish_early():
        for end, place in ((Q - 1, 0), (0, Q - 1)):
            @pl.when(q == end)
            def _():
                wait_shares(place)

        finish_ends(range(PIECES - 1))

    for i in range(PIECES):
        arrive(Q - 1, i, finish_early if i == PIECES - 1 else None)
    finish_ends([PIECES - 1])

    @pl.when((q > 0) & (q < Q - 1))
    def _():
        for i in range(PIECES):
            finish(i, None)

    for d in range(1, B):
        other = lax.rem(b + d, B)
        stat_copy(b, other).wait_send()

    @pl.loop(0, Q)
    def _(s):
        below, above = b - 2 * s, b + 2 * s
        from_below, from_above = q - s >= 0, q + s < Q

        for i in range(PIECES):
            @pl.when(from_below & has_up)
            def _():
                piece_copy(below, i, up_send, b + 2).wait_send()

            @pl.when(from_above & has_down)
            def _():
                piece_copy(above, i, down_send, b - 2).wait_send()

            @pl.when(from_below)
            def _():
                piece_copy(below, i, mate_send, mate).wait_send()

            @pl.when(from_above & (s > 0))
            def _():
                piece_copy(above, i, mate_send, mate).wait_send()

    @pl.loop(0, B)
    def _(k):
        for d in range(1, L):
            other = lax.rem(l + d, L)
            share_copy(k, l, other).wait_send()


F, M2, M1, C, N1, N2, D = range(7)


def line_kernel(L, B, x_hbm, o_ref, zbuf, shr, acc_lo, acc_hi, acc_mid, tile_send, tile_recv, shift_ref, place_ref,
                cols, stats, x_ref, raw,
                z_recv, out_send, in_send, mate_send, own_send, own_out, own_in, first_send, raw_recv, raw_send, shr_recv, shr_send, diag_recv, diag_send, t_recv, t_send,
                st_recv, st_send, x_sem):
    R, T = x_hbm.shape
    total = T * B
    share = R // B
    half = 2 * share
    SP = shr.shape[2]
    pad = share - 128
    W = min(up_to(share + 15, 16), R)
    low, high = R - (3 * half - pad) // 16 * 16, (3 * half - pad) // 16 * 16
    split = (3 * half - share) // 16 * 16
    edges = [0, low, R - split, (R // 2 - pad) // 16 * 16]
    edges = edges + [R - x for x in reversed(edges)]
    size = [edges[p + 1] - edges[p] for p in range(7)]
    far = R - size[M2] - size[M1] - size[N1]
    tile = largest_tile(R, 352)
    RAW = raw.shape[1]
    WS = acc_lo.shape[1]
    hi_lane, mid_lane = R - WS, WS // 128 * 128
    WM = acc_mid.shape[1]
    l, b = lax.axis_index("loop"), lax.axis_index("bulk")
    q, c = b // 2, b % 2
    mate = q * 2 + (1 - c)
    upper = q >= 2
    inner = (q == 1) | (q == 2)
    outer = (q == 0) | (q == 3)
    step = jnp.where(upper, 1, -1)
    H = [jnp.where(upper, h, 3 - h) for h in range(4)]
    out_nbr, in_nbr = b + 2 * step, b - 2 * step
    lx, ly, ld = l + 1 - 2 * (l % 2), lax.rem(l + 2, 4), 3 - l

    def align(value, unit=16):
        return pl.multiple_of(value, unit)

    start = [align(jnp.where(upper, edges[p], edges[6 - p])) for p in range(7)]

    barrier = pltpu.get_barrier_semaphore()
    for d in range(1, B):
        pl.semaphore_signal(barrier, inc=1, device_id=(l, lax.rem(b + d, B)), device_id_type=MESH)
    for line in (lx, ly):
        pl.semaphore_signal(barrier, inc=1, device_id=(line, b), device_id_type=MESH)

    def load(i):
        rows = pl.ds(pl.multiple_of(i * tile, tile), tile)
        return pltpu.make_async_copy(x_hbm.at[rows, :], x_ref.at[rows, :], x_sem.at[i])

    @pl.loop(0, R // tile)
    def _(i):
        load(i).start()

    lane = lax.broadcasted_iota(jnp.int32, (tile, 128), 1)

    @pl.loop(0, R // tile)
    def _(i):
        rows = pl.ds(pl.multiple_of(i * tile, tile), tile)
        load(i).wait()
        v = x_ref[rows, :]
        mean = jnp.sum(v, axis=1, keepdims=True) / T
        dev = v - mean
        m2 = jnp.sum(dev * dev, axis=1, keepdims=True)
        cols[rows, :] = jnp.where(lane == 0, mean, jnp.where(lane == 1, m2, 0.0))

    pick = (lax.broadcasted_iota(jnp.int32, (8, 128), 0)
            == lax.broadcasted_iota(jnp.int32, (8, 128), 1)).astype(jnp.float32)
    line = lax.dot_general(pick, cols[...], NT, precision=lax.Precision.HIGHEST,
                           preferred_element_type=jnp.float32)
    stats[b] = line[:2]

    pl.semaphore_wait(barrier, B - 1 + 2)

    def stat_copy(source, peer):
        return pltpu.make_async_remote_copy(
            src_ref=stats.at[source], dst_ref=stats.at[source],
            send_sem=st_send, recv_sem=st_recv,
            device_id=(l, peer), device_id_type=MESH)

    for d in range(1, B):
        stat_copy(b, lax.rem(b + d, B)).start()
    def raw_copy(p, slot, peer):
        return pltpu.make_async_remote_copy(
            src_ref=x_ref.at[pl.ds(start[p], RAW), :], dst_ref=raw.at[slot], send_sem=raw_send,
            recv_sem=raw_recv.at[slot], device_id=(l, peer), device_id_type=MESH)

    @pl.when(inner)
    def _():
        raw_copy(D, 0, out_nbr).start()
        raw_copy(F, 0, in_nbr).start()

    @pl.when(outer)
    def _():
        raw_copy(D, 1, in_nbr).start()

    gathered = stats.at[pl.ds(0, B - 1)]
    all_stats = pltpu.make_async_remote_copy(
        src_ref=gathered, dst_ref=gathered, send_sem=st_send, recv_sem=st_recv,
        device_id=(l, b), device_id_type=MESH)
    all_stats.wait_recv()

    mean = stats[0, 0:1]
    for k in range(1, B):
        mean = mean + stats[k, 0:1]
    mean = mean / B
    square = jnp.zeros_like(mean)
    for k in range(B):
        shift = stats[k, 0:1] - mean
        square = square + (stats[k, 1:2] + T * (shift * shift))
    scale = lax.rsqrt(square / total + epsilon)
    sub = lax.broadcasted_iota(jnp.int32, (8, R), 0)
    both = jnp.where(sub == 0, mean, jnp.where(sub == 1, scale, 0.0))
    cols[...] = lax.dot_general(both, pick, TN, precision=lax.Precision.HIGHEST,
                                preferred_element_type=jnp.float32)

    def normalise(begin, count):
        unit = count if count <= 288 else largest_tile(count, 128)

        def chunk(i):
            rows = pl.ds(pl.multiple_of(begin + i * unit, 16), unit)
            z = (x_ref[rows, :] - cols[rows, 0:1]) * cols[rows, 1:2]
            zbuf[b, rows, :] = z.astype(jnp.bfloat16)

        if unit == count:
            chunk(0)
        else:
            pl.loop(0, count // unit)(chunk)

    def z_copy(k, p, send_sem, peer, skip=0):
        part = zbuf.at[k, pl.ds(align(start[p] + skip), size[p] - skip), :]
        return pltpu.make_async_remote_copy(
            src_ref=part, dst_ref=part, send_sem=send_sem,
            recv_sem=z_recv.at[k, jnp.where(upper, p, 6 - p)], device_id=(l, peer), device_id_type=MESH)

    def first_copy(k, p, peer):
        return z_copy(k, p, first_send, peer, RAW)

    def unpack(slot, k):
        raw_copy(D, slot, b).wait_recv()
        rows = pl.ds(start[D], RAW)
        z = (raw[slot] - cols[rows, 0:1]) * cols[rows, 1:2]
        zbuf[k, rows, :] = z.astype(jnp.bfloat16)

    def send_out(k, p):
        return z_copy(k, p, out_send, out_nbr)

    def send_in(k, p):
        return z_copy(k, p, in_send, in_nbr)

    def mate_copy(k, p):
        return z_copy(k, p, mate_send, mate)

    def mate_own(k):
        part = zbuf.at[k]
        return pltpu.make_async_remote_copy(
            src_ref=part, dst_ref=part, send_sem=own_send, recv_sem=z_recv.at[k, 0],
            device_id=(l, mate), device_id_type=MESH)

    def share_copy(k, block, peer, way):
        part = shr.at[k, block, pl.ds(0, SR), :]
        return pltpu.make_async_remote_copy(
            src_ref=part, dst_ref=part, send_sem=shr_send,
            recv_sem=shr_recv.at[k, way], device_id=(peer, b), device_id_type=MESH)

    SR = up_to(share, 8)
    cut = up_to(share // 2, 16)

    def diag_copy(k, block, peer, way):
        rows = pl.ds(0, cut) if way == 0 else pl.ds(cut, SR - cut)
        part = shr.at[k, block, rows, :]
        return pltpu.make_async_remote_copy(
            src_ref=part, dst_ref=part, send_sem=diag_send,
            recv_sem=diag_recv.at[k // 2], device_id=(peer, b), device_id_type=MESH)

    first = align(jnp.minimum(b * share // 16 * 16, jnp.where(q == 0, size[D], R) - W))

    def extract_one(k):
        window = zbuf[k, pl.ds(first, W), :]
        row = lax.broadcasted_iota(jnp.int32, (SP, W), 0)
        hot = lax.broadcasted_iota(jnp.int32, (SP, W), 1) == row + (b * share - first)
        hot = jnp.where(hot & (row < share), 1.0, 0.0).astype(jnp.bfloat16)
        rows = lax.dot_general(hot, window, (((1,), (0,)), ((), ())),
                               preferred_element_type=jnp.float32)
        shr[k, l] = rows.astype(jnp.bfloat16)
        share_copy(k, l, lx, 0).start()
        share_copy(k, l, ly, 1).start()

    def extract(place):
        @pl.loop(0, 2)
        def _(core):
            extract_one(place * 2 + core)

    def pass_on(place):
        @pl.loop(0, 2)
        def _(core):
            k = place * 2 + core
            share_copy(k, lx, lx, 0).wait_recv()
            diag_copy(k, lx, ly, 0).start()
            share_copy(k, ly, ly, 1).wait_recv()
            diag_copy(k, ly, lx, 1).start()

    def wait_diag(place):
        part = shr.at[pl.ds(place * 2, 2), ld, pl.ds(0, SR), :]
        pltpu.make_async_remote_copy(
            src_ref=part, dst_ref=part, send_sem=diag_send, recv_sem=diag_recv.at[place],
            device_id=(l, b), device_id_type=MESH).wait_recv()

    def product(place, begin, width):
        part = None
        for core in range(2):
            k = place * 2 + core
            term = lax.dot_general(shr[k].reshape(L * SP, T), zbuf[k, begin:begin + width, :], NT,
                                   preferred_element_type=jnp.float32)
            part = term if part is None else part + term
        return part

    def add_sides(place):
        acc_lo[...] += product(place, 0, WS)
        acc_hi[...] += product(place, hi_lane, WS)

    def add_middle(place):
        acc_mid[...] += product(place, mid_lane, WM)

    def own(h):
        return H[h] * 2 + c

    def other(h):
        return H[h] * 2 + (1 - c)

    def take(h, p, onward=None, first=False):
        if first:
            first_copy(own(h), p, mate).wait_recv()
        else:
            mate_copy(own(h), p).wait_recv()
        if onward is not None:
            onward(own(h), p).start()
        mate_copy(own(h), p).start()

    def mate_take(h, pieces):
        for p in pieces:
            mate_copy(other(h), p).wait_recv()

    def tile_copy(side, j, core, block, slot):
        return pltpu.make_async_remote_copy(
            src_ref=tile_send.at[side, j, core, pl.ds(0, SR), :],
            dst_ref=tile_recv.at[block, pl.ds(0, SR), pl.ds(pl.multiple_of(slot * 128, 128), 128)],
            send_sem=t_send, recv_sem=t_recv.at[block],
            device_id=(j, 6 * side + core), device_id_type=MESH)

    def make_hot():
        shift = (lax.broadcasted_iota(jnp.int32, (SR, 128), 0)
                 == lax.broadcasted_iota(jnp.int32, (SR, 128), 1) + jnp.where(c == 0, pad, 0))
        shift_ref[...] = jnp.where(shift, 1.0, 0.0).astype(jnp.bfloat16)
        row = lax.broadcasted_iota(jnp.int32, (512, WM), 0)
        lane = jnp.where(row < 256, row + half + pad, row - 256 + R // 2 + pad) - mid_lane
        hot = lax.broadcasted_iota(jnp.int32, (512, WM), 1) == lane
        place_ref[...] = jnp.where(hot, 1.0, 0.0).astype(jnp.bfloat16)
        for side, slot in ((0, 0), (3, 3)):
            @pl.when(q == side)
            def _():
                tile_recv[:, :, slot * 128:slot * 128 + 128] = jnp.zeros((L, SP, 128), jnp.bfloat16)

    def finish_tiles(j):
        rows = pl.ds(pl.multiple_of(j * SP, SP), SP)
        for side, acc, begin in ((0, acc_lo, 0), (1, acc_hi, hi_lane)):
            value = acc[rows, :]
            for core in range(2):
                k = H[0] * 2 + core
                value = value + lax.dot_general(shr[k, j], zbuf[k, begin:begin + WS, :], NT,
                                                preferred_element_type=jnp.float32)
            acc[rows, :] = value
            turned = lax.dot_general((value[:SR] / total).astype(jnp.bfloat16), shift_ref[...], TN,
                                     preferred_element_type=jnp.float32)
            for core in range(2):
                at = (WS - half if side else 0) + core * share
                tile_send[side, j, core, :share, :] = turned[at:at + share].astype(jnp.bfloat16)

    def tile_copies(j, act):
        for side, skipped in ((0, 2), (1, 5)):
            @pl.when(b != skipped)
            def _():
                for core in range(2):
                    act(tile_copy(side, j, core, l, b - 2))

    def start_tiles(j):
        tile_copies(j, lambda copy: copy.start())

    def wait_tile(block):
        part = tile_recv.at[block, pl.ds(0, SR), pl.ds(0, 384)]
        pltpu.make_async_remote_copy(
            src_ref=part, dst_ref=part, send_sem=t_send, recv_sem=t_recv.at[block],
            device_id=(l, b), device_id_type=MESH).wait_recv()

    normalise(start[D], size[D])

    @pl.when(inner)
    def _():
        first_copy(b, D, out_nbr).start()

    @pl.when(outer)
    def _():
        first_copy(b, D, in_nbr).start()
    normalise(start[F], size[F])

    @pl.when(inner)
    def _():
        first_copy(b, F, in_nbr).start()
    normalise(low, high - low)

    @pl.when(inner)
    def _():
        for p in (M2, M1, C, D):
            z_copy(b, p, own_in, in_nbr).start()
        for p in (F, C, N2):
            z_copy(b, p, own_out, out_nbr).start()

    @pl.when(outer)
    def _():
        for p in (N2, N1, C, F, M1, M2):
            z_copy(b, p, own_in, in_nbr).start()
    mate_own(b).start()
    extract_one(b)
    make_hot()
    mate_own(mate).wait_recv()
    extract_one(mate)

    @pl.when(inner)
    def _():
        unpack(0, own(1))
        unpack(1, own(3))
        take(1, D, send_out, True)
        take(3, D, None, True)
        pass_on(q)
        take(1, N2, send_out)
        take(3, N2)
        take(1, N1)
        take(3, N1)
        take(1, C, send_out)
        take(3, C)
        mate_take(3, (D, N2, N1, C))
        extract(H[3])
        mate_take(1, (D, N2, N1, C))
        extract(H[1])
        take(1, F, send_out)
        take(3, F, send_in)
        send_in(own(3), C).start()

    @pl.when(outer)
    def _():
        unpack(0, own(2))
        take(2, D, None, True)
        mate_take(2, (D,))
        extract(H[2])
        pass_on(q)
        take(2, F)
        take(2, C)
        take(2, N2)
        pass_on(H[2])
        take(1, D)
        mate_take(1, (D,))
        extract(H[1])
        mate_take(2, (F, C, N2))
    wait_diag(q)
    acc_lo[...] = product(q, 0, WS)
    acc_hi[...] = product(q, hi_lane, WS)
    acc_mid[...] = product(q, mid_lane, WM)

    second, third = jnp.where(inner, H[3], H[2]), H[1]

    @pl.when(inner)
    def _():
        pass_on(H[3])
        take(3, M1, send_in)
        take(3, M2, send_in)
        send_in(own(3), D).start()
        take(0, D, send_out)
        take(0, C, send_out)
        for p in (N1, N2):
            z_copy(b, p, own_in, in_nbr).start()
        pass_on(H[1])
        take(0, N1)
        take(0, N2, send_out)
        mate_take(3, (F, M1, M2))
        mate_take(0, (D, C, N1, N2))
        extract(H[0])
        mate_take(1, (F,))

    @pl.when(outer)
    def _():
        take(1, N2)
        take(1, C)
        take(1, F)
        pass_on(H[1])
        mate_take(1, (N2, C, F))
    wait_diag(second)
    add_sides(second)

    @pl.when(inner)
    def _():
        take(0, F, send_out)

    @pl.when(outer)
    def _():
        take(0, D)
        mate_take(0, (D,))
        extract(H[0])
    wait_diag(third)
    add_sides(third)

    @pl.when(inner)
    def _():
        mate_take(0, (F,))
        finish_tiles(l)
        start_tiles(l)

    @pl.when(outer)
    def _():
        take(0, C)
        take(0, N2)
    pass_on(H[0])

    @pl.when(inner)
    def _():
        @pl.loop(0, 2)
        def _(n):
            j = jnp.where(n == 0, lx, ly)
            finish_tiles(j)
            start_tiles(j)
        for p in (N1, N2):
            send_in(own(3), p).start()
        wait_diag(H[0])
        finish_tiles(ld)
        start_tiles(ld)
        for p in (M1, M2):
            take(1, p)
        mate_take(1, (M1, M2))
    add_middle(second)
    add_middle(third)

    @pl.when(inner)
    def _():
        for p in (M1, M2):
            take(0, p)
        mate_take(0, (M1, M2))

    @pl.when(outer)
    def _():
        take(0, F)
        mate_take(0, (C, N2, F))
        wait_diag(H[0])
        add_sides(H[0])
    add_middle(H[0])

    for j in range(L):
        rows = slice(j * SP, j * SP + share)
        o_ref[:, j, :mid_lane] = acc_lo[rows, :mid_lane] / total
        o_ref[:, j, mid_lane:mid_lane + WM] = acc_mid[rows, :] / total
        o_ref[:, j, mid_lane + WM:] = acc_hi[rows, :][:, mid_lane + WM - hi_lane:] / total

    @pl.when(outer)
    def _():
        place = lax.broadcasted_iota(jnp.int32, (share, WM), 1) + mid_lane
        first_lane = half + pad + jnp.where(upper, 0, 128)
        last_lane = R // 2 + pad + jnp.where(upper, 128, 256)
        inside = ((place >= first_lane) & (place < half + pad + 256)
                  | (place >= R // 2 + pad) & (place < last_lane))
        for d in (l, lx, ly, ld):
            wait_tile(d)
            placed = lax.dot_general(tile_recv[d], place_ref[...], (((1,), (0,)), ((), ())),
                                     preferred_element_type=jnp.float32)[:share]
            middle = pl.ds(mid_lane, WM)
            o_ref[:, d, middle] = jnp.where(inside, placed, o_ref[:, d, middle])

    all_stats.wait_send()
    mate_own(b).wait_send()

    def sent(part, sem):
        pltpu.make_async_remote_copy(
            src_ref=part, dst_ref=part, send_sem=sem, recv_sem=st_recv,
            device_id=(l, b), device_id_type=MESH).wait_send()

    @pl.when(inner)
    def _():
        sent(zbuf.at[0, pl.ds(0, size[F] + size[C] + size[N2]), :], own_out)
        sent(zbuf.at[pl.ds(0, 2), pl.ds(0, size[D] - RAW), :], first_send)
        sent(raw, raw_send)
        sent(zbuf.at[pl.ds(0, 2), pl.ds(0, far), :], out_send)
        sent(zbuf.at[0], in_send)
        sent(zbuf.at[pl.ds(0, 3)], mate_send)
        for skipped in (True, False):
            @pl.when(((b == 2) | (b == 5)) == skipped)
            def _():
                sides = 1 if skipped else 2
                sent(tile_send.at[pl.ds(0, sides), :, :, pl.ds(0, SR), :], t_send)

    @pl.when(outer)
    def _():
        sent(zbuf.at[0, pl.ds(0, size[D] - RAW), :], first_send)
        sent(raw.at[0], raw_send)
        sent(zbuf.at[pl.ds(0, 3), pl.ds(0, far), :], mate_send)

    sent(zbuf.at[0, pl.ds(0, R - size[D]), :], own_in)
    sent(shr.at[pl.ds(0, L), :, pl.ds(0, SR), :], shr_send)
    sent(shr.at[pl.ds(0, B // L), :, pl.ds(0, SR), :], diag_send)


def line_call(L, B, series):
    R, T = series.shape
    share = R // B
    SP = up_to(share, 16)
    pad = share - 128
    high = (3 * 2 * share - pad) // 16 * 16
    WS = R - high
    mid_lane = WS // 128 * 128
    WM = up_to(R // 2 + pad + 256, 128) - mid_lane
    vmem = pl.BlockSpec(memory_space=pltpu.VMEM)
    dma = pltpu.SemaphoreType.DMA
    return pl.pallas_call(
        functools.partial(line_kernel, L, B),
        out_shape=jax.ShapeDtypeStruct((share, L, R), jnp.float32),
        in_specs=[pl.BlockSpec(memory_space=pltpu.HBM)],
        out_specs=vmem,
        scratch_shapes=[
            pltpu.VMEM((B, R, T), jnp.bfloat16),
            pltpu.VMEM((B, L, SP, T), jnp.bfloat16),
            pltpu.VMEM((L * SP, WS), jnp.float32),
            pltpu.VMEM((L * SP, WS), jnp.float32),
            pltpu.VMEM((L * SP, WM), jnp.float32),
            pltpu.VMEM((2, L, 2, SP, 128), jnp.bfloat16),
            pltpu.VMEM((L, SP, 512), jnp.bfloat16),
            pltpu.VMEM((up_to(share, 8), 128), jnp.bfloat16),
            pltpu.VMEM((512, WM), jnp.bfloat16),
            pltpu.VMEM((R, 128), jnp.float32),
            pltpu.VMEM((B, 2, R), jnp.float32),
            pltpu.VMEM((R, T), jnp.float32),
            pltpu.VMEM((2, (R - high) // 32 * 16, T), jnp.float32),
            dma((B, 7)), dma, dma, dma, dma, dma, dma, dma, dma((2,)), dma,
            dma((B, 2)), dma, dma((B // 2,)), dma, dma((L,)), dma,
            dma, dma, dma((R // largest_tile(R, 352),)),
        ],
        compiler_params=pltpu.CompilerParams(
            collective_id=0, has_side_effects=True, vmem_limit_bytes=34 * 1024 * 1024),
    )(pltpu.with_memory_space_constraint(series, pltpu.HBM)).transpose(1, 0, 2)


def solution(mesh):
    L, B = mesh.shape["loop"], mesh.shape["bulk"]

    def on_device(series):
        R, T = series.shape
        share = R // B
        if L == 4 and B == 8 and R % 16 == 0 and T % 128 == 0 and 128 <= share <= 144:
            return line_call(L, B, series)
        SP = up_to(share, 16)
        pieces = 3
        vmem = pl.BlockSpec(memory_space=pltpu.VMEM)
        dma = pltpu.SemaphoreType.DMA
        return pl.pallas_call(
            functools.partial(kernel, L, B, pieces),
            out_shape=jax.ShapeDtypeStruct((share, L, R), jnp.float32),
            in_specs=[pl.BlockSpec(memory_space=pltpu.HBM)],
            out_specs=vmem,
            scratch_shapes=[
                pltpu.VMEM((B, R, T), jnp.bfloat16),
                pltpu.VMEM((B, L, SP, T), jnp.bfloat16),
                pltpu.VMEM((L * SP, R), jnp.float32),
                pltpu.VMEM((R, 128), jnp.float32),
                pltpu.VMEM((B, 2, R), jnp.float32),
                pltpu.VMEM((R, T), jnp.float32),
                dma((B, pieces)), dma((B, pieces)), dma((B, pieces)), dma((B, pieces)),
                dma((B, L)), dma((B, L)), dma((B,)), dma((B,)), dma((R // largest_tile(R, 128),)),
            ],
            compiler_params=pltpu.CompilerParams(
                collective_id=0, has_side_effects=True, vmem_limit_bytes=26 * 1024 * 1024),
        )(pltpu.with_memory_space_constraint(series, pltpu.HBM)).transpose(1, 0, 2)

    return jax.shard_map(
        on_device, mesh=mesh, in_specs=(P("loop", "bulk"),),
        out_specs=P(None, "bulk", "loop"), check_vma=False)
```

```python
import functools
import jax
import jax.numpy as jnp
from jax import lax
from jax.experimental import pallas as pl
from jax.experimental.pallas import tpu as pltpu
from jax.sharding import PartitionSpec as P

epsilon = 1e-06
MESH = pl.DeviceIdType.MESH
NT = (((1,), (1,)), ((), ()))
TN = (((0,), (0,)), ((), ()))


def up_to(value, unit):
    return -(-value // unit) * unit


def largest_tile(rows, limit):
    return max(t for t in range(16, limit + 1, 16) if rows % t == 0)


def kernel(L, B, PIECES, x_hbm, o_ref, zbuf, shr, acc, cols, stats, x_ref,
           z_recv, up_send, down_send, mate_send, shr_recv, shr_send, st_recv, st_send, x_sem):
    R, T = x_hbm.shape
    total = T * B
    Q = B // 2
    share = R // B
    SP = shr.shape[2]
    W = min(up_to(share + 15, 16), R)
    bounds = [up_to(R * i // PIECES, 128) for i in range(PIECES)] + [R]
    tile = largest_tile(R, 128)
    l, b = lax.axis_index("loop"), lax.axis_index("bulk")
    q, c = b // 2, b % 2
    mate = q * 2 + (1 - c)

    barrier = pltpu.get_barrier_semaphore()
    for d in range(1, B):
        pl.semaphore_signal(barrier, inc=1, device_id=(l, lax.rem(b + d, B)), device_id_type=MESH)
    for d in range(1, L):
        pl.semaphore_signal(barrier, inc=1, device_id=(lax.rem(l + d, L), b), device_id_type=MESH)

    def load(i):
        rows = pl.ds(pl.multiple_of(i * tile, tile), tile)
        return pltpu.make_async_copy(x_hbm.at[rows, :], x_ref.at[rows, :], x_sem.at[i])

    @pl.loop(0, R // tile)
    def _(i):
        load(i).start()

    lane = lax.broadcasted_iota(jnp.int32, (tile, 128), 1)

    @pl.loop(0, R // tile)
    def _(i):
        rows = pl.ds(pl.multiple_of(i * tile, tile), tile)
        load(i).wait()
        v = x_ref[rows, :]
        mean = jnp.sum(v, axis=1, keepdims=True) / T
        dev = v - mean
        m2 = jnp.sum(dev * dev, axis=1, keepdims=True)
        cols[rows, :] = jnp.where(lane == 0, mean, jnp.where(lane == 1, m2, 0.0))

    pick = (lax.broadcasted_iota(jnp.int32, (8, 128), 0)
            == lax.broadcasted_iota(jnp.int32, (8, 128), 1)).astype(jnp.float32)
    line = lax.dot_general(pick, cols[...], NT, precision=lax.Precision.HIGHEST,
                           preferred_element_type=jnp.float32)
    stats[b] = line[:2]

    pl.semaphore_wait(barrier, B - 1 + L - 1)

    def stat_copy(source, peer):
        return pltpu.make_async_remote_copy(
            src_ref=stats.at[source], dst_ref=stats.at[source],
            send_sem=st_send.at[peer], recv_sem=st_recv.at[source],
            device_id=(l, peer), device_id_type=MESH)

    for d in range(1, B):
        stat_copy(b, lax.rem(b + d, B)).start()
    for d in range(1, B):
        other = lax.rem(b + d, B)
        stat_copy(other, other).wait_recv()

    mean = stats[0, 0:1]
    for k in range(1, B):
        mean = mean + stats[k, 0:1]
    mean = mean / B
    square = jnp.zeros_like(mean)
    for k in range(B):
        shift = stats[k, 0:1] - mean
        square = square + (stats[k, 1:2] + T * (shift * shift))
    scale = lax.rsqrt(square / total + epsilon)
    sub = lax.broadcasted_iota(jnp.int32, (8, R), 0)
    both = jnp.where(sub == 0, mean, jnp.where(sub == 1, scale, 0.0))
    cols[...] = lax.dot_general(both, pick, TN, precision=lax.Precision.HIGHEST,
                                preferred_element_type=jnp.float32)

    def normalise(piece):
        size = bounds[piece + 1] - bounds[piece]
        step = largest_tile(size, 128)

        @pl.loop(0, size // step)
        def _(i):
            rows = pl.ds(pl.multiple_of(bounds[piece] + i * step, 16), step)
            z = (x_ref[rows, :] - cols[rows, 0:1]) * cols[rows, 1:2]
            zbuf[b, rows, :] = z.astype(jnp.bfloat16)

    def piece_copy(k, piece, send_sem, peer):
        part = zbuf.at[k, pl.ds(bounds[piece], bounds[piece + 1] - bounds[piece]), :]
        return pltpu.make_async_remote_copy(
            src_ref=part, dst_ref=part, send_sem=send_sem.at[k, piece],
            recv_sem=z_recv.at[k, piece], device_id=(l, peer), device_id_type=MESH)

    def share_copy(k, block, peer):
        return pltpu.make_async_remote_copy(
            src_ref=shr.at[k, block], dst_ref=shr.at[k, block], send_sem=shr_send.at[k, peer],
            recv_sem=shr_recv.at[k, block], device_id=(peer, b), device_id_type=MESH)

    has_up, has_down = q + 1 < Q, q >= 1
    start = b * share
    first = pl.multiple_of(jnp.minimum(start // 16 * 16, R - W), 16)
    need_below = PIECES - 1 - sum((first >= x).astype(jnp.int32) for x in bounds[1:-1])
    need_above = sum((first + W > x).astype(jnp.int32) for x in bounds[1:-1])

    def extract(k):
        window = zbuf[k, pl.ds(first, W), :]
        hot = (lax.broadcasted_iota(jnp.int32, (SP, W), 1)
               == lax.broadcasted_iota(jnp.int32, (SP, W), 0) + (start - first))
        inside = lax.broadcasted_iota(jnp.int32, (SP, W), 0) < share
        hot = jnp.where(hot & inside, 1.0, 0.0).astype(jnp.bfloat16)
        rows = lax.dot_general(hot, window, (((1,), (0,)), ((), ())),
                               preferred_element_type=jnp.float32)
        shr[k, l] = rows.astype(jnp.bfloat16)
        for d in range(1, L):
            share_copy(k, l, lax.rem(l + d, L)).start()

    def wait_shares(place):
        for core in range(2):
            k = place * 2 + core
            for d in range(1, L):
                other = lax.rem(l + d, L)
                share_copy(k, other, other).wait_recv()

    def multiply(place):
        part = None
        wait_shares(place)
        for core in range(2):
            k = place * 2 + core
            a = shr[k].reshape(L * SP, T)
            term = lax.dot_general(a, zbuf[k], NT, preferred_element_type=jnp.float32)
            part = term if part is None else part + term
        acc[...] += part

    def multiply_step(s):
        @pl.loop(0, 2)
        def _(n):
            place = q - (1 - 2 * n) * s

            @pl.when((place >= 0) & (place < Q) & ((s > 0) | (n < 1)))
            def _():
                multiply(place)

    def send_own(up_first):
        done = set()

        def send(up, i):
            piece = PIECES - 1 - i if up else i
            if piece not in done:
                done.add(piece)
                normalise(piece)

            @pl.when(has_up if up else has_down)
            def _():
                if up:
                    piece_copy(b, piece, up_send, b + 2).start()
                else:
                    piece_copy(b, piece, down_send, b - 2).start()

        for i in range(PIECES):
            send(up_first, i)
            send(not up_first, i)

    @pl.when(q >= Q // 2)
    def _():
        send_own(True)

    @pl.when(q < Q // 2)
    def _():
        send_own(False)

    for i in range(PIECES):
        piece_copy(b, i, mate_send, mate).start()

    acc[...] = jnp.zeros_like(acc)
    extract(b)

    for i in range(PIECES):
        piece_copy(mate, i, mate_send, mate).wait_recv()

    extract(mate)

    def arrive(s, i, between=None):
        below, above = b - 2 * s, b + 2 * s
        from_below, from_above = q - s >= 0, q + s < Q
        down_piece = PIECES - 1 - i

        @pl.when(from_below)
        def _():
            piece_copy(below, down_piece, up_send, b).wait_recv()

            @pl.when(has_up)
            def _():
                piece_copy(below, down_piece, up_send, b + 2).start()
            piece_copy(below, down_piece, mate_send, mate).start()

        @pl.when(from_above)
        def _():
            piece_copy(above, i, down_send, b).wait_recv()

            @pl.when(has_down)
            def _():
                piece_copy(above, i, down_send, b - 2).start()
            piece_copy(above, i, mate_send, mate).start()

        @pl.when(from_below & (i == need_below))
        def _():
            extract(below)

        @pl.when(from_above & (i == need_above))
        def _():
            extract(above)

        if between is not None:
            between()

        @pl.when(from_below)
        def _():
            piece_copy(mate - 2 * s, down_piece, mate_send, mate).wait_recv()

            @pl.when(i == need_below)
            def _():
                extract(mate - 2 * s)

        @pl.when(from_above)
        def _():
            piece_copy(mate + 2 * s, i, mate_send, mate).wait_recv()

            @pl.when(i == need_above)
            def _():
                extract(mate + 2 * s)

        if i == 0:
            multiply_step(s - 1)

    def finish(piece, place):
        lo, hi = bounds[piece], bounds[piece + 1]
        part = acc[:, lo:hi]
        if place is not None:
            for core in range(2):
                k = place * 2 + core
                a = shr[k].reshape(L * SP, T)
                part = part + lax.dot_general(a, zbuf[k, lo:hi, :], NT,
                                              preferred_element_type=jnp.float32)
        part = part / total
        for j in range(L):
            o_ref[:, j, lo:hi] = part[j * SP:j * SP + share]

    @pl.loop(1, Q - 1)
    def _(s):
        for i in range(PIECES):
            arrive(s, i)

    def finish_ends(steps):
        for end, place in ((Q - 1, 0), (0, Q - 1)):
            @pl.when(q == end)
            def _():
                for i in steps:
                    finish(PIECES - 1 - i if end else i, place)

    def finish_early():
        for end, place in ((Q - 1, 0), (0, Q - 1)):
            @pl.when(q == end)
            def _():
                wait_shares(place)

        finish_ends(range(PIECES - 1))

    for i in range(PIECES):
        arrive(Q - 1, i, finish_early if i == PIECES - 1 else None)
    finish_ends([PIECES - 1])

    @pl.when((q > 0) & (q < Q - 1))
    def _():
        for i in range(PIECES):
            finish(i, None)

    for d in range(1, B):
        other = lax.rem(b + d, B)
        stat_copy(b, other).wait_send()

    @pl.loop(0, Q)
    def _(s):
        below, above = b - 2 * s, b + 2 * s
        from_below, from_above = q - s >= 0, q + s < Q

        for i in range(PIECES):
            @pl.when(from_below & has_up)
            def _():
                piece_copy(below, i, up_send, b + 2).wait_send()

            @pl.when(from_above & has_down)
            def _():
                piece_copy(above, i, down_send, b - 2).wait_send()

            @pl.when(from_below)
            def _():
                piece_copy(below, i, mate_send, mate).wait_send()

            @pl.when(from_above & (s > 0))
            def _():
                piece_copy(above, i, mate_send, mate).wait_send()

    @pl.loop(0, B)
    def _(k):
        for d in range(1, L):
            other = lax.rem(l + d, L)
            share_copy(k, l, other).wait_send()


F, M2, M1, C, N1, N2, D = range(7)


def line_kernel(L, B, x_hbm, o_ref, zbuf, shr, acc_lo, acc_hi, acc_mid, tile_send, tile_recv, shift_ref, place_ref,
                cols, stats, x_ref, raw,
                z_recv, out_send, in_send, mate_send, own_send, own_out, own_in, first_send, raw_recv, raw_send, shr_recv, shr_send, diag_recv, diag_send, t_recv, t_send,
                st_recv, st_send, x_sem):
    R, T = x_hbm.shape
    total = T * B
    share = R // B
    half = 2 * share
    SP = shr.shape[2]
    pad = share - 128
    W = min(up_to(share + 15, 16), R)
    low, high = R - (3 * half - pad) // 16 * 16, (3 * half - pad) // 16 * 16
    split = (3 * half - share) // 16 * 16
    edges = [0, low, R - split, (R // 2 - pad) // 16 * 16]
    edges = edges + [R - x for x in reversed(edges)]
    size = [edges[p + 1] - edges[p] for p in range(7)]
    far = R - size[M2] - size[M1] - size[N1]
    tile = largest_tile(R, 352)
    RAW = raw.shape[1]
    WS = acc_lo.shape[1]
    hi_lane, mid_lane = R - WS, WS // 128 * 128
    WM = acc_mid.shape[1]
    l, b = lax.axis_index("loop"), lax.axis_index("bulk")
    q, c = b // 2, b % 2
    mate = q * 2 + (1 - c)
    upper = q >= 2
    inner = (q == 1) | (q == 2)
    outer = (q == 0) | (q == 3)
    step = jnp.where(upper, 1, -1)
    H = [jnp.where(upper, h, 3 - h) for h in range(4)]
    out_nbr, in_nbr = b + 2 * step, b - 2 * step
    lx, ly, ld = l + 1 - 2 * (l % 2), lax.rem(l + 2, 4), 3 - l

    def align(value, unit=16):
        return pl.multiple_of(value, unit)

    start = [align(jnp.where(upper, edges[p], edges[6 - p])) for p in range(7)]

    barrier = pltpu.get_barrier_semaphore()
    for d in range(1, B):
        pl.semaphore_signal(barrier, inc=1, device_id=(l, lax.rem(b + d, B)), device_id_type=MESH)
    for line in (lx, ly):
        pl.semaphore_signal(barrier, inc=1, device_id=(line, b), device_id_type=MESH)

    def load(i):
        rows = pl.ds(pl.multiple_of(i * tile, tile), tile)
        return pltpu.make_async_copy(x_hbm.at[rows, :], x_ref.at[rows, :], x_sem.at[i])

    @pl.loop(0, R // tile)
    def _(i):
        load(i).start()

    lane = lax.broadcasted_iota(jnp.int32, (tile, 128), 1)

    @pl.loop(0, R // tile)
    def _(i):
        rows = pl.ds(pl.multiple_of(i * tile, tile), tile)
        load(i).wait()
        v = x_ref[rows, :]
        mean = jnp.sum(v, axis=1, keepdims=True) / T
        dev = v - mean
        m2 = jnp.sum(dev * dev, axis=1, keepdims=True)
        cols[rows, :] = jnp.where(lane == 0, mean, jnp.where(lane == 1, m2, 0.0))

    pick = (lax.broadcasted_iota(jnp.int32, (8, 128), 0)
            == lax.broadcasted_iota(jnp.int32, (8, 128), 1)).astype(jnp.float32)
    line = lax.dot_general(pick, cols[...], NT, precision=lax.Precision.HIGHEST,
                           preferred_element_type=jnp.float32)
    stats[b] = line[:2]

    pl.semaphore_wait(barrier, B - 1 + 2)

    def stat_copy(source, peer):
        return pltpu.make_async_remote_copy(
            src_ref=stats.at[source], dst_ref=stats.at[source],
            send_sem=st_send, recv_sem=st_recv,
            device_id=(l, peer), device_id_type=MESH)

    for d in range(1, B):
        stat_copy(b, lax.rem(b + d, B)).start()
    def raw_copy(p, slot, peer):
        return pltpu.make_async_remote_copy(
            src_ref=x_ref.at[pl.ds(start[p], RAW), :], dst_ref=raw.at[slot], send_sem=raw_send,
            recv_sem=raw_recv.at[slot], device_id=(l, peer), device_id_type=MESH)

    @pl.when(inner)
    def _():
        raw_copy(D, 0, out_nbr).start()
        raw_copy(F, 0, in_nbr).start()

    @pl.when(outer)
    def _():
        raw_copy(F, 1, in_nbr).start()

    gathered = stats.at[pl.ds(0, B - 1)]
    all_stats = pltpu.make_async_remote_copy(
        src_ref=gathered, dst_ref=gathered, send_sem=st_send, recv_sem=st_recv,
        device_id=(l, b), device_id_type=MESH)
    all_stats.wait_recv()

    mean = stats[0, 0:1]
    for k in range(1, B):
        mean = mean + stats[k, 0:1]
    mean = mean / B
    square = jnp.zeros_like(mean)
    for k in range(B):
        shift = stats[k, 0:1] - mean
        square = square + (stats[k, 1:2] + T * (shift * shift))
    scale = lax.rsqrt(square / total + epsilon)
    sub = lax.broadcasted_iota(jnp.int32, (8, R), 0)
    both = jnp.where(sub == 0, mean, jnp.where(sub == 1, scale, 0.0))
    cols[...] = lax.dot_general(both, pick, TN, precision=lax.Precision.HIGHEST,
                                preferred_element_type=jnp.float32)

    def normalise(begin, count):
        unit = count if count <= 288 else largest_tile(count, 128)

        def chunk(i):
            rows = pl.ds(pl.multiple_of(begin + i * unit, 16), unit)
            z = (x_ref[rows, :] - cols[rows, 0:1]) * cols[rows, 1:2]
            zbuf[b, rows, :] = z.astype(jnp.bfloat16)

        if unit == count:
            chunk(0)
        else:
            pl.loop(0, count // unit)(chunk)

    def z_copy(k, p, send_sem, peer, skip=0):
        part = zbuf.at[k, pl.ds(align(start[p] + skip), size[p] - skip), :]
        return pltpu.make_async_remote_copy(
            src_ref=part, dst_ref=part, send_sem=send_sem,
            recv_sem=z_recv.at[k, jnp.where(upper, p, 6 - p)], device_id=(l, peer), device_id_type=MESH)

    def first_copy(k, p, peer):
        return z_copy(k, p, first_send, peer, RAW)

    def unpack(slot, k, p):
        raw_copy(p, slot, b).wait_recv()
        rows = pl.ds(start[p], RAW)
        z = (raw[slot] - cols[rows, 0:1]) * cols[rows, 1:2]
        zbuf[k, rows, :] = z.astype(jnp.bfloat16)

    def send_out(k, p):
        return z_copy(k, p, out_send, out_nbr)

    def send_in(k, p):
        return z_copy(k, p, in_send, in_nbr)

    def mate_copy(k, p):
        return z_copy(k, p, mate_send, mate)

    def mate_own(k):
        part = zbuf.at[k]
        return pltpu.make_async_remote_copy(
            src_ref=part, dst_ref=part, send_sem=own_send, recv_sem=z_recv.at[k, 0],
            device_id=(l, mate), device_id_type=MESH)

    def share_copy(k, block, peer, way):
        part = shr.at[k, block, pl.ds(0, SR), :]
        return pltpu.make_async_remote_copy(
            src_ref=part, dst_ref=part, send_sem=shr_send,
            recv_sem=shr_recv.at[k, way], device_id=(peer, b), device_id_type=MESH)

    SR = up_to(share, 8)
    cut = up_to(share // 2, 16)

    def diag_copy(k, block, peer, way):
        rows = pl.ds(0, cut) if way == 0 else pl.ds(cut, SR - cut)
        part = shr.at[k, block, rows, :]
        return pltpu.make_async_remote_copy(
            src_ref=part, dst_ref=part, send_sem=diag_send,
            recv_sem=diag_recv.at[k // 2], device_id=(peer, b), device_id_type=MESH)

    first = align(jnp.minimum(b * share // 16 * 16, jnp.where(q == 0, size[D], R) - W))

    def extract_one(k):
        window = zbuf[k, pl.ds(first, W), :]
        row = lax.broadcasted_iota(jnp.int32, (SP, W), 0)
        hot = lax.broadcasted_iota(jnp.int32, (SP, W), 1) == row + (b * share - first)
        hot = jnp.where(hot & (row < share), 1.0, 0.0).astype(jnp.bfloat16)
        rows = lax.dot_general(hot, window, (((1,), (0,)), ((), ())),
                               preferred_element_type=jnp.float32)
        shr[k, l] = rows.astype(jnp.bfloat16)
        share_copy(k, l, lx, 0).start()
        share_copy(k, l, ly, 1).start()

    def extract(place):
        @pl.loop(0, 2)
        def _(core):
            extract_one(place * 2 + core)

    def pass_on(place):
        @pl.loop(0, 2)
        def _(core):
            k = place * 2 + core
            share_copy(k, lx, lx, 0).wait_recv()
            diag_copy(k, lx, ly, 0).start()
            share_copy(k, ly, ly, 1).wait_recv()
            diag_copy(k, ly, lx, 1).start()

    def wait_diag(place):
        part = shr.at[pl.ds(place * 2, 2), ld, pl.ds(0, SR), :]
        pltpu.make_async_remote_copy(
            src_ref=part, dst_ref=part, send_sem=diag_send, recv_sem=diag_recv.at[place],
            device_id=(l, b), device_id_type=MESH).wait_recv()

    def product(place, begin, width):
        part = None
        for core in range(2):
            k = place * 2 + core
            term = lax.dot_general(shr[k].reshape(L * SP, T), zbuf[k, begin:begin + width, :], NT,
                                   preferred_element_type=jnp.float32)
            part = term if part is None else part + term
        return part

    def add_sides(place):
        acc_lo[...] += product(place, 0, WS)
        acc_hi[...] += product(place, hi_lane, WS)

    def add_middle(place):
        acc_mid[...] += product(place, mid_lane, WM)

    def own(h):
        return H[h] * 2 + c

    def other(h):
        return H[h] * 2 + (1 - c)

    def take(h, p, onward=None, first=False):
        if first:
            first_copy(own(h), p, mate).wait_recv()
        else:
            mate_copy(own(h), p).wait_recv()
        if onward is not None:
            onward(own(h), p).start()
        mate_copy(own(h), p).start()

    def mate_take(h, pieces):
        for p in pieces:
            mate_copy(other(h), p).wait_recv()

    def tile_copy(side, j, core, block, slot):
        return pltpu.make_async_remote_copy(
            src_ref=tile_send.at[side, j, core, pl.ds(0, SR), :],
            dst_ref=tile_recv.at[block, pl.ds(0, SR), pl.ds(pl.multiple_of(slot * 128, 128), 128)],
            send_sem=t_send, recv_sem=t_recv.at[block],
            device_id=(j, 6 * side + core), device_id_type=MESH)

    def make_hot():
        shift = (lax.broadcasted_iota(jnp.int32, (SR, 128), 0)
                 == lax.broadcasted_iota(jnp.int32, (SR, 128), 1) + jnp.where(c == 0, pad, 0))
        shift_ref[...] = jnp.where(shift, 1.0, 0.0).astype(jnp.bfloat16)
        row = lax.broadcasted_iota(jnp.int32, (512, WM), 0)
        lane = jnp.where(row < 256, row + half + pad, row - 256 + R // 2 + pad) - mid_lane
        hot = lax.broadcasted_iota(jnp.int32, (512, WM), 1) == lane
        place_ref[...] = jnp.where(hot, 1.0, 0.0).astype(jnp.bfloat16)
        for side, slot in ((0, 0), (3, 3)):
            @pl.when(q == side)
            def _():
                tile_recv[:, :, slot * 128:slot * 128 + 128] = jnp.zeros((L, SP, 128), jnp.bfloat16)

    def finish_tiles(j):
        rows = pl.ds(pl.multiple_of(j * SP, SP), SP)
        for side, acc, begin in ((0, acc_lo, 0), (1, acc_hi, hi_lane)):
            value = acc[rows, :]
            for k in (H[3] * 2, H[3] * 2 + 1, H[0] * 2, H[0] * 2 + 1):
                value = value + lax.dot_general(shr[k, j], zbuf[k, begin:begin + WS, :], NT,
                                                preferred_element_type=jnp.float32)
            acc[rows, :] = value
            turned = lax.dot_general((value[:SR] / total).astype(jnp.bfloat16), shift_ref[...], TN,
                                     preferred_element_type=jnp.float32)
            for core in range(2):
                at = (WS - half if side else 0) + core * share
                tile_send[side, j, core, :share, :] = turned[at:at + share].astype(jnp.bfloat16)

    def tile_copies(j, act):
        for side, skipped in ((0, 2), (1, 5)):
            @pl.when(b != skipped)
            def _():
                for core in range(2):
                    act(tile_copy(side, j, core, l, b - 2))

    def start_tiles(j):
        tile_copies(j, lambda copy: copy.start())

    def wait_tile(block):
        part = tile_recv.at[block, pl.ds(0, SR), pl.ds(0, 384)]
        pltpu.make_async_remote_copy(
            src_ref=part, dst_ref=part, send_sem=t_send, recv_sem=t_recv.at[block],
            device_id=(l, b), device_id_type=MESH).wait_recv()

    normalise(start[D], size[D])

    @pl.when(inner)
    def _():
        first_copy(b, D, out_nbr).start()

    normalise(start[F], size[F])

    first_copy(b, F, in_nbr).start()
    normalise(low, high - low)

    @pl.when(inner)
    def _():
        for p in (M2, M1, C):
            z_copy(b, p, own_in, in_nbr).start()
        for p in (F, C, N2):
            z_copy(b, p, own_out, out_nbr).start()

    @pl.when(outer)
    def _():
        for p in (M2, M1, C, D, N2, N1):
            z_copy(b, p, own_in, in_nbr).start()
    mate_own(b).start()
    extract_one(b)
    make_hot()
    mate_own(mate).wait_recv()
    extract_one(mate)

    @pl.when(inner)
    def _():
        unpack(0, own(1), D)
        unpack(1, own(3), F)
        take(1, D, send_out, True)
        take(3, F, send_in, True)
        pass_on(q)
        take(1, N2, send_out)
        take(3, M2, send_in)
        take(1, N1)
        take(3, M1, send_in)
        take(1, C, send_out)
        take(3, C, send_in)
        z_copy(b, D, own_in, in_nbr).start()
        mate_take(1, (D, N2, N1, C))
        extract(H[1])
        take(0, D, send_out)
        take(3, D, send_in)

    @pl.when(outer)
    def _():
        unpack(0, own(2), D)
        take(2, D, None, True)
        mate_take(2, (D,))
        extract(H[2])
        pass_on(q)
        take(2, F)
        take(2, C)
        take(2, N2)
        pass_on(H[2])
        take(1, D)
        mate_take(1, (D,))
        extract(H[1])
        mate_take(2, (F, C, N2))
    wait_diag(q)
    acc_lo[...] = product(q, 0, WS)
    acc_hi[...] = product(q, hi_lane, WS)
    acc_mid[...] = product(q, mid_lane, WM)

    second, third = jnp.where(inner, H[1], H[2]), jnp.where(inner, H[3], H[1])

    @pl.when(inner)
    def _():
        pass_on(H[1])
        take(0, N2, send_out)
        take(0, N1)
        take(0, C, send_out)
        mate_take(0, (D, N2, N1, C))
        extract(H[0])
        take(3, N2)
        take(3, N1)
        mate_take(3, (C, D, N2, N1))
        extract(H[3])
        take(1, F, send_out)
        mate_take(1, (F,))

    @pl.when(outer)
    def _():
        take(1, N2)
        take(1, C)
        pass_on(H[1])
    wait_diag(second)
    add_sides(second)

    @pl.when(outer)
    def _():
        take(0, D)
        mate_take(0, (D,))
        extract(H[0])
        take(0, N2)
        take(0, C)
        take(1, F)
        mate_take(1, (N2, C, F))
        wait_diag(H[1])
        add_sides(H[1])
    pass_on(H[0])

    @pl.when(inner)
    def _():
        take(0, F, send_out)
        for p in (N1, N2):
            z_copy(b, p, own_in, in_nbr).start()
        mate_take(3, (F, M1, M2))
        mate_take(0, (F,))
        finish_tiles(l)
        start_tiles(l)
        pass_on(H[3])

        @pl.loop(0, 2)
        def _(n):
            j = jnp.where(n == 0, lx, ly)
            finish_tiles(j)
            start_tiles(j)
        for p in (N1, N2):
            send_in(own(3), p).start()
        wait_diag(H[0])
        wait_diag(H[3])
        finish_tiles(ld)
        start_tiles(ld)
        for p in (M1, M2):
            take(1, p)
        mate_take(1, (M1, M2))
    add_middle(second)
    add_middle(third)

    @pl.when(inner)
    def _():
        for p in (M1, M2):
            take(0, p)
        mate_take(0, (M1, M2))

    @pl.when(outer)
    def _():
        take(0, F)
        mate_take(0, (C, N2, F))
        wait_diag(H[0])
        add_sides(H[0])
    add_middle(H[0])

    for j in range(L):
        rows = slice(j * SP, j * SP + share)
        o_ref[:, j, :mid_lane] = acc_lo[rows, :mid_lane] / total
        o_ref[:, j, mid_lane:mid_lane + WM] = acc_mid[rows, :] / total
        o_ref[:, j, mid_lane + WM:] = acc_hi[rows, :][:, mid_lane + WM - hi_lane:] / total

    @pl.when(outer)
    def _():
        place = lax.broadcasted_iota(jnp.int32, (share, WM), 1) + mid_lane
        first_lane = half + pad + jnp.where(upper, 0, 128)
        last_lane = R // 2 + pad + jnp.where(upper, 128, 256)
        inside = ((place >= first_lane) & (place < half + pad + 256)
                  | (place >= R // 2 + pad) & (place < last_lane))
        for d in (l, lx, ly, ld):
            wait_tile(d)
            placed = lax.dot_general(tile_recv[d], place_ref[...], (((1,), (0,)), ((), ())),
                                     preferred_element_type=jnp.float32)[:share]
            middle = pl.ds(mid_lane, WM)
            o_ref[:, d, middle] = jnp.where(inside, placed, o_ref[:, d, middle])

    all_stats.wait_send()
    mate_own(b).wait_send()

    def sent(part, sem):
        pltpu.make_async_remote_copy(
            src_ref=part, dst_ref=part, send_sem=sem, recv_sem=st_recv,
            device_id=(l, b), device_id_type=MESH).wait_send()

    @pl.when(inner)
    def _():
        sent(zbuf.at[0, pl.ds(0, size[F] + size[C] + size[N2]), :], own_out)
        sent(zbuf.at[pl.ds(0, 2), pl.ds(0, size[D] - RAW), :], first_send)
        sent(raw, raw_send)
        sent(zbuf.at[pl.ds(0, 2), pl.ds(0, far), :], out_send)
        sent(zbuf.at[0], in_send)
        sent(zbuf.at[pl.ds(0, 3)], mate_send)
        for skipped in (True, False):
            @pl.when(((b == 2) | (b == 5)) == skipped)
            def _():
                sides = 1 if skipped else 2
                sent(tile_send.at[pl.ds(0, sides), :, :, pl.ds(0, SR), :], t_send)

    @pl.when(outer)
    def _():
        sent(zbuf.at[0, pl.ds(0, size[D] - RAW), :], first_send)
        sent(raw.at[0], raw_send)
        sent(zbuf.at[pl.ds(0, 3), pl.ds(0, far), :], mate_send)

    sent(zbuf.at[0, pl.ds(0, R - size[D]), :], own_in)
    sent(shr.at[pl.ds(0, L), :, pl.ds(0, SR), :], shr_send)
    sent(shr.at[pl.ds(0, B // L), :, pl.ds(0, SR), :], diag_send)


def line_call(L, B, series):
    R, T = series.shape
    share = R // B
    SP = up_to(share, 16)
    pad = share - 128
    high = (3 * 2 * share - pad) // 16 * 16
    WS = R - high
    mid_lane = WS // 128 * 128
    WM = up_to(R // 2 + pad + 256, 128) - mid_lane
    vmem = pl.BlockSpec(memory_space=pltpu.VMEM)
    dma = pltpu.SemaphoreType.DMA
    return pl.pallas_call(
        functools.partial(line_kernel, L, B),
        out_shape=jax.ShapeDtypeStruct((share, L, R), jnp.float32),
        in_specs=[pl.BlockSpec(memory_space=pltpu.HBM)],
        out_specs=vmem,
        scratch_shapes=[
            pltpu.VMEM((B, R, T), jnp.bfloat16),
            pltpu.VMEM((B, L, SP, T), jnp.bfloat16),
            pltpu.VMEM((L * SP, WS), jnp.float32),
            pltpu.VMEM((L * SP, WS), jnp.float32),
            pltpu.VMEM((L * SP, WM), jnp.float32),
            pltpu.VMEM((2, L, 2, SP, 128), jnp.bfloat16),
            pltpu.VMEM((L, SP, 512), jnp.bfloat16),
            pltpu.VMEM((up_to(share, 8), 128), jnp.bfloat16),
            pltpu.VMEM((512, WM), jnp.bfloat16),
            pltpu.VMEM((R, 128), jnp.float32),
            pltpu.VMEM((B, 2, R), jnp.float32),
            pltpu.VMEM((R, T), jnp.float32),
            pltpu.VMEM((2, (R - high) // 32 * 16, T), jnp.float32),
            dma((B, 7)), dma, dma, dma, dma, dma, dma, dma, dma((2,)), dma,
            dma((B, 2)), dma, dma((B // 2,)), dma, dma((L,)), dma,
            dma, dma, dma((R // largest_tile(R, 352),)),
        ],
        compiler_params=pltpu.CompilerParams(
            collective_id=0, has_side_effects=True, vmem_limit_bytes=34 * 1024 * 1024),
    )(pltpu.with_memory_space_constraint(series, pltpu.HBM)).transpose(1, 0, 2)


def solution(mesh):
    L, B = mesh.shape["loop"], mesh.shape["bulk"]

    def on_device(series):
        R, T = series.shape
        share = R // B
        if L == 4 and B == 8 and R % 16 == 0 and T % 128 == 0 and 128 <= share <= 144:
            return line_call(L, B, series)
        SP = up_to(share, 16)
        pieces = 3
        vmem = pl.BlockSpec(memory_space=pltpu.VMEM)
        dma = pltpu.SemaphoreType.DMA
        return pl.pallas_call(
            functools.partial(kernel, L, B, pieces),
            out_shape=jax.ShapeDtypeStruct((share, L, R), jnp.float32),
            in_specs=[pl.BlockSpec(memory_space=pltpu.HBM)],
            out_specs=vmem,
            scratch_shapes=[
                pltpu.VMEM((B, R, T), jnp.bfloat16),
                pltpu.VMEM((B, L, SP, T), jnp.bfloat16),
                pltpu.VMEM((L * SP, R), jnp.float32),
                pltpu.VMEM((R, 128), jnp.float32),
                pltpu.VMEM((B, 2, R), jnp.float32),
                pltpu.VMEM((R, T), jnp.float32),
                dma((B, pieces)), dma((B, pieces)), dma((B, pieces)), dma((B, pieces)),
                dma((B, L)), dma((B, L)), dma((B,)), dma((B,)), dma((R // largest_tile(R, 128),)),
            ],
            compiler_params=pltpu.CompilerParams(
                collective_id=0, has_side_effects=True, vmem_limit_bytes=26 * 1024 * 1024),
        )(pltpu.with_memory_space_constraint(series, pltpu.HBM)).transpose(1, 0, 2)

    return jax.shard_map(
        on_device, mesh=mesh, in_specs=(P("loop", "bulk"),),
        out_specs=P(None, "bulk", "loop"), check_vma=False)
```

```python
import functools
import jax
import jax.numpy as jnp
from jax import lax
from jax.experimental import pallas as pl
from jax.experimental.pallas import tpu as pltpu
from jax.sharding import PartitionSpec as P

epsilon = 1e-06
MESH = pl.DeviceIdType.MESH
NT = (((1,), (1,)), ((), ()))
TN = (((0,), (0,)), ((), ()))


def up_to(value, unit):
    return -(-value // unit) * unit


def largest_tile(rows, limit):
    return max(t for t in range(16, limit + 1, 16) if rows % t == 0)


def kernel(L, B, PIECES, x_hbm, o_ref, zbuf, shr, acc, cols, stats, x_ref,
           z_recv, up_send, down_send, mate_send, shr_recv, shr_send, st_recv, st_send, x_sem):
    R, T = x_hbm.shape
    total = T * B
    Q = B // 2
    share = R // B
    SP = shr.shape[2]
    W = min(up_to(share + 15, 16), R)
    bounds = [up_to(R * i // PIECES, 128) for i in range(PIECES)] + [R]
    tile = largest_tile(R, 128)
    l, b = lax.axis_index("loop"), lax.axis_index("bulk")
    q, c = b // 2, b % 2
    mate = q * 2 + (1 - c)

    barrier = pltpu.get_barrier_semaphore()
    for d in range(1, B):
        pl.semaphore_signal(barrier, inc=1, device_id=(l, lax.rem(b + d, B)), device_id_type=MESH)
    for d in range(1, L):
        pl.semaphore_signal(barrier, inc=1, device_id=(lax.rem(l + d, L), b), device_id_type=MESH)

    def load(i):
        rows = pl.ds(pl.multiple_of(i * tile, tile), tile)
        return pltpu.make_async_copy(x_hbm.at[rows, :], x_ref.at[rows, :], x_sem.at[i])

    @pl.loop(0, R // tile)
    def _(i):
        load(i).start()

    lane = lax.broadcasted_iota(jnp.int32, (tile, 128), 1)

    @pl.loop(0, R // tile)
    def _(i):
        rows = pl.ds(pl.multiple_of(i * tile, tile), tile)
        load(i).wait()
        v = x_ref[rows, :]
        mean = jnp.sum(v, axis=1, keepdims=True) / T
        dev = v - mean
        m2 = jnp.sum(dev * dev, axis=1, keepdims=True)
        cols[rows, :] = jnp.where(lane == 0, mean, jnp.where(lane == 1, m2, 0.0))

    pick = (lax.broadcasted_iota(jnp.int32, (8, 128), 0)
            == lax.broadcasted_iota(jnp.int32, (8, 128), 1)).astype(jnp.float32)
    line = lax.dot_general(pick, cols[...], NT, precision=lax.Precision.HIGHEST,
                           preferred_element_type=jnp.float32)
    stats[b] = line[:2]

    pl.semaphore_wait(barrier, B - 1 + L - 1)

    def stat_copy(source, peer):
        return pltpu.make_async_remote_copy(
            src_ref=stats.at[source], dst_ref=stats.at[source],
            send_sem=st_send.at[peer], recv_sem=st_recv.at[source],
            device_id=(l, peer), device_id_type=MESH)

    for d in range(1, B):
        stat_copy(b, lax.rem(b + d, B)).start()
    for d in range(1, B):
        other = lax.rem(b + d, B)
        stat_copy(other, other).wait_recv()

    mean = stats[0, 0:1]
    for k in range(1, B):
        mean = mean + stats[k, 0:1]
    mean = mean / B
    square = jnp.zeros_like(mean)
    for k in range(B):
        shift = stats[k, 0:1] - mean
        square = square + (stats[k, 1:2] + T * (shift * shift))
    scale = lax.rsqrt(square / total + epsilon)
    sub = lax.broadcasted_iota(jnp.int32, (8, R), 0)
    both = jnp.where(sub == 0, mean, jnp.where(sub == 1, scale, 0.0))
    cols[...] = lax.dot_general(both, pick, TN, precision=lax.Precision.HIGHEST,
                                preferred_element_type=jnp.float32)

    def normalise(piece):
        size = bounds[piece + 1] - bounds[piece]
        step = largest_tile(size, 128)

        @pl.loop(0, size // step)
        def _(i):
            rows = pl.ds(pl.multiple_of(bounds[piece] + i * step, 16), step)
            z = (x_ref[rows, :] - cols[rows, 0:1]) * cols[rows, 1:2]
            zbuf[b, rows, :] = z.astype(jnp.bfloat16)

    def piece_copy(k, piece, send_sem, peer):
        part = zbuf.at[k, pl.ds(bounds[piece], bounds[piece + 1] - bounds[piece]), :]
        return pltpu.make_async_remote_copy(
            src_ref=part, dst_ref=part, send_sem=send_sem.at[k, piece],
            recv_sem=z_recv.at[k, piece], device_id=(l, peer), device_id_type=MESH)

    def share_copy(k, block, peer):
        return pltpu.make_async_remote_copy(
            src_ref=shr.at[k, block], dst_ref=shr.at[k, block], send_sem=shr_send.at[k, peer],
            recv_sem=shr_recv.at[k, block], device_id=(peer, b), device_id_type=MESH)

    has_up, has_down = q + 1 < Q, q >= 1
    start = b * share
    first = pl.multiple_of(jnp.minimum(start // 16 * 16, R - W), 16)
    need_below = PIECES - 1 - sum((first >= x).astype(jnp.int32) for x in bounds[1:-1])
    need_above = sum((first + W > x).astype(jnp.int32) for x in bounds[1:-1])

    def extract(k):
        window = zbuf[k, pl.ds(first, W), :]
        hot = (lax.broadcasted_iota(jnp.int32, (SP, W), 1)
               == lax.broadcasted_iota(jnp.int32, (SP, W), 0) + (start - first))
        inside = lax.broadcasted_iota(jnp.int32, (SP, W), 0) < share
        hot = jnp.where(hot & inside, 1.0, 0.0).astype(jnp.bfloat16)
        rows = lax.dot_general(hot, window, (((1,), (0,)), ((), ())),
                               preferred_element_type=jnp.float32)
        shr[k, l] = rows.astype(jnp.bfloat16)
        for d in range(1, L):
            share_copy(k, l, lax.rem(l + d, L)).start()

    def wait_shares(place):
        for core in range(2):
            k = place * 2 + core
            for d in range(1, L):
                other = lax.rem(l + d, L)
                share_copy(k, other, other).wait_recv()

    def multiply(place):
        part = None
        wait_shares(place)
        for core in range(2):
            k = place * 2 + core
            a = shr[k].reshape(L * SP, T)
            term = lax.dot_general(a, zbuf[k], NT, preferred_element_type=jnp.float32)
            part = term if part is None else part + term
        acc[...] += part

    def multiply_step(s):
        @pl.loop(0, 2)
        def _(n):
            place = q - (1 - 2 * n) * s

            @pl.when((place >= 0) & (place < Q) & ((s > 0) | (n < 1)))
            def _():
                multiply(place)

    def send_own(up_first):
        done = set()

        def send(up, i):
            piece = PIECES - 1 - i if up else i
            if piece not in done:
                done.add(piece)
                normalise(piece)

            @pl.when(has_up if up else has_down)
            def _():
                if up:
                    piece_copy(b, piece, up_send, b + 2).start()
                else:
                    piece_copy(b, piece, down_send, b - 2).start()

        for i in range(PIECES):
            send(up_first, i)
            send(not up_first, i)

    @pl.when(q >= Q // 2)
    def _():
        send_own(True)

    @pl.when(q < Q // 2)
    def _():
        send_own(False)

    for i in range(PIECES):
        piece_copy(b, i, mate_send, mate).start()

    acc[...] = jnp.zeros_like(acc)
    extract(b)

    for i in range(PIECES):
        piece_copy(mate, i, mate_send, mate).wait_recv()

    extract(mate)

    def arrive(s, i, between=None):
        below, above = b - 2 * s, b + 2 * s
        from_below, from_above = q - s >= 0, q + s < Q
        down_piece = PIECES - 1 - i

        @pl.when(from_below)
        def _():
            piece_copy(below, down_piece, up_send, b).wait_recv()

            @pl.when(has_up)
            def _():
                piece_copy(below, down_piece, up_send, b + 2).start()
            piece_copy(below, down_piece, mate_send, mate).start()

        @pl.when(from_above)
        def _():
            piece_copy(above, i, down_send, b).wait_recv()

            @pl.when(has_down)
            def _():
                piece_copy(above, i, down_send, b - 2).start()
            piece_copy(above, i, mate_send, mate).start()

        @pl.when(from_below & (i == need_below))
        def _():
            extract(below)

        @pl.when(from_above & (i == need_above))
        def _():
            extract(above)

        if between is not None:
            between()

        @pl.when(from_below)
        def _():
            piece_copy(mate - 2 * s, down_piece, mate_send, mate).wait_recv()

            @pl.when(i == need_below)
            def _():
                extract(mate - 2 * s)

        @pl.when(from_above)
        def _():
            piece_copy(mate + 2 * s, i, mate_send, mate).wait_recv()

            @pl.when(i == need_above)
            def _():
                extract(mate + 2 * s)

        if i == 0:
            multiply_step(s - 1)

    def finish(piece, place):
        lo, hi = bounds[piece], bounds[piece + 1]
        part = acc[:, lo:hi]
        if place is not None:
            for core in range(2):
                k = place * 2 + core
                a = shr[k].reshape(L * SP, T)
                part = part + lax.dot_general(a, zbuf[k, lo:hi, :], NT,
                                              preferred_element_type=jnp.float32)
        part = part / total
        for j in range(L):
            o_ref[:, j, lo:hi] = part[j * SP:j * SP + share]

    @pl.loop(1, Q - 1)
    def _(s):
        for i in range(PIECES):
            arrive(s, i)

    def finish_ends(steps):
        for end, place in ((Q - 1, 0), (0, Q - 1)):
            @pl.when(q == end)
            def _():
                for i in steps:
                    finish(PIECES - 1 - i if end else i, place)

    def finish_early():
        for end, place in ((Q - 1, 0), (0, Q - 1)):
            @pl.when(q == end)
            def _():
                wait_shares(place)

        finish_ends(range(PIECES - 1))

    for i in range(PIECES):
        arrive(Q - 1, i, finish_early if i == PIECES - 1 else None)
    finish_ends([PIECES - 1])

    @pl.when((q > 0) & (q < Q - 1))
    def _():
        for i in range(PIECES):
            finish(i, None)

    for d in range(1, B):
        other = lax.rem(b + d, B)
        stat_copy(b, other).wait_send()

    @pl.loop(0, Q)
    def _(s):
        below, above = b - 2 * s, b + 2 * s
        from_below, from_above = q - s >= 0, q + s < Q

        for i in range(PIECES):
            @pl.when(from_below & has_up)
            def _():
                piece_copy(below, i, up_send, b + 2).wait_send()

            @pl.when(from_above & has_down)
            def _():
                piece_copy(above, i, down_send, b - 2).wait_send()

            @pl.when(from_below)
            def _():
                piece_copy(below, i, mate_send, mate).wait_send()

            @pl.when(from_above & (s > 0))
            def _():
                piece_copy(above, i, mate_send, mate).wait_send()

    @pl.loop(0, B)
    def _(k):
        for d in range(1, L):
            other = lax.rem(l + d, L)
            share_copy(k, l, other).wait_send()


F, M2, M1, C, N1, N2, D = range(7)


def line_kernel(L, B, x_hbm, o_ref, zbuf, shr, acc_lo, acc_hi, acc_mid, tile_send, tile_recv, shift_ref, place_ref,
                cols, stats, x_ref, raw,
                z_recv, out_send, in_send, mate_send, own_send, own_out, own_in, first_send, raw_recv, raw_send, shr_recv, shr_send, diag_recv, diag_send, t_recv, t_send,
                st_recv, st_send, x_sem):
    R, T = x_hbm.shape
    total = T * B
    share = R // B
    half = 2 * share
    SP = shr.shape[2]
    pad = share - 128
    W = min(up_to(share + 15, 16), R)
    low, high = R - (3 * half - pad) // 16 * 16, (3 * half - pad) // 16 * 16
    split = (3 * half - share) // 16 * 16
    edges = [0, low, R - split, (R // 2 - pad) // 16 * 16]
    edges = edges + [R - x for x in reversed(edges)]
    size = [edges[p + 1] - edges[p] for p in range(7)]
    far = R - size[M2] - size[M1] - size[N1]
    tile = largest_tile(R, 352)
    RAW = raw.shape[1]
    WS = acc_lo.shape[1]
    hi_lane, mid_lane = R - WS, WS // 128 * 128
    WM = acc_mid.shape[1]
    l, b = lax.axis_index("loop"), lax.axis_index("bulk")
    q, c = b // 2, b % 2
    mate = q * 2 + (1 - c)
    upper = q >= 2
    inner = (q == 1) | (q == 2)
    outer = (q == 0) | (q == 3)
    step = jnp.where(upper, 1, -1)
    H = [jnp.where(upper, h, 3 - h) for h in range(4)]
    out_nbr, in_nbr = b + 2 * step, b - 2 * step
    lx, ly, ld = l + 1 - 2 * (l % 2), lax.rem(l + 2, 4), 3 - l

    def align(value, unit=16):
        return pl.multiple_of(value, unit)

    start = [align(jnp.where(upper, edges[p], edges[6 - p])) for p in range(7)]

    barrier = pltpu.get_barrier_semaphore()
    for d in range(1, B):
        pl.semaphore_signal(barrier, inc=1, device_id=(l, lax.rem(b + d, B)), device_id_type=MESH)
    for line in (lx, ly):
        pl.semaphore_signal(barrier, inc=1, device_id=(line, b), device_id_type=MESH)

    def load(i):
        rows = pl.ds(pl.multiple_of(i * tile, tile), tile)
        return pltpu.make_async_copy(x_hbm.at[rows, :], x_ref.at[rows, :], x_sem.at[i])

    @pl.loop(0, R // tile)
    def _(i):
        load(i).start()

    lane = lax.broadcasted_iota(jnp.int32, (tile, 128), 1)

    @pl.loop(0, R // tile)
    def _(i):
        rows = pl.ds(pl.multiple_of(i * tile, tile), tile)
        load(i).wait()
        v = x_ref[rows, :]
        mean = jnp.sum(v, axis=1, keepdims=True) / T
        dev = v - mean
        m2 = jnp.sum(dev * dev, axis=1, keepdims=True)
        cols[rows, :] = jnp.where(lane == 0, mean, jnp.where(lane == 1, m2, 0.0))

    pick = (lax.broadcasted_iota(jnp.int32, (8, 128), 0)
            == lax.broadcasted_iota(jnp.int32, (8, 128), 1)).astype(jnp.bfloat16)

    def in_parts(x):
        top = x.astype(jnp.bfloat16)
        rest = x - top.astype(jnp.float32)
        middle = rest.astype(jnp.bfloat16)
        return top, middle, (rest - middle.astype(jnp.float32)).astype(jnp.bfloat16)

    def exact_dot(parts, dot):
        top, middle, low_part = [dot(part) for part in parts]
        return top + middle + low_part

    line = exact_dot(in_parts(cols[...]), lambda part: lax.dot_general(
        pick, part, NT, preferred_element_type=jnp.float32))
    stats[b] = line[:2]

    pl.semaphore_wait(barrier, B - 1 + 2)

    def stat_copy(source, peer):
        return pltpu.make_async_remote_copy(
            src_ref=stats.at[source], dst_ref=stats.at[source],
            send_sem=st_send, recv_sem=st_recv,
            device_id=(l, peer), device_id_type=MESH)

    for d in range(1, B):
        stat_copy(b, lax.rem(b + d, B)).start()
    def raw_copy(p, slot, peer):
        return pltpu.make_async_remote_copy(
            src_ref=x_ref.at[pl.ds(start[p], RAW), :], dst_ref=raw.at[slot], send_sem=raw_send,
            recv_sem=raw_recv.at[slot], device_id=(l, peer), device_id_type=MESH)

    @pl.when(inner)
    def _():
        raw_copy(D, 0, out_nbr).start()
        raw_copy(F, 0, in_nbr).start()

    @pl.when(outer)
    def _():
        raw_copy(F, 1, in_nbr).start()

    gathered = stats.at[pl.ds(0, B - 1)]
    all_stats = pltpu.make_async_remote_copy(
        src_ref=gathered, dst_ref=gathered, send_sem=st_send, recv_sem=st_recv,
        device_id=(l, b), device_id_type=MESH)
    all_stats.wait_recv()

    mean = stats[0, 0:1]
    for k in range(1, B):
        mean = mean + stats[k, 0:1]
    mean = mean / B
    square = jnp.zeros_like(mean)
    for k in range(B):
        shift = stats[k, 0:1] - mean
        square = square + (stats[k, 1:2] + T * (shift * shift))
    scale = lax.rsqrt(square / total + epsilon)
    sub = lax.broadcasted_iota(jnp.int32, (8, R), 0)
    both = jnp.where(sub == 0, mean, jnp.where(sub == 1, scale, 0.0))
    cols[...] = exact_dot(in_parts(both), lambda part: lax.dot_general(
        part, pick, TN, preferred_element_type=jnp.float32))

    def normalise(begin, count):
        unit = count if count <= 288 else largest_tile(count, 128)

        def chunk(i):
            rows = pl.ds(pl.multiple_of(begin + i * unit, 16), unit)
            z = (x_ref[rows, :] - cols[rows, 0:1]) * cols[rows, 1:2]
            zbuf[b, rows, :] = z.astype(jnp.bfloat16)

        if unit == count:
            chunk(0)
        else:
            pl.loop(0, count // unit)(chunk)

    def z_copy(k, p, send_sem, peer, skip=0):
        part = zbuf.at[k, pl.ds(align(start[p] + skip), size[p] - skip), :]
        return pltpu.make_async_remote_copy(
            src_ref=part, dst_ref=part, send_sem=send_sem,
            recv_sem=z_recv.at[k, jnp.where(upper, p, 6 - p)], device_id=(l, peer), device_id_type=MESH)

    def first_copy(k, p, peer):
        return z_copy(k, p, first_send, peer, RAW)

    def unpack(slot, k, p):
        raw_copy(p, slot, b).wait_recv()
        rows = pl.ds(start[p], RAW)
        z = (raw[slot] - cols[rows, 0:1]) * cols[rows, 1:2]
        zbuf[k, rows, :] = z.astype(jnp.bfloat16)

    def send_out(k, p):
        return z_copy(k, p, out_send, out_nbr)

    def send_in(k, p):
        return z_copy(k, p, in_send, in_nbr)

    def mate_copy(k, p):
        return z_copy(k, p, mate_send, mate)

    def mate_own(k):
        part = zbuf.at[k]
        return pltpu.make_async_remote_copy(
            src_ref=part, dst_ref=part, send_sem=own_send, recv_sem=z_recv.at[k, 0],
            device_id=(l, mate), device_id_type=MESH)

    def share_copy(k, block, peer, way):
        part = shr.at[k, block, pl.ds(0, SR), :]
        return pltpu.make_async_remote_copy(
            src_ref=part, dst_ref=part, send_sem=shr_send,
            recv_sem=shr_recv.at[k, way], device_id=(peer, b), device_id_type=MESH)

    SR = up_to(share, 8)
    cut = up_to(share // 2, 16)

    def diag_copy(k, block, peer, way):
        rows = pl.ds(0, cut) if way == 0 else pl.ds(cut, SR - cut)
        part = shr.at[k, block, rows, :]
        return pltpu.make_async_remote_copy(
            src_ref=part, dst_ref=part, send_sem=diag_send,
            recv_sem=diag_recv.at[k // 2], device_id=(peer, b), device_id_type=MESH)

    first = align(jnp.minimum(b * share // 16 * 16, jnp.where(q == 0, size[D], R) - W))

    def extract_one(k):
        window = zbuf[k, pl.ds(first, W), :]
        row = lax.broadcasted_iota(jnp.int32, (SP, W), 0)
        hot = lax.broadcasted_iota(jnp.int32, (SP, W), 1) == row + (b * share - first)
        hot = jnp.where(hot & (row < share), 1.0, 0.0).astype(jnp.bfloat16)
        rows = lax.dot_general(hot, window, (((1,), (0,)), ((), ())),
                               preferred_element_type=jnp.float32)
        shr[k, l] = rows.astype(jnp.bfloat16)
        share_copy(k, l, lx, 0).start()
        share_copy(k, l, ly, 1).start()

    def extract(place):
        @pl.loop(0, 2)
        def _(core):
            extract_one(place * 2 + core)

    def pass_on(place):
        @pl.loop(0, 2)
        def _(core):
            k = place * 2 + core
            share_copy(k, lx, lx, 0).wait_recv()
            diag_copy(k, lx, ly, 0).start()
            share_copy(k, ly, ly, 1).wait_recv()
            diag_copy(k, ly, lx, 1).start()

    def wait_diag(place):
        part = shr.at[pl.ds(place * 2, 2), ld, pl.ds(0, SR), :]
        pltpu.make_async_remote_copy(
            src_ref=part, dst_ref=part, send_sem=diag_send, recv_sem=diag_recv.at[place],
            device_id=(l, b), device_id_type=MESH).wait_recv()

    def product(place, begin, width):
        part = None
        for core in range(2):
            k = place * 2 + core
            term = lax.dot_general(shr[k].reshape(L * SP, T), zbuf[k, begin:begin + width, :], NT,
                                   preferred_element_type=jnp.float32)
            part = term if part is None else part + term
        return part

    def add_sides(place):
        acc_lo[...] += product(place, 0, WS)
        acc_hi[...] += product(place, hi_lane, WS)

    def add_middle(place):
        acc_mid[...] += product(place, mid_lane, WM)

    def own(h):
        return H[h] * 2 + c

    def other(h):
        return H[h] * 2 + (1 - c)

    def take(h, p, onward=None, first=False):
        if first:
            first_copy(own(h), p, mate).wait_recv()
        else:
            mate_copy(own(h), p).wait_recv()
        if onward is not None:
            onward(own(h), p).start()
        mate_copy(own(h), p).start()

    def mate_take(h, pieces):
        for p in pieces:
            mate_copy(other(h), p).wait_recv()

    def tile_copy(side, j, core, block, slot):
        return pltpu.make_async_remote_copy(
            src_ref=tile_send.at[side, j, core, pl.ds(0, SR), :],
            dst_ref=tile_recv.at[block, pl.ds(0, SR), pl.ds(pl.multiple_of(slot * 128, 128), 128)],
            send_sem=t_send, recv_sem=t_recv.at[block],
            device_id=(j, 6 * side + core), device_id_type=MESH)

    def make_hot():
        shift = (lax.broadcasted_iota(jnp.int32, (SR, 128), 0)
                 == lax.broadcasted_iota(jnp.int32, (SR, 128), 1) + jnp.where(c == 0, pad, 0))
        shift_ref[...] = jnp.where(shift, 1.0, 0.0).astype(jnp.bfloat16)
        row = lax.broadcasted_iota(jnp.int32, (512, WM), 0)
        lane = jnp.where(row < 256, row + half + pad, row - 256 + R // 2 + pad) - mid_lane
        hot = lax.broadcasted_iota(jnp.int32, (512, WM), 1) == lane
        place_ref[...] = jnp.where(hot, 1.0, 0.0).astype(jnp.bfloat16)
        for side, slot in ((0, 0), (3, 3)):
            @pl.when(q == side)
            def _():
                tile_recv[:, :, slot * 128:slot * 128 + 128] = jnp.zeros((L, SP, 128), jnp.bfloat16)

    def add_rows(j, place):
        rows = pl.ds(pl.multiple_of(j * SP, SP), SP)
        for acc, begin in ((acc_lo, 0), (acc_hi, hi_lane)):
            value = acc[rows, :]
            for core in range(2):
                k = place * 2 + core
                value = value + lax.dot_general(shr[k, j], zbuf[k, begin:begin + WS, :], NT,
                                                preferred_element_type=jnp.float32)
            acc[rows, :] = value

    def turn_tiles(j):
        rows = pl.ds(pl.multiple_of(j * SP, SP), SP)
        for side, acc in ((0, acc_lo), (1, acc_hi)):
            turned = lax.dot_general((acc[rows, :][:SR] / total).astype(jnp.bfloat16), shift_ref[...], TN,
                                     preferred_element_type=jnp.float32)
            for core in range(2):
                at = (WS - half if side else 0) + core * share
                tile_send[side, j, core, :share, :] = turned[at:at + share].astype(jnp.bfloat16)

    def tile_copies(j, act):
        for side, skipped in ((0, 2), (1, 5)):
            @pl.when(b != skipped)
            def _():
                for core in range(2):
                    act(tile_copy(side, j, core, l, b - 2))

    def start_tiles(j):
        tile_copies(j, lambda copy: copy.start())

    def wait_tile(block):
        part = tile_recv.at[block, pl.ds(0, SR), pl.ds(0, 384)]
        pltpu.make_async_remote_copy(
            src_ref=part, dst_ref=part, send_sem=t_send, recv_sem=t_recv.at[block],
            device_id=(l, b), device_id_type=MESH).wait_recv()

    normalise(start[D], size[D])

    @pl.when(inner)
    def _():
        first_copy(b, D, out_nbr).start()

    normalise(start[F], size[F])

    first_copy(b, F, in_nbr).start()
    normalise(low, high - low)

    @pl.when(inner)
    def _():
        for p in (M2, M1, C):
            z_copy(b, p, own_in, in_nbr).start()
        for p in (F, C, N2):
            z_copy(b, p, own_out, out_nbr).start()

    @pl.when(outer)
    def _():
        for p in (M2, M1, C, D, N2, N1):
            z_copy(b, p, own_in, in_nbr).start()
    mate_own(b).start()
    extract_one(b)
    make_hot()
    mate_own(mate).wait_recv()
    extract_one(mate)

    @pl.when(inner)
    def _():
        unpack(0, own(1), D)
        unpack(1, own(3), F)
        take(1, D, send_out, True)
        take(3, F, send_in, True)
        pass_on(q)
        take(1, N2, send_out)
        take(3, M2, send_in)
        take(1, N1)
        take(3, M1, send_in)
        take(1, C, send_out)
        take(3, C, send_in)
        z_copy(b, D, own_in, in_nbr).start()
        mate_take(1, (D, N2, N1, C))
        extract(H[1])
        take(0, D, send_out)
        take(3, D, send_in)

    @pl.when(outer)
    def _():
        unpack(0, own(2), D)
        take(2, D, None, True)
        mate_take(2, (D,))
        extract(H[2])
        pass_on(q)
        take(2, F)
        take(2, C)
        take(2, N2)
        pass_on(H[2])
        take(1, D)
        mate_take(1, (D,))
        extract(H[1])
        mate_take(2, (F, C, N2))
    wait_diag(q)
    acc_lo[...] = product(q, 0, WS)
    acc_hi[...] = product(q, hi_lane, WS)
    acc_mid[...] = product(q, mid_lane, WM)

    second, third = jnp.where(inner, H[1], H[2]), jnp.where(inner, H[3], H[1])

    @pl.when(inner)
    def _():
        pass_on(H[1])
        take(0, N2, send_out)
        take(0, N1)
        take(0, C, send_out)
        mate_take(0, (D, N2, N1, C))
        extract(H[0])
        take(3, N2)
        take(3, N1)
        mate_take(3, (C, D, N2, N1))
        extract(H[3])
        take(1, F, send_out)
        mate_take(1, (F,))

    @pl.when(outer)
    def _():
        take(1, N2)
        take(1, C)
        pass_on(H[1])
    wait_diag(second)
    add_sides(second)

    @pl.when(outer)
    def _():
        take(0, D)
        mate_take(0, (D,))
        extract(H[0])
        take(0, N2)
        take(0, C)
        take(1, F)
        mate_take(1, (N2, C, F))
        wait_diag(H[1])
        add_sides(H[1])
    pass_on(H[0])

    @pl.when(inner)
    def _():
        take(0, F, send_out)
        for p in (N1, N2):
            z_copy(b, p, own_in, in_nbr).start()
        mate_take(3, (F, M1, M2))
        mate_take(0, (F,))
        add_rows(l, H[3])
        add_rows(l, H[0])
        turn_tiles(l)
        start_tiles(l)
        pass_on(H[3])

        @pl.loop(0, 2)
        def _(n):
            j = jnp.where(n == 0, lx, ly)
            add_rows(j, H[3])
            add_rows(j, H[0])
            turn_tiles(j)
            start_tiles(j)
        for p in (N1, N2):
            send_in(own(3), p).start()
        wait_diag(H[0])
        add_rows(ld, H[0])
        wait_diag(H[3])
        add_rows(ld, H[3])
        turn_tiles(ld)
        start_tiles(ld)
        for p in (M1, M2):
            take(1, p)
        mate_take(1, (M1, M2))
    add_middle(second)
    add_middle(third)

    def put(lanes, acc, begin=0):
        for j in range(L):
            part = acc[j * SP:j * SP + share, :][:, begin:begin + lanes.stop - lanes.start]
            o_ref[:, j, lanes] = part / total

    @pl.when(inner)
    def _():
        for p in (M1, M2):
            take(0, p)
        mate_take(0, (M1, M2))
        add_middle(H[0])
        put(slice(0, mid_lane), acc_lo)
        put(slice(mid_lane, mid_lane + WM), acc_mid)
        put(slice(mid_lane + WM, R), acc_hi, mid_lane + WM - hi_lane)

    lanes_lo = mid_lane, up_to(R // 2 + pad, 128)
    lanes_hi = (R // 2 - pad) // 128 * 128, mid_lane + WM

    @pl.when(outer)
    def _():
        mate_take(0, (N2, C))
        wait_diag(H[0])
        for end, acc, begin, (first_mid, last_mid) in ((0, acc_lo, 0, lanes_lo), (3, acc_hi, hi_lane, lanes_hi)):
            @pl.when(q == end)
            def _():
                acc[...] += product(H[0], begin, WS)
                inner_lanes = slice(first_mid - mid_lane, last_mid - mid_lane)
                acc_mid[:, inner_lanes] += product(H[0], first_mid, last_mid - first_mid)
                put(slice(first_mid, last_mid), acc_mid, first_mid - mid_lane)
                if end:
                    put(slice(last_mid, R), acc, last_mid - hi_lane)
                else:
                    put(slice(0, first_mid), acc)
        take(0, F)
        mate_take(0, (F,))
        for end, acc, begin in ((3, acc_lo, 0), (0, acc_hi, hi_lane)):
            @pl.when(q == end)
            def _():
                acc[...] += product(H[0], begin, WS)
                put(slice(begin, begin + WS), acc)
        place = lax.broadcasted_iota(jnp.int32, (share, WM), 1) + mid_lane
        first_lane = half + pad + jnp.where(upper, 0, 128)
        last_lane = R // 2 + pad + jnp.where(upper, 128, 256)
        inside = ((place >= first_lane) & (place < half + pad + 256)
                  | (place >= R // 2 + pad) & (place < last_lane))
        for d in (l, lx, ly, ld):
            wait_tile(d)
            placed = lax.dot_general(tile_recv[d], place_ref[...], (((1,), (0,)), ((), ())),
                                     preferred_element_type=jnp.float32)[:share]
            middle = pl.ds(mid_lane, WM)
            o_ref[:, d, middle] = jnp.where(inside, placed, o_ref[:, d, middle])

    all_stats.wait_send()
    mate_own(b).wait_send()

    def sent(part, sem):
        pltpu.make_async_remote_copy(
            src_ref=part, dst_ref=part, send_sem=sem, recv_sem=st_recv,
            device_id=(l, b), device_id_type=MESH).wait_send()

    @pl.when(inner)
    def _():
        sent(zbuf.at[0, pl.ds(0, size[F] + size[C] + size[N2]), :], own_out)
        sent(zbuf.at[pl.ds(0, 2), pl.ds(0, size[D] - RAW), :], first_send)
        sent(raw, raw_send)
        sent(zbuf.at[pl.ds(0, 2), pl.ds(0, far), :], out_send)
        sent(zbuf.at[0], in_send)
        sent(zbuf.at[pl.ds(0, 3)], mate_send)
        for skipped in (True, False):
            @pl.when(((b == 2) | (b == 5)) == skipped)
            def _():
                sides = 1 if skipped else 2
                sent(tile_send.at[pl.ds(0, sides), :, :, pl.ds(0, SR), :], t_send)

    @pl.when(outer)
    def _():
        sent(zbuf.at[0, pl.ds(0, size[D] - RAW), :], first_send)
        sent(raw.at[0], raw_send)
        sent(zbuf.at[pl.ds(0, 3), pl.ds(0, far), :], mate_send)

    sent(zbuf.at[0, pl.ds(0, R - size[D]), :], own_in)
    sent(shr.at[pl.ds(0, L), :, pl.ds(0, SR), :], shr_send)
    sent(shr.at[pl.ds(0, B // L), :, pl.ds(0, SR), :], diag_send)


def line_call(L, B, series):
    R, T = series.shape
    share = R // B
    SP = up_to(share, 16)
    pad = share - 128
    high = (3 * 2 * share - pad) // 16 * 16
    WS = R - high
    mid_lane = WS // 128 * 128
    WM = up_to(R // 2 + pad + 256, 128) - mid_lane
    vmem = pl.BlockSpec(memory_space=pltpu.VMEM)
    dma = pltpu.SemaphoreType.DMA
    return pl.pallas_call(
        functools.partial(line_kernel, L, B),
        out_shape=jax.ShapeDtypeStruct((share, L, R), jnp.float32),
        in_specs=[pl.BlockSpec(memory_space=pltpu.HBM)],
        out_specs=vmem,
        scratch_shapes=[
            pltpu.VMEM((B, R, T), jnp.bfloat16),
            pltpu.VMEM((B, L, SP, T), jnp.bfloat16),
            pltpu.VMEM((L * SP, WS), jnp.float32),
            pltpu.VMEM((L * SP, WS), jnp.float32),
            pltpu.VMEM((L * SP, WM), jnp.float32),
            pltpu.VMEM((2, L, 2, SP, 128), jnp.bfloat16),
            pltpu.VMEM((L, SP, 512), jnp.bfloat16),
            pltpu.VMEM((up_to(share, 8), 128), jnp.bfloat16),
            pltpu.VMEM((512, WM), jnp.bfloat16),
            pltpu.VMEM((R, 128), jnp.float32),
            pltpu.VMEM((B, 2, R), jnp.float32),
            pltpu.VMEM((R, T), jnp.float32),
            pltpu.VMEM((2, (R - high) // 32 * 16, T), jnp.float32),
            dma((B, 7)), dma, dma, dma, dma, dma, dma, dma, dma((2,)), dma,
            dma((B, 2)), dma, dma((B // 2,)), dma, dma((L,)), dma,
            dma, dma, dma((R // largest_tile(R, 352),)),
        ],
        compiler_params=pltpu.CompilerParams(
            collective_id=0, has_side_effects=True, vmem_limit_bytes=34 * 1024 * 1024),
    )(pltpu.with_memory_space_constraint(series, pltpu.HBM)).transpose(1, 0, 2)


def solution(mesh):
    L, B = mesh.shape["loop"], mesh.shape["bulk"]

    def on_device(series):
        R, T = series.shape
        share = R // B
        if L == 4 and B == 8 and R % 16 == 0 and T % 128 == 0 and 128 <= share <= 144:
            return line_call(L, B, series)
        SP = up_to(share, 16)
        pieces = 3
        vmem = pl.BlockSpec(memory_space=pltpu.VMEM)
        dma = pltpu.SemaphoreType.DMA
        return pl.pallas_call(
            functools.partial(kernel, L, B, pieces),
            out_shape=jax.ShapeDtypeStruct((share, L, R), jnp.float32),
            in_specs=[pl.BlockSpec(memory_space=pltpu.HBM)],
            out_specs=vmem,
            scratch_shapes=[
                pltpu.VMEM((B, R, T), jnp.bfloat16),
                pltpu.VMEM((B, L, SP, T), jnp.bfloat16),
                pltpu.VMEM((L * SP, R), jnp.float32),
                pltpu.VMEM((R, 128), jnp.float32),
                pltpu.VMEM((B, 2, R), jnp.float32),
                pltpu.VMEM((R, T), jnp.float32),
                dma((B, pieces)), dma((B, pieces)), dma((B, pieces)), dma((B, pieces)),
                dma((B, L)), dma((B, L)), dma((B,)), dma((B,)), dma((R // largest_tile(R, 128),)),
            ],
            compiler_params=pltpu.CompilerParams(
                collective_id=0, has_side_effects=True, vmem_limit_bytes=26 * 1024 * 1024),
        )(pltpu.with_memory_space_constraint(series, pltpu.HBM)).transpose(1, 0, 2)

    return jax.shard_map(
        on_device, mesh=mesh, in_specs=(P("loop", "bulk"),),
        out_specs=P(None, "bulk", "loop"), check_vma=False)
```

```python
import functools
import jax
import jax.numpy as jnp
from jax import lax
from jax.experimental import pallas as pl
from jax.experimental.pallas import tpu as pltpu
from jax.sharding import PartitionSpec as P

epsilon = 1e-06
MESH = pl.DeviceIdType.MESH
NT = (((1,), (1,)), ((), ()))
TN = (((0,), (0,)), ((), ()))


def up_to(value, unit):
    return -(-value // unit) * unit


def largest_tile(rows, limit):
    return max(t for t in range(16, limit + 1, 16) if rows % t == 0)


def kernel(L, B, PIECES, x_hbm, o_ref, zbuf, shr, acc, cols, stats, x_ref,
           z_recv, up_send, down_send, mate_send, shr_recv, shr_send, st_recv, st_send, x_sem):
    R, T = x_hbm.shape
    total = T * B
    Q = B // 2
    share = R // B
    SP = shr.shape[2]
    W = min(up_to(share + 15, 16), R)
    bounds = [up_to(R * i // PIECES, 128) for i in range(PIECES)] + [R]
    tile = largest_tile(R, 128)
    l, b = lax.axis_index("loop"), lax.axis_index("bulk")
    q, c = b // 2, b % 2
    mate = q * 2 + (1 - c)

    barrier = pltpu.get_barrier_semaphore()
    for d in range(1, B):
        pl.semaphore_signal(barrier, inc=1, device_id=(l, lax.rem(b + d, B)), device_id_type=MESH)
    for d in range(1, L):
        pl.semaphore_signal(barrier, inc=1, device_id=(lax.rem(l + d, L), b), device_id_type=MESH)

    def load(i):
        rows = pl.ds(pl.multiple_of(i * tile, tile), tile)
        return pltpu.make_async_copy(x_hbm.at[rows, :], x_ref.at[rows, :], x_sem.at[i])

    @pl.loop(0, R // tile)
    def _(i):
        load(i).start()

    lane = lax.broadcasted_iota(jnp.int32, (tile, 128), 1)

    @pl.loop(0, R // tile)
    def _(i):
        rows = pl.ds(pl.multiple_of(i * tile, tile), tile)
        load(i).wait()
        v = x_ref[rows, :]
        mean = jnp.sum(v, axis=1, keepdims=True) / T
        dev = v - mean
        m2 = jnp.sum(dev * dev, axis=1, keepdims=True)
        cols[rows, :] = jnp.where(lane == 0, mean, jnp.where(lane == 1, m2, 0.0))

    pick = (lax.broadcasted_iota(jnp.int32, (8, 128), 0)
            == lax.broadcasted_iota(jnp.int32, (8, 128), 1)).astype(jnp.float32)
    line = lax.dot_general(pick, cols[...], NT, precision=lax.Precision.HIGHEST,
                           preferred_element_type=jnp.float32)
    stats[b] = line[:2]

    pl.semaphore_wait(barrier, B - 1 + L - 1)

    def stat_copy(source, peer):
        return pltpu.make_async_remote_copy(
            src_ref=stats.at[source], dst_ref=stats.at[source],
            send_sem=st_send.at[peer], recv_sem=st_recv.at[source],
            device_id=(l, peer), device_id_type=MESH)

    for d in range(1, B):
        stat_copy(b, lax.rem(b + d, B)).start()
    for d in range(1, B):
        other = lax.rem(b + d, B)
        stat_copy(other, other).wait_recv()

    mean = stats[0, 0:1]
    for k in range(1, B):
        mean = mean + stats[k, 0:1]
    mean = mean / B
    square = jnp.zeros_like(mean)
    for k in range(B):
        shift = stats[k, 0:1] - mean
        square = square + (stats[k, 1:2] + T * (shift * shift))
    scale = lax.rsqrt(square / total + epsilon)
    sub = lax.broadcasted_iota(jnp.int32, (8, R), 0)
    both = jnp.where(sub == 0, mean, jnp.where(sub == 1, scale, 0.0))
    cols[...] = lax.dot_general(both, pick, TN, precision=lax.Precision.HIGHEST,
                                preferred_element_type=jnp.float32)

    def normalise(piece):
        size = bounds[piece + 1] - bounds[piece]
        step = largest_tile(size, 128)

        @pl.loop(0, size // step)
        def _(i):
            rows = pl.ds(pl.multiple_of(bounds[piece] + i * step, 16), step)
            z = (x_ref[rows, :] - cols[rows, 0:1]) * cols[rows, 1:2]
            zbuf[b, rows, :] = z.astype(jnp.bfloat16)

    def piece_copy(k, piece, send_sem, peer):
        part = zbuf.at[k, pl.ds(bounds[piece], bounds[piece + 1] - bounds[piece]), :]
        return pltpu.make_async_remote_copy(
            src_ref=part, dst_ref=part, send_sem=send_sem.at[k, piece],
            recv_sem=z_recv.at[k, piece], device_id=(l, peer), device_id_type=MESH)

    def share_copy(k, block, peer):
        return pltpu.make_async_remote_copy(
            src_ref=shr.at[k, block], dst_ref=shr.at[k, block], send_sem=shr_send.at[k, peer],
            recv_sem=shr_recv.at[k, block], device_id=(peer, b), device_id_type=MESH)

    has_up, has_down = q + 1 < Q, q >= 1
    start = b * share
    first = pl.multiple_of(jnp.minimum(start // 16 * 16, R - W), 16)
    need_below = PIECES - 1 - sum((first >= x).astype(jnp.int32) for x in bounds[1:-1])
    need_above = sum((first + W > x).astype(jnp.int32) for x in bounds[1:-1])

    def extract(k):
        window = zbuf[k, pl.ds(first, W), :]
        hot = (lax.broadcasted_iota(jnp.int32, (SP, W), 1)
               == lax.broadcasted_iota(jnp.int32, (SP, W), 0) + (start - first))
        inside = lax.broadcasted_iota(jnp.int32, (SP, W), 0) < share
        hot = jnp.where(hot & inside, 1.0, 0.0).astype(jnp.bfloat16)
        rows = lax.dot_general(hot, window, (((1,), (0,)), ((), ())),
                               preferred_element_type=jnp.float32)
        shr[k, l] = rows.astype(jnp.bfloat16)
        for d in range(1, L):
            share_copy(k, l, lax.rem(l + d, L)).start()

    def wait_shares(place):
        for core in range(2):
            k = place * 2 + core
            for d in range(1, L):
                other = lax.rem(l + d, L)
                share_copy(k, other, other).wait_recv()

    def multiply(place):
        part = None
        wait_shares(place)
        for core in range(2):
            k = place * 2 + core
            a = shr[k].reshape(L * SP, T)
            term = lax.dot_general(a, zbuf[k], NT, preferred_element_type=jnp.float32)
            part = term if part is None else part + term
        acc[...] += part

    def multiply_step(s):
        @pl.loop(0, 2)
        def _(n):
            place = q - (1 - 2 * n) * s

            @pl.when((place >= 0) & (place < Q) & ((s > 0) | (n < 1)))
            def _():
                multiply(place)

    def send_own(up_first):
        done = set()

        def send(up, i):
            piece = PIECES - 1 - i if up else i
            if piece not in done:
                done.add(piece)
                normalise(piece)

            @pl.when(has_up if up else has_down)
            def _():
                if up:
                    piece_copy(b, piece, up_send, b + 2).start()
                else:
                    piece_copy(b, piece, down_send, b - 2).start()

        for i in range(PIECES):
            send(up_first, i)
            send(not up_first, i)

    @pl.when(q >= Q // 2)
    def _():
        send_own(True)

    @pl.when(q < Q // 2)
    def _():
        send_own(False)

    for i in range(PIECES):
        piece_copy(b, i, mate_send, mate).start()

    acc[...] = jnp.zeros_like(acc)
    extract(b)

    for i in range(PIECES):
        piece_copy(mate, i, mate_send, mate).wait_recv()

    extract(mate)

    def arrive(s, i, between=None):
        below, above = b - 2 * s, b + 2 * s
        from_below, from_above = q - s >= 0, q + s < Q
        down_piece = PIECES - 1 - i

        @pl.when(from_below)
        def _():
            piece_copy(below, down_piece, up_send, b).wait_recv()

            @pl.when(has_up)
            def _():
                piece_copy(below, down_piece, up_send, b + 2).start()
            piece_copy(below, down_piece, mate_send, mate).start()

        @pl.when(from_above)
        def _():
            piece_copy(above, i, down_send, b).wait_recv()

            @pl.when(has_down)
            def _():
                piece_copy(above, i, down_send, b - 2).start()
            piece_copy(above, i, mate_send, mate).start()

        @pl.when(from_below & (i == need_below))
        def _():
            extract(below)

        @pl.when(from_above & (i == need_above))
        def _():
            extract(above)

        if between is not None:
            between()

        @pl.when(from_below)
        def _():
            piece_copy(mate - 2 * s, down_piece, mate_send, mate).wait_recv()

            @pl.when(i == need_below)
            def _():
                extract(mate - 2 * s)

        @pl.when(from_above)
        def _():
            piece_copy(mate + 2 * s, i, mate_send, mate).wait_recv()

            @pl.when(i == need_above)
            def _():
                extract(mate + 2 * s)

        if i == 0:
            multiply_step(s - 1)

    def finish(piece, place):
        lo, hi = bounds[piece], bounds[piece + 1]
        part = acc[:, lo:hi]
        if place is not None:
            for core in range(2):
                k = place * 2 + core
                a = shr[k].reshape(L * SP, T)
                part = part + lax.dot_general(a, zbuf[k, lo:hi, :], NT,
                                              preferred_element_type=jnp.float32)
        part = part / total
        for j in range(L):
            o_ref[:, j, lo:hi] = part[j * SP:j * SP + share]

    @pl.loop(1, Q - 1)
    def _(s):
        for i in range(PIECES):
            arrive(s, i)

    def finish_ends(steps):
        for end, place in ((Q - 1, 0), (0, Q - 1)):
            @pl.when(q == end)
            def _():
                for i in steps:
                    finish(PIECES - 1 - i if end else i, place)

    def finish_early():
        for end, place in ((Q - 1, 0), (0, Q - 1)):
            @pl.when(q == end)
            def _():
                wait_shares(place)

        finish_ends(range(PIECES - 1))

    for i in range(PIECES):
        arrive(Q - 1, i, finish_early if i == PIECES - 1 else None)
    finish_ends([PIECES - 1])

    @pl.when((q > 0) & (q < Q - 1))
    def _():
        for i in range(PIECES):
            finish(i, None)

    for d in range(1, B):
        other = lax.rem(b + d, B)
        stat_copy(b, other).wait_send()

    @pl.loop(0, Q)
    def _(s):
        below, above = b - 2 * s, b + 2 * s
        from_below, from_above = q - s >= 0, q + s < Q

        for i in range(PIECES):
            @pl.when(from_below & has_up)
            def _():
                piece_copy(below, i, up_send, b + 2).wait_send()

            @pl.when(from_above & has_down)
            def _():
                piece_copy(above, i, down_send, b - 2).wait_send()

            @pl.when(from_below)
            def _():
                piece_copy(below, i, mate_send, mate).wait_send()

            @pl.when(from_above & (s > 0))
            def _():
                piece_copy(above, i, mate_send, mate).wait_send()

    @pl.loop(0, B)
    def _(k):
        for d in range(1, L):
            other = lax.rem(l + d, L)
            share_copy(k, l, other).wait_send()


F, M2, M1, C, N1, N2, D = range(7)


def line_kernel(L, B, x_hbm, o_ref, zbuf, shr, acc_lo, acc_hi, acc_mid, tile_send, tile_recv, shift_ref, place_ref,
                cols, stats, x_ref, raw,
                z_recv, out_send, in_send, mate_send, own_send, own_out, own_in, first_send, raw_recv, raw_send, shr_recv, shr_send, diag_recv, diag_send, t_recv, t_send,
                st_recv, st_send, x_sem):
    R, T = x_hbm.shape
    total = T * B
    share = R // B
    half = 2 * share
    SP = shr.shape[2]
    pad = share - 128
    W = min(up_to(share + 15, 16), R)
    low, high = R - (3 * half - pad) // 16 * 16, (3 * half - pad) // 16 * 16
    split = (3 * half - share) // 16 * 16
    edges = [0, low, R - split, (R // 2 - pad) // 16 * 16]
    edges = edges + [R - x for x in reversed(edges)]
    size = [edges[p + 1] - edges[p] for p in range(7)]
    narrow = size[C] // 2
    far = R - size[M2] - size[M1] - size[N1] - narrow
    tile = largest_tile(R, 352)
    RAW = raw.shape[1]
    WS = acc_lo.shape[1]
    hi_lane, mid_lane = R - WS, WS // 128 * 128
    WM = acc_mid.shape[1]
    l, b = lax.axis_index("loop"), lax.axis_index("bulk")
    q, c = b // 2, b % 2
    mate = q * 2 + (1 - c)
    upper = q >= 2
    inner = (q == 1) | (q == 2)
    outer = (q == 0) | (q == 3)
    step = jnp.where(upper, 1, -1)
    H = [jnp.where(upper, h, 3 - h) for h in range(4)]
    out_nbr, in_nbr = b + 2 * step, b - 2 * step
    lx, ly, ld = l + 1 - 2 * (l % 2), lax.rem(l + 2, 4), 3 - l

    def align(value, unit=16):
        return pl.multiple_of(value, unit)

    start = [align(jnp.where(upper, edges[p], edges[6 - p])) for p in range(7)]
    narrow_start = align(jnp.where(upper, R // 2 - narrow, R // 2))

    barrier = pltpu.get_barrier_semaphore()
    for d in range(1, B):
        pl.semaphore_signal(barrier, inc=1, device_id=(l, lax.rem(b + d, B)), device_id_type=MESH)
    for line in (lx, ly):
        pl.semaphore_signal(barrier, inc=1, device_id=(line, b), device_id_type=MESH)

    def load(i):
        rows = pl.ds(pl.multiple_of(i * tile, tile), tile)
        return pltpu.make_async_copy(x_hbm.at[rows, :], x_ref.at[rows, :], x_sem.at[i])

    @pl.loop(0, R // tile)
    def _(i):
        load(i).start()

    lane = lax.broadcasted_iota(jnp.int32, (tile, 128), 1)

    @pl.loop(0, R // tile)
    def _(i):
        rows = pl.ds(pl.multiple_of(i * tile, tile), tile)
        load(i).wait()
        v = x_ref[rows, :]
        mean = jnp.sum(v, axis=1, keepdims=True) / T
        dev = v - mean
        m2 = jnp.sum(dev * dev, axis=1, keepdims=True)
        cols[rows, :] = jnp.where(lane == 0, mean, jnp.where(lane == 1, m2, 0.0))

    pick = (lax.broadcasted_iota(jnp.int32, (8, 128), 0)
            == lax.broadcasted_iota(jnp.int32, (8, 128), 1)).astype(jnp.bfloat16)

    def in_parts(x):
        top = x.astype(jnp.bfloat16)
        rest = x - top.astype(jnp.float32)
        middle = rest.astype(jnp.bfloat16)
        return top, middle, (rest - middle.astype(jnp.float32)).astype(jnp.bfloat16)

    def exact_dot(parts, dot):
        top, middle, low_part = [dot(part) for part in parts]
        return top + middle + low_part

    line = exact_dot(in_parts(cols[...]), lambda part: lax.dot_general(
        pick, part, NT, preferred_element_type=jnp.float32))
    stats[b] = line[:2]

    pl.semaphore_wait(barrier, B - 1 + 2)

    def stat_copy(source, peer):
        return pltpu.make_async_remote_copy(
            src_ref=stats.at[source], dst_ref=stats.at[source],
            send_sem=st_send, recv_sem=st_recv,
            device_id=(l, peer), device_id_type=MESH)

    for d in range(1, B):
        stat_copy(b, lax.rem(b + d, B)).start()
    def raw_copy(p, slot, peer):
        return pltpu.make_async_remote_copy(
            src_ref=x_ref.at[pl.ds(start[p], RAW), :], dst_ref=raw.at[slot], send_sem=raw_send,
            recv_sem=raw_recv.at[slot], device_id=(l, peer), device_id_type=MESH)

    @pl.when(inner)
    def _():
        raw_copy(D, 0, out_nbr).start()
        raw_copy(F, 0, in_nbr).start()

    @pl.when(outer)
    def _():
        raw_copy(F, 1, in_nbr).start()

    gathered = stats.at[pl.ds(0, B - 1)]
    all_stats = pltpu.make_async_remote_copy(
        src_ref=gathered, dst_ref=gathered, send_sem=st_send, recv_sem=st_recv,
        device_id=(l, b), device_id_type=MESH)
    all_stats.wait_recv()

    mean = stats[0, 0:1]
    for k in range(1, B):
        mean = mean + stats[k, 0:1]
    mean = mean / B
    square = jnp.zeros_like(mean)
    for k in range(B):
        shift = stats[k, 0:1] - mean
        square = square + (stats[k, 1:2] + T * (shift * shift))
    scale = lax.rsqrt(square / total + epsilon)
    sub = lax.broadcasted_iota(jnp.int32, (8, R), 0)
    both = jnp.where(sub == 0, mean, jnp.where(sub == 1, scale, 0.0))
    cols[...] = exact_dot(in_parts(both), lambda part: lax.dot_general(
        part, pick, TN, preferred_element_type=jnp.float32))

    def normalise(begin, count):
        unit = count if count <= 288 else largest_tile(count, 128)

        def chunk(i):
            rows = pl.ds(pl.multiple_of(begin + i * unit, 16), unit)
            z = (x_ref[rows, :] - cols[rows, 0:1]) * cols[rows, 1:2]
            zbuf[b, rows, :] = z.astype(jnp.bfloat16)

        if unit == count:
            chunk(0)
        else:
            pl.loop(0, count // unit)(chunk)

    def z_copy(k, p, send_sem, peer, skip=0, to_end=False):
        begin, rows = align(start[p] + skip), size[p] - skip
        if to_end and p == C:
            begin, rows = narrow_start, narrow
        part = zbuf.at[k, pl.ds(begin, rows), :]
        return pltpu.make_async_remote_copy(
            src_ref=part, dst_ref=part, send_sem=send_sem,
            recv_sem=z_recv.at[k, jnp.where(upper, p, 6 - p)], device_id=(l, peer), device_id_type=MESH)

    def first_copy(k, p, peer):
        return z_copy(k, p, first_send, peer, RAW)

    def unpack(slot, k, p):
        raw_copy(p, slot, b).wait_recv()
        rows = pl.ds(start[p], RAW)
        z = (raw[slot] - cols[rows, 0:1]) * cols[rows, 1:2]
        zbuf[k, rows, :] = z.astype(jnp.bfloat16)

    def send_out(k, p):
        return z_copy(k, p, out_send, out_nbr, 0, True)

    def send_in(k, p):
        return z_copy(k, p, in_send, in_nbr)

    def mate_copy(k, p, to_end=False):
        return z_copy(k, p, mate_send, mate, 0, to_end)

    def mate_own(k):
        part = zbuf.at[k]
        return pltpu.make_async_remote_copy(
            src_ref=part, dst_ref=part, send_sem=own_send, recv_sem=z_recv.at[k, 0],
            device_id=(l, mate), device_id_type=MESH)

    def share_copy(k, block, peer, way):
        part = shr.at[k, block, pl.ds(0, SR), :]
        return pltpu.make_async_remote_copy(
            src_ref=part, dst_ref=part, send_sem=shr_send,
            recv_sem=shr_recv.at[k, way], device_id=(peer, b), device_id_type=MESH)

    SR = up_to(share, 8)
    cut = up_to(share // 2, 16)

    def diag_copy(k, block, peer, way):
        rows = pl.ds(0, cut) if way == 0 else pl.ds(cut, SR - cut)
        part = shr.at[k, block, rows, :]
        return pltpu.make_async_remote_copy(
            src_ref=part, dst_ref=part, send_sem=diag_send,
            recv_sem=diag_recv.at[k // 2], device_id=(peer, b), device_id_type=MESH)

    first = align(jnp.minimum(b * share // 16 * 16, jnp.where(q == 0, size[D], R) - W))

    def extract_one(k):
        window = zbuf[k, pl.ds(first, W), :]
        row = lax.broadcasted_iota(jnp.int32, (SP, W), 0)
        hot = lax.broadcasted_iota(jnp.int32, (SP, W), 1) == row + (b * share - first)
        hot = jnp.where(hot & (row < share), 1.0, 0.0).astype(jnp.bfloat16)
        rows = lax.dot_general(hot, window, (((1,), (0,)), ((), ())),
                               preferred_element_type=jnp.float32)
        shr[k, l] = rows.astype(jnp.bfloat16)
        share_copy(k, l, lx, 0).start()
        share_copy(k, l, ly, 1).start()

    def extract(place):
        @pl.loop(0, 2)
        def _(core):
            extract_one(place * 2 + core)

    def pass_on(place):
        @pl.loop(0, 2)
        def _(core):
            k = place * 2 + core
            share_copy(k, lx, lx, 0).wait_recv()
            diag_copy(k, lx, ly, 0).start()
            share_copy(k, ly, ly, 1).wait_recv()
            diag_copy(k, ly, lx, 1).start()

    def wait_diag(place):
        part = shr.at[pl.ds(place * 2, 2), ld, pl.ds(0, SR), :]
        pltpu.make_async_remote_copy(
            src_ref=part, dst_ref=part, send_sem=diag_send, recv_sem=diag_recv.at[place],
            device_id=(l, b), device_id_type=MESH).wait_recv()

    def product(place, begin, width):
        part = None
        for core in range(2):
            k = place * 2 + core
            term = lax.dot_general(shr[k].reshape(L * SP, T), zbuf[k, begin:begin + width, :], NT,
                                   preferred_element_type=jnp.float32)
            part = term if part is None else part + term
        return part

    def add_sides(place):
        acc_lo[...] += product(place, 0, WS)
        acc_hi[...] += product(place, hi_lane, WS)

    def add_middle(place):
        acc_mid[...] += product(place, mid_lane, WM)

    def own(h):
        return H[h] * 2 + c

    def other(h):
        return H[h] * 2 + (1 - c)

    def take(h, p, onward=None, first=False, to_end=False):
        if first:
            first_copy(own(h), p, mate).wait_recv()
        else:
            mate_copy(own(h), p, to_end).wait_recv()
        if onward is not None:
            onward(own(h), p).start()
        mate_copy(own(h), p, to_end).start()

    def mate_take(h, pieces, to_end=False):
        for p in pieces:
            mate_copy(other(h), p, to_end).wait_recv()

    def take_end(h, p):
        take(h, p, to_end=True)

    def mate_take_end(h, pieces):
        mate_take(h, pieces, True)

    def tile_copy(side, j, core, block, slot):
        return pltpu.make_async_remote_copy(
            src_ref=tile_send.at[side, j, core, pl.ds(0, SR), :],
            dst_ref=tile_recv.at[block, pl.ds(0, SR), pl.ds(pl.multiple_of(slot * 128, 128), 128)],
            send_sem=t_send, recv_sem=t_recv.at[block],
            device_id=(j, 6 * side + core), device_id_type=MESH)

    def make_hot():
        for side, skip in ((0, jnp.where(b == 5, 0, pad)), (1, jnp.where(b == 2, pad, 0))):
            shift = (lax.broadcasted_iota(jnp.int32, (SR, 128), 0)
                     == lax.broadcasted_iota(jnp.int32, (SR, 128), 1) + skip)
            shift_ref[side] = jnp.where(shift, 1.0, 0.0).astype(jnp.bfloat16)
        row = lax.broadcasted_iota(jnp.int32, (512, WM), 0)
        slot = row // 128
        shifted = slot < jnp.where(upper, 1, 3)
        lane = half - mid_lane + slot * (share - 128) + row + jnp.where(shifted, pad, 0)
        hot = lax.broadcasted_iota(jnp.int32, (512, WM), 1) == lane
        place_ref[...] = jnp.where(hot, 1.0, 0.0).astype(jnp.bfloat16)
        for side, slot in ((0, 0), (3, 3)):
            @pl.when(q == side)
            def _():
                tile_recv[:, :, slot * 128:slot * 128 + 128] = jnp.zeros((L, SP, 128), jnp.bfloat16)

    def add_rows(j, place):
        rows = pl.ds(pl.multiple_of(j * SP, SP), SP)
        for acc, begin in ((acc_lo, 0), (acc_hi, hi_lane)):
            value = acc[rows, :]
            for core in range(2):
                k = place * 2 + core
                value = value + lax.dot_general(shr[k, j], zbuf[k, begin:begin + WS, :], NT,
                                                preferred_element_type=jnp.float32)
            acc[rows, :] = value

    def turn_tiles(j):
        rows = pl.ds(pl.multiple_of(j * SP, SP), SP)
        for side, acc in ((0, acc_lo), (1, acc_hi)):
            turned = lax.dot_general((acc[rows, :][:SR] / total).astype(jnp.bfloat16), shift_ref[side], TN,
                                     preferred_element_type=jnp.float32)
            for core in range(2):
                at = (WS - half if side else 0) + core * share
                tile_send[side, j, core, :share, :] = turned[at:at + share].astype(jnp.bfloat16)

    def tile_copies(j, act):
        for side, skipped in ((0, 2), (1, 5)):
            @pl.when(b != skipped)
            def _():
                for core in range(2):
                    act(tile_copy(side, j, core, l, b - 2))

    def start_tiles(j):
        tile_copies(j, lambda copy: copy.start())

    def wait_tile(block):
        part = tile_recv.at[block, pl.ds(0, SR), pl.ds(0, 384)]
        pltpu.make_async_remote_copy(
            src_ref=part, dst_ref=part, send_sem=t_send, recv_sem=t_recv.at[block],
            device_id=(l, b), device_id_type=MESH).wait_recv()

    normalise(start[D], size[D])

    @pl.when(inner)
    def _():
        first_copy(b, D, out_nbr).start()

    normalise(start[F], size[F])

    first_copy(b, F, in_nbr).start()
    normalise(low, high - low)

    @pl.when(inner)
    def _():
        for p in (M2, M1, C):
            z_copy(b, p, own_in, in_nbr).start()
        for p in (F, C, N2):
            z_copy(b, p, own_out, out_nbr, 0, True).start()

    @pl.when(outer)
    def _():
        for p in (M2, M1, C, D, N2, N1):
            z_copy(b, p, own_in, in_nbr).start()
    mate_own(b).start()
    extract_one(b)
    make_hot()
    mate_own(mate).wait_recv()
    extract_one(mate)

    @pl.when(inner)
    def _():
        unpack(0, own(1), D)
        unpack(1, own(3), F)
        take(1, D, send_out, True)
        take(3, F, send_in, True)
        pass_on(q)
        take(1, N2, send_out)
        take(3, M2, send_in)
        take(1, N1)
        take(3, M1, send_in)
        take(1, C, send_out)
        take(3, C, send_in)
        z_copy(b, D, own_in, in_nbr).start()
        mate_take(1, (D, N2, N1, C))
        extract(H[1])
        take(0, D, send_out)
        take(3, D, send_in)

    @pl.when(outer)
    def _():
        unpack(0, own(2), D)
        take(2, D, None, True)
        mate_take(2, (D,))
        extract(H[2])
        pass_on(q)
        take_end(2, F)
        take_end(2, C)
        take_end(2, N2)
        pass_on(H[2])
        take(1, D)
        mate_take(1, (D,))
        extract(H[1])
        mate_take_end(2, (F, C, N2))
    wait_diag(q)
    acc_lo[...] = product(q, 0, WS)
    acc_hi[...] = product(q, hi_lane, WS)
    acc_mid[...] = product(q, mid_lane, WM)

    second, third = jnp.where(inner, H[1], H[2]), jnp.where(inner, H[3], H[1])

    @pl.when(inner)
    def _():
        pass_on(H[1])
        take(0, N2, send_out)
        take(0, N1)
        take(0, C, send_out)
        mate_take(0, (D, N2, N1, C))
        extract(H[0])
        take(3, N2)
        take(3, N1)
        mate_take(3, (C, D, N2, N1))
        extract(H[3])
        take(1, F, send_out)
        mate_take(1, (F,))

    @pl.when(outer)
    def _():
        take_end(1, N2)
        take_end(1, C)
        pass_on(H[1])
    wait_diag(second)
    add_sides(second)

    @pl.when(outer)
    def _():
        take(0, D)
        mate_take(0, (D,))
        extract(H[0])
        take_end(0, N2)
        take_end(0, C)
        take_end(1, F)
        mate_take_end(1, (N2, C, F))
        wait_diag(H[1])
        add_sides(H[1])
    pass_on(H[0])

    @pl.when(inner)
    def _():
        take(0, F, send_out)
        for p in (N1, N2):
            z_copy(b, p, own_in, in_nbr).start()
        mate_take(3, (F, M1, M2))
        mate_take(0, (F,))
        add_rows(l, H[3])
        add_rows(l, H[0])
        turn_tiles(l)
        start_tiles(l)
        pass_on(H[3])

        @pl.loop(0, 2)
        def _(n):
            j = jnp.where(n == 0, lx, ly)
            add_rows(j, H[3])
            add_rows(j, H[0])
            turn_tiles(j)
            start_tiles(j)
        for p in (N1, N2):
            send_in(own(3), p).start()
        wait_diag(H[0])
        add_rows(ld, H[0])
        wait_diag(H[3])
        add_rows(ld, H[3])
        turn_tiles(ld)
        start_tiles(ld)
        for p in (M1, M2):
            take(1, p)
        mate_take(1, (M1, M2))
    add_middle(second)
    add_middle(third)

    def put(lanes, acc, begin=0):
        for j in range(L):
            part = acc[j * SP:j * SP + share, :][:, begin:begin + lanes.stop - lanes.start]
            o_ref[:, j, lanes] = part / total

    @pl.when(inner)
    def _():
        for p in (M1, M2):
            take(0, p)
        put(slice(0, mid_lane), acc_lo)
        put(slice(mid_lane + WM, R), acc_hi, mid_lane + WM - hi_lane)
        mate_take(0, (M1, M2))
        add_middle(H[0])
        put(slice(mid_lane, mid_lane + WM), acc_mid)

    lanes_lo = mid_lane, up_to(R // 2 + pad, 128)
    lanes_hi = (R // 2 - pad) // 128 * 128, mid_lane + WM

    @pl.when(outer)
    def _():
        mate_take_end(0, (N2, C))
        wait_diag(H[0])
        for end, acc, begin, (first_mid, last_mid) in ((0, acc_lo, 0, lanes_lo), (3, acc_hi, hi_lane, lanes_hi)):
            @pl.when(q == end)
            def _():
                acc[...] += product(H[0], begin, WS)
                inner_lanes = slice(first_mid - mid_lane, last_mid - mid_lane)
                acc_mid[:, inner_lanes] += product(H[0], first_mid, last_mid - first_mid)
                put(slice(first_mid, last_mid), acc_mid, first_mid - mid_lane)
                if end:
                    put(slice(last_mid, R), acc, last_mid - hi_lane)
                else:
                    put(slice(0, first_mid), acc)
        take(0, F)
        mate_take(0, (F,))
        for end, acc, begin in ((3, acc_lo, 0), (0, acc_hi, hi_lane)):
            @pl.when(q == end)
            def _():
                acc[...] += product(H[0], begin, WS)
                put(slice(begin, begin + WS), acc)
        place = lax.broadcasted_iota(jnp.int32, (share, WM), 1) + mid_lane
        low_first = half + pad + jnp.where(upper, 0, share)
        high_first = R // 2 + jnp.where(upper, 0, pad)
        inside = ((place >= low_first) & (place < low_first + jnp.where(upper, 256, 128))
                  | (place >= high_first) & (place < high_first + jnp.where(upper, 128, 256)))
        for d in (l, lx, ly, ld):
            wait_tile(d)
            placed = lax.dot_general(tile_recv[d], place_ref[...], (((1,), (0,)), ((), ())),
                                     preferred_element_type=jnp.float32)[:share]
            middle = pl.ds(mid_lane, WM)
            o_ref[:, d, middle] = jnp.where(inside, placed, o_ref[:, d, middle])

    all_stats.wait_send()
    mate_own(b).wait_send()

    def sent(part, sem):
        pltpu.make_async_remote_copy(
            src_ref=part, dst_ref=part, send_sem=sem, recv_sem=st_recv,
            device_id=(l, b), device_id_type=MESH).wait_send()

    @pl.when(inner)
    def _():
        sent(zbuf.at[0, pl.ds(0, size[F] + narrow + size[N2]), :], own_out)
        sent(zbuf.at[pl.ds(0, 2), pl.ds(0, size[D] - RAW), :], first_send)
        sent(raw, raw_send)
        sent(zbuf.at[pl.ds(0, 2), pl.ds(0, far), :], out_send)
        sent(zbuf.at[0], in_send)
        sent(zbuf.at[pl.ds(0, 3)], mate_send)
        for skipped in (True, False):
            @pl.when(((b == 2) | (b == 5)) == skipped)
            def _():
                sides = 1 if skipped else 2
                sent(tile_send.at[pl.ds(0, sides), :, :, pl.ds(0, SR), :], t_send)

    @pl.when(outer)
    def _():
        sent(zbuf.at[0, pl.ds(0, size[D] - RAW), :], first_send)
        sent(raw.at[0], raw_send)
        sent(zbuf.at[pl.ds(0, 3), pl.ds(0, far), :], mate_send)

    sent(zbuf.at[0, pl.ds(0, R - size[D]), :], own_in)
    sent(shr.at[pl.ds(0, L), :, pl.ds(0, SR), :], shr_send)
    sent(shr.at[pl.ds(0, B // L), :, pl.ds(0, SR), :], diag_send)


def line_call(L, B, series):
    R, T = series.shape
    share = R // B
    SP = up_to(share, 16)
    pad = share - 128
    high = (3 * 2 * share - pad) // 16 * 16
    WS = R - high
    mid_lane = WS // 128 * 128
    WM = up_to(R // 2 + pad + 256, 128) - mid_lane
    vmem = pl.BlockSpec(memory_space=pltpu.VMEM)
    dma = pltpu.SemaphoreType.DMA
    return pl.pallas_call(
        functools.partial(line_kernel, L, B),
        out_shape=jax.ShapeDtypeStruct((share, L, R), jnp.float32),
        in_specs=[pl.BlockSpec(memory_space=pltpu.HBM)],
        out_specs=vmem,
        scratch_shapes=[
            pltpu.VMEM((B, R, T), jnp.bfloat16),
            pltpu.VMEM((B, L, SP, T), jnp.bfloat16),
            pltpu.VMEM((L * SP, WS), jnp.float32),
            pltpu.VMEM((L * SP, WS), jnp.float32),
            pltpu.VMEM((L * SP, WM), jnp.float32),
            pltpu.VMEM((2, L, 2, SP, 128), jnp.bfloat16),
            pltpu.VMEM((L, SP, 512), jnp.bfloat16),
            pltpu.VMEM((2, up_to(share, 8), 128), jnp.bfloat16),
            pltpu.VMEM((512, WM), jnp.bfloat16),
            pltpu.VMEM((R, 128), jnp.float32),
            pltpu.VMEM((B, 2, R), jnp.float32),
            pltpu.VMEM((R, T), jnp.float32),
            pltpu.VMEM((2, (R - high) * 7 // 256 * 16, T), jnp.float32),
            dma((B, 7)), dma, dma, dma, dma, dma, dma, dma, dma((2,)), dma,
            dma((B, 2)), dma, dma((B // 2,)), dma, dma((L,)), dma,
            dma, dma, dma((R // largest_tile(R, 352),)),
        ],
        compiler_params=pltpu.CompilerParams(
            collective_id=0, has_side_effects=True, vmem_limit_bytes=34 * 1024 * 1024),
    )(pltpu.with_memory_space_constraint(series, pltpu.HBM)).transpose(1, 0, 2)


def solution(mesh):
    L, B = mesh.shape["loop"], mesh.shape["bulk"]

    def on_device(series):
        R, T = series.shape
        share = R // B
        if L == 4 and B == 8 and R % 16 == 0 and T % 128 == 0 and 128 <= share <= 144:
            return line_call(L, B, series)
        SP = up_to(share, 16)
        pieces = 3
        vmem = pl.BlockSpec(memory_space=pltpu.VMEM)
        dma = pltpu.SemaphoreType.DMA
        return pl.pallas_call(
            functools.partial(kernel, L, B, pieces),
            out_shape=jax.ShapeDtypeStruct((share, L, R), jnp.float32),
            in_specs=[pl.BlockSpec(memory_space=pltpu.HBM)],
            out_specs=vmem,
            scratch_shapes=[
                pltpu.VMEM((B, R, T), jnp.bfloat16),
                pltpu.VMEM((B, L, SP, T), jnp.bfloat16),
                pltpu.VMEM((L * SP, R), jnp.float32),
                pltpu.VMEM((R, 128), jnp.float32),
                pltpu.VMEM((B, 2, R), jnp.float32),
                pltpu.VMEM((R, T), jnp.float32),
                dma((B, pieces)), dma((B, pieces)), dma((B, pieces)), dma((B, pieces)),
                dma((B, L)), dma((B, L)), dma((B,)), dma((B,)), dma((R // largest_tile(R, 128),)),
            ],
            compiler_params=pltpu.CompilerParams(
                collective_id=0, has_side_effects=True, vmem_limit_bytes=26 * 1024 * 1024),
        )(pltpu.with_memory_space_constraint(series, pltpu.HBM)).transpose(1, 0, 2)

    return jax.shard_map(
        on_device, mesh=mesh, in_specs=(P("loop", "bulk"),),
        out_specs=P(None, "bulk", "loop"), check_vma=False)
```

```python
import functools
import jax
import jax.numpy as jnp
from jax import lax
from jax.experimental import pallas as pl
from jax.experimental.pallas import tpu as pltpu
from jax.sharding import PartitionSpec as P

epsilon = 1e-06
MESH = pl.DeviceIdType.MESH
NT = (((1,), (1,)), ((), ()))
TN = (((0,), (0,)), ((), ()))


def up_to(value, unit):
    return -(-value // unit) * unit


def largest_tile(rows, limit):
    return max(t for t in range(16, limit + 1, 16) if rows % t == 0)


def kernel(L, B, PIECES, x_hbm, o_ref, zbuf, shr, acc, cols, stats, x_ref,
           z_recv, up_send, down_send, mate_send, shr_recv, shr_send, st_recv, st_send, x_sem):
    R, T = x_hbm.shape
    total = T * B
    Q = B // 2
    share = R // B
    SP = shr.shape[2]
    W = min(up_to(share + 15, 16), R)
    bounds = [up_to(R * i // PIECES, 128) for i in range(PIECES)] + [R]
    tile = largest_tile(R, 128)
    l, b = lax.axis_index("loop"), lax.axis_index("bulk")
    q, c = b // 2, b % 2
    mate = q * 2 + (1 - c)

    barrier = pltpu.get_barrier_semaphore()
    for d in range(1, B):
        pl.semaphore_signal(barrier, inc=1, device_id=(l, lax.rem(b + d, B)), device_id_type=MESH)
    for d in range(1, L):
        pl.semaphore_signal(barrier, inc=1, device_id=(lax.rem(l + d, L), b), device_id_type=MESH)

    def load(i):
        rows = pl.ds(pl.multiple_of(i * tile, tile), tile)
        return pltpu.make_async_copy(x_hbm.at[rows, :], x_ref.at[rows, :], x_sem.at[i])

    @pl.loop(0, R // tile)
    def _(i):
        load(i).start()

    lane = lax.broadcasted_iota(jnp.int32, (tile, 128), 1)

    @pl.loop(0, R // tile)
    def _(i):
        rows = pl.ds(pl.multiple_of(i * tile, tile), tile)
        load(i).wait()
        v = x_ref[rows, :]
        mean = jnp.sum(v, axis=1, keepdims=True) / T
        dev = v - mean
        m2 = jnp.sum(dev * dev, axis=1, keepdims=True)
        cols[rows, :] = jnp.where(lane == 0, mean, jnp.where(lane == 1, m2, 0.0))

    pick = (lax.broadcasted_iota(jnp.int32, (8, 128), 0)
            == lax.broadcasted_iota(jnp.int32, (8, 128), 1)).astype(jnp.float32)
    line = lax.dot_general(pick, cols[...], NT, precision=lax.Precision.HIGHEST,
                           preferred_element_type=jnp.float32)
    stats[b] = line[:2]

    pl.semaphore_wait(barrier, B - 1 + L - 1)

    def stat_copy(source, peer):
        return pltpu.make_async_remote_copy(
            src_ref=stats.at[source], dst_ref=stats.at[source],
            send_sem=st_send.at[peer], recv_sem=st_recv.at[source],
            device_id=(l, peer), device_id_type=MESH)

    for d in range(1, B):
        stat_copy(b, lax.rem(b + d, B)).start()
    for d in range(1, B):
        other = lax.rem(b + d, B)
        stat_copy(other, other).wait_recv()

    mean = stats[0, 0:1]
    for k in range(1, B):
        mean = mean + stats[k, 0:1]
    mean = mean / B
    square = jnp.zeros_like(mean)
    for k in range(B):
        shift = stats[k, 0:1] - mean
        square = square + (stats[k, 1:2] + T * (shift * shift))
    scale = lax.rsqrt(square / total + epsilon)
    sub = lax.broadcasted_iota(jnp.int32, (8, R), 0)
    both = jnp.where(sub == 0, mean, jnp.where(sub == 1, scale, 0.0))
    cols[...] = lax.dot_general(both, pick, TN, precision=lax.Precision.HIGHEST,
                                preferred_element_type=jnp.float32)

    def normalise(piece):
        size = bounds[piece + 1] - bounds[piece]
        step = largest_tile(size, 128)

        @pl.loop(0, size // step)
        def _(i):
            rows = pl.ds(pl.multiple_of(bounds[piece] + i * step, 16), step)
            z = (x_ref[rows, :] - cols[rows, 0:1]) * cols[rows, 1:2]
            zbuf[b, rows, :] = z.astype(jnp.bfloat16)

    def piece_copy(k, piece, send_sem, peer):
        part = zbuf.at[k, pl.ds(bounds[piece], bounds[piece + 1] - bounds[piece]), :]
        return pltpu.make_async_remote_copy(
            src_ref=part, dst_ref=part, send_sem=send_sem.at[k, piece],
            recv_sem=z_recv.at[k, piece], device_id=(l, peer), device_id_type=MESH)

    def share_copy(k, block, peer):
        return pltpu.make_async_remote_copy(
            src_ref=shr.at[k, block], dst_ref=shr.at[k, block], send_sem=shr_send.at[k, peer],
            recv_sem=shr_recv.at[k, block], device_id=(peer, b), device_id_type=MESH)

    has_up, has_down = q + 1 < Q, q >= 1
    start = b * share
    first = pl.multiple_of(jnp.minimum(start // 16 * 16, R - W), 16)
    need_below = PIECES - 1 - sum((first >= x).astype(jnp.int32) for x in bounds[1:-1])
    need_above = sum((first + W > x).astype(jnp.int32) for x in bounds[1:-1])

    def extract(k):
        window = zbuf[k, pl.ds(first, W), :]
        hot = (lax.broadcasted_iota(jnp.int32, (SP, W), 1)
               == lax.broadcasted_iota(jnp.int32, (SP, W), 0) + (start - first))
        inside = lax.broadcasted_iota(jnp.int32, (SP, W), 0) < share
        hot = jnp.where(hot & inside, 1.0, 0.0).astype(jnp.bfloat16)
        rows = lax.dot_general(hot, window, (((1,), (0,)), ((), ())),
                               preferred_element_type=jnp.float32)
        shr[k, l] = rows.astype(jnp.bfloat16)
        for d in range(1, L):
            share_copy(k, l, lax.rem(l + d, L)).start()

    def wait_shares(place):
        for core in range(2):
            k = place * 2 + core
            for d in range(1, L):
                other = lax.rem(l + d, L)
                share_copy(k, other, other).wait_recv()

    def multiply(place):
        part = None
        wait_shares(place)
        for core in range(2):
            k = place * 2 + core
            a = shr[k].reshape(L * SP, T)
            term = lax.dot_general(a, zbuf[k], NT, preferred_element_type=jnp.float32)
            part = term if part is None else part + term
        acc[...] += part

    def multiply_step(s):
        @pl.loop(0, 2)
        def _(n):
            place = q - (1 - 2 * n) * s

            @pl.when((place >= 0) & (place < Q) & ((s > 0) | (n < 1)))
            def _():
                multiply(place)

    def send_own(up_first):
        done = set()

        def send(up, i):
            piece = PIECES - 1 - i if up else i
            if piece not in done:
                done.add(piece)
                normalise(piece)

            @pl.when(has_up if up else has_down)
            def _():
                if up:
                    piece_copy(b, piece, up_send, b + 2).start()
                else:
                    piece_copy(b, piece, down_send, b - 2).start()

        for i in range(PIECES):
            send(up_first, i)
            send(not up_first, i)

    @pl.when(q >= Q // 2)
    def _():
        send_own(True)

    @pl.when(q < Q // 2)
    def _():
        send_own(False)

    for i in range(PIECES):
        piece_copy(b, i, mate_send, mate).start()

    acc[...] = jnp.zeros_like(acc)
    extract(b)

    for i in range(PIECES):
        piece_copy(mate, i, mate_send, mate).wait_recv()

    extract(mate)

    def arrive(s, i, between=None):
        below, above = b - 2 * s, b + 2 * s
        from_below, from_above = q - s >= 0, q + s < Q
        down_piece = PIECES - 1 - i

        @pl.when(from_below)
        def _():
            piece_copy(below, down_piece, up_send, b).wait_recv()

            @pl.when(has_up)
            def _():
                piece_copy(below, down_piece, up_send, b + 2).start()
            piece_copy(below, down_piece, mate_send, mate).start()

        @pl.when(from_above)
        def _():
            piece_copy(above, i, down_send, b).wait_recv()

            @pl.when(has_down)
            def _():
                piece_copy(above, i, down_send, b - 2).start()
            piece_copy(above, i, mate_send, mate).start()

        @pl.when(from_below & (i == need_below))
        def _():
            extract(below)

        @pl.when(from_above & (i == need_above))
        def _():
            extract(above)

        if between is not None:
            between()

        @pl.when(from_below)
        def _():
            piece_copy(mate - 2 * s, down_piece, mate_send, mate).wait_recv()

            @pl.when(i == need_below)
            def _():
                extract(mate - 2 * s)

        @pl.when(from_above)
        def _():
            piece_copy(mate + 2 * s, i, mate_send, mate).wait_recv()

            @pl.when(i == need_above)
            def _():
                extract(mate + 2 * s)

        if i == 0:
            multiply_step(s - 1)

    def finish(piece, place):
        lo, hi = bounds[piece], bounds[piece + 1]
        part = acc[:, lo:hi]
        if place is not None:
            for core in range(2):
                k = place * 2 + core
                a = shr[k].reshape(L * SP, T)
                part = part + lax.dot_general(a, zbuf[k, lo:hi, :], NT,
                                              preferred_element_type=jnp.float32)
        part = part / total
        for j in range(L):
            o_ref[:, j, lo:hi] = part[j * SP:j * SP + share]

    @pl.loop(1, Q - 1)
    def _(s):
        for i in range(PIECES):
            arrive(s, i)

    def finish_ends(steps):
        for end, place in ((Q - 1, 0), (0, Q - 1)):
            @pl.when(q == end)
            def _():
                for i in steps:
                    finish(PIECES - 1 - i if end else i, place)

    def finish_early():
        for end, place in ((Q - 1, 0), (0, Q - 1)):
            @pl.when(q == end)
            def _():
                wait_shares(place)

        finish_ends(range(PIECES - 1))

    for i in range(PIECES):
        arrive(Q - 1, i, finish_early if i == PIECES - 1 else None)
    finish_ends([PIECES - 1])

    @pl.when((q > 0) & (q < Q - 1))
    def _():
        for i in range(PIECES):
            finish(i, None)

    for d in range(1, B):
        other = lax.rem(b + d, B)
        stat_copy(b, other).wait_send()

    @pl.loop(0, Q)
    def _(s):
        below, above = b - 2 * s, b + 2 * s
        from_below, from_above = q - s >= 0, q + s < Q

        for i in range(PIECES):
            @pl.when(from_below & has_up)
            def _():
                piece_copy(below, i, up_send, b + 2).wait_send()

            @pl.when(from_above & has_down)
            def _():
                piece_copy(above, i, down_send, b - 2).wait_send()

            @pl.when(from_below)
            def _():
                piece_copy(below, i, mate_send, mate).wait_send()

            @pl.when(from_above & (s > 0))
            def _():
                piece_copy(above, i, mate_send, mate).wait_send()

    @pl.loop(0, B)
    def _(k):
        for d in range(1, L):
            other = lax.rem(l + d, L)
            share_copy(k, l, other).wait_send()


F, M2, M1, C, N1, N2, D = range(7)


def line_kernel(L, B, x_hbm, o_ref, zbuf, shr, acc_lo, acc_hi, acc_mid, tile_send, tile_recv, shift_ref, place_ref,
                cols, stats, x_ref, raw,
                z_recv, out_send, in_send, mate_send, own_send, own_out, own_in, first_send, raw_recv, raw_send, shr_recv, shr_send, diag_recv, diag_send, t_recv, t_send,
                st_recv, st_send, x_sem):
    R, T = x_hbm.shape
    total = T * B
    share = R // B
    half = 2 * share
    SP = shr.shape[2]
    pad = share - 128
    W = min(up_to(share + 15, 16), R)
    low, high = R - (3 * half - pad) // 16 * 16, (3 * half - pad) // 16 * 16
    split = (3 * half - share) // 16 * 16
    edges = [0, low, R - split, (R // 2 - pad) // 16 * 16]
    edges = edges + [R - x for x in reversed(edges)]
    size = [edges[p + 1] - edges[p] for p in range(7)]
    narrow = size[C] // 2
    far = R - size[M2] - size[M1] - size[N1] - narrow
    tile = largest_tile(R, 352)
    RAW = raw.shape[1]
    WS = acc_lo.shape[1]
    hi_lane, mid_lane = R - WS, WS // 128 * 128
    WM = acc_mid.shape[1]
    l, b = lax.axis_index("loop"), lax.axis_index("bulk")
    q, c = b // 2, b % 2
    mate = q * 2 + (1 - c)
    upper = q >= 2
    inner = (q == 1) | (q == 2)
    outer = (q == 0) | (q == 3)
    step = jnp.where(upper, 1, -1)
    H = [jnp.where(upper, h, 3 - h) for h in range(4)]
    out_nbr, in_nbr = b + 2 * step, b - 2 * step
    lx, ly, ld = l + 1 - 2 * (l % 2), lax.rem(l + 2, 4), 3 - l

    def align(value, unit=16):
        return pl.multiple_of(value, unit)

    start = [align(jnp.where(upper, edges[p], edges[6 - p])) for p in range(7)]
    narrow_start = align(jnp.where(upper, R // 2 - narrow, R // 2))

    barrier = pltpu.get_barrier_semaphore()
    for d in range(1, B):
        pl.semaphore_signal(barrier, inc=1, device_id=(l, lax.rem(b + d, B)), device_id_type=MESH)
    for line in (lx, ly):
        pl.semaphore_signal(barrier, inc=1, device_id=(line, b), device_id_type=MESH)

    def load(i):
        rows = pl.ds(pl.multiple_of(i * tile, tile), tile)
        return pltpu.make_async_copy(x_hbm.at[rows, :], x_ref.at[rows, :], x_sem.at[i])

    @pl.loop(0, R // tile)
    def _(i):
        load(i).start()

    lane = lax.broadcasted_iota(jnp.int32, (tile, 128), 1)

    @pl.loop(0, R // tile)
    def _(i):
        rows = pl.ds(pl.multiple_of(i * tile, tile), tile)
        load(i).wait()
        v = x_ref[rows, :]
        mean = jnp.sum(v, axis=1, keepdims=True) / T
        dev = v - mean
        m2 = jnp.sum(dev * dev, axis=1, keepdims=True)
        cols[rows, :] = jnp.where(lane == 0, mean, jnp.where(lane == 1, m2, 0.0))

    pick = (lax.broadcasted_iota(jnp.int32, (8, 128), 0)
            == lax.broadcasted_iota(jnp.int32, (8, 128), 1)).astype(jnp.bfloat16)

    def in_parts(x):
        top = x.astype(jnp.bfloat16)
        rest = x - top.astype(jnp.float32)
        middle = rest.astype(jnp.bfloat16)
        return top, middle, (rest - middle.astype(jnp.float32)).astype(jnp.bfloat16)

    def exact_dot(parts, dot):
        top, middle, low_part = [dot(part) for part in parts]
        return top + middle + low_part

    line = exact_dot(in_parts(cols[...]), lambda part: lax.dot_general(
        pick, part, NT, preferred_element_type=jnp.float32))
    stats[b] = line[:2]

    pl.semaphore_wait(barrier, B - 1 + 2)

    def stat_copy(source, peer):
        return pltpu.make_async_remote_copy(
            src_ref=stats.at[source], dst_ref=stats.at[source],
            send_sem=st_send, recv_sem=st_recv,
            device_id=(l, peer), device_id_type=MESH)

    for d in range(1, B):
        stat_copy(b, lax.rem(b + d, B)).start()
    def raw_copy(p, slot, peer):
        return pltpu.make_async_remote_copy(
            src_ref=x_ref.at[pl.ds(start[p], RAW), :], dst_ref=raw.at[slot], send_sem=raw_send,
            recv_sem=raw_recv.at[slot], device_id=(l, peer), device_id_type=MESH)

    @pl.when(inner)
    def _():
        raw_copy(D, 0, out_nbr).start()
        raw_copy(F, 0, in_nbr).start()

    @pl.when(outer)
    def _():
        raw_copy(F, 1, in_nbr).start()

    gathered = stats.at[pl.ds(0, B - 1)]
    all_stats = pltpu.make_async_remote_copy(
        src_ref=gathered, dst_ref=gathered, send_sem=st_send, recv_sem=st_recv,
        device_id=(l, b), device_id_type=MESH)
    all_stats.wait_recv()

    mean = stats[0, 0:1]
    for k in range(1, B):
        mean = mean + stats[k, 0:1]
    mean = mean / B
    square = jnp.zeros_like(mean)
    for k in range(B):
        shift = stats[k, 0:1] - mean
        square = square + (stats[k, 1:2] + T * (shift * shift))
    scale = lax.rsqrt(square / total + epsilon)
    sub = lax.broadcasted_iota(jnp.int32, (8, R), 0)
    both = jnp.where(sub == 0, mean, jnp.where(sub == 1, scale, 0.0))
    cols[...] = exact_dot(in_parts(both), lambda part: lax.dot_general(
        part, pick, TN, preferred_element_type=jnp.float32))

    def normalise(begin, count):
        unit = count if count <= 288 else largest_tile(count, 128)

        def chunk(i):
            rows = pl.ds(pl.multiple_of(begin + i * unit, 16), unit)
            z = (x_ref[rows, :] - cols[rows, 0:1]) * cols[rows, 1:2]
            zbuf[b, rows, :] = z.astype(jnp.bfloat16)

        if unit == count:
            chunk(0)
        else:
            pl.loop(0, count // unit)(chunk)

    def z_copy(k, p, send_sem, peer, skip=0, to_end=False):
        begin, rows = align(start[p] + skip), size[p] - skip
        if to_end and p == C:
            begin, rows = narrow_start, narrow
        part = zbuf.at[k, pl.ds(begin, rows), :]
        return pltpu.make_async_remote_copy(
            src_ref=part, dst_ref=part, send_sem=send_sem,
            recv_sem=z_recv.at[k, jnp.where(upper, p, 6 - p)], device_id=(l, peer), device_id_type=MESH)

    def first_copy(k, p, peer):
        return z_copy(k, p, first_send, peer, RAW)

    def unpack(slot, k, p):
        raw_copy(p, slot, b).wait_recv()
        rows = pl.ds(start[p], RAW)
        z = (raw[slot] - cols[rows, 0:1]) * cols[rows, 1:2]
        zbuf[k, rows, :] = z.astype(jnp.bfloat16)

    def send_out(k, p):
        return z_copy(k, p, out_send, out_nbr, 0, True)

    def send_in(k, p):
        return z_copy(k, p, in_send, in_nbr)

    def mate_copy(k, p, to_end=False):
        return z_copy(k, p, mate_send, mate, 0, to_end)

    def mate_own(k):
        part = zbuf.at[k]
        return pltpu.make_async_remote_copy(
            src_ref=part, dst_ref=part, send_sem=own_send, recv_sem=z_recv.at[k, 0],
            device_id=(l, mate), device_id_type=MESH)

    def share_copy(k, block, peer, way):
        part = shr.at[k, block, pl.ds(0, SR), :]
        return pltpu.make_async_remote_copy(
            src_ref=part, dst_ref=part, send_sem=shr_send,
            recv_sem=shr_recv.at[k, way], device_id=(peer, b), device_id_type=MESH)

    SR = up_to(share, 8)
    cut = up_to(share // 2, 16)

    def diag_copy(k, block, peer, way):
        rows = pl.ds(0, cut) if way == 0 else pl.ds(cut, SR - cut)
        part = shr.at[k, block, rows, :]
        return pltpu.make_async_remote_copy(
            src_ref=part, dst_ref=part, send_sem=diag_send,
            recv_sem=diag_recv.at[k // 2], device_id=(peer, b), device_id_type=MESH)

    first = align(jnp.minimum(b * share // 16 * 16, jnp.where(q == 0, size[D], R) - W))

    def extract_one(k):
        window = zbuf[k, pl.ds(first, W), :]
        row = lax.broadcasted_iota(jnp.int32, (SP, W), 0)
        hot = lax.broadcasted_iota(jnp.int32, (SP, W), 1) == row + (b * share - first)
        hot = jnp.where(hot & (row < share), 1.0, 0.0).astype(jnp.bfloat16)
        rows = lax.dot_general(hot, window, (((1,), (0,)), ((), ())),
                               preferred_element_type=jnp.float32)
        shr[k, l] = rows.astype(jnp.bfloat16)
        share_copy(k, l, lx, 0).start()
        share_copy(k, l, ly, 1).start()

    def extract(place):
        @pl.loop(0, 2)
        def _(core):
            extract_one(place * 2 + core)

    def pass_on(place):
        @pl.loop(0, 2)
        def _(core):
            k = place * 2 + core
            share_copy(k, lx, lx, 0).wait_recv()
            diag_copy(k, lx, ly, 0).start()
            share_copy(k, ly, ly, 1).wait_recv()
            diag_copy(k, ly, lx, 1).start()

    def wait_diag(place):
        part = shr.at[pl.ds(place * 2, 2), ld, pl.ds(0, SR), :]
        pltpu.make_async_remote_copy(
            src_ref=part, dst_ref=part, send_sem=diag_send, recv_sem=diag_recv.at[place],
            device_id=(l, b), device_id_type=MESH).wait_recv()

    def product(place, begin, width):
        part = None
        for core in range(2):
            k = place * 2 + core
            term = lax.dot_general(shr[k].reshape(L * SP, T), zbuf[k, begin:begin + width, :], NT,
                                   preferred_element_type=jnp.float32)
            part = term if part is None else part + term
        return part

    def add_sides(place):
        acc_lo[...] += product(place, 0, WS)
        acc_hi[...] += product(place, hi_lane, WS)

    def add_middle(place):
        acc_mid[...] += product(place, mid_lane, WM)

    def own(h):
        return H[h] * 2 + c

    def other(h):
        return H[h] * 2 + (1 - c)

    def take(h, p, onward=None, first=False, to_end=False):
        if first:
            first_copy(own(h), p, mate).wait_recv()
        else:
            mate_copy(own(h), p, to_end).wait_recv()
        if onward is not None:
            onward(own(h), p).start()
        mate_copy(own(h), p, to_end).start()

    def mate_take(h, pieces, to_end=False):
        for p in pieces:
            mate_copy(other(h), p, to_end).wait_recv()

    def take_end(h, p):
        take(h, p, to_end=True)

    def mate_take_end(h, pieces):
        mate_take(h, pieces, True)

    def tile_copy(side, j, core, block, slot):
        return pltpu.make_async_remote_copy(
            src_ref=tile_send.at[side, j, core, pl.ds(0, SR), :],
            dst_ref=tile_recv.at[block, pl.ds(0, SR), pl.ds(pl.multiple_of(slot * 128, 128), 128)],
            send_sem=t_send, recv_sem=t_recv.at[block],
            device_id=(j, 6 * side + core), device_id_type=MESH)

    def make_hot():
        for side, skip in ((0, jnp.where(b == 5, 0, pad)), (1, jnp.where(b == 2, pad, 0))):
            shift = (lax.broadcasted_iota(jnp.int32, (SR, 128), 0)
                     == lax.broadcasted_iota(jnp.int32, (SR, 128), 1) + skip)
            shift_ref[side] = jnp.where(shift, 1.0, 0.0).astype(jnp.bfloat16)
        row = lax.broadcasted_iota(jnp.int32, (512, WM), 0)
        slot = row // 128
        shifted = slot < jnp.where(upper, 1, 3)
        lane = half - mid_lane + slot * (share - 128) + row + jnp.where(shifted, pad, 0)
        hot = lax.broadcasted_iota(jnp.int32, (512, WM), 1) == lane
        place_ref[...] = jnp.where(hot, 1.0, 0.0).astype(jnp.bfloat16)
        for side, slot in ((0, 0), (3, 3)):
            @pl.when(q == side)
            def _():
                tile_recv[:, :, slot * 128:slot * 128 + 128] = jnp.zeros((L, SP, 128), jnp.bfloat16)

    def add_rows(j, place):
        rows = pl.ds(pl.multiple_of(j * SP, SP), SP)
        for acc, begin in ((acc_lo, 0), (acc_hi, hi_lane)):
            value = acc[rows, :]
            for core in range(2):
                k = place * 2 + core
                value = value + lax.dot_general(shr[k, j], zbuf[k, begin:begin + WS, :], NT,
                                                preferred_element_type=jnp.float32)
            acc[rows, :] = value

    def turn_tiles(j):
        rows = pl.ds(pl.multiple_of(j * SP, SP), SP)
        for side, acc in ((0, acc_lo), (1, acc_hi)):
            turned = lax.dot_general((acc[rows, :][:SR] / total).astype(jnp.bfloat16), shift_ref[side], TN,
                                     preferred_element_type=jnp.float32)
            for core in range(2):
                at = (WS - half if side else 0) + core * share
                tile_send[side, j, core, :share, :] = turned[at:at + share].astype(jnp.bfloat16)

    def tile_copies(j, act):
        for side, skipped in ((0, 2), (1, 5)):
            @pl.when(b != skipped)
            def _():
                for core in range(2):
                    act(tile_copy(side, j, core, l, b - 2))

    def start_tiles(j):
        tile_copies(j, lambda copy: copy.start())

    def wait_tile(block):
        part = tile_recv.at[block, pl.ds(0, SR), pl.ds(0, 384)]
        pltpu.make_async_remote_copy(
            src_ref=part, dst_ref=part, send_sem=t_send, recv_sem=t_recv.at[block],
            device_id=(l, b), device_id_type=MESH).wait_recv()

    normalise(start[D], size[D])

    @pl.when(inner)
    def _():
        first_copy(b, D, out_nbr).start()

    normalise(start[F], size[F])

    first_copy(b, F, in_nbr).start()
    normalise(low, high - low)

    @pl.when(inner)
    def _():
        for p in (M2, M1, C):
            z_copy(b, p, own_in, in_nbr).start()
        for p in (F, C, N2):
            z_copy(b, p, own_out, out_nbr, 0, True).start()

    @pl.when(outer)
    def _():
        for p in (M2, M1, C, D, N2, N1):
            z_copy(b, p, own_in, in_nbr).start()
    mate_own(b).start()
    extract_one(b)
    make_hot()
    mate_own(mate).wait_recv()
    extract_one(mate)

    @pl.when(inner)
    def _():
        unpack(0, own(1), D)
        unpack(1, own(3), F)
        take(1, D, send_out, True)
        take(3, F, send_in, True)
        pass_on(q)
        take(1, N2, send_out)
        take(3, M2, send_in)
        take(1, N1)
        take(3, M1, send_in)
        take(1, C, send_out)
        take(3, C, send_in)
        z_copy(b, D, own_in, in_nbr).start()
        mate_take(1, (D, N2, N1, C))
        extract(H[1])
        take(0, D, send_out)
        take(3, D, send_in)

    @pl.when(outer)
    def _():
        unpack(0, own(2), D)
        take(2, D, None, True)
        mate_take(2, (D,))
        extract(H[2])
        pass_on(q)
        take_end(2, F)
        take_end(2, C)
        take_end(2, N2)
        pass_on(H[2])
        take(1, D)
        mate_take(1, (D,))
        extract(H[1])
        mate_take_end(2, (F, C, N2))
    wait_diag(q)
    acc_lo[...] = product(q, 0, WS)
    acc_hi[...] = product(q, hi_lane, WS)
    acc_mid[...] = product(q, mid_lane, WM)

    second, third = jnp.where(inner, H[1], H[2]), jnp.where(inner, H[3], H[1])

    @pl.when(inner)
    def _():
        pass_on(H[1])
        take(0, N2, send_out)
        take(0, N1)
        take(0, C, send_out)
        mate_take(0, (D, N2, N1, C))
        extract(H[0])
        take(3, N2)
        take(3, N1)
        mate_take(3, (C, D, N2, N1))
        extract(H[3])
        take(1, F, send_out)
        mate_take(1, (F,))

    @pl.when(outer)
    def _():
        take_end(1, N2)
        take_end(1, C)
        pass_on(H[1])
    wait_diag(second)
    add_sides(second)

    @pl.when(outer)
    def _():
        take(0, D)
        mate_take(0, (D,))
        extract(H[0])
        take_end(0, N2)
        take_end(0, C)
        take_end(1, F)
        mate_take_end(1, (N2, C, F))
        wait_diag(H[1])
        add_sides(H[1])
    @pl.when(inner)
    def _():
        mate_take(3, (F, M1, M2))
        add_rows(l, H[3])
    pass_on(H[0])

    @pl.when(inner)
    def _():
        take(0, F, send_out)
        for p in (N1, N2):
            z_copy(b, p, own_in, in_nbr).start()
        mate_take(0, (F,))
        add_rows(l, H[0])
        pass_on(H[3])
        turn_tiles(l)
        start_tiles(l)

        @pl.loop(0, 2)
        def _(n):
            j = jnp.where(n == 0, lx, ly)
            add_rows(j, H[3])
            add_rows(j, H[0])
            turn_tiles(j)
            start_tiles(j)
        for p in (N1, N2):
            send_in(own(3), p).start()
        wait_diag(H[0])
        add_rows(ld, H[0])
        wait_diag(H[3])
        add_rows(ld, H[3])
        turn_tiles(ld)
        start_tiles(ld)
        for p in (M1, M2):
            take(1, p)
        mate_take(1, (M1, M2))
    add_middle(second)
    add_middle(third)

    def put(lanes, acc, begin=0):
        for j in range(L):
            part = acc[j * SP:j * SP + share, :][:, begin:begin + lanes.stop - lanes.start]
            o_ref[:, j, lanes] = part / total

    @pl.when(inner)
    def _():
        for p in (M1, M2):
            take(0, p)
        put(slice(0, mid_lane), acc_lo)
        put(slice(mid_lane + WM, R), acc_hi, mid_lane + WM - hi_lane)
        mate_take(0, (M1, M2))
        add_middle(H[0])
        put(slice(mid_lane, mid_lane + WM), acc_mid)

    lanes_lo = mid_lane, up_to(R // 2 + pad, 128)
    lanes_hi = (R // 2 - pad) // 128 * 128, mid_lane + WM

    @pl.when(outer)
    def _():
        mate_take_end(0, (N2, C))
        wait_diag(H[0])
        for end, acc, begin, (first_mid, last_mid) in ((0, acc_lo, 0, lanes_lo), (3, acc_hi, hi_lane, lanes_hi)):
            @pl.when(q == end)
            def _():
                acc[...] += product(H[0], begin, WS)
                inner_lanes = slice(first_mid - mid_lane, last_mid - mid_lane)
                acc_mid[:, inner_lanes] += product(H[0], first_mid, last_mid - first_mid)
                put(slice(first_mid, last_mid), acc_mid, first_mid - mid_lane)
                if end:
                    put(slice(last_mid, R), acc, last_mid - hi_lane)
                else:
                    put(slice(0, first_mid), acc)
        take(0, F)
        mate_take(0, (F,))
        for end, acc, begin in ((3, acc_lo, 0), (0, acc_hi, hi_lane)):
            @pl.when(q == end)
            def _():
                acc[...] += product(H[0], begin, WS)
                put(slice(begin, begin + WS), acc)
        place = lax.broadcasted_iota(jnp.int32, (share, WM), 1) + mid_lane
        low_first = half + pad + jnp.where(upper, 0, share)
        high_first = R // 2 + jnp.where(upper, 0, pad)
        inside = ((place >= low_first) & (place < low_first + jnp.where(upper, 256, 128))
                  | (place >= high_first) & (place < high_first + jnp.where(upper, 128, 256)))
        for d in (l, lx, ly, ld):
            wait_tile(d)
            placed = lax.dot_general(tile_recv[d], place_ref[...], (((1,), (0,)), ((), ())),
                                     preferred_element_type=jnp.float32)[:share]
            middle = pl.ds(mid_lane, WM)
            o_ref[:, d, middle] = jnp.where(inside, placed, o_ref[:, d, middle])

    all_stats.wait_send()
    mate_own(b).wait_send()

    def sent(part, sem):
        pltpu.make_async_remote_copy(
            src_ref=part, dst_ref=part, send_sem=sem, recv_sem=st_recv,
            device_id=(l, b), device_id_type=MESH).wait_send()

    @pl.when(inner)
    def _():
        sent(zbuf.at[0, pl.ds(0, size[F] + narrow + size[N2]), :], own_out)
        sent(zbuf.at[pl.ds(0, 2), pl.ds(0, size[D] - RAW), :], first_send)
        sent(raw, raw_send)
        sent(zbuf.at[pl.ds(0, 2), pl.ds(0, far), :], out_send)
        sent(zbuf.at[0], in_send)
        sent(zbuf.at[pl.ds(0, 3)], mate_send)
        for skipped in (True, False):
            @pl.when(((b == 2) | (b == 5)) == skipped)
            def _():
                sides = 1 if skipped else 2
                sent(tile_send.at[pl.ds(0, sides), :, :, pl.ds(0, SR), :], t_send)

    @pl.when(outer)
    def _():
        sent(zbuf.at[0, pl.ds(0, size[D] - RAW), :], first_send)
        sent(raw.at[0], raw_send)
        sent(zbuf.at[pl.ds(0, 3), pl.ds(0, far), :], mate_send)

    sent(zbuf.at[0, pl.ds(0, R - size[D]), :], own_in)
    sent(shr.at[pl.ds(0, L), :, pl.ds(0, SR), :], shr_send)
    sent(shr.at[pl.ds(0, B // L), :, pl.ds(0, SR), :], diag_send)


def line_call(L, B, series):
    R, T = series.shape
    share = R // B
    SP = up_to(share, 16)
    pad = share - 128
    high = (3 * 2 * share - pad) // 16 * 16
    WS = R - high
    mid_lane = WS // 128 * 128
    WM = up_to(R // 2 + pad + 256, 128) - mid_lane
    vmem = pl.BlockSpec(memory_space=pltpu.VMEM)
    dma = pltpu.SemaphoreType.DMA
    return pl.pallas_call(
        functools.partial(line_kernel, L, B),
        out_shape=jax.ShapeDtypeStruct((share, L, R), jnp.float32),
        in_specs=[pl.BlockSpec(memory_space=pltpu.HBM)],
        out_specs=vmem,
        scratch_shapes=[
            pltpu.VMEM((B, R, T), jnp.bfloat16),
            pltpu.VMEM((B, L, SP, T), jnp.bfloat16),
            pltpu.VMEM((L * SP, WS), jnp.float32),
            pltpu.VMEM((L * SP, WS), jnp.float32),
            pltpu.VMEM((L * SP, WM), jnp.float32),
            pltpu.VMEM((2, L, 2, SP, 128), jnp.bfloat16),
            pltpu.VMEM((L, SP, 512), jnp.bfloat16),
            pltpu.VMEM((2, up_to(share, 8), 128), jnp.bfloat16),
            pltpu.VMEM((512, WM), jnp.bfloat16),
            pltpu.VMEM((R, 128), jnp.float32),
            pltpu.VMEM((B, 2, R), jnp.float32),
            pltpu.VMEM((R, T), jnp.float32),
            pltpu.VMEM((2, (R - high) * 7 // 256 * 16, T), jnp.float32),
            dma((B, 7)), dma, dma, dma, dma, dma, dma, dma, dma((2,)), dma,
            dma((B, 2)), dma, dma((B // 2,)), dma, dma((L,)), dma,
            dma, dma, dma((R // largest_tile(R, 352),)),
        ],
        compiler_params=pltpu.CompilerParams(
            collective_id=0, has_side_effects=True, vmem_limit_bytes=34 * 1024 * 1024),
    )(pltpu.with_memory_space_constraint(series, pltpu.HBM)).transpose(1, 0, 2)


def solution(mesh):
    L, B = mesh.shape["loop"], mesh.shape["bulk"]

    def on_device(series):
        R, T = series.shape
        share = R // B
        if L == 4 and B == 8 and R % 16 == 0 and T % 128 == 0 and 128 <= share <= 144:
            return line_call(L, B, series)
        SP = up_to(share, 16)
        pieces = 3
        vmem = pl.BlockSpec(memory_space=pltpu.VMEM)
        dma = pltpu.SemaphoreType.DMA
        return pl.pallas_call(
            functools.partial(kernel, L, B, pieces),
            out_shape=jax.ShapeDtypeStruct((share, L, R), jnp.float32),
            in_specs=[pl.BlockSpec(memory_space=pltpu.HBM)],
            out_specs=vmem,
            scratch_shapes=[
                pltpu.VMEM((B, R, T), jnp.bfloat16),
                pltpu.VMEM((B, L, SP, T), jnp.bfloat16),
                pltpu.VMEM((L * SP, R), jnp.float32),
                pltpu.VMEM((R, 128), jnp.float32),
                pltpu.VMEM((B, 2, R), jnp.float32),
                pltpu.VMEM((R, T), jnp.float32),
                dma((B, pieces)), dma((B, pieces)), dma((B, pieces)), dma((B, pieces)),
                dma((B, L)), dma((B, L)), dma((B,)), dma((B,)), dma((R // largest_tile(R, 128),)),
            ],
            compiler_params=pltpu.CompilerParams(
                collective_id=0, has_side_effects=True, vmem_limit_bytes=26 * 1024 * 1024),
        )(pltpu.with_memory_space_constraint(series, pltpu.HBM)).transpose(1, 0, 2)

    return jax.shard_map(
        on_device, mesh=mesh, in_specs=(P("loop", "bulk"),),
        out_specs=P(None, "bulk", "loop"), check_vma=False)
```

```python
import functools
import jax
import jax.numpy as jnp
from jax import lax
from jax.experimental import pallas as pl
from jax.experimental.pallas import tpu as pltpu
from jax.sharding import PartitionSpec as P

epsilon = 1e-06
MESH = pl.DeviceIdType.MESH
NT = (((1,), (1,)), ((), ()))
TN = (((0,), (0,)), ((), ()))


def up_to(value, unit):
    return -(-value // unit) * unit


def largest_tile(rows, limit):
    return max(t for t in range(16, limit + 1, 16) if rows % t == 0)


def kernel(L, B, PIECES, x_hbm, o_ref, zbuf, shr, acc, cols, stats, x_ref,
           z_recv, up_send, down_send, mate_send, shr_recv, shr_send, st_recv, st_send, x_sem):
    R, T = x_hbm.shape
    total = T * B
    Q = B // 2
    share = R // B
    SP = shr.shape[2]
    W = min(up_to(share + 15, 16), R)
    bounds = [up_to(R * i // PIECES, 128) for i in range(PIECES)] + [R]
    tile = largest_tile(R, 128)
    l, b = lax.axis_index("loop"), lax.axis_index("bulk")
    q, c = b // 2, b % 2
    mate = q * 2 + (1 - c)

    barrier = pltpu.get_barrier_semaphore()
    for d in range(1, B):
        pl.semaphore_signal(barrier, inc=1, device_id=(l, lax.rem(b + d, B)), device_id_type=MESH)
    for d in range(1, L):
        pl.semaphore_signal(barrier, inc=1, device_id=(lax.rem(l + d, L), b), device_id_type=MESH)

    def load(i):
        rows = pl.ds(pl.multiple_of(i * tile, tile), tile)
        return pltpu.make_async_copy(x_hbm.at[rows, :], x_ref.at[rows, :], x_sem.at[i])

    @pl.loop(0, R // tile)
    def _(i):
        load(i).start()

    lane = lax.broadcasted_iota(jnp.int32, (tile, 128), 1)

    @pl.loop(0, R // tile)
    def _(i):
        rows = pl.ds(pl.multiple_of(i * tile, tile), tile)
        load(i).wait()
        v = x_ref[rows, :]
        mean = jnp.sum(v, axis=1, keepdims=True) / T
        dev = v - mean
        m2 = jnp.sum(dev * dev, axis=1, keepdims=True)
        cols[rows, :] = jnp.where(lane == 0, mean, jnp.where(lane == 1, m2, 0.0))

    pick = (lax.broadcasted_iota(jnp.int32, (8, 128), 0)
            == lax.broadcasted_iota(jnp.int32, (8, 128), 1)).astype(jnp.float32)
    line = lax.dot_general(pick, cols[...], NT, precision=lax.Precision.HIGHEST,
                           preferred_element_type=jnp.float32)
    stats[b] = line[:2]

    pl.semaphore_wait(barrier, B - 1 + L - 1)

    def stat_copy(source, peer):
        return pltpu.make_async_remote_copy(
            src_ref=stats.at[source], dst_ref=stats.at[source],
            send_sem=st_send.at[peer], recv_sem=st_recv.at[source],
            device_id=(l, peer), device_id_type=MESH)

    for d in range(1, B):
        stat_copy(b, lax.rem(b + d, B)).start()
    for d in range(1, B):
        other = lax.rem(b + d, B)
        stat_copy(other, other).wait_recv()

    mean = stats[0, 0:1]
    for k in range(1, B):
        mean = mean + stats[k, 0:1]
    mean = mean / B
    square = jnp.zeros_like(mean)
    for k in range(B):
        shift = stats[k, 0:1] - mean
        square = square + (stats[k, 1:2] + T * (shift * shift))
    scale = lax.rsqrt(square / total + epsilon)
    sub = lax.broadcasted_iota(jnp.int32, (8, R), 0)
    both = jnp.where(sub == 0, mean, jnp.where(sub == 1, scale, 0.0))
    cols[...] = lax.dot_general(both, pick, TN, precision=lax.Precision.HIGHEST,
                                preferred_element_type=jnp.float32)

    def normalise(piece):
        size = bounds[piece + 1] - bounds[piece]
        step = largest_tile(size, 128)

        @pl.loop(0, size // step)
        def _(i):
            rows = pl.ds(pl.multiple_of(bounds[piece] + i * step, 16), step)
            z = (x_ref[rows, :] - cols[rows, 0:1]) * cols[rows, 1:2]
            zbuf[b, rows, :] = z.astype(jnp.bfloat16)

    def piece_copy(k, piece, send_sem, peer):
        part = zbuf.at[k, pl.ds(bounds[piece], bounds[piece + 1] - bounds[piece]), :]
        return pltpu.make_async_remote_copy(
            src_ref=part, dst_ref=part, send_sem=send_sem.at[k, piece],
            recv_sem=z_recv.at[k, piece], device_id=(l, peer), device_id_type=MESH)

    def share_copy(k, block, peer):
        return pltpu.make_async_remote_copy(
            src_ref=shr.at[k, block], dst_ref=shr.at[k, block], send_sem=shr_send.at[k, peer],
            recv_sem=shr_recv.at[k, block], device_id=(peer, b), device_id_type=MESH)

    has_up, has_down = q + 1 < Q, q >= 1
    start = b * share
    first = pl.multiple_of(jnp.minimum(start // 16 * 16, R - W), 16)
    need_below = PIECES - 1 - sum((first >= x).astype(jnp.int32) for x in bounds[1:-1])
    need_above = sum((first + W > x).astype(jnp.int32) for x in bounds[1:-1])

    def extract(k):
        window = zbuf[k, pl.ds(first, W), :]
        hot = (lax.broadcasted_iota(jnp.int32, (SP, W), 1)
               == lax.broadcasted_iota(jnp.int32, (SP, W), 0) + (start - first))
        inside = lax.broadcasted_iota(jnp.int32, (SP, W), 0) < share
        hot = jnp.where(hot & inside, 1.0, 0.0).astype(jnp.bfloat16)
        rows = lax.dot_general(hot, window, (((1,), (0,)), ((), ())),
                               preferred_element_type=jnp.float32)
        shr[k, l] = rows.astype(jnp.bfloat16)
        for d in range(1, L):
            share_copy(k, l, lax.rem(l + d, L)).start()

    def wait_shares(place):
        for core in range(2):
            k = place * 2 + core
            for d in range(1, L):
                other = lax.rem(l + d, L)
                share_copy(k, other, other).wait_recv()

    def multiply(place):
        part = None
        wait_shares(place)
        for core in range(2):
            k = place * 2 + core
            a = shr[k].reshape(L * SP, T)
            term = lax.dot_general(a, zbuf[k], NT, preferred_element_type=jnp.float32)
            part = term if part is None else part + term
        acc[...] += part

    def multiply_step(s):
        @pl.loop(0, 2)
        def _(n):
            place = q - (1 - 2 * n) * s

            @pl.when((place >= 0) & (place < Q) & ((s > 0) | (n < 1)))
            def _():
                multiply(place)

    def send_own(up_first):
        done = set()

        def send(up, i):
            piece = PIECES - 1 - i if up else i
            if piece not in done:
                done.add(piece)
                normalise(piece)

            @pl.when(has_up if up else has_down)
            def _():
                if up:
                    piece_copy(b, piece, up_send, b + 2).start()
                else:
                    piece_copy(b, piece, down_send, b - 2).start()

        for i in range(PIECES):
            send(up_first, i)
            send(not up_first, i)

    @pl.when(q >= Q // 2)
    def _():
        send_own(True)

    @pl.when(q < Q // 2)
    def _():
        send_own(False)

    for i in range(PIECES):
        piece_copy(b, i, mate_send, mate).start()

    acc[...] = jnp.zeros_like(acc)
    extract(b)

    for i in range(PIECES):
        piece_copy(mate, i, mate_send, mate).wait_recv()

    extract(mate)

    def arrive(s, i, between=None):
        below, above = b - 2 * s, b + 2 * s
        from_below, from_above = q - s >= 0, q + s < Q
        down_piece = PIECES - 1 - i

        @pl.when(from_below)
        def _():
            piece_copy(below, down_piece, up_send, b).wait_recv()

            @pl.when(has_up)
            def _():
                piece_copy(below, down_piece, up_send, b + 2).start()
            piece_copy(below, down_piece, mate_send, mate).start()

        @pl.when(from_above)
        def _():
            piece_copy(above, i, down_send, b).wait_recv()

            @pl.when(has_down)
            def _():
                piece_copy(above, i, down_send, b - 2).start()
            piece_copy(above, i, mate_send, mate).start()

        @pl.when(from_below & (i == need_below))
        def _():
            extract(below)

        @pl.when(from_above & (i == need_above))
        def _():
            extract(above)

        if between is not None:
            between()

        @pl.when(from_below)
        def _():
            piece_copy(mate - 2 * s, down_piece, mate_send, mate).wait_recv()

            @pl.when(i == need_below)
            def _():
                extract(mate - 2 * s)

        @pl.when(from_above)
        def _():
            piece_copy(mate + 2 * s, i, mate_send, mate).wait_recv()

            @pl.when(i == need_above)
            def _():
                extract(mate + 2 * s)

        if i == 0:
            multiply_step(s - 1)

    def finish(piece, place):
        lo, hi = bounds[piece], bounds[piece + 1]
        part = acc[:, lo:hi]
        if place is not None:
            for core in range(2):
                k = place * 2 + core
                a = shr[k].reshape(L * SP, T)
                part = part + lax.dot_general(a, zbuf[k, lo:hi, :], NT,
                                              preferred_element_type=jnp.float32)
        part = part / total
        for j in range(L):
            o_ref[:, j, lo:hi] = part[j * SP:j * SP + share]

    @pl.loop(1, Q - 1)
    def _(s):
        for i in range(PIECES):
            arrive(s, i)

    def finish_ends(steps):
        for end, place in ((Q - 1, 0), (0, Q - 1)):
            @pl.when(q == end)
            def _():
                for i in steps:
                    finish(PIECES - 1 - i if end else i, place)

    def finish_early():
        for end, place in ((Q - 1, 0), (0, Q - 1)):
            @pl.when(q == end)
            def _():
                wait_shares(place)

        finish_ends(range(PIECES - 1))

    for i in range(PIECES):
        arrive(Q - 1, i, finish_early if i == PIECES - 1 else None)
    finish_ends([PIECES - 1])

    @pl.when((q > 0) & (q < Q - 1))
    def _():
        for i in range(PIECES):
            finish(i, None)

    for d in range(1, B):
        other = lax.rem(b + d, B)
        stat_copy(b, other).wait_send()

    @pl.loop(0, Q)
    def _(s):
        below, above = b - 2 * s, b + 2 * s
        from_below, from_above = q - s >= 0, q + s < Q

        for i in range(PIECES):
            @pl.when(from_below & has_up)
            def _():
                piece_copy(below, i, up_send, b + 2).wait_send()

            @pl.when(from_above & has_down)
            def _():
                piece_copy(above, i, down_send, b - 2).wait_send()

            @pl.when(from_below)
            def _():
                piece_copy(below, i, mate_send, mate).wait_send()

            @pl.when(from_above & (s > 0))
            def _():
                piece_copy(above, i, mate_send, mate).wait_send()

    @pl.loop(0, B)
    def _(k):
        for d in range(1, L):
            other = lax.rem(l + d, L)
            share_copy(k, l, other).wait_send()


F, M2, M1, C, N1, N2, D = range(7)


def line_kernel(L, B, x_hbm, o_ref, zbuf, shr, acc_lo, acc_hi, acc_mid, tile_send, tile_recv, shift_ref, place_ref,
                cols, stats, x_ref, raw,
                z_recv, out_send, in_send, mate_send, own_send, own_out, own_in, first_send, raw_recv, raw_send, shr_recv, shr_send, diag_recv, diag_send, t_recv, t_send,
                st_recv, st_send, x_sem):
    R, T = x_hbm.shape
    total = T * B
    share = R // B
    half = 2 * share
    SP = shr.shape[2]
    pad = share - 128
    W = min(up_to(share + 15, 16), R)
    low, high = R - (3 * half - pad) // 16 * 16, (3 * half - pad) // 16 * 16
    split = (3 * half - share) // 16 * 16
    edges = [0, low, R - split, (R // 2 - pad) // 16 * 16]
    edges = edges + [R - x for x in reversed(edges)]
    size = [edges[p + 1] - edges[p] for p in range(7)]
    narrow = size[C] // 2
    far = R - size[M2] - size[M1] - size[N1] - narrow
    tile = largest_tile(R, 352)
    RAW = raw.shape[1]
    WS = acc_lo.shape[1]
    hi_lane, mid_lane = R - WS, WS // 128 * 128
    WM = acc_mid.shape[1]
    l, b = lax.axis_index("loop"), lax.axis_index("bulk")
    q, c = b // 2, b % 2
    mate = q * 2 + (1 - c)
    upper = q >= 2
    inner = (q == 1) | (q == 2)
    outer = (q == 0) | (q == 3)
    step = jnp.where(upper, 1, -1)
    H = [jnp.where(upper, h, 3 - h) for h in range(4)]
    out_nbr, in_nbr = b + 2 * step, b - 2 * step
    lx, ly, ld = l + 1 - 2 * (l % 2), lax.rem(l + 2, 4), 3 - l

    def align(value, unit=16):
        return pl.multiple_of(value, unit)

    start = [align(jnp.where(upper, edges[p], edges[6 - p])) for p in range(7)]
    narrow_start = align(jnp.where(upper, R // 2 - narrow, R // 2))

    barrier = pltpu.get_barrier_semaphore()
    for d in range(1, B):
        pl.semaphore_signal(barrier, inc=1, device_id=(l, lax.rem(b + d, B)), device_id_type=MESH)
    for line in (lx, ly):
        pl.semaphore_signal(barrier, inc=1, device_id=(line, b), device_id_type=MESH)

    def load(i):
        rows = pl.ds(pl.multiple_of(i * tile, tile), tile)
        return pltpu.make_async_copy(x_hbm.at[rows, :], x_ref.at[rows, :], x_sem.at[i])

    @pl.loop(0, R // tile)
    def _(i):
        load(i).start()

    lane = lax.broadcasted_iota(jnp.int32, (tile, 128), 1)

    @pl.loop(0, R // tile)
    def _(i):
        rows = pl.ds(pl.multiple_of(i * tile, tile), tile)
        load(i).wait()
        v = x_ref[rows, :]
        mean = jnp.sum(v, axis=1, keepdims=True) / T
        dev = v - mean
        m2 = jnp.sum(dev * dev, axis=1, keepdims=True)
        cols[rows, :] = jnp.where(lane == 0, mean, jnp.where(lane == 1, m2, 0.0))

    pick = (lax.broadcasted_iota(jnp.int32, (8, 128), 0)
            == lax.broadcasted_iota(jnp.int32, (8, 128), 1)).astype(jnp.bfloat16)

    def in_parts(x):
        top = x.astype(jnp.bfloat16)
        rest = x - top.astype(jnp.float32)
        middle = rest.astype(jnp.bfloat16)
        return top, middle, (rest - middle.astype(jnp.float32)).astype(jnp.bfloat16)

    def exact_dot(parts, dot):
        top, middle, low_part = [dot(part) for part in parts]
        return top + middle + low_part

    line = exact_dot(in_parts(cols[...]), lambda part: lax.dot_general(
        pick, part, NT, preferred_element_type=jnp.float32))
    stats[b] = line[:2]

    pl.semaphore_wait(barrier, B - 1 + 2)

    def stat_copy(source, peer):
        return pltpu.make_async_remote_copy(
            src_ref=stats.at[source], dst_ref=stats.at[source],
            send_sem=st_send, recv_sem=st_recv,
            device_id=(l, peer), device_id_type=MESH)

    for d in range(1, B):
        stat_copy(b, lax.rem(b + d, B)).start()
    def raw_copy(p, slot, peer):
        return pltpu.make_async_remote_copy(
            src_ref=x_ref.at[pl.ds(start[p], RAW), :], dst_ref=raw.at[slot], send_sem=raw_send,
            recv_sem=raw_recv.at[slot], device_id=(l, peer), device_id_type=MESH)

    @pl.when(inner)
    def _():
        raw_copy(D, 0, out_nbr).start()
        raw_copy(F, 0, in_nbr).start()

    @pl.when(outer)
    def _():
        raw_copy(F, 1, in_nbr).start()

    gathered = stats.at[pl.ds(0, B - 1)]
    all_stats = pltpu.make_async_remote_copy(
        src_ref=gathered, dst_ref=gathered, send_sem=st_send, recv_sem=st_recv,
        device_id=(l, b), device_id_type=MESH)
    all_stats.wait_recv()

    mean = stats[0, 0:1]
    for k in range(1, B):
        mean = mean + stats[k, 0:1]
    mean = mean / B
    square = jnp.zeros_like(mean)
    for k in range(B):
        shift = stats[k, 0:1] - mean
        square = square + (stats[k, 1:2] + T * (shift * shift))
    scale = lax.rsqrt(square / total + epsilon)
    sub = lax.broadcasted_iota(jnp.int32, (8, R), 0)
    both = jnp.where(sub == 0, mean, jnp.where(sub == 1, scale, 0.0))
    cols[...] = exact_dot(in_parts(both), lambda part: lax.dot_general(
        part, pick, TN, preferred_element_type=jnp.float32))

    def normalise(begin, count):
        unit = count if count <= 288 else largest_tile(count, 128)

        def chunk(i):
            rows = pl.ds(pl.multiple_of(begin + i * unit, 16), unit)
            z = (x_ref[rows, :] - cols[rows, 0:1]) * cols[rows, 1:2]
            zbuf[b, rows, :] = z.astype(jnp.bfloat16)

        if unit == count:
            chunk(0)
        else:
            pl.loop(0, count // unit)(chunk)

    def z_copy(k, p, send_sem, peer, skip=0, to_end=False):
        begin, rows = align(start[p] + skip), size[p] - skip
        if to_end and p == C:
            begin, rows = narrow_start, narrow
        part = zbuf.at[k, pl.ds(begin, rows), :]
        return pltpu.make_async_remote_copy(
            src_ref=part, dst_ref=part, send_sem=send_sem,
            recv_sem=z_recv.at[k, jnp.where(upper, p, 6 - p)], device_id=(l, peer), device_id_type=MESH)

    def first_copy(k, p, peer):
        return z_copy(k, p, first_send, peer, RAW)

    def unpack(slot, k, p):
        raw_copy(p, slot, b).wait_recv()
        rows = pl.ds(start[p], RAW)
        z = (raw[slot] - cols[rows, 0:1]) * cols[rows, 1:2]
        zbuf[k, rows, :] = z.astype(jnp.bfloat16)

    def send_out(k, p):
        return z_copy(k, p, out_send, out_nbr, 0, True)

    def send_in(k, p):
        return z_copy(k, p, in_send, in_nbr)

    def mate_copy(k, p, to_end=False):
        return z_copy(k, p, mate_send, mate, 0, to_end)

    def mate_own(k):
        part = zbuf.at[k]
        return pltpu.make_async_remote_copy(
            src_ref=part, dst_ref=part, send_sem=own_send, recv_sem=z_recv.at[k, 0],
            device_id=(l, mate), device_id_type=MESH)

    def share_copy(k, block, peer, way):
        part = shr.at[k, block, pl.ds(0, SR), :]
        return pltpu.make_async_remote_copy(
            src_ref=part, dst_ref=part, send_sem=shr_send,
            recv_sem=shr_recv.at[k, way], device_id=(peer, b), device_id_type=MESH)

    SR = up_to(share, 8)
    cut = up_to(share // 2, 16)

    def diag_copy(k, block, peer, way):
        rows = pl.ds(0, cut) if way == 0 else pl.ds(cut, SR - cut)
        part = shr.at[k, block, rows, :]
        return pltpu.make_async_remote_copy(
            src_ref=part, dst_ref=part, send_sem=diag_send,
            recv_sem=diag_recv.at[k // 2], device_id=(peer, b), device_id_type=MESH)

    first = align(jnp.minimum(b * share // 16 * 16, jnp.where(q == 0, size[D], R) - W))

    def extract_one(k):
        window = zbuf[k, pl.ds(first, W), :]
        row = lax.broadcasted_iota(jnp.int32, (SP, W), 0)
        hot = lax.broadcasted_iota(jnp.int32, (SP, W), 1) == row + (b * share - first)
        hot = jnp.where(hot & (row < share), 1.0, 0.0).astype(jnp.bfloat16)
        rows = lax.dot_general(hot, window, (((1,), (0,)), ((), ())),
                               preferred_element_type=jnp.float32)
        shr[k, l] = rows.astype(jnp.bfloat16)
        share_copy(k, l, lx, 0).start()
        share_copy(k, l, ly, 1).start()

    def extract(place):
        @pl.loop(0, 2)
        def _(core):
            extract_one(place * 2 + core)

    def pass_on(place):
        @pl.loop(0, 2)
        def _(core):
            k = place * 2 + core
            share_copy(k, lx, lx, 0).wait_recv()
            diag_copy(k, lx, ly, 0).start()
            share_copy(k, ly, ly, 1).wait_recv()
            diag_copy(k, ly, lx, 1).start()

    def wait_diag(place):
        part = shr.at[pl.ds(place * 2, 2), ld, pl.ds(0, SR), :]
        pltpu.make_async_remote_copy(
            src_ref=part, dst_ref=part, send_sem=diag_send, recv_sem=diag_recv.at[place],
            device_id=(l, b), device_id_type=MESH).wait_recv()

    def product(place, begin, width):
        part = None
        for core in range(2):
            k = place * 2 + core
            term = lax.dot_general(shr[k].reshape(L * SP, T), zbuf[k, begin:begin + width, :], NT,
                                   preferred_element_type=jnp.float32)
            part = term if part is None else part + term
        return part

    def add_sides(place):
        acc_lo[...] += product(place, 0, WS)
        acc_hi[...] += product(place, hi_lane, WS)

    def add_middle(place):
        acc_mid[...] += product(place, mid_lane, WM)

    def own(h):
        return H[h] * 2 + c

    def other(h):
        return H[h] * 2 + (1 - c)

    def take(h, p, onward=None, first=False, to_end=False):
        if first:
            first_copy(own(h), p, mate).wait_recv()
        else:
            mate_copy(own(h), p, to_end).wait_recv()
        if onward is not None:
            onward(own(h), p).start()
        mate_copy(own(h), p, to_end).start()

    def mate_take(h, pieces, to_end=False):
        for p in pieces:
            mate_copy(other(h), p, to_end).wait_recv()

    def take_end(h, p):
        take(h, p, to_end=True)

    def mate_take_end(h, pieces):
        mate_take(h, pieces, True)

    def tile_copy(side, j, core, block, slot):
        return pltpu.make_async_remote_copy(
            src_ref=tile_send.at[side, j, core, pl.ds(0, SR), :],
            dst_ref=tile_recv.at[block, pl.ds(0, SR), pl.ds(pl.multiple_of(slot * 128, 128), 128)],
            send_sem=t_send, recv_sem=t_recv.at[block],
            device_id=(j, 6 * side + core), device_id_type=MESH)

    def make_hot():
        for side, skip in ((0, jnp.where(b == 5, 0, pad)), (1, jnp.where(b == 2, pad, 0))):
            shift = (lax.broadcasted_iota(jnp.int32, (SR, 128), 0)
                     == lax.broadcasted_iota(jnp.int32, (SR, 128), 1) + skip)
            shift_ref[side] = jnp.where(shift, 1.0, 0.0).astype(jnp.bfloat16)
        row = lax.broadcasted_iota(jnp.int32, (512, WM), 0)
        slot = row // 128
        shifted = slot < jnp.where(upper, 1, 3)
        lane = half - mid_lane + slot * (share - 128) + row + jnp.where(shifted, pad, 0)
        hot = lax.broadcasted_iota(jnp.int32, (512, WM), 1) == lane
        place_ref[...] = jnp.where(hot, 1.0, 0.0).astype(jnp.bfloat16)
        for side, slot in ((0, 0), (3, 3)):
            @pl.when(q == side)
            def _():
                tile_recv[:, :, slot * 128:slot * 128 + 128] = jnp.zeros((L, SP, 128), jnp.bfloat16)

    def add_rows(j, place):
        rows = pl.ds(pl.multiple_of(j * SP, SP), SP)
        for acc, begin in ((acc_lo, 0), (acc_hi, hi_lane)):
            value = acc[rows, :]
            for core in range(2):
                k = place * 2 + core
                value = value + lax.dot_general(shr[k, j], zbuf[k, begin:begin + WS, :], NT,
                                                preferred_element_type=jnp.float32)
            acc[rows, :] = value

    def turn_tiles(j):
        rows = pl.ds(pl.multiple_of(j * SP, SP), SP)
        for side, acc in ((0, acc_lo), (1, acc_hi)):
            turned = lax.dot_general((acc[rows, :][:SR] / total).astype(jnp.bfloat16), shift_ref[side], TN,
                                     preferred_element_type=jnp.float32)
            for core in range(2):
                at = (WS - half if side else 0) + core * share
                tile_send[side, j, core, :share, :] = turned[at:at + share].astype(jnp.bfloat16)

    def tile_copies(j, act):
        for side, skipped in ((0, 2), (1, 5)):
            @pl.when(b != skipped)
            def _():
                for core in range(2):
                    act(tile_copy(side, j, core, l, b - 2))

    def start_tiles(j):
        tile_copies(j, lambda copy: copy.start())

    def wait_tile(block):
        part = tile_recv.at[block, pl.ds(0, SR), pl.ds(0, 384)]
        pltpu.make_async_remote_copy(
            src_ref=part, dst_ref=part, send_sem=t_send, recv_sem=t_recv.at[block],
            device_id=(l, b), device_id_type=MESH).wait_recv()

    normalise(start[D], size[D])

    @pl.when(inner)
    def _():
        first_copy(b, D, out_nbr).start()

    normalise(start[F], size[F])

    first_copy(b, F, in_nbr).start()
    normalise(low, high - low)

    @pl.when(inner)
    def _():
        for p in (M2, M1, C):
            z_copy(b, p, own_in, in_nbr).start()
        for p in (F, C, N2):
            z_copy(b, p, own_out, out_nbr, 0, True).start()

    @pl.when(outer)
    def _():
        for p in (M2, M1, C, D, N2, N1):
            z_copy(b, p, own_in, in_nbr).start()
    mate_own(b).start()
    extract_one(b)
    make_hot()
    mate_own(mate).wait_recv()
    extract_one(mate)

    @pl.when(inner)
    def _():
        unpack(0, own(1), D)
        unpack(1, own(3), F)
        take(1, D, send_out, True)
        take(3, F, send_in, True)
        pass_on(q)
        take(1, N2, send_out)
        take(3, M2, send_in)
        take(1, N1)
        take(3, M1, send_in)
        take(1, C, send_out)
        take(3, C, send_in)
        z_copy(b, D, own_in, in_nbr).start()
        mate_take(1, (D, N2, N1, C))
        extract(H[1])
        take(0, D, send_out)
        take(3, D, send_in)

    @pl.when(outer)
    def _():
        unpack(0, own(2), D)
        take(2, D, None, True)
        mate_take(2, (D,))
        extract(H[2])
        pass_on(q)
        take_end(2, F)
        take_end(2, C)
        take_end(2, N2)
        pass_on(H[2])
        take(1, D)
        mate_take(1, (D,))
        extract(H[1])
        mate_take_end(2, (F, C, N2))
    wait_diag(q)
    acc_lo[...] = product(q, 0, WS)
    acc_hi[...] = product(q, hi_lane, WS)
    acc_mid[...] = product(q, mid_lane, WM)

    second, third = jnp.where(inner, H[1], H[2]), jnp.where(inner, H[3], H[1])

    @pl.when(inner)
    def _():
        pass_on(H[1])
        take(0, N2, send_out)
        take(0, N1)
        take(0, C, send_out)
        mate_take(0, (D, N2, N1, C))
        extract(H[0])
        take(3, N2)
        take(3, N1)
        mate_take(3, (C, D, N2, N1))
        extract(H[3])
        take(1, F, send_out)
        mate_take(1, (F,))

    @pl.when(outer)
    def _():
        take_end(1, N2)
        take_end(1, C)
        pass_on(H[1])
    wait_diag(second)
    add_sides(second)

    @pl.when(outer)
    def _():
        take(0, D)
        mate_take(0, (D,))
        extract(H[0])
        take_end(0, N2)
        take_end(0, C)
        take_end(1, F)
        mate_take_end(1, (N2, C, F))
        wait_diag(H[1])
        add_sides(H[1])
    @pl.when(inner)
    def _():
        mate_take(3, (F, M1, M2))
        add_rows(l, H[3])
    pass_on(H[0])

    @pl.when(inner)
    def _():
        take(0, F, send_out)
        for p in (N1, N2):
            z_copy(b, p, own_in, in_nbr).start()
        mate_take(0, (F,))
        add_rows(l, H[0])
        turn_tiles(l)
        start_tiles(l)

        @pl.loop(0, 2)
        def _(n):
            add_rows(jnp.where(n == 0, lx, ly), H[0])
        pass_on(H[3])

        @pl.loop(0, 2)
        def _(n):
            j = jnp.where(n == 0, lx, ly)
            add_rows(j, H[3])
            turn_tiles(j)
            start_tiles(j)
        for p in (N1, N2):
            send_in(own(3), p).start()
        wait_diag(H[0])
        add_rows(ld, H[0])
        wait_diag(H[3])
        add_rows(ld, H[3])
        turn_tiles(ld)
        start_tiles(ld)
        for p in (M1, M2):
            take(1, p)
        mate_take(1, (M1, M2))
    add_middle(second)
    add_middle(third)

    def put(lanes, acc, begin=0):
        for j in range(L):
            part = acc[j * SP:j * SP + share, :][:, begin:begin + lanes.stop - lanes.start]
            o_ref[:, j, lanes] = part / total

    @pl.when(inner)
    def _():
        for p in (M1, M2):
            take(0, p)
        put(slice(0, mid_lane), acc_lo)
        put(slice(mid_lane + WM, R), acc_hi, mid_lane + WM - hi_lane)
        mate_take(0, (M1, M2))
        add_middle(H[0])
        put(slice(mid_lane, mid_lane + WM), acc_mid)

    lanes_lo = mid_lane, up_to(R // 2 + pad, 128)
    lanes_hi = (R // 2 - pad) // 128 * 128, mid_lane + WM

    @pl.when(outer)
    def _():
        mate_take_end(0, (N2, C))
        wait_diag(H[0])
        for end, acc, begin, (first_mid, last_mid) in ((0, acc_lo, 0, lanes_lo), (3, acc_hi, hi_lane, lanes_hi)):
            @pl.when(q == end)
            def _():
                acc[...] += product(H[0], begin, WS)
                inner_lanes = slice(first_mid - mid_lane, last_mid - mid_lane)
                acc_mid[:, inner_lanes] += product(H[0], first_mid, last_mid - first_mid)
                put(slice(first_mid, last_mid), acc_mid, first_mid - mid_lane)
                if end:
                    put(slice(last_mid, R), acc, last_mid - hi_lane)
                else:
                    put(slice(0, first_mid), acc)
        take(0, F)
        mate_take(0, (F,))
        for end, acc, begin in ((3, acc_lo, 0), (0, acc_hi, hi_lane)):
            @pl.when(q == end)
            def _():
                acc[...] += product(H[0], begin, WS)
                put(slice(begin, begin + WS), acc)
        place = lax.broadcasted_iota(jnp.int32, (share, WM), 1) + mid_lane
        low_first = half + pad + jnp.where(upper, 0, share)
        high_first = R // 2 + jnp.where(upper, 0, pad)
        inside = ((place >= low_first) & (place < low_first + jnp.where(upper, 256, 128))
                  | (place >= high_first) & (place < high_first + jnp.where(upper, 128, 256)))
        for d in (l, lx, ly, ld):
            wait_tile(d)
            placed = lax.dot_general(tile_recv[d], place_ref[...], (((1,), (0,)), ((), ())),
                                     preferred_element_type=jnp.float32)[:share]
            middle = pl.ds(mid_lane, WM)
            o_ref[:, d, middle] = jnp.where(inside, placed, o_ref[:, d, middle])

    all_stats.wait_send()
    mate_own(b).wait_send()

    def sent(part, sem):
        pltpu.make_async_remote_copy(
            src_ref=part, dst_ref=part, send_sem=sem, recv_sem=st_recv,
            device_id=(l, b), device_id_type=MESH).wait_send()

    @pl.when(inner)
    def _():
        sent(zbuf.at[0, pl.ds(0, size[F] + narrow + size[N2]), :], own_out)
        sent(zbuf.at[pl.ds(0, 2), pl.ds(0, size[D] - RAW), :], first_send)
        sent(raw, raw_send)
        sent(zbuf.at[pl.ds(0, 2), pl.ds(0, far), :], out_send)
        sent(zbuf.at[0], in_send)
        sent(zbuf.at[pl.ds(0, 3)], mate_send)
        for skipped in (True, False):
            @pl.when(((b == 2) | (b == 5)) == skipped)
            def _():
                sides = 1 if skipped else 2
                sent(tile_send.at[pl.ds(0, sides), :, :, pl.ds(0, SR), :], t_send)

    @pl.when(outer)
    def _():
        sent(zbuf.at[0, pl.ds(0, size[D] - RAW), :], first_send)
        sent(raw.at[0], raw_send)
        sent(zbuf.at[pl.ds(0, 3), pl.ds(0, far), :], mate_send)

    sent(zbuf.at[0, pl.ds(0, R - size[D]), :], own_in)
    sent(shr.at[pl.ds(0, L), :, pl.ds(0, SR), :], shr_send)
    sent(shr.at[pl.ds(0, B // L), :, pl.ds(0, SR), :], diag_send)


def line_call(L, B, series):
    R, T = series.shape
    share = R // B
    SP = up_to(share, 16)
    pad = share - 128
    high = (3 * 2 * share - pad) // 16 * 16
    WS = R - high
    mid_lane = WS // 128 * 128
    WM = up_to(R // 2 + pad + 256, 128) - mid_lane
    vmem = pl.BlockSpec(memory_space=pltpu.VMEM)
    dma = pltpu.SemaphoreType.DMA
    return pl.pallas_call(
        functools.partial(line_kernel, L, B),
        out_shape=jax.ShapeDtypeStruct((share, L, R), jnp.float32),
        in_specs=[pl.BlockSpec(memory_space=pltpu.HBM)],
        out_specs=vmem,
        scratch_shapes=[
            pltpu.VMEM((B, R, T), jnp.bfloat16),
            pltpu.VMEM((B, L, SP, T), jnp.bfloat16),
            pltpu.VMEM((L * SP, WS), jnp.float32),
            pltpu.VMEM((L * SP, WS), jnp.float32),
            pltpu.VMEM((L * SP, WM), jnp.float32),
            pltpu.VMEM((2, L, 2, SP, 128), jnp.bfloat16),
            pltpu.VMEM((L, SP, 512), jnp.bfloat16),
            pltpu.VMEM((2, up_to(share, 8), 128), jnp.bfloat16),
            pltpu.VMEM((512, WM), jnp.bfloat16),
            pltpu.VMEM((R, 128), jnp.float32),
            pltpu.VMEM((B, 2, R), jnp.float32),
            pltpu.VMEM((R, T), jnp.float32),
            pltpu.VMEM((2, (R - high) * 7 // 256 * 16, T), jnp.float32),
            dma((B, 7)), dma, dma, dma, dma, dma, dma, dma, dma((2,)), dma,
            dma((B, 2)), dma, dma((B // 2,)), dma, dma((L,)), dma,
            dma, dma, dma((R // largest_tile(R, 352),)),
        ],
        compiler_params=pltpu.CompilerParams(
            collective_id=0, has_side_effects=True, vmem_limit_bytes=34 * 1024 * 1024),
    )(pltpu.with_memory_space_constraint(series, pltpu.HBM)).transpose(1, 0, 2)


def solution(mesh):
    L, B = mesh.shape["loop"], mesh.shape["bulk"]

    def on_device(series):
        R, T = series.shape
        share = R // B
        if L == 4 and B == 8 and R % 16 == 0 and T % 128 == 0 and 128 <= share <= 144:
            return line_call(L, B, series)
        SP = up_to(share, 16)
        pieces = 3
        vmem = pl.BlockSpec(memory_space=pltpu.VMEM)
        dma = pltpu.SemaphoreType.DMA
        return pl.pallas_call(
            functools.partial(kernel, L, B, pieces),
            out_shape=jax.ShapeDtypeStruct((share, L, R), jnp.float32),
            in_specs=[pl.BlockSpec(memory_space=pltpu.HBM)],
            out_specs=vmem,
            scratch_shapes=[
                pltpu.VMEM((B, R, T), jnp.bfloat16),
                pltpu.VMEM((B, L, SP, T), jnp.bfloat16),
                pltpu.VMEM((L * SP, R), jnp.float32),
                pltpu.VMEM((R, 128), jnp.float32),
                pltpu.VMEM((B, 2, R), jnp.float32),
                pltpu.VMEM((R, T), jnp.float32),
                dma((B, pieces)), dma((B, pieces)), dma((B, pieces)), dma((B, pieces)),
                dma((B, L)), dma((B, L)), dma((B,)), dma((B,)), dma((R // largest_tile(R, 128),)),
            ],
            compiler_params=pltpu.CompilerParams(
                collective_id=0, has_side_effects=True, vmem_limit_bytes=26 * 1024 * 1024),
        )(pltpu.with_memory_space_constraint(series, pltpu.HBM)).transpose(1, 0, 2)

    return jax.shard_map(
        on_device, mesh=mesh, in_specs=(P("loop", "bulk"),),
        out_specs=P(None, "bulk", "loop"), check_vma=False)
```

```python
import functools
import jax
import jax.numpy as jnp
from jax import lax
from jax.experimental import pallas as pl
from jax.experimental.pallas import tpu as pltpu
from jax.sharding import PartitionSpec as P

epsilon = 1e-06
MESH = pl.DeviceIdType.MESH
NT = (((1,), (1,)), ((), ()))
TN = (((0,), (0,)), ((), ()))


def up_to(value, unit):
    return -(-value // unit) * unit


def largest_tile(rows, limit):
    return max(t for t in range(16, limit + 1, 16) if rows % t == 0)


def kernel(L, B, PIECES, x_hbm, o_ref, zbuf, shr, acc, cols, stats, x_ref,
           z_recv, up_send, down_send, mate_send, shr_recv, shr_send, st_recv, st_send, x_sem):
    R, T = x_hbm.shape
    total = T * B
    Q = B // 2
    share = R // B
    SP = shr.shape[2]
    W = min(up_to(share + 15, 16), R)
    bounds = [up_to(R * i // PIECES, 128) for i in range(PIECES)] + [R]
    tile = largest_tile(R, 128)
    l, b = lax.axis_index("loop"), lax.axis_index("bulk")
    q, c = b // 2, b % 2
    mate = q * 2 + (1 - c)

    barrier = pltpu.get_barrier_semaphore()
    for d in range(1, B):
        pl.semaphore_signal(barrier, inc=1, device_id=(l, lax.rem(b + d, B)), device_id_type=MESH)
    for d in range(1, L):
        pl.semaphore_signal(barrier, inc=1, device_id=(lax.rem(l + d, L), b), device_id_type=MESH)

    def load(i):
        rows = pl.ds(pl.multiple_of(i * tile, tile), tile)
        return pltpu.make_async_copy(x_hbm.at[rows, :], x_ref.at[rows, :], x_sem.at[i])

    @pl.loop(0, R // tile)
    def _(i):
        load(i).start()

    lane = lax.broadcasted_iota(jnp.int32, (tile, 128), 1)

    @pl.loop(0, R // tile)
    def _(i):
        rows = pl.ds(pl.multiple_of(i * tile, tile), tile)
        load(i).wait()
        v = x_ref[rows, :]
        mean = jnp.sum(v, axis=1, keepdims=True) / T
        dev = v - mean
        m2 = jnp.sum(dev * dev, axis=1, keepdims=True)
        cols[rows, :] = jnp.where(lane == 0, mean, jnp.where(lane == 1, m2, 0.0))

    pick = (lax.broadcasted_iota(jnp.int32, (8, 128), 0)
            == lax.broadcasted_iota(jnp.int32, (8, 128), 1)).astype(jnp.float32)
    line = lax.dot_general(pick, cols[...], NT, precision=lax.Precision.HIGHEST,
                           preferred_element_type=jnp.float32)
    stats[b] = line[:2]

    pl.semaphore_wait(barrier, B - 1 + L - 1)

    def stat_copy(source, peer):
        return pltpu.make_async_remote_copy(
            src_ref=stats.at[source], dst_ref=stats.at[source],
            send_sem=st_send.at[peer], recv_sem=st_recv.at[source],
            device_id=(l, peer), device_id_type=MESH)

    for d in range(1, B):
        stat_copy(b, lax.rem(b + d, B)).start()
    for d in range(1, B):
        other = lax.rem(b + d, B)
        stat_copy(other, other).wait_recv()

    mean = stats[0, 0:1]
    for k in range(1, B):
        mean = mean + stats[k, 0:1]
    mean = mean / B
    square = jnp.zeros_like(mean)
    for k in range(B):
        shift = stats[k, 0:1] - mean
        square = square + (stats[k, 1:2] + T * (shift * shift))
    scale = lax.rsqrt(square / total + epsilon)
    sub = lax.broadcasted_iota(jnp.int32, (8, R), 0)
    both = jnp.where(sub == 0, mean, jnp.where(sub == 1, scale, 0.0))
    cols[...] = lax.dot_general(both, pick, TN, precision=lax.Precision.HIGHEST,
                                preferred_element_type=jnp.float32)

    def normalise(piece):
        size = bounds[piece + 1] - bounds[piece]
        step = largest_tile(size, 128)

        @pl.loop(0, size // step)
        def _(i):
            rows = pl.ds(pl.multiple_of(bounds[piece] + i * step, 16), step)
            z = (x_ref[rows, :] - cols[rows, 0:1]) * cols[rows, 1:2]
            zbuf[b, rows, :] = z.astype(jnp.bfloat16)

    def piece_copy(k, piece, send_sem, peer):
        part = zbuf.at[k, pl.ds(bounds[piece], bounds[piece + 1] - bounds[piece]), :]
        return pltpu.make_async_remote_copy(
            src_ref=part, dst_ref=part, send_sem=send_sem.at[k, piece],
            recv_sem=z_recv.at[k, piece], device_id=(l, peer), device_id_type=MESH)

    def share_copy(k, block, peer):
        return pltpu.make_async_remote_copy(
            src_ref=shr.at[k, block], dst_ref=shr.at[k, block], send_sem=shr_send.at[k, peer],
            recv_sem=shr_recv.at[k, block], device_id=(peer, b), device_id_type=MESH)

    has_up, has_down = q + 1 < Q, q >= 1
    start = b * share
    first = pl.multiple_of(jnp.minimum(start // 16 * 16, R - W), 16)
    need_below = PIECES - 1 - sum((first >= x).astype(jnp.int32) for x in bounds[1:-1])
    need_above = sum((first + W > x).astype(jnp.int32) for x in bounds[1:-1])

    def extract(k):
        window = zbuf[k, pl.ds(first, W), :]
        hot = (lax.broadcasted_iota(jnp.int32, (SP, W), 1)
               == lax.broadcasted_iota(jnp.int32, (SP, W), 0) + (start - first))
        inside = lax.broadcasted_iota(jnp.int32, (SP, W), 0) < share
        hot = jnp.where(hot & inside, 1.0, 0.0).astype(jnp.bfloat16)
        rows = lax.dot_general(hot, window, (((1,), (0,)), ((), ())),
                               preferred_element_type=jnp.float32)
        shr[k, l] = rows.astype(jnp.bfloat16)
        for d in range(1, L):
            share_copy(k, l, lax.rem(l + d, L)).start()

    def wait_shares(place):
        for core in range(2):
            k = place * 2 + core
            for d in range(1, L):
                other = lax.rem(l + d, L)
                share_copy(k, other, other).wait_recv()

    def multiply(place):
        part = None
        wait_shares(place)
        for core in range(2):
            k = place * 2 + core
            a = shr[k].reshape(L * SP, T)
            term = lax.dot_general(a, zbuf[k], NT, preferred_element_type=jnp.float32)
            part = term if part is None else part + term
        acc[...] += part

    def multiply_step(s):
        @pl.loop(0, 2)
        def _(n):
            place = q - (1 - 2 * n) * s

            @pl.when((place >= 0) & (place < Q) & ((s > 0) | (n < 1)))
            def _():
                multiply(place)

    def send_own(up_first):
        done = set()

        def send(up, i):
            piece = PIECES - 1 - i if up else i
            if piece not in done:
                done.add(piece)
                normalise(piece)

            @pl.when(has_up if up else has_down)
            def _():
                if up:
                    piece_copy(b, piece, up_send, b + 2).start()
                else:
                    piece_copy(b, piece, down_send, b - 2).start()

        for i in range(PIECES):
            send(up_first, i)
            send(not up_first, i)

    @pl.when(q >= Q // 2)
    def _():
        send_own(True)

    @pl.when(q < Q // 2)
    def _():
        send_own(False)

    for i in range(PIECES):
        piece_copy(b, i, mate_send, mate).start()

    acc[...] = jnp.zeros_like(acc)
    extract(b)

    for i in range(PIECES):
        piece_copy(mate, i, mate_send, mate).wait_recv()

    extract(mate)

    def arrive(s, i, between=None):
        below, above = b - 2 * s, b + 2 * s
        from_below, from_above = q - s >= 0, q + s < Q
        down_piece = PIECES - 1 - i

        @pl.when(from_below)
        def _():
            piece_copy(below, down_piece, up_send, b).wait_recv()

            @pl.when(has_up)
            def _():
                piece_copy(below, down_piece, up_send, b + 2).start()
            piece_copy(below, down_piece, mate_send, mate).start()

        @pl.when(from_above)
        def _():
            piece_copy(above, i, down_send, b).wait_recv()

            @pl.when(has_down)
            def _():
                piece_copy(above, i, down_send, b - 2).start()
            piece_copy(above, i, mate_send, mate).start()

        @pl.when(from_below & (i == need_below))
        def _():
            extract(below)

        @pl.when(from_above & (i == need_above))
        def _():
            extract(above)

        if between is not None:
            between()

        @pl.when(from_below)
        def _():
            piece_copy(mate - 2 * s, down_piece, mate_send, mate).wait_recv()

            @pl.when(i == need_below)
            def _():
                extract(mate - 2 * s)

        @pl.when(from_above)
        def _():
            piece_copy(mate + 2 * s, i, mate_send, mate).wait_recv()

            @pl.when(i == need_above)
            def _():
                extract(mate + 2 * s)

        if i == 0:
            multiply_step(s - 1)

    def finish(piece, place):
        lo, hi = bounds[piece], bounds[piece + 1]
        part = acc[:, lo:hi]
        if place is not None:
            for core in range(2):
                k = place * 2 + core
                a = shr[k].reshape(L * SP, T)
                part = part + lax.dot_general(a, zbuf[k, lo:hi, :], NT,
                                              preferred_element_type=jnp.float32)
        part = part / total
        for j in range(L):
            o_ref[:, j, lo:hi] = part[j * SP:j * SP + share]

    @pl.loop(1, Q - 1)
    def _(s):
        for i in range(PIECES):
            arrive(s, i)

    def finish_ends(steps):
        for end, place in ((Q - 1, 0), (0, Q - 1)):
            @pl.when(q == end)
            def _():
                for i in steps:
                    finish(PIECES - 1 - i if end else i, place)

    def finish_early():
        for end, place in ((Q - 1, 0), (0, Q - 1)):
            @pl.when(q == end)
            def _():
                wait_shares(place)

        finish_ends(range(PIECES - 1))

    for i in range(PIECES):
        arrive(Q - 1, i, finish_early if i == PIECES - 1 else None)
    finish_ends([PIECES - 1])

    @pl.when((q > 0) & (q < Q - 1))
    def _():
        for i in range(PIECES):
            finish(i, None)

    for d in range(1, B):
        other = lax.rem(b + d, B)
        stat_copy(b, other).wait_send()

    @pl.loop(0, Q)
    def _(s):
        below, above = b - 2 * s, b + 2 * s
        from_below, from_above = q - s >= 0, q + s < Q

        for i in range(PIECES):
            @pl.when(from_below & has_up)
            def _():
                piece_copy(below, i, up_send, b + 2).wait_send()

            @pl.when(from_above & has_down)
            def _():
                piece_copy(above, i, down_send, b - 2).wait_send()

            @pl.when(from_below)
            def _():
                piece_copy(below, i, mate_send, mate).wait_send()

            @pl.when(from_above & (s > 0))
            def _():
                piece_copy(above, i, mate_send, mate).wait_send()

    @pl.loop(0, B)
    def _(k):
        for d in range(1, L):
            other = lax.rem(l + d, L)
            share_copy(k, l, other).wait_send()


F, M2, M1, C, N1, N2, D = range(7)


def line_kernel(L, B, x_hbm, o_ref, zbuf, shr, acc_lo, acc_hi, acc_mid, tile_send, tile_recv, shift_ref, place_ref,
                cols, stats, x_ref, raw,
                z_recv, out_send, in_send, mate_send, own_send, own_out, own_in, first_send, raw_recv, raw_send, shr_recv, shr_send, diag_recv, diag_send, t_recv, t_send,
                st_recv, st_send, x_sem):
    R, T = x_hbm.shape
    total = T * B
    share = R // B
    half = 2 * share
    SP = shr.shape[2]
    pad = share - 128
    W = min(up_to(share + 15, 16), R)
    low, high = R - (3 * half - pad) // 16 * 16, (3 * half - pad) // 16 * 16
    split = (3 * half - share) // 16 * 16
    edges = [0, low, R - split, (R // 2 - pad) // 16 * 16]
    edges = edges + [R - x for x in reversed(edges)]
    size = [edges[p + 1] - edges[p] for p in range(7)]
    narrow = size[C] // 2
    far = R - size[M2] - size[M1] - size[N1] - narrow
    tile = largest_tile(R, 352)
    RAW = raw.shape[1]
    WS = acc_lo.shape[1]
    hi_lane, mid_lane = R - WS, WS // 128 * 128
    WM = acc_mid.shape[1]
    l, b = lax.axis_index("loop"), lax.axis_index("bulk")
    q, c = b // 2, b % 2
    mate = q * 2 + (1 - c)
    upper = q >= 2
    inner = (q == 1) | (q == 2)
    outer = (q == 0) | (q == 3)
    step = jnp.where(upper, 1, -1)
    H = [jnp.where(upper, h, 3 - h) for h in range(4)]
    out_nbr, in_nbr = b + 2 * step, b - 2 * step
    lx, ly, ld = l + 1 - 2 * (l % 2), lax.rem(l + 2, 4), 3 - l

    def align(value, unit=16):
        return pl.multiple_of(value, unit)

    start = [align(jnp.where(upper, edges[p], edges[6 - p])) for p in range(7)]
    narrow_start = align(jnp.where(upper, R // 2 - narrow, R // 2))

    barrier = pltpu.get_barrier_semaphore()
    for d in range(1, B):
        pl.semaphore_signal(barrier, inc=1, device_id=(l, lax.rem(b + d, B)), device_id_type=MESH)
    for line in (lx, ly):
        pl.semaphore_signal(barrier, inc=1, device_id=(line, b), device_id_type=MESH)

    def load(i):
        rows = pl.ds(pl.multiple_of(i * tile, tile), tile)
        return pltpu.make_async_copy(x_hbm.at[rows, :], x_ref.at[rows, :], x_sem.at[i])

    @pl.loop(0, R // tile)
    def _(i):
        load(i).start()

    lane = lax.broadcasted_iota(jnp.int32, (tile, 128), 1)

    @pl.loop(0, R // tile)
    def _(i):
        rows = pl.ds(pl.multiple_of(i * tile, tile), tile)
        load(i).wait()
        v = x_ref[rows, :]
        mean = jnp.sum(v, axis=1, keepdims=True) / T
        dev = v - mean
        m2 = jnp.sum(dev * dev, axis=1, keepdims=True)
        cols[rows, :] = jnp.where(lane == 0, mean, jnp.where(lane == 1, m2, 0.0))

    pick = (lax.broadcasted_iota(jnp.int32, (8, 128), 0)
            == lax.broadcasted_iota(jnp.int32, (8, 128), 1)).astype(jnp.bfloat16)

    def in_parts(x):
        top = x.astype(jnp.bfloat16)
        rest = x - top.astype(jnp.float32)
        middle = rest.astype(jnp.bfloat16)
        return top, middle, (rest - middle.astype(jnp.float32)).astype(jnp.bfloat16)

    def exact_dot(parts, dot):
        top, middle, low_part = [dot(part) for part in parts]
        return top + middle + low_part

    line = exact_dot(in_parts(cols[...]), lambda part: lax.dot_general(
        pick, part, NT, preferred_element_type=jnp.float32))
    stats[b] = line[:2]

    pl.semaphore_wait(barrier, B - 1 + 2)

    def stat_copy(source, peer):
        return pltpu.make_async_remote_copy(
            src_ref=stats.at[source], dst_ref=stats.at[source],
            send_sem=st_send, recv_sem=st_recv,
            device_id=(l, peer), device_id_type=MESH)

    for d in range(1, B):
        stat_copy(b, lax.rem(b + d, B)).start()
    def raw_copy(p, slot, peer):
        return pltpu.make_async_remote_copy(
            src_ref=x_ref.at[pl.ds(start[p], RAW), :], dst_ref=raw.at[slot], send_sem=raw_send,
            recv_sem=raw_recv.at[slot], device_id=(l, peer), device_id_type=MESH)

    @pl.when(inner)
    def _():
        raw_copy(D, 0, out_nbr).start()
        raw_copy(F, 0, in_nbr).start()

    @pl.when(outer)
    def _():
        raw_copy(F, 1, in_nbr).start()

    gathered = stats.at[pl.ds(0, B - 1)]
    all_stats = pltpu.make_async_remote_copy(
        src_ref=gathered, dst_ref=gathered, send_sem=st_send, recv_sem=st_recv,
        device_id=(l, b), device_id_type=MESH)
    all_stats.wait_recv()

    mean = stats[0, 0:1]
    for k in range(1, B):
        mean = mean + stats[k, 0:1]
    mean = mean / B
    square = jnp.zeros_like(mean)
    for k in range(B):
        shift = stats[k, 0:1] - mean
        square = square + (stats[k, 1:2] + T * (shift * shift))
    scale = lax.rsqrt(square / total + epsilon)
    sub = lax.broadcasted_iota(jnp.int32, (8, R), 0)
    both = jnp.where(sub == 0, mean, jnp.where(sub == 1, scale, 0.0))
    cols[...] = exact_dot(in_parts(both), lambda part: lax.dot_general(
        part, pick, TN, preferred_element_type=jnp.float32))

    def normalise(begin, count):
        unit = count if count <= 288 else largest_tile(count, 128)

        def chunk(i):
            rows = pl.ds(pl.multiple_of(begin + i * unit, 16), unit)
            z = (x_ref[rows, :] - cols[rows, 0:1]) * cols[rows, 1:2]
            zbuf[b, rows, :] = z.astype(jnp.bfloat16)

        if unit == count:
            chunk(0)
        else:
            pl.loop(0, count // unit)(chunk)

    def z_copy(k, p, send_sem, peer, skip=0, to_end=False):
        begin, rows = align(start[p] + skip), size[p] - skip
        if to_end and p == C:
            begin, rows = narrow_start, narrow
        part = zbuf.at[k, pl.ds(begin, rows), :]
        return pltpu.make_async_remote_copy(
            src_ref=part, dst_ref=part, send_sem=send_sem,
            recv_sem=z_recv.at[k, jnp.where(upper, p, 6 - p)], device_id=(l, peer), device_id_type=MESH)

    def first_copy(k, p, peer):
        return z_copy(k, p, first_send, peer, RAW)

    def unpack(slot, k, p):
        raw_copy(p, slot, b).wait_recv()
        rows = pl.ds(start[p], RAW)
        z = (raw[slot] - cols[rows, 0:1]) * cols[rows, 1:2]
        zbuf[k, rows, :] = z.astype(jnp.bfloat16)

    def send_out(k, p):
        return z_copy(k, p, out_send, out_nbr, 0, True)

    def send_in(k, p):
        return z_copy(k, p, in_send, in_nbr)

    def mate_copy(k, p, to_end=False):
        return z_copy(k, p, mate_send, mate, 0, to_end)

    def mate_own(k):
        part = zbuf.at[k]
        return pltpu.make_async_remote_copy(
            src_ref=part, dst_ref=part, send_sem=own_send, recv_sem=z_recv.at[k, 0],
            device_id=(l, mate), device_id_type=MESH)

    def share_copy(k, block, peer, way):
        part = shr.at[k, block, pl.ds(0, SR), :]
        return pltpu.make_async_remote_copy(
            src_ref=part, dst_ref=part, send_sem=shr_send,
            recv_sem=shr_recv.at[k, way], device_id=(peer, b), device_id_type=MESH)

    SR = up_to(share, 8)
    cut = up_to(share // 2, 16)

    def diag_copy(k, block, peer, way):
        rows = pl.ds(0, cut) if way == 0 else pl.ds(cut, SR - cut)
        part = shr.at[k, block, rows, :]
        return pltpu.make_async_remote_copy(
            src_ref=part, dst_ref=part, send_sem=diag_send,
            recv_sem=diag_recv.at[k // 2], device_id=(peer, b), device_id_type=MESH)

    first = align(jnp.minimum(b * share // 16 * 16, jnp.where(q == 0, size[D], R) - W))

    def extract_one(k):
        window = zbuf[k, pl.ds(first, W), :]
        row = lax.broadcasted_iota(jnp.int32, (SP, W), 0)
        hot = lax.broadcasted_iota(jnp.int32, (SP, W), 1) == row + (b * share - first)
        hot = jnp.where(hot & (row < share), 1.0, 0.0).astype(jnp.bfloat16)
        rows = lax.dot_general(hot, window, (((1,), (0,)), ((), ())),
                               preferred_element_type=jnp.float32)
        shr[k, l] = rows.astype(jnp.bfloat16)
        share_copy(k, l, lx, 0).start()
        share_copy(k, l, ly, 1).start()

    def extract(place):
        @pl.loop(0, 2)
        def _(core):
            extract_one(place * 2 + core)

    def pass_on(place):
        @pl.loop(0, 2)
        def _(core):
            k = place * 2 + core
            share_copy(k, lx, lx, 0).wait_recv()
            diag_copy(k, lx, ly, 0).start()
            share_copy(k, ly, ly, 1).wait_recv()
            diag_copy(k, ly, lx, 1).start()

    def wait_diag(place):
        part = shr.at[pl.ds(place * 2, 2), ld, pl.ds(0, SR), :]
        pltpu.make_async_remote_copy(
            src_ref=part, dst_ref=part, send_sem=diag_send, recv_sem=diag_recv.at[place],
            device_id=(l, b), device_id_type=MESH).wait_recv()

    def product(place, begin, width):
        part = None
        for core in range(2):
            k = place * 2 + core
            term = lax.dot_general(shr[k].reshape(L * SP, T), zbuf[k, begin:begin + width, :], NT,
                                   preferred_element_type=jnp.float32)
            part = term if part is None else part + term
        return part

    def add_sides(place):
        acc_lo[...] += product(place, 0, WS)
        acc_hi[...] += product(place, hi_lane, WS)

    def add_middle(place):
        acc_mid[...] += product(place, mid_lane, WM)

    def own(h):
        return H[h] * 2 + c

    def other(h):
        return H[h] * 2 + (1 - c)

    def take(h, p, onward=None, first=False, to_end=False):
        if first:
            first_copy(own(h), p, mate).wait_recv()
        else:
            mate_copy(own(h), p, to_end).wait_recv()
        if onward is not None:
            onward(own(h), p).start()
        mate_copy(own(h), p, to_end).start()

    def mate_take(h, pieces, to_end=False):
        for p in pieces:
            mate_copy(other(h), p, to_end).wait_recv()

    def take_end(h, p):
        take(h, p, to_end=True)

    def mate_take_end(h, pieces):
        mate_take(h, pieces, True)

    def tile_copy(side, j, core, block, slot):
        return pltpu.make_async_remote_copy(
            src_ref=tile_send.at[side, j, core, pl.ds(0, SR), :],
            dst_ref=tile_recv.at[block, pl.ds(0, SR), pl.ds(pl.multiple_of(slot * 128, 128), 128)],
            send_sem=t_send, recv_sem=t_recv.at[block],
            device_id=(j, 6 * side + core), device_id_type=MESH)

    def make_hot():
        for side, skip in ((0, jnp.where(b == 5, 0, pad)), (1, jnp.where(b == 2, pad, 0))):
            shift = (lax.broadcasted_iota(jnp.int32, (SR, 128), 0)
                     == lax.broadcasted_iota(jnp.int32, (SR, 128), 1) + skip)
            shift_ref[side] = jnp.where(shift, 1.0, 0.0).astype(jnp.bfloat16)
        row = lax.broadcasted_iota(jnp.int32, (512, WM), 0)
        slot = row // 128
        shifted = slot < jnp.where(upper, 1, 3)
        lane = half - mid_lane + slot * (share - 128) + row + jnp.where(shifted, pad, 0)
        hot = lax.broadcasted_iota(jnp.int32, (512, WM), 1) == lane
        place_ref[...] = jnp.where(hot, 1.0, 0.0).astype(jnp.bfloat16)
        for side, slot in ((0, 0), (3, 3)):
            @pl.when(q == side)
            def _():
                tile_recv[:, :, slot * 128:slot * 128 + 128] = jnp.zeros((L, SP, 128), jnp.bfloat16)

    def add_rows(j, place):
        rows = pl.ds(pl.multiple_of(j * SP, SP), SP)
        for acc, begin in ((acc_lo, 0), (acc_hi, hi_lane)):
            value = acc[rows, :]
            for core in range(2):
                k = place * 2 + core
                value = value + lax.dot_general(shr[k, j], zbuf[k, begin:begin + WS, :], NT,
                                                preferred_element_type=jnp.float32)
            acc[rows, :] = value

    def turn_tiles(j):
        rows = pl.ds(pl.multiple_of(j * SP, SP), SP)
        for side, acc in ((0, acc_lo), (1, acc_hi)):
            turned = lax.dot_general((acc[rows, :][:SR] / total).astype(jnp.bfloat16), shift_ref[side], TN,
                                     preferred_element_type=jnp.float32)
            for core in range(2):
                at = (WS - half if side else 0) + core * share
                tile_send[side, j, core, :share, :] = turned[at:at + share].astype(jnp.bfloat16)

    def tile_copies(j, act):
        for side, skipped in ((0, 2), (1, 5)):
            @pl.when(b != skipped)
            def _():
                for core in range(2):
                    act(tile_copy(side, j, core, l, b - 2))

    def start_tiles(j):
        tile_copies(j, lambda copy: copy.start())

    def wait_tile(block):
        part = tile_recv.at[block, pl.ds(0, SR), pl.ds(0, 384)]
        pltpu.make_async_remote_copy(
            src_ref=part, dst_ref=part, send_sem=t_send, recv_sem=t_recv.at[block],
            device_id=(l, b), device_id_type=MESH).wait_recv()

    normalise(start[D], size[D])

    @pl.when(inner)
    def _():
        first_copy(b, D, out_nbr).start()

    normalise(start[F], size[F])

    first_copy(b, F, in_nbr).start()
    normalise(low, high - low)

    @pl.when(inner)
    def _():
        for p in (M2, M1, C):
            z_copy(b, p, own_in, in_nbr).start()
        for p in (F, C, N2):
            z_copy(b, p, own_out, out_nbr, 0, True).start()

    @pl.when(outer)
    def _():
        for p in (M2, M1, C, D, N2, N1):
            z_copy(b, p, own_in, in_nbr).start()
    mate_own(b).start()
    extract_one(b)
    make_hot()
    mate_own(mate).wait_recv()
    extract_one(mate)

    @pl.when(inner)
    def _():
        unpack(0, own(1), D)
        unpack(1, own(3), F)
        take(1, D, send_out, True)
        take(3, F, send_in, True)
        pass_on(q)
        take(1, N2, send_out)
        take(3, M2, send_in)
        take(1, N1)
        take(3, M1, send_in)
        take(1, C, send_out)
        take(3, C, send_in)
        z_copy(b, D, own_in, in_nbr).start()
        mate_take(1, (D, N2, N1, C))
        extract(H[1])
        take(0, D, send_out)
        take(3, D, send_in)

    @pl.when(outer)
    def _():
        unpack(0, own(2), D)
        take(2, D, None, True)
        mate_take(2, (D,))
        extract(H[2])
        pass_on(q)
        take_end(2, F)
        take_end(2, C)
        take_end(2, N2)
        pass_on(H[2])
        take(1, D)
        mate_take(1, (D,))
        extract(H[1])
        mate_take_end(2, (F, C, N2))
    wait_diag(q)
    acc_lo[...] = product(q, 0, WS)
    acc_hi[...] = product(q, hi_lane, WS)
    acc_mid[...] = product(q, mid_lane, WM)

    second, third = jnp.where(inner, H[1], H[2]), jnp.where(inner, H[3], H[1])

    @pl.when(inner)
    def _():
        pass_on(H[1])
        take(0, N2, send_out)
        take(0, N1)
        take(0, C, send_out)
        mate_take(0, (D, N2, N1, C))
        extract(H[0])
        take(3, N2)
        take(3, N1)
        mate_take(3, (C, D, N2, N1))
        extract(H[3])
        take(1, F, send_out)
        mate_take(1, (F,))

    @pl.when(outer)
    def _():
        take_end(1, N2)
        take_end(1, C)
        pass_on(H[1])
    wait_diag(second)
    add_sides(second)

    @pl.when(outer)
    def _():
        take(0, D)
        mate_take(0, (D,))
        extract(H[0])
        take_end(0, N2)
        take_end(0, C)
        take_end(1, F)
        mate_take_end(1, (N2, C, F))
        wait_diag(H[1])
        add_sides(H[1])
    @pl.when(inner)
    def _():
        mate_take(3, (F, M1, M2))
        add_rows(l, H[3])
    pass_on(H[0])

    @pl.when(inner)
    def _():
        take(0, F, send_out)
        for p in (N1, N2):
            z_copy(b, p, own_in, in_nbr).start()
        mate_take(0, (F,))
        add_rows(l, H[0])
        turn_tiles(l)
        start_tiles(l)

        @pl.loop(0, 2)
        def _(n):
            add_rows(jnp.where(n == 0, lx, ly), H[0])
        pass_on(H[3])

        @pl.loop(0, 2)
        def _(n):
            j = jnp.where(n == 0, lx, ly)
            add_rows(j, H[3])
            turn_tiles(j)
            start_tiles(j)
        for p in (N1, N2):
            send_in(own(3), p).start()
        wait_diag(H[0])
        add_rows(ld, H[0])
        wait_diag(H[3])
        add_rows(ld, H[3])
        turn_tiles(ld)
        start_tiles(ld)
        for p in (M1, M2):
            take(1, p)
        mate_take(1, (M1, M2))
    add_middle(second)
    add_middle(third)

    def put(lanes, acc, begin=0):
        for j in range(L):
            part = acc[j * SP:j * SP + share, :][:, begin:begin + lanes.stop - lanes.start]
            o_ref[:, j, lanes] = part / total

    @pl.when(inner)
    def _():
        for p in (M1, M2):
            take(0, p)
        put(slice(0, mid_lane), acc_lo)
        put(slice(mid_lane + WM, R), acc_hi, mid_lane + WM - hi_lane)
        mate_take(0, (M1, M2))
        add_middle(H[0])
        put(slice(mid_lane, mid_lane + WM), acc_mid)

    lanes_lo = mid_lane, up_to(R // 2 + pad, 128)
    lanes_hi = (R // 2 - pad) // 128 * 128, mid_lane + WM

    @pl.when(outer)
    def _():
        mate_take_end(0, (N2, C))
        wait_diag(H[0])
        for end, acc, begin, (first_mid, last_mid) in ((0, acc_lo, 0, lanes_lo), (3, acc_hi, hi_lane, lanes_hi)):
            @pl.when(q == end)
            def _():
                acc[...] += product(H[0], begin, WS)
                inner_lanes = slice(first_mid - mid_lane, last_mid - mid_lane)
                acc_mid[:, inner_lanes] += product(H[0], first_mid, last_mid - first_mid)
                put(slice(first_mid, last_mid), acc_mid, first_mid - mid_lane)
                if end:
                    put(slice(last_mid, R), acc, last_mid - hi_lane)
                else:
                    put(slice(0, first_mid), acc)
        place = lax.broadcasted_iota(jnp.int32, (share, WM), 1) + mid_lane
        low_first = half + pad + jnp.where(upper, 0, share)
        high_first = R // 2 + jnp.where(upper, 0, pad)
        inside = ((place >= low_first) & (place < low_first + jnp.where(upper, 256, 128))
                  | (place >= high_first) & (place < high_first + jnp.where(upper, 128, 256)))
        def place_tile(d):
            wait_tile(d)
            placed = lax.dot_general(tile_recv[d], place_ref[...], (((1,), (0,)), ((), ())),
                                     preferred_element_type=jnp.float32)[:share]
            middle = pl.ds(mid_lane, WM)
            o_ref[:, d, middle] = jnp.where(inside, placed, o_ref[:, d, middle])

        take(0, F)
        place_tile(l)
        place_tile(lx)
        mate_take(0, (F,))
        for end, acc, begin in ((3, acc_lo, 0), (0, acc_hi, hi_lane)):
            @pl.when(q == end)
            def _():
                acc[...] += product(H[0], begin, WS)
                put(slice(begin, begin + WS), acc)
        place_tile(ly)
        place_tile(ld)

    all_stats.wait_send()
    mate_own(b).wait_send()

    def sent(part, sem):
        pltpu.make_async_remote_copy(
            src_ref=part, dst_ref=part, send_sem=sem, recv_sem=st_recv,
            device_id=(l, b), device_id_type=MESH).wait_send()

    @pl.when(inner)
    def _():
        sent(zbuf.at[0, pl.ds(0, size[F] + narrow + size[N2]), :], own_out)
        sent(zbuf.at[pl.ds(0, 2), pl.ds(0, size[D] - RAW), :], first_send)
        sent(raw, raw_send)
        sent(zbuf.at[pl.ds(0, 2), pl.ds(0, far), :], out_send)
        sent(zbuf.at[0], in_send)
        sent(zbuf.at[pl.ds(0, 3)], mate_send)
        for skipped in (True, False):
            @pl.when(((b == 2) | (b == 5)) == skipped)
            def _():
                sides = 1 if skipped else 2
                sent(tile_send.at[pl.ds(0, sides), :, :, pl.ds(0, SR), :], t_send)

    @pl.when(outer)
    def _():
        sent(zbuf.at[0, pl.ds(0, size[D] - RAW), :], first_send)
        sent(raw.at[0], raw_send)
        sent(zbuf.at[pl.ds(0, 3), pl.ds(0, far), :], mate_send)

    sent(zbuf.at[0, pl.ds(0, R - size[D]), :], own_in)
    sent(shr.at[pl.ds(0, L), :, pl.ds(0, SR), :], shr_send)
    sent(shr.at[pl.ds(0, B // L), :, pl.ds(0, SR), :], diag_send)


def line_call(L, B, series):
    R, T = series.shape
    share = R // B
    SP = up_to(share, 16)
    pad = share - 128
    high = (3 * 2 * share - pad) // 16 * 16
    WS = R - high
    mid_lane = WS // 128 * 128
    WM = up_to(R // 2 + pad + 256, 128) - mid_lane
    vmem = pl.BlockSpec(memory_space=pltpu.VMEM)
    dma = pltpu.SemaphoreType.DMA
    return pl.pallas_call(
        functools.partial(line_kernel, L, B),
        out_shape=jax.ShapeDtypeStruct((share, L, R), jnp.float32),
        in_specs=[pl.BlockSpec(memory_space=pltpu.HBM)],
        out_specs=vmem,
        scratch_shapes=[
            pltpu.VMEM((B, R, T), jnp.bfloat16),
            pltpu.VMEM((B, L, SP, T), jnp.bfloat16),
            pltpu.VMEM((L * SP, WS), jnp.float32),
            pltpu.VMEM((L * SP, WS), jnp.float32),
            pltpu.VMEM((L * SP, WM), jnp.float32),
            pltpu.VMEM((2, L, 2, SP, 128), jnp.bfloat16),
            pltpu.VMEM((L, SP, 512), jnp.bfloat16),
            pltpu.VMEM((2, up_to(share, 8), 128), jnp.bfloat16),
            pltpu.VMEM((512, WM), jnp.bfloat16),
            pltpu.VMEM((R, 128), jnp.float32),
            pltpu.VMEM((B, 2, R), jnp.float32),
            pltpu.VMEM((R, T), jnp.float32),
            pltpu.VMEM((2, (R - high) * 7 // 256 * 16, T), jnp.float32),
            dma((B, 7)), dma, dma, dma, dma, dma, dma, dma, dma((2,)), dma,
            dma((B, 2)), dma, dma((B // 2,)), dma, dma((L,)), dma,
            dma, dma, dma((R // largest_tile(R, 352),)),
        ],
        compiler_params=pltpu.CompilerParams(
            collective_id=0, has_side_effects=True, vmem_limit_bytes=34 * 1024 * 1024),
    )(pltpu.with_memory_space_constraint(series, pltpu.HBM)).transpose(1, 0, 2)


def solution(mesh):
    L, B = mesh.shape["loop"], mesh.shape["bulk"]

    def on_device(series):
        R, T = series.shape
        share = R // B
        if L == 4 and B == 8 and R % 16 == 0 and T % 128 == 0 and 128 <= share <= 144:
            return line_call(L, B, series)
        SP = up_to(share, 16)
        pieces = 3
        vmem = pl.BlockSpec(memory_space=pltpu.VMEM)
        dma = pltpu.SemaphoreType.DMA
        return pl.pallas_call(
            functools.partial(kernel, L, B, pieces),
            out_shape=jax.ShapeDtypeStruct((share, L, R), jnp.float32),
            in_specs=[pl.BlockSpec(memory_space=pltpu.HBM)],
            out_specs=vmem,
            scratch_shapes=[
                pltpu.VMEM((B, R, T), jnp.bfloat16),
                pltpu.VMEM((B, L, SP, T), jnp.bfloat16),
                pltpu.VMEM((L * SP, R), jnp.float32),
                pltpu.VMEM((R, 128), jnp.float32),
                pltpu.VMEM((B, 2, R), jnp.float32),
                pltpu.VMEM((R, T), jnp.float32),
                dma((B, pieces)), dma((B, pieces)), dma((B, pieces)), dma((B, pieces)),
                dma((B, L)), dma((B, L)), dma((B,)), dma((B,)), dma((R // largest_tile(R, 128),)),
            ],
            compiler_params=pltpu.CompilerParams(
                collective_id=0, has_side_effects=True, vmem_limit_bytes=26 * 1024 * 1024),
        )(pltpu.with_memory_space_constraint(series, pltpu.HBM)).transpose(1, 0, 2)

    return jax.shard_map(
        on_device, mesh=mesh, in_specs=(P("loop", "bulk"),),
        out_specs=P(None, "bulk", "loop"), check_vma=False)
```

```python
import functools
import jax
import jax.numpy as jnp
from jax import lax
from jax.experimental import pallas as pl
from jax.experimental.pallas import tpu as pltpu
from jax.sharding import PartitionSpec as P

epsilon = 1e-06
MESH = pl.DeviceIdType.MESH
NT = (((1,), (1,)), ((), ()))
TN = (((0,), (0,)), ((), ()))


def up_to(value, unit):
    return -(-value // unit) * unit


def largest_tile(rows, limit):
    return max(t for t in range(16, limit + 1, 16) if rows % t == 0)


def kernel(L, B, PIECES, x_hbm, o_ref, zbuf, shr, acc, cols, stats, x_ref,
           z_recv, up_send, down_send, mate_send, shr_recv, shr_send, st_recv, st_send, x_sem):
    R, T = x_hbm.shape
    total = T * B
    Q = B // 2
    share = R // B
    SP = shr.shape[2]
    W = min(up_to(share + 15, 16), R)
    bounds = [up_to(R * i // PIECES, 128) for i in range(PIECES)] + [R]
    tile = largest_tile(R, 128)
    l, b = lax.axis_index("loop"), lax.axis_index("bulk")
    q, c = b // 2, b % 2
    mate = q * 2 + (1 - c)

    barrier = pltpu.get_barrier_semaphore()
    for d in range(1, B):
        pl.semaphore_signal(barrier, inc=1, device_id=(l, lax.rem(b + d, B)), device_id_type=MESH)
    for d in range(1, L):
        pl.semaphore_signal(barrier, inc=1, device_id=(lax.rem(l + d, L), b), device_id_type=MESH)

    def load(i):
        rows = pl.ds(pl.multiple_of(i * tile, tile), tile)
        return pltpu.make_async_copy(x_hbm.at[rows, :], x_ref.at[rows, :], x_sem.at[i])

    @pl.loop(0, R // tile)
    def _(i):
        load(i).start()

    lane = lax.broadcasted_iota(jnp.int32, (tile, 128), 1)

    @pl.loop(0, R // tile)
    def _(i):
        rows = pl.ds(pl.multiple_of(i * tile, tile), tile)
        load(i).wait()
        v = x_ref[rows, :]
        mean = jnp.sum(v, axis=1, keepdims=True) / T
        dev = v - mean
        m2 = jnp.sum(dev * dev, axis=1, keepdims=True)
        cols[rows, :] = jnp.where(lane == 0, mean, jnp.where(lane == 1, m2, 0.0))

    pick = (lax.broadcasted_iota(jnp.int32, (8, 128), 0)
            == lax.broadcasted_iota(jnp.int32, (8, 128), 1)).astype(jnp.float32)
    line = lax.dot_general(pick, cols[...], NT, precision=lax.Precision.HIGHEST,
                           preferred_element_type=jnp.float32)
    stats[b] = line[:2]

    pl.semaphore_wait(barrier, B - 1 + L - 1)

    def stat_copy(source, peer):
        return pltpu.make_async_remote_copy(
            src_ref=stats.at[source], dst_ref=stats.at[source],
            send_sem=st_send.at[peer], recv_sem=st_recv.at[source],
            device_id=(l, peer), device_id_type=MESH)

    for d in range(1, B):
        stat_copy(b, lax.rem(b + d, B)).start()
    for d in range(1, B):
        other = lax.rem(b + d, B)
        stat_copy(other, other).wait_recv()

    mean = stats[0, 0:1]
    for k in range(1, B):
        mean = mean + stats[k, 0:1]
    mean = mean / B
    square = jnp.zeros_like(mean)
    for k in range(B):
        shift = stats[k, 0:1] - mean
        square = square + (stats[k, 1:2] + T * (shift * shift))
    scale = lax.rsqrt(square / total + epsilon)
    sub = lax.broadcasted_iota(jnp.int32, (8, R), 0)
    both = jnp.where(sub == 0, mean, jnp.where(sub == 1, scale, 0.0))
    cols[...] = lax.dot_general(both, pick, TN, precision=lax.Precision.HIGHEST,
                                preferred_element_type=jnp.float32)

    def normalise(piece):
        size = bounds[piece + 1] - bounds[piece]
        step = largest_tile(size, 128)

        @pl.loop(0, size // step)
        def _(i):
            rows = pl.ds(pl.multiple_of(bounds[piece] + i * step, 16), step)
            z = (x_ref[rows, :] - cols[rows, 0:1]) * cols[rows, 1:2]
            zbuf[b, rows, :] = z.astype(jnp.bfloat16)

    def piece_copy(k, piece, send_sem, peer):
        part = zbuf.at[k, pl.ds(bounds[piece], bounds[piece + 1] - bounds[piece]), :]
        return pltpu.make_async_remote_copy(
            src_ref=part, dst_ref=part, send_sem=send_sem.at[k, piece],
            recv_sem=z_recv.at[k, piece], device_id=(l, peer), device_id_type=MESH)

    def share_copy(k, block, peer):
        return pltpu.make_async_remote_copy(
            src_ref=shr.at[k, block], dst_ref=shr.at[k, block], send_sem=shr_send.at[k, peer],
            recv_sem=shr_recv.at[k, block], device_id=(peer, b), device_id_type=MESH)

    has_up, has_down = q + 1 < Q, q >= 1
    start = b * share
    first = pl.multiple_of(jnp.minimum(start // 16 * 16, R - W), 16)
    need_below = PIECES - 1 - sum((first >= x).astype(jnp.int32) for x in bounds[1:-1])
    need_above = sum((first + W > x).astype(jnp.int32) for x in bounds[1:-1])

    def extract(k):
        window = zbuf[k, pl.ds(first, W), :]
        hot = (lax.broadcasted_iota(jnp.int32, (SP, W), 1)
               == lax.broadcasted_iota(jnp.int32, (SP, W), 0) + (start - first))
        inside = lax.broadcasted_iota(jnp.int32, (SP, W), 0) < share
        hot = jnp.where(hot & inside, 1.0, 0.0).astype(jnp.bfloat16)
        rows = lax.dot_general(hot, window, (((1,), (0,)), ((), ())),
                               preferred_element_type=jnp.float32)
        shr[k, l] = rows.astype(jnp.bfloat16)
        for d in range(1, L):
            share_copy(k, l, lax.rem(l + d, L)).start()

    def wait_shares(place):
        for core in range(2):
            k = place * 2 + core
            for d in range(1, L):
                other = lax.rem(l + d, L)
                share_copy(k, other, other).wait_recv()

    def multiply(place):
        part = None
        wait_shares(place)
        for core in range(2):
            k = place * 2 + core
            a = shr[k].reshape(L * SP, T)
            term = lax.dot_general(a, zbuf[k], NT, preferred_element_type=jnp.float32)
            part = term if part is None else part + term
        acc[...] += part

    def multiply_step(s):
        @pl.loop(0, 2)
        def _(n):
            place = q - (1 - 2 * n) * s

            @pl.when((place >= 0) & (place < Q) & ((s > 0) | (n < 1)))
            def _():
                multiply(place)

    def send_own(up_first):
        done = set()

        def send(up, i):
            piece = PIECES - 1 - i if up else i
            if piece not in done:
                done.add(piece)
                normalise(piece)

            @pl.when(has_up if up else has_down)
            def _():
                if up:
                    piece_copy(b, piece, up_send, b + 2).start()
                else:
                    piece_copy(b, piece, down_send, b - 2).start()

        for i in range(PIECES):
            send(up_first, i)
            send(not up_first, i)

    @pl.when(q >= Q // 2)
    def _():
        send_own(True)

    @pl.when(q < Q // 2)
    def _():
        send_own(False)

    for i in range(PIECES):
        piece_copy(b, i, mate_send, mate).start()

    acc[...] = jnp.zeros_like(acc)
    extract(b)

    for i in range(PIECES):
        piece_copy(mate, i, mate_send, mate).wait_recv()

    extract(mate)

    def arrive(s, i, between=None):
        below, above = b - 2 * s, b + 2 * s
        from_below, from_above = q - s >= 0, q + s < Q
        down_piece = PIECES - 1 - i

        @pl.when(from_below)
        def _():
            piece_copy(below, down_piece, up_send, b).wait_recv()

            @pl.when(has_up)
            def _():
                piece_copy(below, down_piece, up_send, b + 2).start()
            piece_copy(below, down_piece, mate_send, mate).start()

        @pl.when(from_above)
        def _():
            piece_copy(above, i, down_send, b).wait_recv()

            @pl.when(has_down)
            def _():
                piece_copy(above, i, down_send, b - 2).start()
            piece_copy(above, i, mate_send, mate).start()

        @pl.when(from_below & (i == need_below))
        def _():
            extract(below)

        @pl.when(from_above & (i == need_above))
        def _():
            extract(above)

        if between is not None:
            between()

        @pl.when(from_below)
        def _():
            piece_copy(mate - 2 * s, down_piece, mate_send, mate).wait_recv()

            @pl.when(i == need_below)
            def _():
                extract(mate - 2 * s)

        @pl.when(from_above)
        def _():
            piece_copy(mate + 2 * s, i, mate_send, mate).wait_recv()

            @pl.when(i == need_above)
            def _():
                extract(mate + 2 * s)

        if i == 0:
            multiply_step(s - 1)

    def finish(piece, place):
        lo, hi = bounds[piece], bounds[piece + 1]
        part = acc[:, lo:hi]
        if place is not None:
            for core in range(2):
                k = place * 2 + core
                a = shr[k].reshape(L * SP, T)
                part = part + lax.dot_general(a, zbuf[k, lo:hi, :], NT,
                                              preferred_element_type=jnp.float32)
        part = part / total
        for j in range(L):
            o_ref[:, j, lo:hi] = part[j * SP:j * SP + share]

    @pl.loop(1, Q - 1)
    def _(s):
        for i in range(PIECES):
            arrive(s, i)

    def finish_ends(steps):
        for end, place in ((Q - 1, 0), (0, Q - 1)):
            @pl.when(q == end)
            def _():
                for i in steps:
                    finish(PIECES - 1 - i if end else i, place)

    def finish_early():
        for end, place in ((Q - 1, 0), (0, Q - 1)):
            @pl.when(q == end)
            def _():
                wait_shares(place)

        finish_ends(range(PIECES - 1))

    for i in range(PIECES):
        arrive(Q - 1, i, finish_early if i == PIECES - 1 else None)
    finish_ends([PIECES - 1])

    @pl.when((q > 0) & (q < Q - 1))
    def _():
        for i in range(PIECES):
            finish(i, None)

    for d in range(1, B):
        other = lax.rem(b + d, B)
        stat_copy(b, other).wait_send()

    @pl.loop(0, Q)
    def _(s):
        below, above = b - 2 * s, b + 2 * s
        from_below, from_above = q - s >= 0, q + s < Q

        for i in range(PIECES):
            @pl.when(from_below & has_up)
            def _():
                piece_copy(below, i, up_send, b + 2).wait_send()

            @pl.when(from_above & has_down)
            def _():
                piece_copy(above, i, down_send, b - 2).wait_send()

            @pl.when(from_below)
            def _():
                piece_copy(below, i, mate_send, mate).wait_send()

            @pl.when(from_above & (s > 0))
            def _():
                piece_copy(above, i, mate_send, mate).wait_send()

    @pl.loop(0, B)
    def _(k):
        for d in range(1, L):
            other = lax.rem(l + d, L)
            share_copy(k, l, other).wait_send()


F, M2, M1, C, N1, N2, D = range(7)


def line_kernel(L, B, x_hbm, o_ref, zbuf, shr, acc_lo, acc_hi, acc_mid, tile_send, tile_recv, shift_ref, place_ref,
                cols, stats, x_ref, raw,
                z_recv, out_send, in_send, mate_send, own_send, own_out, own_in, first_send, raw_recv, raw_send, shr_recv, shr_send, diag_recv, diag_send, t_recv, t_send,
                st_recv, st_send, x_sem):
    R, T = x_hbm.shape
    total = T * B
    share = R // B
    half = 2 * share
    SP = shr.shape[2]
    pad = share - 128
    W = min(up_to(share + 15, 16), R)
    low, high = R - (3 * half - pad) // 16 * 16, (3 * half - pad) // 16 * 16
    split = (3 * half - share) // 16 * 16
    edges = [0, low, R - split, (R // 2 - pad) // 16 * 16]
    edges = edges + [R - x for x in reversed(edges)]
    size = [edges[p + 1] - edges[p] for p in range(7)]
    narrow = size[C] // 2
    far = R - size[M2] - size[M1] - size[N1] - narrow
    tile = largest_tile(R, 528)
    RAW = raw.shape[1]
    WS = acc_lo.shape[1]
    hi_lane, mid_lane = R - WS, WS // 128 * 128
    WM = acc_mid.shape[1]
    l, b = lax.axis_index("loop"), lax.axis_index("bulk")
    q, c = b // 2, b % 2
    mate = q * 2 + (1 - c)
    upper = q >= 2
    inner = (q == 1) | (q == 2)
    outer = (q == 0) | (q == 3)
    step = jnp.where(upper, 1, -1)
    H = [jnp.where(upper, h, 3 - h) for h in range(4)]
    out_nbr, in_nbr = b + 2 * step, b - 2 * step
    lx, ly, ld = l + 1 - 2 * (l % 2), lax.rem(l + 2, 4), 3 - l

    def align(value, unit=16):
        return pl.multiple_of(value, unit)

    start = [align(jnp.where(upper, edges[p], edges[6 - p])) for p in range(7)]
    narrow_start = align(jnp.where(upper, R // 2 - narrow, R // 2))

    barrier = pltpu.get_barrier_semaphore()
    for d in range(1, B):
        pl.semaphore_signal(barrier, inc=1, device_id=(l, lax.rem(b + d, B)), device_id_type=MESH)
    for line in (lx, ly):
        pl.semaphore_signal(barrier, inc=1, device_id=(line, b), device_id_type=MESH)

    def load(i):
        rows = pl.ds(pl.multiple_of(i * tile, tile), tile)
        return pltpu.make_async_copy(x_hbm.at[rows, :], x_ref.at[rows, :], x_sem.at[i])

    @pl.loop(0, R // tile)
    def _(i):
        load(i).start()

    lane = lax.broadcasted_iota(jnp.int32, (tile, 128), 1)

    @pl.loop(0, R // tile)
    def _(i):
        rows = pl.ds(pl.multiple_of(i * tile, tile), tile)
        load(i).wait()
        v = x_ref[rows, :]
        mean = jnp.sum(v, axis=1, keepdims=True) / T
        dev = v - mean
        m2 = jnp.sum(dev * dev, axis=1, keepdims=True)
        cols[rows, :] = jnp.where(lane == 0, mean, jnp.where(lane == 1, m2, 0.0))

    pick = (lax.broadcasted_iota(jnp.int32, (8, 128), 0)
            == lax.broadcasted_iota(jnp.int32, (8, 128), 1)).astype(jnp.bfloat16)

    def in_parts(x):
        top = x.astype(jnp.bfloat16)
        rest = x - top.astype(jnp.float32)
        middle = rest.astype(jnp.bfloat16)
        return top, middle, (rest - middle.astype(jnp.float32)).astype(jnp.bfloat16)

    def exact_dot(parts, dot):
        top, middle, low_part = [dot(part) for part in parts]
        return top + middle + low_part

    line = exact_dot(in_parts(cols[...]), lambda part: lax.dot_general(
        pick, part, NT, preferred_element_type=jnp.float32))
    stats[b] = line[:2]

    pl.semaphore_wait(barrier, B - 1 + 2)

    def stat_copy(source, peer):
        return pltpu.make_async_remote_copy(
            src_ref=stats.at[source], dst_ref=stats.at[source],
            send_sem=st_send, recv_sem=st_recv,
            device_id=(l, peer), device_id_type=MESH)

    for d in range(1, B):
        stat_copy(b, lax.rem(b + d, B)).start()
    def raw_copy(p, slot, peer):
        return pltpu.make_async_remote_copy(
            src_ref=x_ref.at[pl.ds(start[p], RAW), :], dst_ref=raw.at[slot], send_sem=raw_send,
            recv_sem=raw_recv.at[slot], device_id=(l, peer), device_id_type=MESH)

    @pl.when(inner)
    def _():
        raw_copy(D, 0, out_nbr).start()
        raw_copy(F, 0, in_nbr).start()

    @pl.when(outer)
    def _():
        raw_copy(F, 1, in_nbr).start()

    gathered = stats.at[pl.ds(0, B - 1)]
    all_stats = pltpu.make_async_remote_copy(
        src_ref=gathered, dst_ref=gathered, send_sem=st_send, recv_sem=st_recv,
        device_id=(l, b), device_id_type=MESH)
    all_stats.wait_recv()

    mean = stats[0, 0:1]
    for k in range(1, B):
        mean = mean + stats[k, 0:1]
    mean = mean / B
    square = jnp.zeros_like(mean)
    for k in range(B):
        shift = stats[k, 0:1] - mean
        square = square + (stats[k, 1:2] + T * (shift * shift))
    scale = lax.rsqrt(square / total + epsilon)
    sub = lax.broadcasted_iota(jnp.int32, (8, R), 0)
    both = jnp.where(sub == 0, mean, jnp.where(sub == 1, scale, 0.0))
    cols[...] = exact_dot(in_parts(both), lambda part: lax.dot_general(
        part, pick, TN, preferred_element_type=jnp.float32))

    def normalise(begin, count):
        unit = count if count <= 288 else largest_tile(count, 128)

        def chunk(i):
            rows = pl.ds(pl.multiple_of(begin + i * unit, 16), unit)
            z = (x_ref[rows, :] - cols[rows, 0:1]) * cols[rows, 1:2]
            zbuf[b, rows, :] = z.astype(jnp.bfloat16)

        if unit == count:
            chunk(0)
        else:
            pl.loop(0, count // unit)(chunk)

    def z_copy(k, p, send_sem, peer, skip=0, to_end=False):
        begin, rows = align(start[p] + skip), size[p] - skip
        if to_end and p == C:
            begin, rows = narrow_start, narrow
        part = zbuf.at[k, pl.ds(begin, rows), :]
        return pltpu.make_async_remote_copy(
            src_ref=part, dst_ref=part, send_sem=send_sem,
            recv_sem=z_recv.at[k, jnp.where(upper, p, 6 - p)], device_id=(l, peer), device_id_type=MESH)

    def first_copy(k, p, peer):
        return z_copy(k, p, first_send, peer, RAW)

    def unpack(slot, k, p):
        raw_copy(p, slot, b).wait_recv()
        rows = pl.ds(start[p], RAW)
        z = (raw[slot] - cols[rows, 0:1]) * cols[rows, 1:2]
        zbuf[k, rows, :] = z.astype(jnp.bfloat16)

    def send_out(k, p):
        return z_copy(k, p, out_send, out_nbr, 0, True)

    def send_in(k, p):
        return z_copy(k, p, in_send, in_nbr)

    def mate_copy(k, p, to_end=False):
        return z_copy(k, p, mate_send, mate, 0, to_end)

    def mate_own(k):
        part = zbuf.at[k]
        return pltpu.make_async_remote_copy(
            src_ref=part, dst_ref=part, send_sem=own_send, recv_sem=z_recv.at[k, 0],
            device_id=(l, mate), device_id_type=MESH)

    def share_copy(k, block, peer, way):
        part = shr.at[k, block, pl.ds(0, SR), :]
        return pltpu.make_async_remote_copy(
            src_ref=part, dst_ref=part, send_sem=shr_send,
            recv_sem=shr_recv.at[k // 2, way], device_id=(peer, b), device_id_type=MESH)

    SR = up_to(share, 8)
    cut = up_to(share // 2, 16)

    def diag_copy(k, block, peer, way):
        rows = pl.ds(0, cut) if way == 0 else pl.ds(cut, SR - cut)
        part = shr.at[k, block, rows, :]
        return pltpu.make_async_remote_copy(
            src_ref=part, dst_ref=part, send_sem=diag_send,
            recv_sem=diag_recv.at[k // 2], device_id=(peer, b), device_id_type=MESH)

    first = align(jnp.minimum(b * share // 16 * 16, jnp.where(q == 0, size[D], R) - W))

    def extract_one(k):
        window = zbuf[k, pl.ds(first, W), :]
        row = lax.broadcasted_iota(jnp.int32, (SP, W), 0)
        hot = lax.broadcasted_iota(jnp.int32, (SP, W), 1) == row + (b * share - first)
        hot = jnp.where(hot & (row < share), 1.0, 0.0).astype(jnp.bfloat16)
        rows = lax.dot_general(hot, window, (((1,), (0,)), ((), ())),
                               preferred_element_type=jnp.float32)
        shr[k, l] = rows.astype(jnp.bfloat16)
        share_copy(k, l, lx, 0).start()
        share_copy(k, l, ly, 1).start()

    def extract(place):
        @pl.loop(0, 2)
        def _(core):
            extract_one(place * 2 + core)

    def pass_on(place):
        for way, near, onward in ((0, lx, ly), (1, ly, lx)):
            part = shr.at[pl.ds(place * 2, 2), near, pl.ds(0, SR), :]
            pltpu.make_async_remote_copy(
                src_ref=part, dst_ref=part, send_sem=shr_send, recv_sem=shr_recv.at[place, way],
                device_id=(l, b), device_id_type=MESH).wait_recv()
            for core in range(2):
                diag_copy(place * 2 + core, near, onward, way).start()

    def wait_diag(place):
        part = shr.at[pl.ds(place * 2, 2), ld, pl.ds(0, SR), :]
        pltpu.make_async_remote_copy(
            src_ref=part, dst_ref=part, send_sem=diag_send, recv_sem=diag_recv.at[place],
            device_id=(l, b), device_id_type=MESH).wait_recv()

    def product(place, begin, width):
        part = None
        for core in range(2):
            k = place * 2 + core
            term = lax.dot_general(shr[k].reshape(L * SP, T), zbuf[k, begin:begin + width, :], NT,
                                   preferred_element_type=jnp.float32)
            part = term if part is None else part + term
        return part

    def add_sides(place):
        acc_lo[...] += product(place, 0, WS)
        acc_hi[...] += product(place, hi_lane, WS)

    def add_middle(place):
        acc_mid[...] += product(place, mid_lane, WM)

    def own(h):
        return H[h] * 2 + c

    def other(h):
        return H[h] * 2 + (1 - c)

    def take(h, p, onward=None, first=False, to_end=False):
        if first:
            first_copy(own(h), p, mate).wait_recv()
        else:
            mate_copy(own(h), p, to_end).wait_recv()
        if onward is not None:
            onward(own(h), p).start()
        mate_copy(own(h), p, to_end).start()

    def mate_take(h, pieces, to_end=False):
        for p in pieces:
            mate_copy(other(h), p, to_end).wait_recv()

    def take_end(h, p):
        take(h, p, to_end=True)

    def mate_take_end(h, pieces):
        mate_take(h, pieces, True)

    def tile_copy(side, j, core, block, slot):
        return pltpu.make_async_remote_copy(
            src_ref=tile_send.at[side, j, core, pl.ds(0, SR), :],
            dst_ref=tile_recv.at[block, pl.ds(0, SR), pl.ds(pl.multiple_of(slot * 128, 128), 128)],
            send_sem=t_send, recv_sem=t_recv.at[block],
            device_id=(j, 6 * side + core), device_id_type=MESH)

    def make_hot():
        for side, skip in ((0, jnp.where(b == 5, 0, pad)), (1, jnp.where(b == 2, pad, 0))):
            shift = (lax.broadcasted_iota(jnp.int32, (SR, 128), 0)
                     == lax.broadcasted_iota(jnp.int32, (SR, 128), 1) + skip)
            shift_ref[side] = jnp.where(shift, 1.0, 0.0).astype(jnp.bfloat16)
        row = lax.broadcasted_iota(jnp.int32, (512, WM), 0)
        slot = row // 128
        shifted = slot < jnp.where(upper, 1, 3)
        lane = half - mid_lane + slot * (share - 128) + row + jnp.where(shifted, pad, 0)
        hot = lax.broadcasted_iota(jnp.int32, (512, WM), 1) == lane
        place_ref[...] = jnp.where(hot, 1.0, 0.0).astype(jnp.bfloat16)
        for side, slot in ((0, 0), (3, 3)):
            @pl.when(q == side)
            def _():
                tile_recv[:, :, slot * 128:slot * 128 + 128] = jnp.zeros((L, SP, 128), jnp.bfloat16)

    def add_rows(j, place):
        rows = pl.ds(pl.multiple_of(j * SP, SP), SP)
        for acc, begin in ((acc_lo, 0), (acc_hi, hi_lane)):
            value = acc[rows, :]
            for core in range(2):
                k = place * 2 + core
                value = value + lax.dot_general(shr[k, j], zbuf[k, begin:begin + WS, :], NT,
                                                preferred_element_type=jnp.float32)
            acc[rows, :] = value

    def turn_tiles(j):
        rows = pl.ds(pl.multiple_of(j * SP, SP), SP)
        for side, acc in ((0, acc_lo), (1, acc_hi)):
            turned = lax.dot_general((acc[rows, :][:SR] / total).astype(jnp.bfloat16), shift_ref[side], TN,
                                     preferred_element_type=jnp.float32)
            for core in range(2):
                at = (WS - half if side else 0) + core * share
                tile_send[side, j, core, :share, :] = turned[at:at + share].astype(jnp.bfloat16)

    def tile_copies(j, act):
        for side, skipped in ((0, 2), (1, 5)):
            @pl.when(b != skipped)
            def _():
                for core in range(2):
                    act(tile_copy(side, j, core, l, b - 2))

    def start_tiles(j):
        tile_copies(j, lambda copy: copy.start())

    def wait_tile(block):
        part = tile_recv.at[block, pl.ds(0, SR), pl.ds(0, 384)]
        pltpu.make_async_remote_copy(
            src_ref=part, dst_ref=part, send_sem=t_send, recv_sem=t_recv.at[block],
            device_id=(l, b), device_id_type=MESH).wait_recv()

    normalise(start[D], size[D])

    @pl.when(inner)
    def _():
        first_copy(b, D, out_nbr).start()

    normalise(start[F], size[F])

    first_copy(b, F, in_nbr).start()
    normalise(low, high - low)

    @pl.when(inner)
    def _():
        for p in (M2, M1, C):
            z_copy(b, p, own_in, in_nbr).start()
        for p in (F, C, N2):
            z_copy(b, p, own_out, out_nbr, 0, True).start()

    @pl.when(outer)
    def _():
        for p in (M2, M1, C, D, N2, N1):
            z_copy(b, p, own_in, in_nbr).start()
    mate_own(b).start()
    extract_one(b)
    make_hot()
    mate_own(mate).wait_recv()
    extract_one(mate)

    @pl.when(inner)
    def _():
        unpack(0, own(1), D)
        unpack(1, own(3), F)
        take(1, D, send_out, True)
        take(3, F, send_in, True)
        pass_on(q)
        take(1, N2, send_out)
        take(3, M2, send_in)
        take(1, N1)
        take(3, M1, send_in)
        take(1, C, send_out)
        take(3, C, send_in)
        z_copy(b, D, own_in, in_nbr).start()
        mate_take(1, (D, N2, N1, C))
        extract(H[1])
        take(0, D, send_out)
        take(3, D, send_in)

    @pl.when(outer)
    def _():
        unpack(0, own(2), D)
        take(2, D, None, True)
        mate_take(2, (D,))
        extract(H[2])
        pass_on(q)
        take_end(2, F)
        take_end(2, C)
        take_end(2, N2)
        pass_on(H[2])
        take(1, D)
        mate_take(1, (D,))
        extract(H[1])
        mate_take_end(2, (F, C, N2))
    wait_diag(q)
    acc_lo[...] = product(q, 0, WS)
    acc_hi[...] = product(q, hi_lane, WS)
    acc_mid[...] = product(q, mid_lane, WM)

    second, third = jnp.where(inner, H[1], H[2]), jnp.where(inner, H[3], H[1])

    @pl.when(inner)
    def _():
        pass_on(H[1])
        take(0, N2, send_out)
        take(0, N1)
        take(0, C, send_out)
        mate_take(0, (D, N2, N1, C))
        extract(H[0])
        take(3, N2)
        take(3, N1)
        mate_take(3, (C, D, N2, N1))
        extract(H[3])
        take(1, F, send_out)
        mate_take(1, (F,))

    @pl.when(outer)
    def _():
        take_end(1, N2)
        take_end(1, C)
        pass_on(H[1])
    wait_diag(second)
    add_sides(second)

    @pl.when(outer)
    def _():
        take(0, D)
        mate_take(0, (D,))
        extract(H[0])
        take_end(0, N2)
        take_end(0, C)
        take_end(1, F)
        mate_take_end(1, (N2, C, F))
        wait_diag(H[1])
        add_sides(H[1])
    @pl.when(inner)
    def _():
        mate_take(3, (F, M1, M2))
        add_rows(l, H[3])
    pass_on(H[0])

    @pl.when(inner)
    def _():
        take(0, F, send_out)
        for p in (N1, N2):
            z_copy(b, p, own_in, in_nbr).start()
        mate_take(0, (F,))
        add_rows(l, H[0])
        turn_tiles(l)
        start_tiles(l)

        @pl.loop(0, 2)
        def _(n):
            add_rows(jnp.where(n == 0, lx, ly), H[0])
        pass_on(H[3])

        @pl.loop(0, 2)
        def _(n):
            j = jnp.where(n == 0, lx, ly)
            add_rows(j, H[3])
            turn_tiles(j)
            start_tiles(j)
        for p in (N1, N2):
            send_in(own(3), p).start()
        wait_diag(H[0])
        add_rows(ld, H[0])
        wait_diag(H[3])
        add_rows(ld, H[3])
        turn_tiles(ld)
        start_tiles(ld)
        for p in (M1, M2):
            take(1, p)
        mate_take(1, (M1, M2))
    add_middle(second)
    add_middle(third)

    def put(lanes, acc, begin=0):
        for j in range(L):
            part = acc[j * SP:j * SP + share, :][:, begin:begin + lanes.stop - lanes.start]
            o_ref[:, j, lanes] = part / total

    @pl.when(inner)
    def _():
        for p in (M1, M2):
            take(0, p)
        put(slice(0, mid_lane), acc_lo)
        put(slice(mid_lane + WM, R), acc_hi, mid_lane + WM - hi_lane)
        mate_take(0, (M1, M2))
        add_middle(H[0])
        put(slice(mid_lane, mid_lane + WM), acc_mid)

    lanes_lo = mid_lane, up_to(R // 2 + pad, 128)
    lanes_hi = (R // 2 - pad) // 128 * 128, mid_lane + WM

    @pl.when(outer)
    def _():
        mate_take_end(0, (N2, C))
        wait_diag(H[0])
        for end, acc, begin, (first_mid, last_mid) in ((0, acc_lo, 0, lanes_lo), (3, acc_hi, hi_lane, lanes_hi)):
            @pl.when(q == end)
            def _():
                acc[...] += product(H[0], begin, WS)
                inner_lanes = slice(first_mid - mid_lane, last_mid - mid_lane)
                acc_mid[:, inner_lanes] += product(H[0], first_mid, last_mid - first_mid)
                put(slice(first_mid, last_mid), acc_mid, first_mid - mid_lane)
                if end:
                    put(slice(last_mid, R), acc, last_mid - hi_lane)
                else:
                    put(slice(0, first_mid), acc)
        take(0, F)
        mate_take(0, (F,))
        for end, acc, begin in ((3, acc_lo, 0), (0, acc_hi, hi_lane)):
            @pl.when(q == end)
            def _():
                acc[...] += product(H[0], begin, WS)
                put(slice(begin, begin + WS), acc)
        place = lax.broadcasted_iota(jnp.int32, (share, WM), 1) + mid_lane
        low_first = half + pad + jnp.where(upper, 0, share)
        high_first = R // 2 + jnp.where(upper, 0, pad)
        inside = ((place >= low_first) & (place < low_first + jnp.where(upper, 256, 128))
                  | (place >= high_first) & (place < high_first + jnp.where(upper, 128, 256)))
        for d in (l, lx, ly, ld):
            wait_tile(d)
            placed = lax.dot_general(tile_recv[d], place_ref[...], (((1,), (0,)), ((), ())),
                                     preferred_element_type=jnp.float32)[:share]
            middle = pl.ds(mid_lane, WM)
            o_ref[:, d, middle] = jnp.where(inside, placed, o_ref[:, d, middle])

    all_stats.wait_send()
    mate_own(b).wait_send()

    def sent(part, sem):
        pltpu.make_async_remote_copy(
            src_ref=part, dst_ref=part, send_sem=sem, recv_sem=st_recv,
            device_id=(l, b), device_id_type=MESH).wait_send()

    @pl.when(inner)
    def _():
        sent(zbuf.at[0, pl.ds(0, size[F] + narrow + size[N2]), :], own_out)
        sent(zbuf.at[pl.ds(0, 2), pl.ds(0, size[D] - RAW), :], first_send)
        sent(raw, raw_send)
        sent(zbuf.at[pl.ds(0, 2), pl.ds(0, far), :], out_send)
        sent(zbuf.at[0], in_send)
        sent(zbuf.at[pl.ds(0, 3)], mate_send)
        for skipped in (True, False):
            @pl.when(((b == 2) | (b == 5)) == skipped)
            def _():
                sides = 1 if skipped else 2
                sent(tile_send.at[pl.ds(0, sides), :, :, pl.ds(0, SR), :], t_send)

    @pl.when(outer)
    def _():
        sent(zbuf.at[0, pl.ds(0, size[D] - RAW), :], first_send)
        sent(raw.at[0], raw_send)
        sent(zbuf.at[pl.ds(0, 3), pl.ds(0, far), :], mate_send)

    sent(zbuf.at[0, pl.ds(0, R - size[D]), :], own_in)
    sent(shr.at[pl.ds(0, L), :, pl.ds(0, SR), :], shr_send)
    sent(shr.at[pl.ds(0, B // L), :, pl.ds(0, SR), :], diag_send)


def line_call(L, B, series):
    R, T = series.shape
    share = R // B
    SP = up_to(share, 16)
    pad = share - 128
    high = (3 * 2 * share - pad) // 16 * 16
    WS = R - high
    mid_lane = WS // 128 * 128
    WM = up_to(R // 2 + pad + 256, 128) - mid_lane
    vmem = pl.BlockSpec(memory_space=pltpu.VMEM)
    dma = pltpu.SemaphoreType.DMA
    return pl.pallas_call(
        functools.partial(line_kernel, L, B),
        out_shape=jax.ShapeDtypeStruct((share, L, R), jnp.float32),
        in_specs=[pl.BlockSpec(memory_space=pltpu.HBM)],
        out_specs=vmem,
        scratch_shapes=[
            pltpu.VMEM((B, R, T), jnp.bfloat16),
            pltpu.VMEM((B, L, SP, T), jnp.bfloat16),
            pltpu.VMEM((L * SP, WS), jnp.float32),
            pltpu.VMEM((L * SP, WS), jnp.float32),
            pltpu.VMEM((L * SP, WM), jnp.float32),
            pltpu.VMEM((2, L, 2, SP, 128), jnp.bfloat16),
            pltpu.VMEM((L, SP, 512), jnp.bfloat16),
            pltpu.VMEM((2, up_to(share, 8), 128), jnp.bfloat16),
            pltpu.VMEM((512, WM), jnp.bfloat16),
            pltpu.VMEM((R, 128), jnp.float32),
            pltpu.VMEM((B, 2, R), jnp.float32),
            pltpu.VMEM((R, T), jnp.float32),
            pltpu.VMEM((2, (R - high) * 7 // 256 * 16, T), jnp.float32),
            dma((B, 7)), dma, dma, dma, dma, dma, dma, dma, dma((2,)), dma,
            dma((B // 2, 2)), dma, dma((B // 2,)), dma, dma((L,)), dma,
            dma, dma, dma((R // largest_tile(R, 528),)),
        ],
        compiler_params=pltpu.CompilerParams(
            collective_id=0, has_side_effects=True, vmem_limit_bytes=34 * 1024 * 1024),
    )(pltpu.with_memory_space_constraint(series, pltpu.HBM)).transpose(1, 0, 2)


def solution(mesh):
    L, B = mesh.shape["loop"], mesh.shape["bulk"]

    def on_device(series):
        R, T = series.shape
        share = R // B
        if L == 4 and B == 8 and R % 16 == 0 and T % 128 == 0 and 128 <= share <= 144:
            return line_call(L, B, series)
        SP = up_to(share, 16)
        pieces = 3
        vmem = pl.BlockSpec(memory_space=pltpu.VMEM)
        dma = pltpu.SemaphoreType.DMA
        return pl.pallas_call(
            functools.partial(kernel, L, B, pieces),
            out_shape=jax.ShapeDtypeStruct((share, L, R), jnp.float32),
            in_specs=[pl.BlockSpec(memory_space=pltpu.HBM)],
            out_specs=vmem,
            scratch_shapes=[
                pltpu.VMEM((B, R, T), jnp.bfloat16),
                pltpu.VMEM((B, L, SP, T), jnp.bfloat16),
                pltpu.VMEM((L * SP, R), jnp.float32),
                pltpu.VMEM((R, 128), jnp.float32),
                pltpu.VMEM((B, 2, R), jnp.float32),
                pltpu.VMEM((R, T), jnp.float32),
                dma((B, pieces)), dma((B, pieces)), dma((B, pieces)), dma((B, pieces)),
                dma((B, L)), dma((B, L)), dma((B,)), dma((B,)), dma((R // largest_tile(R, 128),)),
            ],
            compiler_params=pltpu.CompilerParams(
                collective_id=0, has_side_effects=True, vmem_limit_bytes=26 * 1024 * 1024),
        )(pltpu.with_memory_space_constraint(series, pltpu.HBM)).transpose(1, 0, 2)

    return jax.shard_map(
        on_device, mesh=mesh, in_specs=(P("loop", "bulk"),),
        out_specs=P(None, "bulk", "loop"), check_vma=False)
```
